256 devices in a mesh: slab: 4 (over x), space: 64 (over y, z, core).
Axes of the slice: x: 4, y: 4, z: 8, core: 2. Of those that a mesh axis runs over, the one named last changes fastest.
Arguments:
- dipoles: float32 [3, 131072], P(None, ('slab', 'space')), may hold values from -3 to 3
- residual: float32 [3, 131072], P(None, ('slab', 'space')), may hold values from -12 to 12, as said below
- cells: int32 [3, 131072], P(None, ('slab', 'space')), may hold values from 0 to 255, as said below
- fraction: float32 [3, 131072], P(None, ('slab', 'space')), may hold values from 0.25 to 0.75
- polarizability: float32 [131072], P(('slab', 'space')), may hold values from 0.3 to 2.5
- tile_order: int32 [256, 512], P(('slab', 'space')), may hold values from 0 to 511, as said below
- send_tiles: int32 [256, 2], P(('slab', 'space')), may hold values from 0 to 3, as said below
- tile_lists: int32 [256, 4, 8], P(('slab', 'space')), may hold values from 0 to 19, as said below
- tile_counts: int32 [256, 4], P(('slab', 'space')), may hold values from 1 to 8, as said below
Outputs:
- dipoles_next: float32 [3, 131072], P(None, ('slab', 'space'))
- residual_next: float32 [3, 131072], P(None, ('slab', 'space'))
- direction: float32 [3, 131072], P(None, ('slab', 'space'))
The draws below stay inside these ranges and needn't reach their ends.
Inputs may be any that keep to these rules, and one draw needn't show every extreme that they name: The residual's entries stay within the stated range. `cells`: the first component is below 64 and the second below 4; no two atoms of one device share a cell. `tile_order`: each device's row holds every number of 0 to 511 once. `send_tiles`: the 2 tile numbers of each device are distinct. `tile_lists`: entry 0 of the list of tile t is t itself; the 8 entries of one list are distinct. `tile_counts`: on some devices every tile has 8 live entries.
All inputs are finite; a program needn't handle non-finite values.
Results may differ from the reference program's by a relative error of at most 0.0003.
Values sent between devices are 32-bit elements; how exact they have to be, the bound alone decides.
No kernel may reach another device: no remote copies, remote signals or barrier semaphores. Data moves between devices by JAX's collectives and lax.ppermute only.
A program may use at most 64 MiB of HBM per device.

```python
import math
import jax
import jax.numpy as jnp
from jax import lax

G = 256
TILE = 128
TILES_DEV = 4
MAXN = 8
XL = 64
YL = 4
SEND = 2
POOL = 20
ATOM_DEV = 512
ATOMS = 131072
N_SLAB = 4
N_SPACE = 64
DEVICES = 256


def tile_layout():
    aspect_ratio = max(G // XL, 1)
    tiles_across = 1
    for doubling in range(6):
        candidate = tiles_across * 2
        if TILES_DEV % candidate == 0 and candidate * candidate * aspect_ratio <= TILES_DEV:
            tiles_across = candidate
    tiles_depth = TILES_DEV // tiles_across
    return (tiles_depth, XL // tiles_across, G // tiles_depth)


def atom_layout(key):
    tiles_depth, box_width, box_depth = tile_layout()
    box_cells = box_width * YL * box_depth
    device_keys = jax.random.split(jax.random.fold_in(key, 101), DEVICES)
    tile_ids = jnp.arange(TILES_DEV, dtype=jnp.int32)
    anchor_x = tile_ids // tiles_depth * box_width
    anchor_z = tile_ids % tiles_depth * box_depth

    def one_tile(tile_key):
        return jax.random.permutation(tile_key, box_cells)[:TILE]

    def one_device(device_key):
        order_key, place_key = jax.random.split(device_key)
        ordering = jax.random.permutation(order_key, ATOM_DEV).astype(jnp.int32)
        picked = jax.vmap(one_tile)(jax.random.split(place_key, TILES_DEV)).astype(jnp.int32)
        cell_x = anchor_x[:, None] + picked // (YL * box_depth)
        cell_y = picked // box_depth % YL
        cell_z = anchor_z[:, None] + picked % box_depth
        ordered = jnp.stack([cell_x, cell_y, cell_z]).reshape(3, ATOM_DEV)
        placed = jnp.zeros((3, ATOM_DEV), jnp.int32).at[:, ordering].set(ordered)
        return (ordering, placed)
    orderings, placed = jax.vmap(one_device)(device_keys)
    return (orderings.astype(jnp.int32), jnp.transpose(placed, (1, 0, 2)).reshape(3, ATOMS).astype(jnp.int32))


def shared_tiles(key):
    device_keys = jax.random.split(jax.random.fold_in(key, 202), DEVICES)

    def one_device(device_key):
        return jax.random.permutation(device_key, TILES_DEV)[:SEND]
    return jax.vmap(one_device)(device_keys).astype(jnp.int32)


def draw_residual(key, part):
    device_rank = (jnp.arange(ATOMS) // ATOM_DEV).astype(jnp.float32) / max(DEVICES - 1, 1)
    rising = 1.0 + 2.0 * device_rank
    samples = jnp.clip(jax.random.normal(key, (3, ATOMS), jnp.float32), -4.0, 4.0)
    return samples * rising[None]


def draw_cells(key, part):
    return atom_layout(key)[1]


def draw_tile_order(key, part):
    return atom_layout(key)[0]


def draw_send_tiles(key, part):
    return shared_tiles(key)


def draw_tile_lists(key, part):
    tiles_depth, box_width, box_depth = tile_layout()
    sending = shared_tiles(key)
    count_slab = G // XL
    count_space = G // YL
    device_ids = jnp.arange(DEVICES, dtype=jnp.int32)
    slab_ids = device_ids // count_space
    space_ids = device_ids % count_space
    offset_a = jnp.array([0, 0, 0, 1, 1, 2, 2, 2], jnp.int32)
    offset_b = jnp.array([0, 1, 2, 0, 2, 0, 1, 2], jnp.int32)
    beside_all = (slab_ids[:, None] + offset_a[None] - 1 + count_slab) % count_slab * count_space + (space_ids[:, None] + offset_b[None] - 1 + count_space) % count_space
    remote = sending[beside_all].reshape(DEVICES, 8 * SEND)
    own_tiles = jnp.broadcast_to(jnp.arange(TILES_DEV, dtype=jnp.int32)[None], (DEVICES, TILES_DEV))
    pool_tiles = jnp.concatenate([own_tiles, remote], 1)
    shift_x = jnp.concatenate([jnp.zeros((TILES_DEV,), jnp.int32), jnp.repeat(offset_a - 1, SEND)]) * XL
    low_x = pool_tiles // tiles_depth * box_width + shift_x[None]
    low_z = pool_tiles % tiles_depth * box_depth
    apart_x = jnp.abs(low_x[:, None, :] - low_x[:, :TILES_DEV, None])
    gap_x = jnp.maximum(apart_x - box_width, 0)
    apart_z = (low_z[:, None, :] - low_z[:, :TILES_DEV, None]) % G
    apart_z = jnp.minimum(apart_z, G - apart_z)
    gap_z = jnp.maximum(apart_z - box_depth, 0)
    rank_keys = jax.random.split(jax.random.fold_in(key, 303), DEVICES * TILES_DEV)

    def one_rank(rank_key):
        return jax.random.permutation(rank_key, POOL)
    ranks = jax.vmap(one_rank)(rank_keys).reshape(DEVICES, TILES_DEV, POOL).astype(jnp.int32)
    scores = (gap_x * gap_x + gap_z * gap_z) * POOL + ranks
    itself = jnp.arange(POOL, dtype=jnp.int32)[None, None, :] == jnp.arange(TILES_DEV, dtype=jnp.int32)[None, :, None]
    scores = jnp.where(itself, -1, scores)
    ordering = jnp.argsort(scores, axis=2, stable=True)
    return ordering[:, :, :MAXN].astype(jnp.int32)


def draw_tile_counts(key, part):
    first_key, second_key = jax.random.split(jax.random.fold_in(key, 5))
    heavy = jax.random.randint(first_key, (DEVICES, 1), 0, 8) == 0
    heavy = heavy.at[0].set(True)
    light = jax.random.randint(second_key, (DEVICES, TILES_DEV), 1, MAXN // 2 + 1)
    return jnp.where(heavy, MAXN, light).astype(jnp.int32)


def shard_levels(rng, dims, shards, smallest, largest):
    gain = 1.0
    for position, blocks in shards:
        heights = jax.random.uniform(jax.random.fold_in(jax.random.fold_in(rng, 6), position), (blocks,), jnp.float32, smallest / len(shards), largest / len(shards))
        gain = gain * jnp.repeat(jnp.exp(heights), dims[position] // blocks).reshape((-1,) + (1,) * (len(dims) - 1 - position))
    return gain


def centred(rng, extent, deviation, most, pieces=(), held_as=jnp.bfloat16):
    drawn = jax.random.normal(rng, extent, jnp.float32) * deviation
    if len(pieces) > 0:
        drawn = shard_levels(rng, extent, pieces, -0.22, 0.18) * drawn
    return jnp.clip(drawn, min=-most, max=most).astype(held_as)


def setup_inputs(seed: int = 0) -> dict:
    streams_of = jax.random.split(jax.random.key(seed), 10)
    return {
        "dipoles": centred(streams_of[0], (3, ATOMS), 0.5, 3.0, ((1, 256),), jnp.float32),
        "residual": draw_residual(jax.random.fold_in(streams_of[9], 71), 0),
        "cells": draw_cells(jax.random.fold_in(streams_of[9], 71), 0),
        "fraction": jnp.clip(0.25 + 0.5 * jax.random.uniform(streams_of[3], (3, ATOMS), jnp.float32) ** shard_levels(streams_of[3], (3, ATOMS), ((1, 256),), -0.2, 0.2), 0.25, 0.75),
        "polarizability": jnp.clip(jnp.exp(math.log(2.5) - 2.1202635 * jax.random.uniform(streams_of[4], (ATOMS,), jnp.float32) ** shard_levels(streams_of[4], (ATOMS,), ((0, 256),), -0.2, 0.2)), 0.3, 2.5),
        "tile_order": draw_tile_order(jax.random.fold_in(streams_of[9], 71), 0),
        "send_tiles": draw_send_tiles(jax.random.fold_in(streams_of[9], 71), 0),
        "tile_lists": draw_tile_lists(jax.random.fold_in(streams_of[9], 71), 0),
        "tile_counts": draw_tile_counts(jax.random.fold_in(streams_of[9], 71), 0),
    }


EWALD_BETA = 0.4
THOLE_SCALE = 0.39
SELF_FIELD = 4.0 * EWALD_BETA ** 3 / (3.0 * math.sqrt(math.pi))

def spline(fraction):
    centre_arg = fraction - 0.5
    lower_one = fraction + 0.5
    upper_one = 1.5 - fraction
    lower_two = fraction + 1.5
    upper_two = 2.5 - fraction

    def middle(amount):
        return (55.0 + 20.0 * amount - 120.0 * amount ** 2 + 80.0 * amount ** 3 - 16.0 * amount ** 4) / 96.0

    def middle_slope(amount):
        return (20.0 - 240.0 * amount + 240.0 * amount ** 2 - 64.0 * amount ** 3) / 96.0

    def outer_piece(amount):
        return (5.0 - 2.0 * amount) ** 4 / 384.0

    def outer_slope(amount):
        return -(5.0 - 2.0 * amount) ** 3 / 48.0
    centre = 115.0 / 192.0 - 0.625 * centre_arg ** 2 + 0.25 * centre_arg ** 4
    centre_slope = -1.25 * centre_arg + centre_arg ** 3
    weights = jnp.stack([outer_piece(lower_two), middle(lower_one), centre, middle(upper_one), outer_piece(upper_two)])
    slopes = jnp.stack([outer_slope(lower_two), middle_slope(lower_one), centre_slope, -middle_slope(upper_one), -outer_slope(upper_two)])
    return (weights, slopes)

def wave_factors(freq_ids):
    wrapped = jnp.where(freq_ids > G // 2, freq_ids - G, freq_ids).astype(jnp.float32) / G
    angles = 2.0 * math.pi / G * freq_ids.astype(jnp.float32)
    modulus = 115.0 / 192.0 + 19.0 / 48.0 * jnp.cos(angles) + 1.0 / 192.0 * jnp.cos(2.0 * angles)
    return (wrapped * wrapped, jnp.exp(-(math.pi / EWALD_BETA) ** 2 * wrapped * wrapped) / (modulus * modulus))

def multiplier(freq_x, freq_y, freq_z):
    square_x, factor_x = wave_factors(freq_x)
    square_y, factor_y = wave_factors(freq_y)
    square_z, factor_z = wave_factors(freq_z)
    square_sum = square_x + square_y + square_z
    anchor = ((freq_x == 0) & (freq_y == 0) & (freq_z == 0)).astype(jnp.float32)
    return (1.0 - anchor) * factor_x * factor_y * factor_z / (math.pi * float(G) ** 3 * (square_sum + anchor))

def short_field(own_geometry, pool_geometry, pool_dipoles, neighbour_ids, neighbour_counts):
    count_tiles = own_geometry.shape[0]
    tile_width = own_geometry.shape[2]
    slots = neighbour_ids.shape[1]
    tile_ids = jnp.arange(count_tiles, dtype=jnp.int32)
    diagonal = (jnp.arange(tile_width)[:, None] == jnp.arange(tile_width)[None, :]).astype(jnp.float32)
    slot_ids = jnp.arange(slots, dtype=jnp.int32)

    def per_tile(inputs):
        tile_id, own_tile, picked, live_count = inputs
        geometry = pool_geometry[picked]
        dipole = pool_dipoles[picked]
        displacement = geometry[:, :3, None, :] - own_tile[None, :3, :, None]
        half_box = 0.5 * G
        depth_z = displacement[:, 2]
        depth_z = jnp.where(depth_z > half_box, depth_z - G, jnp.where(depth_z < -half_box, depth_z + G, depth_z))
        displacement = jnp.stack([displacement[:, 0], displacement[:, 1], depth_z], 1)
        itself = (picked == tile_id).astype(jnp.float32)[:, None, None] * diagonal[None]
        square = lax.optimization_barrier(jnp.sum(displacement * displacement, 1)) + itself
        distance = jnp.sqrt(square)
        inverse = 1.0 / distance
        inverse_sq = inverse * inverse
        gauss = jnp.exp(-EWALD_BETA ** 2 * square)
        bare_zero = lax.erfc(EWALD_BETA * distance) * inverse
        bare_one = (bare_zero + 2.0 * EWALD_BETA / math.sqrt(math.pi) * gauss) * inverse_sq
        bare_two = (3.0 * bare_one + 4.0 * EWALD_BETA ** 3 / math.sqrt(math.pi) * gauss) * inverse_sq
        damping = THOLE_SCALE * square * distance * lax.rsqrt(own_tile[3][None, :, None] * geometry[:, 3][:, None, :])
        decay = jnp.exp(-damping)
        rank_three = bare_one - decay * inverse * inverse_sq
        rank_five = bare_two - 3.0 * (1.0 + damping) * decay * inverse * inverse_sq * inverse_sq
        weight_pair = (slot_ids < live_count).astype(jnp.float32)[:, None, None] * (1.0 - itself)
        projection = lax.optimization_barrier(jnp.sum(displacement * dipole[:, :, None, :], 1))
        terms = rank_five[:, None] * displacement * projection[:, None] - rank_three[:, None] * dipole[:, :, None, :]
        return lax.optimization_barrier(jnp.sum(weight_pair[:, None] * terms, (0, 3)))
    return lax.map(per_tile, (tile_ids, own_geometry, neighbour_ids, neighbour_counts))

def tiled(values, tile_order):
    channels = values.shape[0]
    blocks = values.reshape(channels, DEVICES, ATOM_DEV).transpose(1, 0, 2)
    ordered = jnp.take_along_axis(blocks, tile_order[:, None, :], axis=2)
    return ordered.reshape(DEVICES, channels, TILES_DEV, TILE).transpose(0, 2, 1, 3)

def untiled(tile_values, tile_order):
    channels = tile_values.shape[2]
    ordered = tile_values.transpose(0, 2, 1, 3).reshape(DEVICES, channels, ATOM_DEV)

    def restore(row_values, row_order):
        return jnp.zeros_like(row_values).at[:, row_order].set(row_values)
    blocks = jax.vmap(restore)(ordered, tile_order)
    return blocks.transpose(1, 0, 2).reshape(channels, ATOMS)

def recip_field(direction, cells, fraction):
    device_ids = jnp.arange(ATOMS, dtype=jnp.int32) // ATOM_DEV
    base_x = cells[0] + device_ids // N_SPACE * XL
    base_y = cells[1] + device_ids % N_SPACE * YL
    base_z = cells[2]
    weight_x, slope_x = spline(fraction[0])
    weight_y, slope_y = spline(fraction[1])
    weight_z, slope_z = spline(fraction[2])
    points_z = (base_z[None] + jnp.arange(5, dtype=jnp.int32)[:, None] - 2 + G) % G
    density = jnp.zeros((G, G, G), jnp.float32)
    for step_x in range(5):
        for step_y in range(5):
            points_x = (base_x + step_x - 2 + G) % G
            points_y = (base_y + step_y - 2 + G) % G
            values = (direction[0] * slope_x[step_x] * weight_y[step_y])[None] * weight_z
            values = values + (direction[1] * weight_x[step_x] * slope_y[step_y])[None] * weight_z
            values = values + (direction[2] * weight_x[step_x] * weight_y[step_y])[None] * slope_z
            density = density.at[points_x[None], points_y[None], points_z].add(values)
    freq_ids = jnp.arange(G, dtype=jnp.int32)
    factor = multiplier(freq_ids[:, None, None], freq_ids[None, :, None], freq_ids[None, None, :])
    potential = jnp.real(jnp.fft.ifftn(factor * jnp.fft.fftn(density))) * float(G) ** 3
    field_x = jnp.zeros((ATOMS,), potential.dtype)
    field_y = jnp.zeros((ATOMS,), potential.dtype)
    field_z = jnp.zeros((ATOMS,), potential.dtype)
    for step_x in range(5):
        for step_y in range(5):
            points_x = (base_x + step_x - 2 + G) % G
            points_y = (base_y + step_y - 2 + G) % G
            values = potential[points_x[None], points_y[None], points_z]
            field_x = field_x - lax.optimization_barrier(jnp.sum((slope_x[step_x] * weight_y[step_y])[None] * weight_z * values, 0))
            field_y = field_y - lax.optimization_barrier(jnp.sum((weight_x[step_x] * slope_y[step_y])[None] * weight_z * values, 0))
            field_z = field_z - lax.optimization_barrier(jnp.sum((weight_x[step_x] * weight_y[step_y])[None] * slope_z * values, 0))
    return jnp.stack([field_x, field_y, field_z])

def reference(dipoles, residual, cells, fraction, polarizability, tile_order, send_tiles, tile_lists, tile_counts):
    positions = cells.astype(jnp.float32) + fraction
    geometry_tiles = tiled(jnp.concatenate([positions, polarizability[None]], 0), tile_order)
    device_ids = jnp.arange(DEVICES, dtype=jnp.int32)
    slab_ids = device_ids // N_SPACE
    space_ids = device_ids % N_SPACE
    beside_all = [(step_a, step_b) for step_a in range(3) for step_b in range(3) if (step_a, step_b) != (1, 1)]
    neighbours = jnp.stack([(slab_ids + step_a - 1 + N_SLAB) % N_SLAB * N_SPACE + (space_ids + step_b - 1 + N_SPACE) % N_SPACE for step_a, step_b in beside_all], 1)
    shifts = jnp.array([[float((step_a - 1) * XL), float((step_b - 1) * YL), 0.0, 0.0] for step_a, step_b in beside_all], jnp.float32)
    sent_geometry = jnp.take_along_axis(geometry_tiles, send_tiles[:, :, None, None], axis=1)

    def short(values):
        dipole_tiles = tiled(values, tile_order)
        sent_dipoles = jnp.take_along_axis(dipole_tiles, send_tiles[:, :, None, None], axis=1)

        def per_device(device):
            near = neighbours[device]
            pool_geometry = jnp.concatenate([geometry_tiles[device], (sent_geometry[near] + shifts[:, None, :, None]).reshape(8 * SEND, 4, TILE)], 0)
            pool_dipoles = jnp.concatenate([dipole_tiles[device], sent_dipoles[near].reshape(8 * SEND, 3, TILE)], 0)
            return short_field(geometry_tiles[device], pool_geometry, pool_dipoles, tile_lists[device], tile_counts[device])
        return untiled(lax.map(per_device, device_ids), tile_order)
    alphas = polarizability[None]
    search = alphas * residual
    for sweep_id in range(3):
        search = alphas * (residual + short(search))
    direction = search
    search_dot = jnp.sum(residual * direction)
    applied = direction / alphas - short(direction) - SELF_FIELD * direction - recip_field(direction, cells, fraction)
    curve_total = jnp.sum(direction * applied)
    step_size = search_dot / curve_total
    return (dipoles + step_size * direction, residual - step_size * applied, direction)
```

```python
import functools
import math

import jax
import jax.numpy as jnp
import ml_dtypes
import numpy as np
from jax import lax
from jax.experimental import pallas as pl
from jax.experimental.pallas import tpu as pltpu
from jax.sharding import PartitionSpec as P

G = 256
TILE = 128
BOTH = ("slab", "space")
BETA = 0.4
THOLE = 0.39
ROOT_PI = math.sqrt(math.pi)
SELF_FIELD = 4.0 * BETA**3 / (3.0 * ROOT_PI)
F32 = jnp.float32
BF16 = jnp.bfloat16
SCALED_ERFC_T = 0.45
SCALED_ERFC = (
    0.25388532876968384,
    0.25388309359550476,
    0.22827406227588654,
    0.17522020637989044,
    0.1201537474989891,
    -0.023065825924277306,
    0.14381752908229828,
    -0.3022053837776184,
    0.19167575240135193,
    -0.04163854941725731,
)
NT = (((1,), (1,)), ((), ()))
NN = (((1,), (0,)), ((), ()))
TN = (((0,), (0,)), ((), ()))
VMEM_LIMIT = 48 * 1024 * 1024


def halves(values):
    high = values.astype(BF16)
    return (high, (values - high.astype(F32)).astype(BF16))


def product(left, right, dims):
    def one(a, b):
        return lax.dot_general(a, b, dims, preferred_element_type=F32)

    return one(left[0], right[0]) + (one(left[0], right[1]) + one(left[1], right[0]))


def thirds(values):
    high = values.astype(BF16).astype(F32)
    rest = values - high
    middle = rest.astype(BF16).astype(F32)
    return jnp.concatenate([high, middle, rest - middle], 0).astype(BF16)


def selected(values, one_hot, dims):
    rows = values.shape[0]
    picked = lax.dot_general(thirds(values), one_hot, dims, preferred_element_type=F32)
    return picked[:rows] + (picked[rows : 2 * rows] + picked[2 * rows :])


def order_matrix(order_row, count):
    ids = lax.broadcasted_iota(jnp.int32, (count, count), 0)
    return jnp.where(ids == order_row, 1.0, 0.0).astype(BF16)


COUNTS_AT = 32
SEND_AT = 36
PARITY_AT = 38


def tile_at(meta, place):
    first, second = (meta[SEND_AT], meta[SEND_AT + 1])
    if place == 0:
        return first
    if place == 1:
        return second
    third = jnp.where(
        (first != 0) & (second != 0), 0, jnp.where((first != 1) & (second != 1), 1, 2)
    )
    return third if place == 2 else 6 - first - second - third


def pool_slot(meta, entry):
    remote = entry - 4
    pair = remote // 2
    pair = pair + jnp.where(pair >= 4, 1, 0)
    along = jnp.where(pair >= 3, 1, 0) + jnp.where(pair >= 6, 1, 0)
    across = pair - 3 * along
    inner_side = jnp.where(meta[PARITY_AT] == 0, 2, 0)
    base = jnp.where(across == 1, 4, jnp.where(across == inner_side, 10, 16))
    return jnp.where(entry < 4, entry, base + along * 2 + remote % 2)


def call(kernel, outs, flops, smem=0, scratch=()):
    def run(*args):
        in_specs = [pl.BlockSpec(memory_space=pltpu.SMEM)] * smem
        in_specs += [pl.BlockSpec(memory_space=pltpu.VMEM)] * (len(args) - smem)
        return pl.pallas_call(
            kernel,
            out_shape=[jax.ShapeDtypeStruct(shape, dtype) for shape, dtype in outs],
            in_specs=in_specs,
            out_specs=[pl.BlockSpec(memory_space=pltpu.VMEM)] * len(outs),
            scratch_shapes=list(scratch),
            compiler_params=pltpu.CompilerParams(vmem_limit_bytes=VMEM_LIMIT),
            cost_estimate=pl.CostEstimate(
                flops=flops, bytes_accessed=1 << 20, transcendentals=0
            ),
        )(*args)

    return run


def gather_kernel(meta, residual, cells, fraction, alphas, order, own, sent):
    atoms = residual.shape[1]
    position = cells[...].astype(F32) + fraction[...]
    rows = jnp.concatenate(
        [position, alphas[...], residual[...], jnp.zeros((1, atoms), F32)], 0
    )
    picked = selected(rows, order_matrix(order[...], atoms), NN)
    for tile in range(atoms // TILE):
        own[tile] = picked[:, tile * TILE : (tile + 1) * TILE]
    for place in range(2):
        sent[place] = own[meta[SEND_AT + place]]


def search_rows(block):
    return block[3:4] * block[4:7]


def fill_pool(pool, extents, own, straight, inner, outer, meta):
    inner_step = jnp.where(meta[PARITY_AT] == 0, 1.0, -1.0)
    rows = lax.broadcasted_iota(jnp.int32, (8, TILE), 0)
    for tile in range(4):
        pool[tile] = own[tile]
    for base, source, step in ((4, straight, 0.0), (10, inner, inner_step), (16, outer, -inner_step)):
        for along in range(3):
            shift = jnp.where(
                rows == 0,
                float((along - 1) * extents[0]),
                jnp.where(rows == 1, step * float(extents[1]), 0.0),
            )
            for member in range(2):
                pool[base + 2 * along + member] = source[along, member] + shift


def own_columns(columns, block):
    turned = block.T
    for row in range(columns.shape[0]):
        columns[row] = jnp.broadcast_to(turned[:, row : row + 1], (TILE, TILE))


def wrap_depth(depth):
    half = 0.5 * G
    return jnp.where(depth > half, depth - G, jnp.where(depth < -half, depth + G, depth))


PAIR_ROWS = 64


def pair_kernel(places, extents, meta, own, straight, inner, outer, pool, pairs, found, columns, totals):
    fill_pool(pool, extents, own, straight, inner, outer, meta)
    for at, place in enumerate(places):
        tile = tile_at(meta, place)
        block = own[tile]
        own_columns(columns, jnp.concatenate([block[:3], lax.rsqrt(block[3:4]), block[4:]], 0))
        live = meta[COUNTS_AT + tile]
        for chunk in range(TILE // PAIR_ROWS):
            rows = slice(chunk * PAIR_ROWS, (chunk + 1) * PAIR_ROWS)
            shape = (PAIR_ROWS, TILE)
            same = lax.broadcasted_iota(jnp.int32, shape, 0) + chunk * PAIR_ROWS
            diagonal = jnp.where(same == lax.broadcasted_iota(jnp.int32, shape, 1), 1.0, 0.0)

            def step(entry, sums):
                listed = meta[tile * 8 + entry]
                other = pool[pool_slot(meta, listed)]
                itself = diagonal * jnp.where(listed == tile, 1.0, 0.0)
                d_x = other[0:1] - columns[0, rows]
                d_y = other[1:2] - columns[1, rows]
                d_z = wrap_depth(other[2:3] - columns[2, rows])
                square = d_x * d_x + d_y * d_y + d_z * d_z + itself
                inverse = lax.rsqrt(square)
                distance = square * inverse
                inverse_sq = inverse * inverse
                gauss = jnp.exp(-(BETA**2) * square)
                t = 1.0 / (1.0 + (SCALED_ERFC_T * BETA) * distance)
                series = jnp.full(shape, SCALED_ERFC[-1], F32)
                for term in SCALED_ERFC[-2::-1]:
                    series = series * t + term
                bare_one = gauss * (series * t * inverse + 2.0 * BETA / ROOT_PI) * inverse_sq
                bare_two = (3.0 * bare_one + (4.0 * BETA**3 / ROOT_PI) * gauss) * inverse_sq
                damping = (square * distance) * (THOLE * columns[3, rows] * lax.rsqrt(other[3:4]))
                decay = jnp.exp(-damping) * inverse * inverse_sq
                keep = 1.0 - itself
                three = keep * (bare_one - decay)
                five = keep * (bare_two - 3.0 * (1.0 + damping) * decay * inverse_sq)
                pairs[0, at * 8 + entry, rows] = five
                pairs[1, at * 8 + entry, rows] = three
                v = search_rows(other)
                along = five * (d_x * v[0:1] + d_y * v[1:2] + d_z * v[2:3])
                return (
                    sums[0] + (along * d_x - three * v[0:1]),
                    sums[1] + (along * d_y - three * v[1:2]),
                    sums[2] + (along * d_z - three * v[2:3]),
                )

            zero = jnp.zeros(shape, F32)
            sums = lax.fori_loop(0, live, step, (zero, zero, zero))
            for part in range(3):
                totals[part, rows] = sums[part]
        found[at] = updated(block, totals)


def field_rows(totals):
    return [jnp.sum(totals[part].T, axis=0, keepdims=True) for part in range(3)]


def updated(block, totals):
    alpha = block[3:4]
    field = field_rows(totals)
    rows = [alpha * (block[4 + part : 5 + part] + field[part]) for part in range(3)]
    return jnp.concatenate(rows + [jnp.zeros((5, TILE), F32)], 0)


APPLY_ROWS = 32


def fill_search(pool, own_first, own_rest, straight, inner, outer, meta):
    for place in range(4):
        pool[tile_at(meta, place)] = own_first[place] if place < 2 else own_rest[place - 2]
    for base, source in ((4, straight), (10, inner), (16, outer)):
        for along in range(3):
            for member in range(2):
                pool[base + 2 * along + member] = source[along, member]


def apply_tile(meta, tile, at, pairs, geometry, pool, columns, totals):
    block = geometry[tile]
    own_columns(columns, block)
    live = meta[COUNTS_AT + tile]
    for chunk in range(TILE // APPLY_ROWS):
        rows = slice(chunk * APPLY_ROWS, (chunk + 1) * APPLY_ROWS)
        x_i, y_i, z_i = (columns[0, rows], columns[1, rows], columns[2, rows])

        def step(entry, sums):
            slot = pool_slot(meta, meta[tile * 8 + entry])
            other = geometry[slot]
            v = pool[slot]
            d_x = other[0:1] - x_i
            d_y = other[1:2] - y_i
            d_z = wrap_depth(other[2:3] - z_i)
            three = pairs[1, at * 8 + entry, rows]
            along = pairs[0, at * 8 + entry, rows] * (d_x * v[0:1] + d_y * v[1:2] + d_z * v[2:3])
            return (
                sums[0] + (along * d_x - three * v[0:1]),
                sums[1] + (along * d_y - three * v[1:2]),
                sums[2] + (along * d_z - three * v[2:3]),
            )

        zero = jnp.zeros((APPLY_ROWS, TILE), F32)
        sums = lax.fori_loop(0, live, step, (zero, zero, zero))
        for part in range(3):
            totals[part, rows] = sums[part]


def sweep_kernel(places, meta, geometry, own_first, own_rest, straight, inner, outer, *rest):
    banks = len(places) // 2
    pairs, found = (rest[:banks], rest[banks])
    pool, columns, totals = rest[banks + 1 :]
    fill_search(pool, own_first, own_rest, straight, inner, outer, meta)
    for at, place in enumerate(places):
        tile = tile_at(meta, place)
        apply_tile(meta, tile, at % 2, pairs[at // 2], geometry, pool, columns, totals)
        found[at] = updated(geometry[tile], totals)


def final_field_kernel(
    meta, geometry, direction, straight, inner, outer, pairs_a, pairs_b, order, applied, sums, pool, columns, totals, local
):
    atoms = order.shape[1]
    fill_search(pool, direction, direction.at[2:4], straight, inner, outer, meta)
    curve = jnp.zeros((1, TILE), F32)
    dots = jnp.zeros((1, TILE), F32)
    for place in range(4):
        tile = tile_at(meta, place)
        apply_tile(meta, tile, place % 2, (pairs_a, pairs_b)[place // 2], geometry, pool, columns, totals)
        block = geometry[tile]
        ahead = direction[place]
        field = field_rows(totals)
        rows = []
        for part in range(3):
            d = ahead[part : part + 1]
            value = d / block[3:4] - field[part] - SELF_FIELD * d
            curve = curve + d * value
            dots = dots + d * block[4 + part : 5 + part]
            rows.append(value)
        local[tile] = jnp.concatenate(rows + [jnp.zeros((5, TILE), F32)], 0)
    in_tiles = jnp.concatenate([local[tile] for tile in range(4)], 1)
    applied[...] = selected(in_tiles, order_matrix(order[...], atoms), NT)
    lane = lax.broadcasted_iota(jnp.int32, (8, TILE), 1)
    curve_sum = jnp.sum(curve, axis=1, keepdims=True)
    dot_sum = jnp.sum(dots, axis=1, keepdims=True)
    sums[...] = jnp.where(lane == 1, curve_sum, jnp.where(lane == 2, dot_sum, 0.0))


def spline(fraction):
    centre_arg = fraction - 0.5

    def middle(u):
        return (55.0 + u * (20.0 + u * (-120.0 + u * (80.0 - 16.0 * u)))) / 96.0

    def middle_slope(u):
        return (20.0 + u * (-240.0 + u * (240.0 - 64.0 * u))) / 96.0

    def outer(u):
        w = 5.0 - 2.0 * u
        return (w * w) * (w * w) / 384.0

    def outer_slope(u):
        w = 5.0 - 2.0 * u
        return -(w * w * w) / 48.0

    sq = centre_arg * centre_arg
    weights = (
        outer(fraction + 1.5),
        middle(fraction + 0.5),
        115.0 / 192.0 - 0.625 * sq + 0.25 * sq * sq,
        middle(1.5 - fraction),
        outer(2.5 - fraction),
    )
    slopes = (
        outer_slope(fraction + 1.5),
        middle_slope(fraction + 0.5),
        -1.25 * centre_arg + centre_arg * sq,
        -middle_slope(1.5 - fraction),
        -outer_slope(2.5 - fraction),
    )
    return (weights, slopes)


def table(cell_row, values, length, wrapped):
    atoms = cell_row.shape[1]
    ids = lax.broadcasted_iota(jnp.int32, (length, atoms), 0)
    if wrapped:
        ahead = ids - cell_row + 2
        ahead = jnp.where(ahead >= G, ahead - G, jnp.where(ahead < 0, ahead + G, ahead))
    else:
        ahead = ids - cell_row
    total = jnp.zeros((length, atoms), F32)
    for step in range(5):
        total = jnp.where(ahead == step, values[step], total)
    return total


def tables_kernel(cells, fraction, cas_high, cas_low, tab_x, tab_y, w_high, w_low, slope_z):
    for dim, out in ((0, tab_x), (1, tab_y)):
        weights, slopes = spline(fraction[dim : dim + 1])
        out[0] = table(cells[dim : dim + 1], weights, out.shape[1], False)
        out[1] = table(cells[dim : dim + 1], slopes, out.shape[1], False)
    weights, slopes = spline(fraction[2:3])
    cas = (cas_high[...], cas_low[...])
    waves = product(cas, halves(table(cells[2:3], weights, G, True)), NN)
    high, low = halves(waves)
    w_high[...] = high
    w_low[...] = low
    slope_z[...] = product(cas, halves(table(cells[2:3], slopes, G, True)), NN)


def spread_kernel(x_rows, meta, direction, order, tab_x, tab_y, w_high, w_low, slope_z, ordered, out, local):
    atoms = order.shape[1]
    y_rows = tab_y.shape[1]
    for place in range(4):
        local[tile_at(meta, place)] = direction[place]
    in_tiles = jnp.concatenate([local[tile] for tile in range(4)], 1)
    d = selected(in_tiles, order_matrix(order[...], atoms), NT)
    ordered[...] = d
    w_z = (w_high[...], w_low[...])
    s_z = halves(slope_z[...] * d[2:3])
    slope_part = tab_x[1] * d[0:1]
    weight_part = tab_x[0] * d[1:2]
    sides = []
    for y in range(y_rows):
        w_y, s_y = (tab_y[0, y : y + 1], tab_y[1, y : y + 1])
        sides.append((slope_part * w_y + weight_part * s_y, tab_x[0] * w_y))
    side = halves(jnp.concatenate([pair[0] for pair in sides], 0))
    flat = halves(jnp.concatenate([pair[1] for pair in sides], 0))
    width = y_rows * x_rows
    out[:, :width] = product(w_z, side, NT) + product(s_z, flat, NT)
    out[:, width:] = jnp.zeros((G, out.shape[1] - width), F32)


def plane_kernel(
    shapes, grid, factor, sums, x_high, x_low, y_high, y_low, yt_high, yt_low, xt_high, xt_low, out, along_x
):
    n_slab, n_space, x_rows, y_rows = shapes
    width = x_rows * y_rows
    for y in range(y_rows):
        total = None
        for s in range(n_slab):
            block = halves(grid[s * n_space : (s + 1) * n_space, y * x_rows : (y + 1) * x_rows])
            rows = slice(s * x_rows, (s + 1) * x_rows)
            term = product(block, (x_high[rows], x_low[rows]), NN)
            total = term if total is None else total + term
        along_x[y * n_space : (y + 1) * n_space] = total
    spectrum = product((yt_high[...], yt_low[...]), halves(along_x[...]), NN)
    scaled = spectrum * factor[...]
    energy = jnp.sum(jnp.sum(spectrum * scaled, axis=0, keepdims=True), axis=1, keepdims=True)
    back = halves(product((y_high[...], y_low[...]), halves(scaled), NN))
    planes = product(back, (xt_high[...], xt_low[...]), NN)
    for s in range(n_slab):
        for y in range(y_rows):
            out[s * n_space : (s + 1) * n_space, y * x_rows : (y + 1) * x_rows] = planes[
                y * n_space : (y + 1) * n_space, s * TILE : s * TILE + x_rows
            ]
    spare = out.shape[1] - width
    lane = lax.broadcasted_iota(jnp.int32, (1, spare), 1)
    tail = jnp.where(lane == 0, energy, sums[0:1, :spare])
    out[:, width:] = jnp.broadcast_to(tail, (out.shape[0], spare))


def finish_kernel(
    x_rows, grid, w_high, w_low, slope_z, tab_x, tab_y, ordered, applied, dipoles, residual, next_dipoles, next_residual, direction
):
    y_rows = tab_y.shape[1]
    width = y_rows * x_rows
    planes = halves(grid[:, :width])
    tail = jnp.sum(grid[:, width:], axis=0, keepdims=True)
    step = tail[:, 2:3] / (tail[:, 0:1] + tail[:, 1:2])
    by_weight = product(planes, (w_high[...], w_low[...]), TN)
    by_slope = product(planes, halves(slope_z[...]), TN)
    fields = [0.0, 0.0, 0.0]
    for y in range(y_rows):
        rows = slice(y * x_rows, (y + 1) * x_rows)
        w_y, s_y = (tab_y[0, y : y + 1], tab_y[1, y : y + 1])
        weighted = by_weight[rows]
        fields[0] += w_y * jnp.sum(tab_x[1] * weighted, axis=0, keepdims=True)
        fields[1] += s_y * jnp.sum(tab_x[0] * weighted, axis=0, keepdims=True)
        fields[2] += w_y * jnp.sum(tab_x[0] * by_slope[rows], axis=0, keepdims=True)
    total = applied[0:3] + jnp.concatenate(fields, 0)
    d = ordered[0:3]
    next_dipoles[...] = dipoles[...] + step * d
    next_residual[...] = residual[...] - step * total
    direction[...] = d


def cas_matrix(first, second):
    angles = 2.0 * np.pi / G * (np.outer(first, second) % G)
    return np.cos(angles) + np.sin(angles)


def split_constant(values):
    whole = values.astype(np.float32)
    high = whole.astype(ml_dtypes.bfloat16)
    low = (values - high.astype(np.float64)).astype(ml_dtypes.bfloat16)
    return (jnp.asarray(high), jnp.asarray(low))


def wave_factors(freq_ids):
    wrapped = jnp.where(freq_ids > G // 2, freq_ids - G, freq_ids).astype(F32) / G
    angles = 2.0 * math.pi / G * freq_ids.astype(F32)
    modulus = 115.0 / 192.0 + 19.0 / 48.0 * jnp.cos(angles) + 1.0 / 192.0 * jnp.cos(2.0 * angles)
    return (
        wrapped * wrapped,
        jnp.exp(-((math.pi / BETA) ** 2) * wrapped * wrapped) / (modulus * modulus),
    )


def multiplier(freq_x, freq_y, freq_z):
    square_x, factor_x = wave_factors(freq_x)
    square_y, factor_y = wave_factors(freq_y)
    square_z, factor_z = wave_factors(freq_z)
    square_sum = square_x + square_y + square_z
    anchor = ((freq_x == 0) & (freq_y == 0) & (freq_z == 0)).astype(F32)
    return (
        (1.0 - anchor)
        * factor_x
        * factor_y
        * factor_z
        / (math.pi * float(G) ** 3 * (square_sum + anchor))
    )


def swap_pairs(n_slab, n_space, odd):
    pairs = []
    for s in range(n_slab):
        for q in range(n_space):
            partner = (q + 1 if (q % 2 == 1) == odd else q - 1) % n_space
            pairs.append((s * n_space + q, s * n_space + partner))
    return pairs


def around(block):
    n_slab, n_space = (lax.axis_size("slab"), lax.axis_size("space"))
    up = [(i, (i + 1) % n_slab) for i in range(n_slab)]
    down = [(j, i) for i, j in up]
    before = lax.ppermute(block, "slab", up)
    after = lax.ppermute(block, "slab", down)
    straight = jnp.stack([before, block, after])
    inner = lax.ppermute(straight, BOTH, swap_pairs(n_slab, n_space, False))
    outer = lax.ppermute(straight, BOTH, swap_pairs(n_slab, n_space, True))
    return (straight, inner, outer)


def local(
    dipoles, residual, cells, fraction, polarizability, tile_order, send_tiles, tile_lists, tile_counts
):
    n_slab, n_space = (lax.axis_size("slab"), lax.axis_size("space"))
    atoms = residual.shape[1]
    extents = (G // n_slab, G // n_space)
    x_rows = -(-(extents[0] + 4) // 8) * 8
    y_rows = extents[1] + 4
    width = x_rows * y_rows
    lanes = -(-(width + 3) // TILE) * TILE
    slab_index, space_index = (lax.axis_index("slab"), lax.axis_index("space"))
    meta = jnp.concatenate(
        [
            tile_lists.reshape(-1),
            tile_counts.reshape(-1),
            send_tiles.reshape(-1),
            (space_index % 2).reshape(1).astype(jnp.int32),
        ]
    )
    tile_shape = ((4, 8, TILE), F32)
    two_shape = ((2, 8, TILE), F32)
    bank_shape = ((2, 16, TILE, TILE), F32)
    pool_scratch = pltpu.VMEM((22, 8, TILE), F32)
    total_scratch = pltpu.VMEM((3, TILE, TILE), F32)
    own, sent = call(gather_kernel, [tile_shape, two_shape], 10**8, smem=1)(
        meta, residual, cells, fraction, polarizability.reshape(1, atoms), tile_order
    )
    first = around(sent)

    def pairs_of(places):
        return call(
            functools.partial(pair_kernel, places, extents),
            [((22, 8, TILE), F32), bank_shape, two_shape],
            10**9,
            smem=1,
            scratch=(pltpu.VMEM((8, TILE, TILE), F32), total_scratch),
        )(meta, own, *first)

    geometry, pairs_a, search_a = pairs_of((0, 1))
    _, pairs_b, search_b = pairs_of((2, 3))
    sweep_scratch = (pool_scratch, pltpu.VMEM((3, TILE, TILE), F32), total_scratch)
    second = around(search_a)

    def sweep(places, mine, others, received, banks):
        return call(
            functools.partial(sweep_kernel, places),
            [((len(places), 8, TILE), F32)],
            10**8,
            smem=1,
            scratch=sweep_scratch,
        )(meta, geometry, mine, others, *received, *banks)[0]

    next_a = sweep((0, 1), search_a, search_b, second, (pairs_a,))
    next_b = sweep((2, 3), search_a, search_b, second, (pairs_b,))
    third = around(next_a)
    direction = sweep((0, 1, 2, 3), next_a, next_b, third, (pairs_a, pairs_b))
    freq = np.arange(G)
    padded_x = np.stack([(s * extents[0] + np.arange(x_rows) - 2) % G for s in range(n_slab)])
    real_x = np.tile(np.arange(x_rows) < extents[0] + 4, n_slab)
    cas_x = cas_matrix(padded_x.reshape(-1), freq) * real_x[:, None]
    rows_y = (np.arange(n_space)[None] * extents[1] + np.arange(y_rows)[:, None] - 2) % G
    cas_y = cas_matrix(rows_y.reshape(-1), freq)
    wide_x = np.zeros((G, n_slab, TILE))
    wide_x[:, :, :x_rows] = cas_x.reshape(n_slab, x_rows, G).transpose(2, 0, 1)
    tab_x, tab_y, w_high, w_low, slope_z = call(
        tables_kernel,
        [
            ((2, x_rows, atoms), F32),
            ((2, y_rows, atoms), F32),
            ((G, atoms), BF16),
            ((G, atoms), BF16),
            ((G, atoms), F32),
        ],
        10**8,
    )(cells, fraction, *split_constant(cas_matrix(freq, freq)))
    ordered, spread = call(
        functools.partial(spread_kernel, x_rows),
        [((8, atoms), F32), ((G, lanes), F32)],
        10**9,
        smem=1,
        scratch=(pltpu.VMEM((4, 8, TILE), F32),),
    )(meta, direction, tile_order, tab_x, tab_y, w_high, w_low, slope_z)
    grid = lax.all_to_all(spread, BOTH, 0, 0, tiled=True)
    last = around(direction[:2])
    applied, sums = call(
        final_field_kernel,
        [((8, atoms), F32), ((8, TILE), F32)],
        10**9,
        smem=1,
        scratch=sweep_scratch + (pltpu.VMEM((4, 8, TILE), F32),),
    )(meta, geometry, direction, *last, pairs_a, pairs_b, tile_order)
    ids = jnp.arange(G, dtype=jnp.int32)
    factor = multiplier(ids[None, :], ids[:, None], slab_index * n_space + space_index)
    planes = call(
        functools.partial(plane_kernel, (n_slab, n_space, x_rows, y_rows)),
        [((G, lanes), F32)],
        10**9,
        scratch=(pltpu.VMEM((y_rows * n_space, G), F32),),
    )(
        grid,
        factor,
        sums,
        *split_constant(cas_x),
        *split_constant(cas_y),
        *split_constant(cas_y.T),
        *split_constant(wide_x.reshape(G, -1)),
    )[0]
    returned = lax.all_to_all(planes, BOTH, 0, 0, tiled=True)
    three = ((3, atoms), F32)
    return tuple(
        call(functools.partial(finish_kernel, x_rows), [three, three, three], 10**9)(
            returned, w_high, w_low, slope_z, tab_x, tab_y, ordered, applied, dipoles, residual
        )
    )


def solution(mesh):
    in_specs = (
        P(None, BOTH),
        P(None, BOTH),
        P(None, BOTH),
        P(None, BOTH),
        P(BOTH),
        P(BOTH, None),
        P(BOTH, None),
        P(BOTH, None, None),
        P(BOTH, None),
    )
    out_specs = (P(None, BOTH), P(None, BOTH), P(None, BOTH))
    return jax.shard_map(local, mesh=mesh, in_specs=in_specs, out_specs=out_specs, check_vma=False)
```

```python
import functools
import math

import jax
import jax.numpy as jnp
import ml_dtypes
import numpy as np
from jax import lax
from jax.experimental import pallas as pl
from jax.experimental.pallas import tpu as pltpu
from jax.sharding import PartitionSpec as P

G = 256
TILE = 128
BOTH = ("slab", "space")
BETA = 0.4
THOLE = 0.39
ROOT_PI = math.sqrt(math.pi)
SELF_FIELD = 4.0 * BETA**3 / (3.0 * ROOT_PI)
F32 = jnp.float32
BF16 = jnp.bfloat16
SCALED_ERFC_T = 0.45
SCALED_ERFC = (
    0.25388532876968384,
    0.25388309359550476,
    0.22827406227588654,
    0.17522020637989044,
    0.1201537474989891,
    -0.023065825924277306,
    0.14381752908229828,
    -0.3022053837776184,
    0.19167575240135193,
    -0.04163854941725731,
)
NT = (((1,), (1,)), ((), ()))
NN = (((1,), (0,)), ((), ()))
TN = (((0,), (0,)), ((), ()))
VMEM_LIMIT = 20 * 1024 * 1024


def halves(values):
    high = values.astype(BF16)
    return (high, (values - high.astype(F32)).astype(BF16))


def product(left, right, dims):
    def one(a, b):
        return lax.dot_general(a, b, dims, preferred_element_type=F32)

    return one(left[0], right[0]) + (one(left[0], right[1]) + one(left[1], right[0]))


def thirds(values):
    high = values.astype(BF16).astype(F32)
    rest = values - high
    middle = rest.astype(BF16).astype(F32)
    return jnp.concatenate([high, middle, rest - middle], 0).astype(BF16)


def selected(values, one_hot, dims):
    rows = values.shape[0]
    picked = lax.dot_general(thirds(values), one_hot, dims, preferred_element_type=F32)
    return picked[:rows] + (picked[rows : 2 * rows] + picked[2 * rows :])


def order_matrix(order_row, count):
    ids = lax.broadcasted_iota(jnp.int32, (count, count), 0)
    return jnp.where(ids == order_row, 1.0, 0.0).astype(BF16)


COUNTS_AT = 32
ORDER_AT = 36
PARITY_AT = 40


def meta_of(tile_lists, tile_counts, send_tiles, parity):
    entry = tile_lists.reshape(-1)
    remote = entry - 4
    pair = remote // 2
    pair = pair + (pair >= 4)
    along = pair // 3
    across = pair % 3
    base = jnp.where(across == 1, 4, jnp.where(across == 2 - 2 * parity, 10, 16))
    slots = jnp.where(entry < 4, entry, base + along * 2 + remote % 2)
    first, second = (send_tiles[0, 0], send_tiles[0, 1])
    third = jnp.where(
        (first != 0) & (second != 0), 0, jnp.where((first != 1) & (second != 1), 1, 2)
    )
    rest = jnp.stack([first, second, third, 6 - first - second - third, parity])
    return jnp.concatenate([slots, tile_counts.reshape(-1), rest]).astype(jnp.int32)


def call(kernel, outs, flops, smem=0, scratch=()):
    def run(*args):
        in_specs = [pl.BlockSpec(memory_space=pltpu.SMEM)] * smem
        in_specs += [pl.BlockSpec(memory_space=pltpu.VMEM)] * (len(args) - smem)
        return pl.pallas_call(
            kernel,
            out_shape=[jax.ShapeDtypeStruct(shape, dtype) for shape, dtype in outs],
            in_specs=in_specs,
            out_specs=[pl.BlockSpec(memory_space=pltpu.VMEM)] * len(outs),
            scratch_shapes=list(scratch),
            compiler_params=pltpu.CompilerParams(vmem_limit_bytes=VMEM_LIMIT),
            cost_estimate=pl.CostEstimate(
                flops=flops, bytes_accessed=1 << 20, transcendentals=0
            ),
        )(*args)

    return run


def gather_kernel(send, *refs):
    sources, own, sent, held, sems = (refs[:5], refs[5], refs[6], refs[7:12], refs[12])
    copies = [
        pltpu.make_async_copy(source, target, sems.at[at])
        for at, (source, target) in enumerate(zip(sources, held))
    ]
    for copy in copies:
        copy.start()
    for copy in copies:
        copy.wait()
    residual, cells, fraction, alphas, order = held
    atoms = residual.shape[1]
    position = cells[...].astype(F32) + fraction[...]
    rows = jnp.concatenate(
        [position, alphas[...].reshape(1, atoms), residual[...], jnp.zeros((1, atoms), F32)], 0
    )
    picked = selected(rows, order_matrix(order[...], atoms), NN)
    for tile in range(atoms // TILE):
        own[tile] = picked[:, tile * TILE : (tile + 1) * TILE]
    for place in range(2):
        sent[place] = own[send[0, place]]


def search_rows(block):
    return block[3:4] * block[4:7]


def fill_pool(pool, extents, own, straight, inner, outer, meta):
    inner_step = jnp.where(meta[PARITY_AT] == 0, 1.0, -1.0)
    rows = lax.broadcasted_iota(jnp.int32, (8, TILE), 0)
    for tile in range(4):
        pool[tile] = own[tile]
    for base, source, step in ((4, straight, 0.0), (10, inner, inner_step), (16, outer, -inner_step)):
        for along in range(3):
            shift = jnp.where(
                rows == 0,
                float((along - 1) * extents[0]),
                jnp.where(rows == 1, step * float(extents[1]), 0.0),
            )
            for member in range(2):
                pool[base + 2 * along + member] = source[along, member] + shift


def own_columns(columns, block, count):
    turned = block.T
    for row in range(count):
        columns[row] = jnp.broadcast_to(turned[:, row : row + 1], (TILE, TILE))


def wrap_depth(depth):
    half = 0.5 * G
    return jnp.where(depth > half, depth - G, jnp.where(depth < -half, depth + G, depth))


PAIR_ROWS = 32
GROUP = 4


def pair_kernel(first_place, extents, meta, own, straight, inner, outer, pool, pairs, found, columns, totals):
    fill_pool(pool, extents, own, straight, inner, outer, meta)

    def tile_step(at, carry):
        tile = meta[ORDER_AT + first_place + at]
        block = own[tile]
        own_columns(columns, jnp.concatenate([block[:3], lax.rsqrt(block[3:4]), block[4:]], 0), 4)
        live = meta[COUNTS_AT + tile]

        def chunk_step(chunk, carry):
            start = pl.multiple_of(chunk * PAIR_ROWS, PAIR_ROWS)
            rows = pl.ds(start, PAIR_ROWS)
            shape = (PAIR_ROWS, TILE)
            ahead = lax.broadcasted_iota(jnp.int32, shape, 0) - lax.broadcasted_iota(
                jnp.int32, shape, 1
            )
            diagonal = jnp.where(ahead == -start, 1.0, 0.0)

            def group_step(group, sums):
                for member in range(GROUP):
                    entry = group * GROUP + member
                    slot = meta[tile * 8 + entry]
                    other = pool[slot]
                    itself = diagonal * jnp.where(slot == tile, 1.0, 0.0)
                    d_x = other[0:1] - columns[0, rows]
                    d_y = other[1:2] - columns[1, rows]
                    d_z = wrap_depth(other[2:3] - columns[2, rows])
                    square = d_x * d_x + d_y * d_y + d_z * d_z + itself
                    inverse = lax.rsqrt(square)
                    distance = square * inverse
                    inverse_sq = inverse * inverse
                    gauss = jnp.exp(-(BETA**2) * square)
                    stretch = 1.0 + (SCALED_ERFC_T * BETA) * distance
                    t = lax.rsqrt(stretch * stretch)
                    series = SCALED_ERFC[-1] * t + SCALED_ERFC[-2]
                    for term in SCALED_ERFC[-3::-1]:
                        series = series * t + term
                    bare_one = gauss * (series * t * inverse + 2.0 * BETA / ROOT_PI) * inverse_sq
                    bare_two = (3.0 * bare_one + (4.0 * BETA**3 / ROOT_PI) * gauss) * inverse_sq
                    damping = (square * distance) * columns[3, rows] * (THOLE * lax.rsqrt(other[3:4]))
                    decay = jnp.exp(-damping) * inverse * inverse_sq
                    keep = jnp.where(entry < live, 1.0, 0.0) * (1.0 - itself)
                    three = keep * (bare_one - decay)
                    five = keep * (bare_two - (3.0 + 3.0 * damping) * decay * inverse_sq)
                    pairs[0, at * 8 + entry, rows] = five
                    pairs[1, at * 8 + entry, rows] = three
                    v = search_rows(other)
                    along = five * (d_x * v[0:1] + d_y * v[1:2] + d_z * v[2:3])
                    sums = (
                        sums[0] + (along * d_x - three * v[0:1]),
                        sums[1] + (along * d_y - three * v[1:2]),
                        sums[2] + (along * d_z - three * v[2:3]),
                    )
                return sums

            zero = jnp.zeros(shape, F32)
            sums = lax.fori_loop(0, (live + GROUP - 1) // GROUP, group_step, (zero, zero, zero))
            for part in range(3):
                totals[part, rows] = sums[part]
            return carry

        lax.fori_loop(0, TILE // PAIR_ROWS, chunk_step, 0)
        found[at] = updated(block, totals)
        return carry

    lax.fori_loop(0, 2, tile_step, 0)


def field_rows(totals):
    return [jnp.sum(totals[part].T, axis=0, keepdims=True) for part in range(3)]


def updated(block, totals):
    alpha = block[3:4]
    field = field_rows(totals)
    rows = [alpha * (block[4 + part : 5 + part] + field[part]) for part in range(3)]
    return jnp.concatenate(rows + [jnp.zeros((5, TILE), F32)], 0)


APPLY_ROWS = 64


def fill_search(pool, own_first, own_rest, straight, inner, outer, meta):
    for place in range(4):
        pool[meta[ORDER_AT + place]] = own_first[place] if place < 2 else own_rest[place - 2]
    for base, source in ((4, straight), (10, inner), (16, outer)):
        for along in range(3):
            for member in range(2):
                pool[base + 2 * along + member] = source[along, member]


def apply_tile(meta, tile, at, pairs, geometry, pool, columns, totals):
    block = geometry[tile]
    own_columns(columns, block, 3)
    live = meta[COUNTS_AT + tile]

    def chunk_step(chunk, carry):
        rows = pl.ds(pl.multiple_of(chunk * APPLY_ROWS, APPLY_ROWS), APPLY_ROWS)

        def group_step(group, sums):
            for member in range(GROUP):
                entry = group * GROUP + member
                slot = meta[tile * 8 + entry]
                other = geometry[slot]
                v = pool[slot]
                d_x = other[0:1] - columns[0, rows]
                d_y = other[1:2] - columns[1, rows]
                d_z = wrap_depth(other[2:3] - columns[2, rows])
                three = pairs[1, at * 8 + entry, rows]
                along = pairs[0, at * 8 + entry, rows] * (d_x * v[0:1] + d_y * v[1:2] + d_z * v[2:3])
                sums = (
                    sums[0] + (along * d_x - three * v[0:1]),
                    sums[1] + (along * d_y - three * v[1:2]),
                    sums[2] + (along * d_z - three * v[2:3]),
                )
            return sums

        zero = jnp.zeros((APPLY_ROWS, TILE), F32)
        sums = lax.fori_loop(0, (live + GROUP - 1) // GROUP, group_step, (zero, zero, zero))
        for part in range(3):
            totals[part, rows] = sums[part]
        return carry

    lax.fori_loop(0, TILE // APPLY_ROWS, chunk_step, 0)


def sweep_kernel(first_place, meta, geometry, own_first, own_rest, straight, inner, outer, *rest):
    banks = len(rest) - 4
    pairs, found = (rest[:banks], rest[banks])
    pool, columns, totals = rest[banks + 1 :]
    fill_search(pool, own_first, own_rest, straight, inner, outer, meta)
    for bank in range(banks):

        def tile_step(at, carry):
            tile = meta[ORDER_AT + first_place + 2 * bank + at]
            apply_tile(meta, tile, at, pairs[bank], geometry, pool, columns, totals)
            found[2 * bank + at] = updated(geometry[tile], totals)
            return carry

        lax.fori_loop(0, 2, tile_step, 0)


def final_field_kernel(
    meta, geometry, direction, straight, inner, outer, pairs_a, pairs_b, order, applied, sums, pool, columns, totals, local
):
    atoms = order.shape[1]
    fill_search(pool, direction, direction.at[2:4], straight, inner, outer, meta)
    both = (jnp.zeros((1, TILE), F32), jnp.zeros((1, TILE), F32))
    for bank, pairs in enumerate((pairs_a, pairs_b)):

        def tile_step(at, both):
            curve, dots = both
            place = 2 * bank + at
            tile = meta[ORDER_AT + place]
            apply_tile(meta, tile, at, pairs, geometry, pool, columns, totals)
            block = geometry[tile]
            ahead = direction[place]
            field = field_rows(totals)
            rows = []
            for part in range(3):
                d = ahead[part : part + 1]
                value = d / block[3:4] - field[part] - SELF_FIELD * d
                curve = curve + d * value
                dots = dots + d * block[4 + part : 5 + part]
                rows.append(value)
            local[tile] = jnp.concatenate(rows + [jnp.zeros((5, TILE), F32)], 0)
            return (curve, dots)

        both = lax.fori_loop(0, 2, tile_step, both)
    in_tiles = jnp.concatenate([local[tile] for tile in range(4)], 1)
    applied[...] = selected(in_tiles, order_matrix(order[...], atoms), NT)
    lane = lax.broadcasted_iota(jnp.int32, (8, TILE), 1)
    curve_sum = jnp.sum(both[0], axis=1, keepdims=True)
    dot_sum = jnp.sum(both[1], axis=1, keepdims=True)
    sums[...] = jnp.where(lane == 1, curve_sum, jnp.where(lane == 2, dot_sum, 0.0))


def spline(fraction):
    centre_arg = fraction - 0.5

    def middle(u):
        return (55.0 + u * (20.0 + u * (-120.0 + u * (80.0 - 16.0 * u)))) / 96.0

    def middle_slope(u):
        return (20.0 + u * (-240.0 + u * (240.0 - 64.0 * u))) / 96.0

    def outer(u):
        w = 5.0 - 2.0 * u
        return (w * w) * (w * w) / 384.0

    def outer_slope(u):
        w = 5.0 - 2.0 * u
        return -(w * w * w) / 48.0

    sq = centre_arg * centre_arg
    weights = (
        outer(fraction + 1.5),
        middle(fraction + 0.5),
        115.0 / 192.0 - 0.625 * sq + 0.25 * sq * sq,
        middle(1.5 - fraction),
        outer(2.5 - fraction),
    )
    slopes = (
        outer_slope(fraction + 1.5),
        middle_slope(fraction + 0.5),
        -1.25 * centre_arg + centre_arg * sq,
        -middle_slope(1.5 - fraction),
        -outer_slope(2.5 - fraction),
    )
    return (weights, slopes)


def table(cell_row, values, length, wrapped):
    atoms = cell_row.shape[1]
    ids = lax.broadcasted_iota(jnp.int32, (length, atoms), 0)
    if wrapped:
        ahead = ids - cell_row + 2
        ahead = jnp.where(ahead >= G, ahead - G, jnp.where(ahead < 0, ahead + G, ahead))
    else:
        ahead = ids - cell_row
    total = jnp.zeros((length, atoms), F32)
    for step in range(5):
        total = jnp.where(ahead == step, values[step], total)
    return total


def tables_kernel(cells, fraction, cas_high, cas_low, tab_x, tab_y, w_high, w_low, slope_z):
    for dim, out in ((0, tab_x), (1, tab_y)):
        weights, slopes = spline(fraction[dim : dim + 1])
        out[0] = table(cells[dim : dim + 1], weights, out.shape[1], False)
        out[1] = table(cells[dim : dim + 1], slopes, out.shape[1], False)
    weights, slopes = spline(fraction[2:3])
    cas = (cas_high[...], cas_low[...])
    waves = product(cas, halves(table(cells[2:3], weights, G, True)), NN)
    high, low = halves(waves)
    w_high[...] = high
    w_low[...] = low
    slope_z[...] = product(cas, halves(table(cells[2:3], slopes, G, True)), NN)


def spread_kernel(x_rows, meta, direction, order, tab_x, tab_y, w_high, w_low, slope_z, ordered, out, local):
    atoms = order.shape[1]
    y_rows = tab_y.shape[1]
    for place in range(4):
        local[meta[ORDER_AT + place]] = direction[place]
    in_tiles = jnp.concatenate([local[tile] for tile in range(4)], 1)
    d = selected(in_tiles, order_matrix(order[...], atoms), NT)
    ordered[...] = d
    w_z = (w_high[...], w_low[...])
    s_z = halves(slope_z[...] * d[2:3])
    slope_part = tab_x[1] * d[0:1]
    weight_part = tab_x[0] * d[1:2]
    sides = []
    for y in range(y_rows):
        w_y, s_y = (tab_y[0, y : y + 1], tab_y[1, y : y + 1])
        sides.append((slope_part * w_y + weight_part * s_y, tab_x[0] * w_y))
    side = halves(jnp.concatenate([pair[0] for pair in sides], 0))
    flat = halves(jnp.concatenate([pair[1] for pair in sides], 0))
    width = y_rows * x_rows
    out[:, :width] = product(w_z, side, NT) + product(s_z, flat, NT)
    out[:, width:] = jnp.zeros((G, out.shape[1] - width), F32)


def plane_kernel(shapes, grid, factor, sums, x_high, x_low, y_high, y_low, out, along_x):
    n_slab, n_space, x_rows, y_rows = shapes
    width = x_rows * y_rows
    for y in range(y_rows):
        total = None
        for s in range(n_slab):
            block = halves(grid[s * n_space : (s + 1) * n_space, y * x_rows : (y + 1) * x_rows])
            rows = slice(s * TILE, s * TILE + x_rows)
            term = product(block, (x_high[rows], x_low[rows]), NN)
            total = term if total is None else total + term
        along_x[y * n_space : (y + 1) * n_space] = total
    cas_y = (y_high[...], y_low[...])
    spectrum = product(cas_y, halves(along_x[...]), TN)
    scaled = spectrum * factor[...]
    energy = jnp.sum(jnp.sum(spectrum * scaled, axis=0, keepdims=True), axis=1, keepdims=True)
    back = halves(product(cas_y, halves(scaled), NN))
    planes = product(back, (x_high[...], x_low[...]), NT)
    for s in range(n_slab):
        for y in range(y_rows):
            out[s * n_space : (s + 1) * n_space, y * x_rows : (y + 1) * x_rows] = planes[
                y * n_space : (y + 1) * n_space, s * TILE : s * TILE + x_rows
            ]
    spare = out.shape[1] - width
    lane = lax.broadcasted_iota(jnp.int32, (1, spare), 1)
    tail = jnp.where(lane == 0, energy, sums[0:1, :spare])
    out[:, width:] = jnp.broadcast_to(tail, (out.shape[0], spare))


def finish_kernel(
    x_rows, grid, w_high, w_low, slope_z, tab_x, tab_y, ordered, applied, dipoles, residual, next_dipoles, next_residual, direction
):
    y_rows = tab_y.shape[1]
    width = y_rows * x_rows
    planes = halves(grid[:, :width])
    tail = jnp.sum(grid[:, width:], axis=0, keepdims=True)
    step = tail[:, 2:3] / (tail[:, 0:1] + tail[:, 1:2])
    by_weight = product(planes, (w_high[...], w_low[...]), TN)
    by_slope = product(planes, halves(slope_z[...]), TN)
    fields = [0.0, 0.0, 0.0]
    for y in range(y_rows):
        rows = slice(y * x_rows, (y + 1) * x_rows)
        w_y, s_y = (tab_y[0, y : y + 1], tab_y[1, y : y + 1])
        weighted = by_weight[rows]
        fields[0] += w_y * jnp.sum(tab_x[1] * weighted, axis=0, keepdims=True)
        fields[1] += s_y * jnp.sum(tab_x[0] * weighted, axis=0, keepdims=True)
        fields[2] += w_y * jnp.sum(tab_x[0] * by_slope[rows], axis=0, keepdims=True)
    total = applied[0:3] + jnp.concatenate(fields, 0)
    d = ordered[0:3]
    next_dipoles[...] = dipoles[...] + step * d
    next_residual[...] = residual[...] - step * total
    direction[...] = d


def cas_matrix(first, second):
    angles = 2.0 * np.pi / G * (np.outer(first, second) % G)
    return np.cos(angles) + np.sin(angles)


def split_constant(values):
    whole = values.astype(np.float32)
    high = whole.astype(ml_dtypes.bfloat16)
    low = (values - high.astype(np.float64)).astype(ml_dtypes.bfloat16)
    return (jnp.asarray(high), jnp.asarray(low))


def wave_factors(freq_ids):
    wrapped = jnp.where(freq_ids > G // 2, freq_ids - G, freq_ids).astype(F32) / G
    angles = 2.0 * math.pi / G * freq_ids.astype(F32)
    modulus = 115.0 / 192.0 + 19.0 / 48.0 * jnp.cos(angles) + 1.0 / 192.0 * jnp.cos(2.0 * angles)
    return (
        wrapped * wrapped,
        jnp.exp(-((math.pi / BETA) ** 2) * wrapped * wrapped) / (modulus * modulus),
    )


def multiplier(freq_x, freq_y, freq_z):
    square_x, factor_x = wave_factors(freq_x)
    square_y, factor_y = wave_factors(freq_y)
    square_z, factor_z = wave_factors(freq_z)
    square_sum = square_x + square_y + square_z
    anchor = ((freq_x == 0) & (freq_y == 0) & (freq_z == 0)).astype(F32)
    return (
        (1.0 - anchor)
        * factor_x
        * factor_y
        * factor_z
        / (math.pi * float(G) ** 3 * (square_sum + anchor))
    )


def swap_pairs(n_slab, n_space, odd):
    pairs = []
    for s in range(n_slab):
        for q in range(n_space):
            partner = (q + 1 if (q % 2 == 1) == odd else q - 1) % n_space
            pairs.append((s * n_space + q, s * n_space + partner))
    return pairs


def around(block):
    n_slab, n_space = (lax.axis_size("slab"), lax.axis_size("space"))
    up = [(i, (i + 1) % n_slab) for i in range(n_slab)]
    down = [(j, i) for i, j in up]
    before = lax.ppermute(block, "slab", up)
    after = lax.ppermute(block, "slab", down)
    straight = jnp.stack([before, block, after])
    inner = lax.ppermute(straight, BOTH, swap_pairs(n_slab, n_space, False))
    outer = lax.ppermute(straight, BOTH, swap_pairs(n_slab, n_space, True))
    return (straight, inner, outer)


def local(
    dipoles, residual, cells, fraction, polarizability, tile_order, send_tiles, tile_lists, tile_counts
):
    n_slab, n_space = (lax.axis_size("slab"), lax.axis_size("space"))
    atoms = residual.shape[1]
    extents = (G // n_slab, G // n_space)
    x_rows = -(-(extents[0] + 4) // 8) * 8
    y_rows = extents[1] + 4
    width = x_rows * y_rows
    lanes = -(-(width + 3) // TILE) * TILE
    slab_index, space_index = (lax.axis_index("slab"), lax.axis_index("space"))
    tile_shape = ((4, 8, TILE), F32)
    two_shape = ((2, 8, TILE), F32)
    bank_shape = ((2, 16, TILE, TILE), F32)
    pool_scratch = pltpu.VMEM((22, 8, TILE), F32)
    total_scratch = pltpu.VMEM((3, TILE, TILE), F32)
    own, sent = pl.pallas_call(
        gather_kernel,
        out_shape=[jax.ShapeDtypeStruct(*tile_shape), jax.ShapeDtypeStruct(*two_shape)],
        in_specs=[pl.BlockSpec(memory_space=pltpu.SMEM)] + [pl.BlockSpec(memory_space=pltpu.HBM)] * 5,
        out_specs=[pl.BlockSpec(memory_space=pltpu.VMEM)] * 2,
        scratch_shapes=[
            pltpu.VMEM((3, atoms), F32),
            pltpu.VMEM((3, atoms), jnp.int32),
            pltpu.VMEM((3, atoms), F32),
            pltpu.VMEM((atoms,), F32),
            pltpu.VMEM((1, atoms), jnp.int32),
            pltpu.SemaphoreType.DMA((5,)),
        ],
        compiler_params=pltpu.CompilerParams(vmem_limit_bytes=VMEM_LIMIT),
    )(send_tiles, residual, cells, fraction, polarizability, tile_order)
    later = lax.optimization_barrier((tile_lists, tile_counts, send_tiles, sent))
    meta = meta_of(*later[:3], space_index % 2)
    first = around(sent)

    def pairs_of(first_place):
        return call(
            functools.partial(pair_kernel, first_place, extents),
            [((22, 8, TILE), F32), bank_shape, two_shape],
            10**9,
            smem=1,
            scratch=(pltpu.VMEM((4, TILE, TILE), F32), total_scratch),
        )(meta, own, *first)

    geometry, pairs_a, search_a = pairs_of(0)
    _, pairs_b, search_b = pairs_of(2)
    sweep_scratch = (pool_scratch, pltpu.VMEM((3, TILE, TILE), F32), total_scratch)
    second = around(search_a)

    def sweep(first_place, mine, others, received, banks):
        return call(
            functools.partial(sweep_kernel, first_place),
            [((2 * len(banks), 8, TILE), F32)],
            10**8,
            smem=1,
            scratch=sweep_scratch,
        )(meta, geometry, mine, others, *received, *banks)[0]

    next_a = sweep(0, search_a, search_b, second, (pairs_a,))
    next_b = sweep(2, search_a, search_b, second, (pairs_b,))
    third = around(next_a)
    direction = sweep(0, next_a, next_b, third, (pairs_a, pairs_b))
    freq = np.arange(G)
    padded_x = np.stack([(s * extents[0] + np.arange(x_rows) - 2) % G for s in range(n_slab)])
    real_x = np.tile(np.arange(x_rows) < extents[0] + 4, n_slab)
    cas_x = cas_matrix(padded_x.reshape(-1), freq) * real_x[:, None]
    rows_y = (np.arange(n_space)[None] * extents[1] + np.arange(y_rows)[:, None] - 2) % G
    cas_y = cas_matrix(rows_y.reshape(-1), freq)
    wide_x = np.zeros((n_slab, TILE, G))
    wide_x[:, :x_rows] = cas_x.reshape(n_slab, x_rows, G)
    tab_x, tab_y, w_high, w_low, slope_z = call(
        tables_kernel,
        [
            ((2, x_rows, atoms), F32),
            ((2, y_rows, atoms), F32),
            ((G, atoms), BF16),
            ((G, atoms), BF16),
            ((G, atoms), F32),
        ],
        10**8,
    )(cells, fraction, *split_constant(cas_matrix(freq, freq)))
    ordered, spread = call(
        functools.partial(spread_kernel, x_rows),
        [((8, atoms), F32), ((G, lanes), F32)],
        10**9,
        smem=1,
        scratch=(pltpu.VMEM((4, 8, TILE), F32),),
    )(meta, direction, tile_order, tab_x, tab_y, w_high, w_low, slope_z)
    grid = lax.all_to_all(spread, BOTH, 0, 0, tiled=True)
    last = around(direction[:2])
    applied, sums = call(
        final_field_kernel,
        [((8, atoms), F32), ((8, TILE), F32)],
        10**9,
        smem=1,
        scratch=sweep_scratch + (pltpu.VMEM((4, 8, TILE), F32),),
    )(meta, geometry, direction, *last, pairs_a, pairs_b, tile_order)
    ids = jnp.arange(G, dtype=jnp.int32)
    factor = multiplier(ids[None, :], ids[:, None], slab_index * n_space + space_index)
    planes = call(
        functools.partial(plane_kernel, (n_slab, n_space, x_rows, y_rows)),
        [((G, lanes), F32)],
        10**9,
        scratch=(pltpu.VMEM((y_rows * n_space, G), F32),),
    )(
        grid,
        factor,
        sums,
        *split_constant(wide_x.reshape(-1, G)),
        *split_constant(cas_y),
    )[0]
    returned = lax.all_to_all(planes, BOTH, 0, 0, tiled=True)
    three = ((3, atoms), F32)
    return tuple(
        call(functools.partial(finish_kernel, x_rows), [three, three, three], 10**9)(
            returned, w_high, w_low, slope_z, tab_x, tab_y, ordered, applied, dipoles, residual
        )
    )


def solution(mesh):
    in_specs = (
        P(None, BOTH),
        P(None, BOTH),
        P(None, BOTH),
        P(None, BOTH),
        P(BOTH),
        P(BOTH, None),
        P(BOTH, None),
        P(BOTH, None, None),
        P(BOTH, None),
    )
    out_specs = (P(None, BOTH), P(None, BOTH), P(None, BOTH))
    return jax.shard_map(local, mesh=mesh, in_specs=in_specs, out_specs=out_specs, check_vma=False)
```

```python
import functools
import math

import jax
import jax.numpy as jnp
import ml_dtypes
import numpy as np
from jax import lax
from jax.experimental import pallas as pl
from jax.experimental.pallas import tpu as pltpu
from jax.sharding import Mesh
from jax.sharding import PartitionSpec as P

G = 256
TILE = 128
SPACE = ("pair", "core")
BOTH = ("slab", "pair", "core")
CHIPS = ("slab", "pair")
BETA = 0.4
THOLE = 0.39
ROOT_PI = math.sqrt(math.pi)
SELF_FIELD = 4.0 * BETA**3 / (3.0 * ROOT_PI)
F32 = jnp.float32
BF16 = jnp.bfloat16
SCALED_ERFC_T = 0.45
SCALED_ERFC = (
    0.25388532876968384,
    0.25388309359550476,
    0.22827406227588654,
    0.17522020637989044,
    0.1201537474989891,
    -0.023065825924277306,
    0.14381752908229828,
    -0.3022053837776184,
    0.19167575240135193,
    -0.04163854941725731,
)
NT = (((1,), (1,)), ((), ()))
NN = (((1,), (0,)), ((), ()))
TN = (((0,), (0,)), ((), ()))
VMEM_LIMIT = 20 * 1024 * 1024


def halves(values):
    high = values.astype(BF16)
    return (high, (values - high.astype(F32)).astype(BF16))


def product(left, right, dims):
    def one(a, b):
        return lax.dot_general(a, b, dims, preferred_element_type=F32)

    return one(left[0], right[0]) + (one(left[0], right[1]) + one(left[1], right[0]))


def thirds(values):
    high = values.astype(BF16).astype(F32)
    rest = values - high
    middle = rest.astype(BF16).astype(F32)
    return jnp.concatenate([high, middle, rest - middle], 0).astype(BF16)


def selected(values, one_hot, dims):
    rows = values.shape[0]
    picked = lax.dot_general(thirds(values), one_hot, dims, preferred_element_type=F32)
    return picked[:rows] + (picked[rows : 2 * rows] + picked[2 * rows :])


def order_matrix(order_row, count):
    ids = lax.broadcasted_iota(jnp.int32, (count, count), 0)
    return jnp.where(ids == order_row, 1.0, 0.0).astype(BF16)


COUNTS_AT = 32
ORDER_AT = 36
PARITY_AT = 40


def meta_of(tile_lists, tile_counts, send_tiles, parity):
    entry = tile_lists.reshape(-1)
    remote = entry - 4
    pair = remote // 2
    pair = pair + (pair >= 4)
    along = pair // 3
    across = pair % 3
    base = jnp.where(across == 1, 4, jnp.where(across == 2 - 2 * parity, 10, 16))
    slots = jnp.where(entry < 4, entry, base + along * 2 + remote % 2)
    first, second = (send_tiles[0, 0], send_tiles[0, 1])
    third = jnp.where(
        (first != 0) & (second != 0), 0, jnp.where((first != 1) & (second != 1), 1, 2)
    )
    rest = jnp.stack([first, second, third, 6 - first - second - third, parity])
    return jnp.concatenate([slots, tile_counts.reshape(-1), rest]).astype(jnp.int32)


def call(kernel, outs, flops, smem=0, scratch=()):
    def run(*args):
        in_specs = [pl.BlockSpec(memory_space=pltpu.SMEM)] * smem
        in_specs += [pl.BlockSpec(memory_space=pltpu.VMEM)] * (len(args) - smem)
        return pl.pallas_call(
            kernel,
            out_shape=[jax.ShapeDtypeStruct(shape, dtype) for shape, dtype in outs],
            in_specs=in_specs,
            out_specs=[pl.BlockSpec(memory_space=pltpu.VMEM)] * len(outs),
            scratch_shapes=list(scratch),
            compiler_params=pltpu.CompilerParams(vmem_limit_bytes=VMEM_LIMIT),
            cost_estimate=pl.CostEstimate(
                flops=flops, bytes_accessed=1 << 20, transcendentals=0
            ),
        )(*args)

    return run


def gather_kernel(send, *refs):
    sources, (own, sent, statics), held, sems = (refs[:5], refs[5:8], refs[8:13], refs[13])
    copies = [
        pltpu.make_async_copy(source, target, sems.at[at])
        for at, (source, target) in enumerate(zip(sources, held))
    ]
    for copy in copies:
        copy.start()
    for copy in copies:
        copy.wait()
    residual, cells, fraction, alphas, order = held
    atoms = residual.shape[1]
    in_cells = cells[...].astype(F32)
    statics[0:3] = in_cells
    statics[3:6] = fraction[...]
    statics[6:8] = jnp.zeros((2, atoms), F32)
    position = in_cells + fraction[...]
    rows = jnp.concatenate(
        [position, alphas[...].reshape(1, atoms), residual[...], jnp.zeros((1, atoms), F32)], 0
    )
    picked = selected(rows, order_matrix(order[...], atoms), NN)
    for tile in range(atoms // TILE):
        own[tile] = picked[:, tile * TILE : (tile + 1) * TILE]
    for place in range(2):
        sent[place] = own[send[0, place]]


def search_rows(block):
    return block[3:4] * block[4:7]


def fill_pool(pool, extents, own, straight, inner, outer, meta):
    inner_step = jnp.where(meta[PARITY_AT] == 0, 1.0, -1.0)
    rows = lax.broadcasted_iota(jnp.int32, (8, TILE), 0)
    for tile in range(4):
        pool[tile] = own[tile]
    for base, source, step in ((4, straight, 0.0), (10, inner, inner_step), (16, outer, -inner_step)):
        for along in range(3):
            shift = jnp.where(
                rows == 0,
                float((along - 1) * extents[0]),
                jnp.where(rows == 1, step * float(extents[1]), 0.0),
            )
            for member in range(2):
                pool[base + 2 * along + member] = source[along, member] + shift


def own_columns(columns, block, count):
    turned = block.T
    for row in range(count):
        columns[row] = jnp.broadcast_to(turned[:, row : row + 1], (TILE, TILE))


def wrap_depth(depth):
    half = 0.5 * G
    return jnp.where(depth > half, depth - G, jnp.where(depth < -half, depth + G, depth))


PAIR_ROWS = 32
GROUP = 4


def pair_kernel(first_place, extents, meta, own, straight, inner, outer, pool, pairs, found, columns, totals):
    fill_pool(pool, extents, own, straight, inner, outer, meta)

    def tile_step(at, carry):
        tile = meta[ORDER_AT + first_place + at]
        block = own[tile]
        own_columns(columns, jnp.concatenate([block[:3], lax.rsqrt(block[3:4]), block[4:]], 0), 4)
        live = meta[COUNTS_AT + tile]

        def chunk_step(chunk, carry):
            start = pl.multiple_of(chunk * PAIR_ROWS, PAIR_ROWS)
            rows = pl.ds(start, PAIR_ROWS)
            shape = (PAIR_ROWS, TILE)
            ahead = lax.broadcasted_iota(jnp.int32, shape, 0) - lax.broadcasted_iota(
                jnp.int32, shape, 1
            )
            diagonal = jnp.where(ahead == -start, 1.0, 0.0)

            def group_step(group, sums):
                for member in range(GROUP):
                    entry = group * GROUP + member
                    slot = meta[tile * 8 + entry]
                    other = pool[slot]
                    itself = diagonal * jnp.where(slot == tile, 1.0, 0.0)
                    d_x = other[0:1] - columns[0, rows]
                    d_y = other[1:2] - columns[1, rows]
                    d_z = wrap_depth(other[2:3] - columns[2, rows])
                    square = d_x * d_x + d_y * d_y + d_z * d_z + itself
                    inverse = lax.rsqrt(square)
                    distance = square * inverse
                    inverse_sq = inverse * inverse
                    gauss = jnp.exp(-(BETA**2) * square)
                    stretch = 1.0 + (SCALED_ERFC_T * BETA) * distance
                    t = lax.rsqrt(stretch * stretch)
                    series = SCALED_ERFC[-1] * t + SCALED_ERFC[-2]
                    for term in SCALED_ERFC[-3::-1]:
                        series = series * t + term
                    bare_one = gauss * (series * t * inverse + 2.0 * BETA / ROOT_PI) * inverse_sq
                    bare_two = (3.0 * bare_one + (4.0 * BETA**3 / ROOT_PI) * gauss) * inverse_sq
                    damping = (square * distance) * columns[3, rows] * (THOLE * lax.rsqrt(other[3:4]))
                    decay = jnp.exp(-damping) * inverse * inverse_sq
                    keep = jnp.where(entry < live, 1.0, 0.0) * (1.0 - itself)
                    three = keep * (bare_one - decay)
                    five = keep * (bare_two - (3.0 + 3.0 * damping) * decay * inverse_sq)
                    pairs[0, at * 8 + entry, rows] = five
                    pairs[1, at * 8 + entry, rows] = three
                    v = search_rows(other)
                    along = five * (d_x * v[0:1] + d_y * v[1:2] + d_z * v[2:3])
                    sums = (
                        sums[0] + (along * d_x - three * v[0:1]),
                        sums[1] + (along * d_y - three * v[1:2]),
                        sums[2] + (along * d_z - three * v[2:3]),
                    )
                return sums

            zero = jnp.zeros(shape, F32)
            sums = lax.fori_loop(0, (live + GROUP - 1) // GROUP, group_step, (zero, zero, zero))
            for part in range(3):
                totals[part, rows] = sums[part]
            return carry

        lax.fori_loop(0, TILE // PAIR_ROWS, chunk_step, 0)
        found[at] = updated(block, totals)
        return carry

    lax.fori_loop(0, 2, tile_step, 0)


def field_rows(totals):
    return [jnp.sum(totals[part].T, axis=0, keepdims=True) for part in range(3)]


def updated(block, totals):
    alpha = block[3:4]
    field = field_rows(totals)
    rows = [alpha * (block[4 + part : 5 + part] + field[part]) for part in range(3)]
    return jnp.concatenate(rows + [jnp.zeros((5, TILE), F32)], 0)


APPLY_ROWS = 64


def fill_search(pool, own_first, own_rest, straight, inner, outer, meta):
    for place in range(4):
        pool[meta[ORDER_AT + place]] = own_first[place] if place < 2 else own_rest[place - 2]
    for base, source in ((4, straight), (10, inner), (16, outer)):
        for along in range(3):
            for member in range(2):
                pool[base + 2 * along + member] = source[along, member]


def apply_tile(meta, tile, at, pairs, geometry, pool, columns, totals):
    block = geometry[tile]
    own_columns(columns, block, 3)
    live = meta[COUNTS_AT + tile]

    def chunk_step(chunk, carry):
        rows = pl.ds(pl.multiple_of(chunk * APPLY_ROWS, APPLY_ROWS), APPLY_ROWS)

        def group_step(group, sums):
            for member in range(GROUP):
                entry = group * GROUP + member
                slot = meta[tile * 8 + entry]
                other = geometry[slot]
                v = pool[slot]
                d_x = other[0:1] - columns[0, rows]
                d_y = other[1:2] - columns[1, rows]
                d_z = wrap_depth(other[2:3] - columns[2, rows])
                three = pairs[1, at * 8 + entry, rows]
                along = pairs[0, at * 8 + entry, rows] * (d_x * v[0:1] + d_y * v[1:2] + d_z * v[2:3])
                sums = (
                    sums[0] + (along * d_x - three * v[0:1]),
                    sums[1] + (along * d_y - three * v[1:2]),
                    sums[2] + (along * d_z - three * v[2:3]),
                )
            return sums

        zero = jnp.zeros((APPLY_ROWS, TILE), F32)
        sums = lax.fori_loop(0, (live + GROUP - 1) // GROUP, group_step, (zero, zero, zero))
        for part in range(3):
            totals[part, rows] = sums[part]
        return carry

    lax.fori_loop(0, TILE // APPLY_ROWS, chunk_step, 0)


def sweep_tiles(first_place, meta, geometry, banks, found, pool, columns, totals, local=None):
    for bank, pairs in enumerate(banks):

        def tile_step(at, carry):
            tile = meta[ORDER_AT + first_place + 2 * bank + at]
            apply_tile(meta, tile, at, pairs, geometry, pool, columns, totals)
            rows = updated(geometry[tile], totals)
            found[2 * bank + at] = rows
            if local is not None:
                local[tile] = rows
            return carry

        lax.fori_loop(0, 2, tile_step, 0)


def sweep_kernel(
    first_place, meta, geometry, own_first, own_rest, straight, inner, outer, pairs, found, pool, columns, totals
):
    fill_search(pool, own_first, own_rest, straight, inner, outer, meta)
    sweep_tiles(first_place, meta, geometry, (pairs,), found, pool, columns, totals)


def direction_kernel(
    meta, geometry, own_first, own_rest, straight, inner, outer, pairs_a, pairs_b, order, found, ordered, pool, columns, totals, local
):
    fill_search(pool, own_first, own_rest, straight, inner, outer, meta)
    sweep_tiles(0, meta, geometry, (pairs_a, pairs_b), found, pool, columns, totals, local)
    in_tiles = jnp.concatenate([local[tile] for tile in range(4)], 1)
    ordered[...] = selected(in_tiles, order_matrix(order[...], order.shape[1]), NT)


def final_field_kernel(
    meta, geometry, direction, straight, inner, outer, pairs_a, pairs_b, order, applied, sums, pool, columns, totals, local
):
    atoms = order.shape[1]
    fill_search(pool, direction, direction.at[2:4], straight, inner, outer, meta)
    both = (jnp.zeros((1, TILE), F32), jnp.zeros((1, TILE), F32))
    for bank, pairs in enumerate((pairs_a, pairs_b)):

        def tile_step(at, both):
            curve, dots = both
            place = 2 * bank + at
            tile = meta[ORDER_AT + place]
            apply_tile(meta, tile, at, pairs, geometry, pool, columns, totals)
            block = geometry[tile]
            ahead = direction[place]
            field = field_rows(totals)
            rows = []
            for part in range(3):
                d = ahead[part : part + 1]
                value = d / block[3:4] - field[part] - SELF_FIELD * d
                curve = curve + d * value
                dots = dots + d * block[4 + part : 5 + part]
                rows.append(value)
            local[tile] = jnp.concatenate(rows + [jnp.zeros((5, TILE), F32)], 0)
            return (curve, dots)

        both = lax.fori_loop(0, 2, tile_step, both)
    in_tiles = jnp.concatenate([local[tile] for tile in range(4)], 1)
    applied[...] = selected(in_tiles, order_matrix(order[...], atoms), NT)
    lane = lax.broadcasted_iota(jnp.int32, (8, TILE), 1)
    curve_sum = jnp.sum(both[0], axis=1, keepdims=True)
    dot_sum = jnp.sum(both[1], axis=1, keepdims=True)
    sums[...] = jnp.where(lane == 1, curve_sum, jnp.where(lane == 2, dot_sum, 0.0))


def spline(fraction):
    centre_arg = fraction - 0.5

    def middle(u):
        return (55.0 + u * (20.0 + u * (-120.0 + u * (80.0 - 16.0 * u)))) / 96.0

    def middle_slope(u):
        return (20.0 + u * (-240.0 + u * (240.0 - 64.0 * u))) / 96.0

    def outer(u):
        w = 5.0 - 2.0 * u
        return (w * w) * (w * w) / 384.0

    def outer_slope(u):
        w = 5.0 - 2.0 * u
        return -(w * w * w) / 48.0

    sq = centre_arg * centre_arg
    weights = (
        outer(fraction + 1.5),
        middle(fraction + 0.5),
        115.0 / 192.0 - 0.625 * sq + 0.25 * sq * sq,
        middle(1.5 - fraction),
        outer(2.5 - fraction),
    )
    slopes = (
        outer_slope(fraction + 1.5),
        middle_slope(fraction + 0.5),
        -1.25 * centre_arg + centre_arg * sq,
        -middle_slope(1.5 - fraction),
        -outer_slope(2.5 - fraction),
    )
    return (weights, slopes)


def table(cell_row, values, length, wrapped):
    atoms = cell_row.shape[1]
    ids = lax.broadcasted_iota(jnp.int32, (length, atoms), 0)
    if wrapped:
        ahead = ids - cell_row + 2
        ahead = jnp.where(ahead >= G, ahead - G, jnp.where(ahead < 0, ahead + G, ahead))
    else:
        ahead = ids - cell_row
    total = jnp.zeros((length, atoms), F32)
    for step in range(5):
        total = jnp.where(ahead == step, values[step], total)
    return total


def tables_kernel(meta, mine, beside, cas_high, cas_low, tab_x, tab_y, w_high, w_low, slope_z):
    cas = (cas_high[meta[PARITY_AT]], cas_low[meta[PARITY_AT]])
    for side, statics in enumerate((mine, beside)):
        cells = statics[0:3].astype(jnp.int32)
        for dim, out in ((0, tab_x), (1, tab_y)):
            weights, slopes = spline(statics[3 + dim : 4 + dim])
            out[side, 0] = table(cells[dim : dim + 1], weights, out.shape[2], False)
            out[side, 1] = table(cells[dim : dim + 1], slopes, out.shape[2], False)
        weights, slopes = spline(statics[5:6])
        high, low = halves(product(cas, halves(table(cells[2:3], weights, G, True)), NN))
        w_high[side] = high
        w_low[side] = low
        slope_z[side] = product(cas, halves(table(cells[2:3], slopes, G, True)), NN)


def spread_part(side, d, tab_x, tab_y, w_high, w_low, slope_z):
    w_z = (w_high[side], w_low[side])
    s_z = halves(slope_z[side] * d[2:3])
    weight_x = tab_x[side, 0]
    slope_part = tab_x[side, 1] * d[0:1]
    weight_part = weight_x * d[1:2]
    sides = []
    for y in range(tab_y.shape[2]):
        w_y, s_y = (tab_y[side, 0, y : y + 1], tab_y[side, 1, y : y + 1])
        sides.append((slope_part * w_y + weight_part * s_y, weight_x * w_y))
    rows = halves(jnp.concatenate([pair[0] for pair in sides], 0))
    flat = halves(jnp.concatenate([pair[1] for pair in sides], 0))
    return product(w_z, rows, NT) + product(s_z, flat, NT)


def spread_own_kernel(ordered, tab_x, tab_y, w_high, w_low, slope_z, out):
    out[...] = spread_part(0, ordered[...], tab_x, tab_y, w_high, w_low, slope_z)


def put_lanes(out, flat):
    for row in range(8):
        out[:, row, :] = flat[:, row * TILE : (row + 1) * TILE]


def get_lanes(grid):
    return jnp.concatenate([grid[:, row, :] for row in range(8)], 1)


def spread_both_kernel(shift, meta, ordered, mine, tab_x, tab_y, w_high, w_low, slope_z, out, flat):
    theirs = spread_part(1, ordered[...], tab_x, tab_y, w_high, w_low, slope_z)
    ours = mine[...]
    width = ours.shape[1]
    even = meta[PARITY_AT] == 0
    lower = jnp.where(even, ours, theirs)
    upper = jnp.where(even, theirs, ours)
    flat[:, :shift] = lower[:, :shift]
    flat[:, shift:width] = lower[:, shift:] + upper[:, : width - shift]
    flat[:, width : width + shift] = upper[:, width - shift :]
    flat[:, width + shift :] = jnp.zeros((flat.shape[0], flat.shape[1] - width - shift), F32)
    put_lanes(out, flat)


def plane_kernel(shapes, grid, factor, sums, x_high, x_low, y_high, y_low, out, flat):
    n_slab, n_pair, x_rows, y_rows = shapes
    width = x_rows * y_rows
    flat[...] = get_lanes(grid)
    along_x = None
    for s in range(n_slab):
        block = jnp.concatenate(
            [
                flat[s * n_pair : (s + 1) * n_pair, y * x_rows : (y + 1) * x_rows]
                for y in range(y_rows)
            ],
            0,
        )
        rows = slice(s * TILE, s * TILE + x_rows)
        term = product(halves(block), (x_high[rows], x_low[rows]), NN)
        along_x = term if along_x is None else along_x + term
    cas_y = (y_high[...], y_low[...])
    spectrum = product(cas_y, halves(along_x), TN)
    scaled = spectrum * factor[...]
    energy = jnp.sum(jnp.sum(spectrum * scaled, axis=0, keepdims=True), axis=1, keepdims=True)
    back = halves(product(cas_y, halves(scaled), NN))
    planes = product(back, (x_high[...], x_low[...]), NT)
    for s in range(n_slab):
        for y in range(y_rows):
            flat[s * n_pair : (s + 1) * n_pair, y * x_rows : (y + 1) * x_rows] = planes[
                y * n_pair : (y + 1) * n_pair, s * TILE : s * TILE + x_rows
            ]
    spare = flat.shape[1] - width
    lane = lax.broadcasted_iota(jnp.int32, (1, spare), 1)
    known = jnp.concatenate([sums[0:1], jnp.zeros((1, spare - TILE), F32)], 1)
    tail = jnp.where(lane == 0, energy, known)
    flat[:, width:] = jnp.broadcast_to(tail, (flat.shape[0], spare))
    put_lanes(out, flat)


def probe_part(side, planes, tab_x, tab_y, w_high, w_low, slope_z):
    x_rows = tab_x.shape[2]
    by_weight = product(planes, (w_high[side], w_low[side]), TN)
    by_slope = product(planes, halves(slope_z[side]), TN)
    weight_x, slope_x = (tab_x[side, 0], tab_x[side, 1])
    fields = [0.0, 0.0, 0.0]
    for y in range(tab_y.shape[2]):
        rows = slice(y * x_rows, (y + 1) * x_rows)
        w_y, s_y = (tab_y[side, 0, y : y + 1], tab_y[side, 1, y : y + 1])
        weighted = by_weight[rows]
        fields[0] += w_y * jnp.sum(slope_x * weighted, axis=0, keepdims=True)
        fields[1] += s_y * jnp.sum(weight_x * weighted, axis=0, keepdims=True)
        fields[2] += w_y * jnp.sum(weight_x * by_slope[rows], axis=0, keepdims=True)
    return fields


def probe_kernel(side, shift, meta, grid, tab_x, tab_y, w_high, w_low, slope_z, out):
    matrix = get_lanes(grid)
    width = tab_x.shape[2] * tab_y.shape[2]
    low_side = 0 if side == 0 else 1
    planes = jnp.where(
        meta[PARITY_AT] == low_side, matrix[:, :width], matrix[:, shift : shift + width]
    )
    fields = probe_part(side, halves(planes), tab_x, tab_y, w_high, w_low, slope_z)
    atoms = out.shape[1]
    scalars = jnp.sum(matrix[:, width + shift :], axis=0, keepdims=True)[:, :TILE]
    padded = jnp.concatenate([scalars, jnp.zeros((1, atoms - TILE), F32)], 1)
    out[...] = jnp.concatenate(fields + [padded, jnp.zeros((4, atoms), F32)], 0)


def finish_kernel(mine, theirs, ordered, applied, dipoles, residual, next_dipoles, next_residual, direction):
    total = mine[...] + theirs[...]
    step = total[3:4, 2:3] / (total[3:4, 0:1] + total[3:4, 1:2])
    d = ordered[0:3]
    next_dipoles[...] = dipoles[...] + step * d
    next_residual[...] = residual[...] - step * (applied[0:3] + total[0:3])
    direction[...] = d


def cas_matrix(first, second):
    angles = 2.0 * np.pi / G * (np.outer(first, second) % G)
    return np.cos(angles) + np.sin(angles)


def split_constant(values):
    whole = values.astype(np.float32)
    high = whole.astype(ml_dtypes.bfloat16)
    low = (values - high.astype(np.float64)).astype(ml_dtypes.bfloat16)
    return (jnp.asarray(high), jnp.asarray(low))


def wave_factors(freq_ids):
    wrapped = jnp.where(freq_ids > G // 2, freq_ids - G, freq_ids).astype(F32) / G
    angles = 2.0 * math.pi / G * freq_ids.astype(F32)
    modulus = 115.0 / 192.0 + 19.0 / 48.0 * jnp.cos(angles) + 1.0 / 192.0 * jnp.cos(2.0 * angles)
    return (
        wrapped * wrapped,
        jnp.exp(-((math.pi / BETA) ** 2) * wrapped * wrapped) / (modulus * modulus),
    )


def multiplier(freq_x, freq_y, freq_z):
    square_x, factor_x = wave_factors(freq_x)
    square_y, factor_y = wave_factors(freq_y)
    square_z, factor_z = wave_factors(freq_z)
    square_sum = square_x + square_y + square_z
    anchor = ((freq_x == 0) & (freq_y == 0) & (freq_z == 0)).astype(F32)
    return (
        (1.0 - anchor)
        * factor_x
        * factor_y
        * factor_z
        / (math.pi * float(G) ** 3 * (square_sum + anchor))
    )


def swap_pairs(n_slab, n_space, odd):
    pairs = []
    for s in range(n_slab):
        for q in range(n_space):
            partner = (q + 1 if (q % 2 == 1) == odd else q - 1) % n_space
            pairs.append((s * n_space + q, s * n_space + partner))
    return pairs


def around(block):
    n_slab, n_space = (lax.axis_size("slab"), lax.axis_size(SPACE))
    up = [(i, (i + 1) % n_slab) for i in range(n_slab)]
    down = [(j, i) for i, j in up]
    before = lax.ppermute(block, "slab", up)
    after = lax.ppermute(block, "slab", down)
    straight = jnp.stack([before, block, after])
    inner = lax.ppermute(straight, BOTH, swap_pairs(n_slab, n_space, False))
    outer = lax.ppermute(straight, BOTH, swap_pairs(n_slab, n_space, True))
    return (straight, inner, outer)


def from_core_beside(block):
    return lax.ppermute(
        block, BOTH, swap_pairs(lax.axis_size("slab"), lax.axis_size(SPACE), False)
    )


def local(
    dipoles, residual, cells, fraction, polarizability, tile_order, send_tiles, tile_lists, tile_counts
):
    n_slab, n_space = (lax.axis_size("slab"), lax.axis_size(SPACE))
    n_pair = n_space // 2
    atoms = residual.shape[1]
    extents = (G // n_slab, G // n_space)
    x_rows = -(-(extents[0] + 4) // 8) * 8
    y_rows = extents[1] + 4
    pair_rows = 2 * extents[1] + 4
    shift = extents[1] * x_rows
    half = G // 2
    slab_index, space_index = (lax.axis_index("slab"), lax.axis_index(SPACE))
    tile_shape = ((4, 8, TILE), F32)
    two_shape = ((2, 8, TILE), F32)
    bank_shape = ((2, 16, TILE, TILE), F32)
    pool_scratch = pltpu.VMEM((22, 8, TILE), F32)
    total_scratch = pltpu.VMEM((3, TILE, TILE), F32)
    own, sent, statics = pl.pallas_call(
        gather_kernel,
        out_shape=[
            jax.ShapeDtypeStruct(*tile_shape),
            jax.ShapeDtypeStruct(*two_shape),
            jax.ShapeDtypeStruct((8, atoms), F32),
        ],
        in_specs=[pl.BlockSpec(memory_space=pltpu.SMEM)] + [pl.BlockSpec(memory_space=pltpu.HBM)] * 5,
        out_specs=[pl.BlockSpec(memory_space=pltpu.VMEM)] * 3,
        scratch_shapes=[
            pltpu.VMEM((3, atoms), F32),
            pltpu.VMEM((3, atoms), jnp.int32),
            pltpu.VMEM((3, atoms), F32),
            pltpu.VMEM((atoms,), F32),
            pltpu.VMEM((1, atoms), jnp.int32),
            pltpu.SemaphoreType.DMA((5,)),
        ],
        compiler_params=pltpu.CompilerParams(vmem_limit_bytes=VMEM_LIMIT),
    )(send_tiles, residual, cells, fraction, polarizability, tile_order)
    later = lax.optimization_barrier((tile_lists, tile_counts, send_tiles, sent))
    meta = meta_of(*later[:3], space_index % 2)
    first = around(sent)

    def pairs_of(first_place):
        return call(
            functools.partial(pair_kernel, first_place, extents),
            [((22, 8, TILE), F32), bank_shape, two_shape],
            10**9,
            smem=1,
            scratch=(pltpu.VMEM((4, TILE, TILE), F32), total_scratch),
        )(meta, own, *first)

    geometry, pairs_a, search_a = pairs_of(0)
    _, pairs_b, search_b = pairs_of(2)
    sweep_scratch = (pool_scratch, pltpu.VMEM((3, TILE, TILE), F32), total_scratch)
    second = around(search_a)

    def sweep(first_place, pairs):
        return call(
            functools.partial(sweep_kernel, first_place),
            [two_shape],
            10**8,
            smem=1,
            scratch=sweep_scratch,
        )(meta, geometry, search_a, search_b, *second, pairs)[0]

    next_a = sweep(0, pairs_a)
    next_b = sweep(2, pairs_b)
    third = around(next_a)
    local_scratch = pltpu.VMEM((4, 8, TILE), F32)
    direction, ordered = call(
        direction_kernel,
        [tile_shape, ((8, atoms), F32)],
        10**8,
        smem=1,
        scratch=sweep_scratch + (local_scratch,),
    )(meta, geometry, next_a, next_b, *third, pairs_a, pairs_b, tile_order)
    ordered_beside = from_core_beside(ordered)
    freq = np.arange(G)
    padded_x = np.stack([(s * extents[0] + np.arange(x_rows) - 2) % G for s in range(n_slab)])
    real_x = np.tile(np.arange(x_rows) < extents[0] + 4, n_slab)
    cas_x = cas_matrix(padded_x.reshape(-1), freq) * real_x[:, None]
    rows_y = (np.arange(n_pair)[None] * 2 * extents[1] + np.arange(pair_rows)[:, None] - 2) % G
    cas_y = cas_matrix(rows_y.reshape(-1), freq)
    freq_by_core = np.stack([freq[0::2], freq[1::2]])
    cas_z = cas_matrix(freq_by_core.reshape(-1), freq).reshape(2, half, G)
    wide_x = np.zeros((n_slab, TILE, G))
    wide_x[:, :x_rows] = cas_x.reshape(n_slab, x_rows, G)
    statics, _ = lax.optimization_barrier((statics, first[1]))
    tables = call(
        tables_kernel,
        [
            ((2, 2, x_rows, atoms), F32),
            ((2, 2, y_rows, atoms), F32),
            ((2, half, atoms), BF16),
            ((2, half, atoms), BF16),
            ((2, half, atoms), F32),
        ],
        10**8,
        smem=1,
    )(meta, statics, from_core_beside(statics), *split_constant(cas_z))
    message = ((half, 8, TILE), F32)
    flat_scratch = pltpu.VMEM((half, 8 * TILE), F32)
    spread_own = call(spread_own_kernel, [((half, x_rows * y_rows), F32)], 10**9)(ordered, *tables)[0]
    spread = call(
        functools.partial(spread_both_kernel, shift),
        [message],
        10**9,
        smem=1,
        scratch=(flat_scratch,),
    )(meta, ordered_beside, spread_own, *tables)[0]
    grid = lax.all_to_all(spread, CHIPS, 0, 0, tiled=True)
    last = around(direction[:2])
    applied, sums = call(
        final_field_kernel,
        [((8, atoms), F32), ((8, TILE), F32)],
        10**9,
        smem=1,
        scratch=sweep_scratch + (local_scratch,),
    )(meta, geometry, direction, *last, pairs_a, pairs_b, tile_order)
    ids = jnp.arange(G, dtype=jnp.int32)
    factor = multiplier(ids[None, :], ids[:, None], slab_index * n_space + space_index)
    planes = call(
        functools.partial(plane_kernel, (n_slab, n_pair, x_rows, pair_rows)),
        [message],
        10**9,
        scratch=(flat_scratch,),
    )(
        grid,
        factor,
        sums,
        *split_constant(wide_x.reshape(-1, G)),
        *split_constant(cas_y),
    )[0]
    returned = lax.all_to_all(planes, CHIPS, 0, 0, tiled=True)

    def probe(side):
        return call(
            functools.partial(probe_kernel, side, shift), [((8, atoms), F32)], 10**9, smem=1
        )(meta, returned, *tables)[0]

    beside = from_core_beside(probe(1))
    three = ((3, atoms), F32)
    return tuple(
        call(finish_kernel, [three, three, three], 10**6)(
            probe(0), beside, ordered, applied, dipoles, residual
        )
    )


def solution(mesh):
    slab, space = (mesh.shape["slab"], mesh.shape["space"])
    mesh = Mesh(mesh.devices.reshape(slab, space // 2, 2), BOTH)
    in_specs = (
        P(None, BOTH),
        P(None, BOTH),
        P(None, BOTH),
        P(None, BOTH),
        P(BOTH),
        P(BOTH, None),
        P(BOTH, None),
        P(BOTH, None, None),
        P(BOTH, None),
    )
    out_specs = (P(None, BOTH), P(None, BOTH), P(None, BOTH))
    return jax.shard_map(local, mesh=mesh, in_specs=in_specs, out_specs=out_specs, check_vma=False)
```

```python
import functools
import math

import jax
import jax.numpy as jnp
import ml_dtypes
import numpy as np
from jax import lax
from jax.experimental import pallas as pl
from jax.experimental.pallas import tpu as pltpu
from jax.sharding import Mesh
from jax.sharding import PartitionSpec as P

G = 256
TILE = 128
SPACE = ("pair", "core")
BOTH = ("slab", "pair", "core")
CHIPS = ("slab", "pair")
BETA = 0.4
THOLE = 0.39
ROOT_PI = math.sqrt(math.pi)
SELF_FIELD = 4.0 * BETA**3 / (3.0 * ROOT_PI)
F32 = jnp.float32
BF16 = jnp.bfloat16
SCALED_ERFC_T = 0.45
SCALED_ERFC = (
    0.25388532876968384,
    0.25388309359550476,
    0.22827406227588654,
    0.17522020637989044,
    0.1201537474989891,
    -0.023065825924277306,
    0.14381752908229828,
    -0.3022053837776184,
    0.19167575240135193,
    -0.04163854941725731,
)
NT = (((1,), (1,)), ((), ()))
NN = (((1,), (0,)), ((), ()))
TN = (((0,), (0,)), ((), ()))
SMALL_VMEM = 6 * 1024 * 1024
LARGE_VMEM = 16 * 1024 * 1024


def halves(values):
    high = values.astype(BF16)
    return (high, (values - high.astype(F32)).astype(BF16))


def product(left, right, dims):
    def one(a, b):
        return lax.dot_general(a, b, dims, preferred_element_type=F32)

    (left_dim,), (right_dim,) = dims[0]
    if left[0].shape[left_dim] % TILE:
        return one(left[0], right[0]) + (one(left[0], right[1]) + one(left[1], right[0]))
    return one(
        jnp.concatenate([left[0], left[0], left[1]], left_dim),
        jnp.concatenate([right[0], right[1], right[0]], right_dim),
    )


def thirds(values):
    high = values.astype(BF16).astype(F32)
    rest = values - high
    middle = rest.astype(BF16).astype(F32)
    return jnp.concatenate([high, middle, rest - middle], 0).astype(BF16)


def selected(values, one_hot, dims):
    rows = values.shape[0]
    picked = lax.dot_general(thirds(values), one_hot, dims, preferred_element_type=F32)
    return picked[:rows] + (picked[rows : 2 * rows] + picked[2 * rows :])


def order_matrix(order_row, count):
    ids = lax.broadcasted_iota(jnp.int32, (count, count), 0)
    return jnp.where(ids == order_row, 1.0, 0.0).astype(BF16)


COUNTS_AT = 32
ORDER_AT = 36
PARITY_AT = 40


def meta_kernel(lists, counts, send, after, meta):
    parity = lax.axis_index("core")
    for tile in range(4):

        def remap(place, carry):
            entry = lists[0, tile, place]
            remote = entry - 4
            pair = lax.shift_right_arithmetic(remote, 1)
            pair = pair + jnp.where(pair >= 4, 1, 0)
            along = jnp.where(pair >= 3, 1, 0) + jnp.where(pair >= 6, 1, 0)
            across = pair - 3 * along
            base = jnp.where(across == 1, 4, jnp.where(across == 2 - 2 * parity, 10, 16))
            slot = base + along * 2 + (remote & 1)
            meta[tile * 8 + place] = jnp.where(entry < 4, entry, slot)
            return carry

        lax.fori_loop(0, 8, remap, 0)
        meta[COUNTS_AT + tile] = counts[0, tile]
    first, second = (send[0, 0], send[0, 1])
    third = jnp.where(
        (first != 0) & (second != 0), 0, jnp.where((first != 1) & (second != 1), 1, 2)
    )
    meta[ORDER_AT] = first
    meta[ORDER_AT + 1] = second
    meta[ORDER_AT + 2] = third
    meta[ORDER_AT + 3] = 6 - first - second - third
    meta[PARITY_AT] = parity


def call(kernel, outs, flops, smem=0, scratch=(), vmem=SMALL_VMEM):
    def run(*args):
        in_specs = [pl.BlockSpec(memory_space=pltpu.SMEM)] * smem
        in_specs += [pl.BlockSpec(memory_space=pltpu.VMEM)] * (len(args) - smem)
        return pl.pallas_call(
            kernel,
            out_shape=[jax.ShapeDtypeStruct(shape, dtype) for shape, dtype in outs],
            in_specs=in_specs,
            out_specs=[pl.BlockSpec(memory_space=pltpu.VMEM)] * len(outs),
            scratch_shapes=list(scratch),
            compiler_params=pltpu.CompilerParams(vmem_limit_bytes=vmem),
            cost_estimate=pl.CostEstimate(
                flops=flops, bytes_accessed=1 << 20, transcendentals=0
            ),
        )(*args)

    return run


def gather_kernel(send, *refs):
    sources, (own, sent, statics), held, sems = (refs[:5], refs[5:8], refs[8:13], refs[13])
    copies = [
        pltpu.make_async_copy(source, target, sems.at[at])
        for at, (source, target) in enumerate(zip(sources, held))
    ]
    for copy in copies:
        copy.start()
    for copy in copies:
        copy.wait()
    residual, cells, fraction, alphas, order = held
    atoms = residual.shape[1]
    in_cells = cells[...].astype(F32)
    statics[0:3] = in_cells
    statics[3:6] = fraction[...]
    statics[6:8] = jnp.zeros((2, atoms), F32)
    position = in_cells + fraction[...]
    rows = jnp.concatenate(
        [position, alphas[...].reshape(1, atoms), residual[...], jnp.zeros((1, atoms), F32)], 0
    )
    picked = selected(rows, order_matrix(order[...], atoms), NN)
    for tile in range(atoms // TILE):
        own[tile] = picked[:, tile * TILE : (tile + 1) * TILE]
    for place in range(2):
        sent[place] = own[send[0, place]]


def search_rows(block):
    return block[3:4] * block[4:7]


def fill_pool(pool, extents, own, straight, inner, outer, meta):
    inner_step = jnp.where(meta[PARITY_AT] == 0, 1.0, -1.0)
    rows = lax.broadcasted_iota(jnp.int32, (8, TILE), 0)
    for tile in range(4):
        pool[tile] = own[tile]
    for base, source, step in ((4, straight, 0.0), (10, inner, inner_step), (16, outer, -inner_step)):
        for along in range(3):
            shift = jnp.where(
                rows == 0,
                float((along - 1) * extents[0]),
                jnp.where(rows == 1, step * float(extents[1]), 0.0),
            )
            for member in range(2):
                pool[base + 2 * along + member] = source[along, member] + shift


def own_columns(columns, block, count):
    turned = block.T
    for row in range(count):
        columns[row] = jnp.broadcast_to(turned[:, row : row + 1], (TILE, TILE))


def wrap_depth(depth):
    half = 0.5 * G
    return jnp.where(depth > half, depth - G, jnp.where(depth < -half, depth + G, depth))


PAIR_ROWS = 32
GROUP = 4


def pair_kernel(first_place, extents, meta, own, straight, inner, outer, pool, pairs, found, columns, totals):
    fill_pool(pool, extents, own, straight, inner, outer, meta)

    def tile_step(at, carry):
        tile = meta[ORDER_AT + first_place + at]
        block = own[tile]
        own_columns(columns, jnp.concatenate([block[:3], lax.rsqrt(block[3:4]), block[4:]], 0), 4)
        live = meta[COUNTS_AT + tile]

        def chunk_step(chunk, carry):
            start = pl.multiple_of(chunk * PAIR_ROWS, PAIR_ROWS)
            rows = pl.ds(start, PAIR_ROWS)
            shape = (PAIR_ROWS, TILE)
            ahead = lax.broadcasted_iota(jnp.int32, shape, 0) - lax.broadcasted_iota(
                jnp.int32, shape, 1
            )
            diagonal = jnp.where(ahead == -start, 1.0, 0.0)

            def group_step(group, sums):
                for member in range(GROUP):
                    entry = group * GROUP + member
                    slot = meta[tile * 8 + entry]
                    other = pool[slot]
                    itself = diagonal * jnp.where(slot == tile, 1.0, 0.0)
                    d_x = other[0:1] - columns[0, rows]
                    d_y = other[1:2] - columns[1, rows]
                    d_z = wrap_depth(other[2:3] - columns[2, rows])
                    square = d_x * d_x + d_y * d_y + d_z * d_z + itself
                    inverse = lax.rsqrt(square)
                    distance = square * inverse
                    inverse_sq = inverse * inverse
                    gauss = jnp.exp(-(BETA**2) * square)
                    stretch = 1.0 + (SCALED_ERFC_T * BETA) * distance
                    t = lax.rsqrt(stretch * stretch)
                    series = SCALED_ERFC[-1] * t + SCALED_ERFC[-2]
                    for term in SCALED_ERFC[-3::-1]:
                        series = series * t + term
                    bare_one = gauss * (series * t * inverse + 2.0 * BETA / ROOT_PI) * inverse_sq
                    bare_two = (3.0 * bare_one + (4.0 * BETA**3 / ROOT_PI) * gauss) * inverse_sq
                    damping = (square * distance) * columns[3, rows] * (THOLE * lax.rsqrt(other[3:4]))
                    decay = jnp.exp(-damping) * inverse * inverse_sq
                    keep = jnp.where(entry < live, 1.0, 0.0) * (1.0 - itself)
                    three = keep * (bare_one - decay)
                    five = keep * (bare_two - (3.0 + 3.0 * damping) * decay * inverse_sq)
                    pairs[0, at * 8 + entry, rows] = five
                    pairs[1, at * 8 + entry, rows] = three
                    pairs[2, at * 8 + entry, rows] = d_z
                    v = search_rows(other)
                    along = five * (d_x * v[0:1] + d_y * v[1:2] + d_z * v[2:3])
                    sums = (
                        sums[0] + (along * d_x - three * v[0:1]),
                        sums[1] + (along * d_y - three * v[1:2]),
                        sums[2] + (along * d_z - three * v[2:3]),
                    )
                return sums

            zero = jnp.zeros(shape, F32)
            sums = lax.fori_loop(0, (live + GROUP - 1) // GROUP, group_step, (zero, zero, zero))
            for part in range(3):
                totals[part, rows] = sums[part]
            return carry

        lax.fori_loop(0, TILE // PAIR_ROWS, chunk_step, 0)
        found[at] = updated(block, totals)
        return carry

    lax.fori_loop(0, 2, tile_step, 0)


def field_rows(totals):
    return [jnp.sum(totals[part].T, axis=0, keepdims=True) for part in range(3)]


def updated(block, totals):
    alpha = block[3:4]
    field = field_rows(totals)
    rows = [alpha * (block[4 + part : 5 + part] + field[part]) for part in range(3)]
    return jnp.concatenate(rows + [jnp.zeros((5, TILE), F32)], 0)


APPLY_ROWS = 64


def fill_search(pool, own_first, own_rest, straight, inner, outer, meta):
    for place in range(4):
        pool[meta[ORDER_AT + place]] = own_first[place] if place < 2 else own_rest[place - 2]
    for base, source in ((4, straight), (10, inner), (16, outer)):
        for along in range(3):
            for member in range(2):
                pool[base + 2 * along + member] = source[along, member]


def apply_tile(meta, tile, at, pairs, geometry, pool, columns, totals):
    block = geometry[tile]
    own_columns(columns, block, 2)
    live = meta[COUNTS_AT + tile]

    def chunk_step(chunk, carry):
        rows = pl.ds(pl.multiple_of(chunk * APPLY_ROWS, APPLY_ROWS), APPLY_ROWS)

        def group_step(group, sums):
            for member in range(GROUP):
                entry = group * GROUP + member
                slot = meta[tile * 8 + entry]
                other = geometry[slot]
                v = pool[slot]
                d_x = other[0:1] - columns[0, rows]
                d_y = other[1:2] - columns[1, rows]
                d_z = pairs[2, at * 8 + entry, rows]
                three = pairs[1, at * 8 + entry, rows]
                along = pairs[0, at * 8 + entry, rows] * (d_x * v[0:1] + d_y * v[1:2] + d_z * v[2:3])
                sums = (
                    sums[0] + (along * d_x - three * v[0:1]),
                    sums[1] + (along * d_y - three * v[1:2]),
                    sums[2] + (along * d_z - three * v[2:3]),
                )
            return sums

        zero = jnp.zeros((APPLY_ROWS, TILE), F32)
        sums = lax.fori_loop(0, (live + GROUP - 1) // GROUP, group_step, (zero, zero, zero))
        for part in range(3):
            totals[part, rows] = sums[part]
        return carry

    lax.fori_loop(0, TILE // APPLY_ROWS, chunk_step, 0)


def sweep_tiles(first_place, meta, geometry, banks, found, pool, columns, totals, local=None):
    for bank, pairs in enumerate(banks):

        def tile_step(at, carry):
            tile = meta[ORDER_AT + first_place + 2 * bank + at]
            apply_tile(meta, tile, at, pairs, geometry, pool, columns, totals)
            rows = updated(geometry[tile], totals)
            found[2 * bank + at] = rows
            if local is not None:
                local[tile] = rows
            return carry

        lax.fori_loop(0, 2, tile_step, 0)


def sweep_kernel(
    first_place, meta, geometry, own_first, own_rest, straight, inner, outer, pairs, found, pool, columns, totals
):
    fill_search(pool, own_first, own_rest, straight, inner, outer, meta)
    sweep_tiles(first_place, meta, geometry, (pairs,), found, pool, columns, totals)


def direction_kernel(
    meta, geometry, own_first, own_rest, straight, inner, outer, pairs_a, pairs_b, order, found, ordered, pool, columns, totals, local
):
    fill_search(pool, own_first, own_rest, straight, inner, outer, meta)
    sweep_tiles(0, meta, geometry, (pairs_a, pairs_b), found, pool, columns, totals, local)
    in_tiles = jnp.concatenate([local[tile] for tile in range(4)], 1)
    ordered[...] = selected(in_tiles, order_matrix(order[...], order.shape[1]), NT)


def final_field_kernel(
    meta, geometry, direction, straight, inner, outer, pairs_a, pairs_b, order, applied, sums, pool, columns, totals, local
):
    atoms = order.shape[1]
    fill_search(pool, direction, direction.at[2:4], straight, inner, outer, meta)
    both = (jnp.zeros((1, TILE), F32), jnp.zeros((1, TILE), F32))
    for bank, pairs in enumerate((pairs_a, pairs_b)):

        def tile_step(at, both):
            curve, dots = both
            place = 2 * bank + at
            tile = meta[ORDER_AT + place]
            apply_tile(meta, tile, at, pairs, geometry, pool, columns, totals)
            block = geometry[tile]
            ahead = direction[place]
            field = field_rows(totals)
            rows = []
            for part in range(3):
                d = ahead[part : part + 1]
                value = d / block[3:4] - field[part] - SELF_FIELD * d
                curve = curve + d * value
                dots = dots + d * block[4 + part : 5 + part]
                rows.append(value)
            local[tile] = jnp.concatenate(rows + [jnp.zeros((5, TILE), F32)], 0)
            return (curve, dots)

        both = lax.fori_loop(0, 2, tile_step, both)
    in_tiles = jnp.concatenate([local[tile] for tile in range(4)], 1)
    applied[...] = selected(in_tiles, order_matrix(order[...], atoms), NT)
    lane = lax.broadcasted_iota(jnp.int32, (8, TILE), 1)
    curve_sum = jnp.sum(both[0], axis=1, keepdims=True)
    dot_sum = jnp.sum(both[1], axis=1, keepdims=True)
    sums[...] = jnp.where(lane == 1, curve_sum, jnp.where(lane == 2, dot_sum, 0.0))


def spline(fraction):
    centre_arg = fraction - 0.5

    def middle(u):
        return (55.0 + u * (20.0 + u * (-120.0 + u * (80.0 - 16.0 * u)))) / 96.0

    def middle_slope(u):
        return (20.0 + u * (-240.0 + u * (240.0 - 64.0 * u))) / 96.0

    def outer(u):
        w = 5.0 - 2.0 * u
        return (w * w) * (w * w) / 384.0

    def outer_slope(u):
        w = 5.0 - 2.0 * u
        return -(w * w * w) / 48.0

    sq = centre_arg * centre_arg
    weights = (
        outer(fraction + 1.5),
        middle(fraction + 0.5),
        115.0 / 192.0 - 0.625 * sq + 0.25 * sq * sq,
        middle(1.5 - fraction),
        outer(2.5 - fraction),
    )
    slopes = (
        outer_slope(fraction + 1.5),
        middle_slope(fraction + 0.5),
        -1.25 * centre_arg + centre_arg * sq,
        -middle_slope(1.5 - fraction),
        -outer_slope(2.5 - fraction),
    )
    return (weights, slopes)


def table(cell_row, values, length, wrapped):
    atoms = cell_row.shape[1]
    ids = lax.broadcasted_iota(jnp.int32, (length, atoms), 0)
    if wrapped:
        ahead = ids - cell_row + 2
        ahead = jnp.where(ahead >= G, ahead - G, jnp.where(ahead < 0, ahead + G, ahead))
    else:
        ahead = ids - cell_row
    total = jnp.zeros((length, atoms), F32)
    for step in range(5):
        total = jnp.where(ahead == step, values[step], total)
    return total


def tables_kernel(meta, mine, beside, cas_high, cas_low, tab_x, tab_y, w_high, w_low, slope_z):
    cas = (cas_high[meta[PARITY_AT]], cas_low[meta[PARITY_AT]])
    for side, statics in enumerate((mine, beside)):
        cells = statics[0:3].astype(jnp.int32)
        for dim, out in ((0, tab_x), (1, tab_y)):
            weights, slopes = spline(statics[3 + dim : 4 + dim])
            out[side, 0] = table(cells[dim : dim + 1], weights, out.shape[2], False)
            out[side, 1] = table(cells[dim : dim + 1], slopes, out.shape[2], False)
        weights, slopes = spline(statics[5:6])
        high, low = halves(product(cas, halves(table(cells[2:3], weights, G, True)), NN))
        w_high[side] = high
        w_low[side] = low
        slope_z[side] = product(cas, halves(table(cells[2:3], slopes, G, True)), NN)


def spread_part(side, d, tab_x, tab_y, w_high, w_low, slope_z):
    w_z = (w_high[side], w_low[side])
    s_z = halves(slope_z[side] * d[2:3])
    weight_x = tab_x[side, 0]
    slope_part = tab_x[side, 1] * d[0:1]
    weight_part = weight_x * d[1:2]
    sides = []
    for y in range(tab_y.shape[2]):
        w_y, s_y = (tab_y[side, 0, y : y + 1], tab_y[side, 1, y : y + 1])
        sides.append((slope_part * w_y + weight_part * s_y, weight_x * w_y))
    rows = halves(jnp.concatenate([pair[0] for pair in sides], 0))
    flat = halves(jnp.concatenate([pair[1] for pair in sides], 0))
    return product(w_z, rows, NT) + product(s_z, flat, NT)


def spread_own_kernel(ordered, tab_x, tab_y, w_high, w_low, slope_z, out):
    out[...] = spread_part(0, ordered[...], tab_x, tab_y, w_high, w_low, slope_z)


def put_lanes(out, flat):
    for row in range(8):
        out[:, row, :] = flat[:, row * TILE : (row + 1) * TILE]


def get_lanes(grid):
    return jnp.concatenate([grid[:, row, :] for row in range(8)], 1)


def spread_both_kernel(shift, meta, ordered, mine, tab_x, tab_y, w_high, w_low, slope_z, out, flat):
    theirs = spread_part(1, ordered[...], tab_x, tab_y, w_high, w_low, slope_z)
    ours = mine[...]
    width = ours.shape[1]
    even = meta[PARITY_AT] == 0
    lower = jnp.where(even, ours, theirs)
    upper = jnp.where(even, theirs, ours)
    flat[:, :shift] = lower[:, :shift]
    flat[:, shift:width] = lower[:, shift:] + upper[:, : width - shift]
    flat[:, width : width + shift] = upper[:, width - shift :]
    flat[:, width + shift :] = jnp.zeros((flat.shape[0], flat.shape[1] - width - shift), F32)
    put_lanes(out, flat)


def plane_kernel(shapes, grid, factor, sums, x_high, x_low, y_high, y_low, out, flat):
    n_slab, n_pair, x_rows, y_rows = shapes
    width = x_rows * y_rows
    flat[...] = get_lanes(grid)
    along_x = None
    for s in range(n_slab):
        block = jnp.concatenate(
            [
                flat[s * n_pair : (s + 1) * n_pair, y * x_rows : (y + 1) * x_rows]
                for y in range(y_rows)
            ],
            0,
        )
        rows = slice(s * TILE, s * TILE + x_rows)
        term = product(halves(block), (x_high[rows], x_low[rows]), NN)
        along_x = term if along_x is None else along_x + term
    cas_y = (y_high[...], y_low[...])
    spectrum = product(cas_y, halves(along_x), TN)
    scaled = spectrum * factor[...]
    energy = jnp.sum(jnp.sum(spectrum * scaled, axis=0, keepdims=True), axis=1, keepdims=True)
    back = halves(product(cas_y, halves(scaled), NN))
    planes = product(back, (x_high[...], x_low[...]), NT)
    for s in range(n_slab):
        for y in range(y_rows):
            flat[s * n_pair : (s + 1) * n_pair, y * x_rows : (y + 1) * x_rows] = planes[
                y * n_pair : (y + 1) * n_pair, s * TILE : s * TILE + x_rows
            ]
    spare = flat.shape[1] - width
    lane = lax.broadcasted_iota(jnp.int32, (1, spare), 1)
    known = jnp.concatenate([sums[0:1], jnp.zeros((1, spare - TILE), F32)], 1)
    tail = jnp.where(lane == 0, energy, known)
    flat[:, width:] = jnp.broadcast_to(tail, (flat.shape[0], spare))
    put_lanes(out, flat)


def probe_part(side, planes, tab_x, tab_y, w_high, w_low, slope_z):
    x_rows = tab_x.shape[2]
    by_weight = product(planes, (w_high[side], w_low[side]), TN)
    by_slope = product(planes, halves(slope_z[side]), TN)
    weight_x, slope_x = (tab_x[side, 0], tab_x[side, 1])
    fields = [0.0, 0.0, 0.0]
    for y in range(tab_y.shape[2]):
        rows = slice(y * x_rows, (y + 1) * x_rows)
        w_y, s_y = (tab_y[side, 0, y : y + 1], tab_y[side, 1, y : y + 1])
        weighted = by_weight[rows]
        fields[0] += w_y * jnp.sum(slope_x * weighted, axis=0, keepdims=True)
        fields[1] += s_y * jnp.sum(weight_x * weighted, axis=0, keepdims=True)
        fields[2] += w_y * jnp.sum(weight_x * by_slope[rows], axis=0, keepdims=True)
    return fields


def probe_kernel(side, shift, meta, grid, tab_x, tab_y, w_high, w_low, slope_z, out):
    matrix = get_lanes(grid)
    width = tab_x.shape[2] * tab_y.shape[2]
    low_side = 0 if side == 0 else 1
    planes = jnp.where(
        meta[PARITY_AT] == low_side, matrix[:, :width], matrix[:, shift : shift + width]
    )
    fields = probe_part(side, halves(planes), tab_x, tab_y, w_high, w_low, slope_z)
    atoms = out.shape[1]
    scalars = jnp.sum(matrix[:, width + shift :], axis=0, keepdims=True)[:, :TILE]
    padded = jnp.concatenate([scalars, jnp.zeros((1, atoms - TILE), F32)], 1)
    out[...] = jnp.concatenate(fields + [padded, jnp.zeros((4, atoms), F32)], 0)


def finish_kernel(mine, theirs, ordered, applied, dipoles, residual, next_dipoles, next_residual, direction):
    total = mine[...] + theirs[...]
    step = total[3:4, 2:3] / (total[3:4, 0:1] + total[3:4, 1:2])
    d = ordered[0:3]
    next_dipoles[...] = dipoles[...] + step * d
    next_residual[...] = residual[...] - step * (applied[0:3] + total[0:3])
    direction[...] = d


def cas_matrix(first, second):
    angles = 2.0 * np.pi / G * (np.outer(first, second) % G)
    return np.cos(angles) + np.sin(angles)


def split_constant(values):
    whole = values.astype(np.float32)
    high = whole.astype(ml_dtypes.bfloat16)
    low = (values - high.astype(np.float64)).astype(ml_dtypes.bfloat16)
    return (jnp.asarray(high), jnp.asarray(low))


def wave_factors(freq_ids):
    wrapped = jnp.where(freq_ids > G // 2, freq_ids - G, freq_ids).astype(F32) / G
    angles = 2.0 * math.pi / G * freq_ids.astype(F32)
    modulus = 115.0 / 192.0 + 19.0 / 48.0 * jnp.cos(angles) + 1.0 / 192.0 * jnp.cos(2.0 * angles)
    return (
        wrapped * wrapped,
        jnp.exp(-((math.pi / BETA) ** 2) * wrapped * wrapped) / (modulus * modulus),
    )


def multiplier(freq_x, freq_y, freq_z):
    square_x, factor_x = wave_factors(freq_x)
    square_y, factor_y = wave_factors(freq_y)
    square_z, factor_z = wave_factors(freq_z)
    square_sum = square_x + square_y + square_z
    anchor = ((freq_x == 0) & (freq_y == 0) & (freq_z == 0)).astype(F32)
    return (
        (1.0 - anchor)
        * factor_x
        * factor_y
        * factor_z
        / (math.pi * float(G) ** 3 * (square_sum + anchor))
    )


def swap_pairs(n_slab, n_space, odd):
    pairs = []
    for s in range(n_slab):
        for q in range(n_space):
            partner = (q + 1 if (q % 2 == 1) == odd else q - 1) % n_space
            pairs.append((s * n_space + q, s * n_space + partner))
    return pairs


def along_slab(block):
    n_slab = lax.axis_size("slab")
    up = [(i, (i + 1) % n_slab) for i in range(n_slab)]
    down = [(j, i) for i, j in up]
    before = lax.ppermute(block, "slab", up)
    after = lax.ppermute(block, "slab", down)
    return jnp.stack([before, block, after])


def across_space(straight):
    n_slab, n_space = (lax.axis_size("slab"), lax.axis_size(SPACE))
    inner = lax.ppermute(straight, BOTH, swap_pairs(n_slab, n_space, False))
    outer = lax.ppermute(straight, BOTH, swap_pairs(n_slab, n_space, True))
    return (straight, inner, outer)


def around(block):
    return across_space(along_slab(block))


def from_core_beside(block):
    return lax.ppermute(
        block, BOTH, swap_pairs(lax.axis_size("slab"), lax.axis_size(SPACE), False)
    )


def local(
    dipoles, residual, cells, fraction, polarizability, tile_order, send_tiles, tile_lists, tile_counts
):
    n_slab, n_space = (lax.axis_size("slab"), lax.axis_size(SPACE))
    n_pair = n_space // 2
    atoms = residual.shape[1]
    extents = (G // n_slab, G // n_space)
    x_rows = -(-(extents[0] + 4) // 8) * 8
    y_rows = extents[1] + 4
    pair_rows = 2 * extents[1] + 4
    shift = extents[1] * x_rows
    half = G // 2
    slab_index, space_index = (lax.axis_index("slab"), lax.axis_index(SPACE))
    tile_shape = ((4, 8, TILE), F32)
    two_shape = ((2, 8, TILE), F32)
    bank_shape = ((3, 16, TILE, TILE), F32)
    pool_scratch = pltpu.VMEM((22, 8, TILE), F32)
    total_scratch = pltpu.VMEM((3, TILE, TILE), F32)
    own, sent, statics = pl.pallas_call(
        gather_kernel,
        out_shape=[
            jax.ShapeDtypeStruct(*tile_shape),
            jax.ShapeDtypeStruct(*two_shape),
            jax.ShapeDtypeStruct((8, atoms), F32),
        ],
        in_specs=[pl.BlockSpec(memory_space=pltpu.SMEM)] + [pl.BlockSpec(memory_space=pltpu.HBM)] * 5,
        out_specs=[pl.BlockSpec(memory_space=pltpu.VMEM)] * 3,
        scratch_shapes=[
            pltpu.VMEM((3, atoms), F32),
            pltpu.VMEM((3, atoms), jnp.int32),
            pltpu.VMEM((3, atoms), F32),
            pltpu.VMEM((atoms,), F32),
            pltpu.VMEM((1, atoms), jnp.int32),
            pltpu.SemaphoreType.DMA((5,)),
        ],
        compiler_params=pltpu.CompilerParams(vmem_limit_bytes=SMALL_VMEM),
    )(
        send_tiles,
        *[
            pltpu.with_memory_space_constraint(array, pltpu.HBM)
            for array in (residual, cells, fraction, polarizability, tile_order)
        ],
    )
    smem, anywhere = (pl.BlockSpec(memory_space=pltpu.SMEM), pl.BlockSpec(memory_space=pltpu.HBM))
    meta = pl.pallas_call(
        meta_kernel,
        out_shape=jax.ShapeDtypeStruct((48,), jnp.int32),
        in_specs=[smem, smem, smem, pl.BlockSpec(memory_space=pltpu.VMEM)],
        out_specs=smem,
        cost_estimate=pl.CostEstimate(flops=10**8, bytes_accessed=1 << 20, transcendentals=0),
    )(tile_lists, tile_counts, send_tiles, sent)
    first = around(sent)

    def pairs_of(first_place):
        return call(
            functools.partial(pair_kernel, first_place, extents),
            [((22, 8, TILE), F32), bank_shape, two_shape],
            10**9,
            smem=1,
            scratch=(pltpu.VMEM((4, TILE, TILE), F32), total_scratch),
        )(meta, own, *first)

    geometry, pairs_a, search_a = pairs_of(0)
    _, pairs_b, search_b = pairs_of(2)
    sweep_scratch = (pool_scratch, pltpu.VMEM((3, TILE, TILE), F32), total_scratch)
    second = around(search_a)

    def sweep(first_place, pairs):
        return call(
            functools.partial(sweep_kernel, first_place),
            [two_shape],
            10**8,
            smem=1,
            scratch=sweep_scratch,
        )(meta, geometry, search_a, search_b, *second, pairs)[0]

    next_a = sweep(0, pairs_a)
    next_b = sweep(2, pairs_b)
    third = around(next_a)
    local_scratch = pltpu.VMEM((4, 8, TILE), F32)
    direction, ordered = call(
        direction_kernel,
        [tile_shape, ((8, atoms), F32)],
        10**8,
        smem=1,
        scratch=sweep_scratch + (local_scratch,),
    )(meta, geometry, next_a, next_b, *third, pairs_a, pairs_b, tile_order)
    ordered_beside = from_core_beside(ordered)
    freq = np.arange(G)
    padded_x = np.stack([(s * extents[0] + np.arange(x_rows) - 2) % G for s in range(n_slab)])
    real_x = np.tile(np.arange(x_rows) < extents[0] + 4, n_slab)
    cas_x = cas_matrix(padded_x.reshape(-1), freq) * real_x[:, None]
    rows_y = (np.arange(n_pair)[None] * 2 * extents[1] + np.arange(pair_rows)[:, None] - 2) % G
    cas_y = cas_matrix(rows_y.reshape(-1), freq)
    freq_by_core = np.stack([freq[0::2], freq[1::2]])
    cas_z = cas_matrix(freq_by_core.reshape(-1), freq).reshape(2, half, G)
    wide_x = np.zeros((n_slab, TILE, G))
    wide_x[:, :x_rows] = cas_x.reshape(n_slab, x_rows, G)
    statics, _ = lax.optimization_barrier((statics, first[1]))
    tables = call(
        tables_kernel,
        [
            ((2, 2, x_rows, atoms), F32),
            ((2, 2, y_rows, atoms), F32),
            ((2, half, atoms), BF16),
            ((2, half, atoms), BF16),
            ((2, half, atoms), F32),
        ],
        10**8,
        smem=1,
        vmem=LARGE_VMEM,
    )(meta, statics, from_core_beside(statics), *split_constant(cas_z))
    message = ((half, 8, TILE), F32)
    flat_scratch = pltpu.VMEM((half, 8 * TILE), F32)
    spread_own = call(spread_own_kernel, [((half, x_rows * y_rows), F32)], 10**9, vmem=LARGE_VMEM)(ordered, *tables)[0]
    spread = call(
        functools.partial(spread_both_kernel, shift),
        [message],
        10**9,
        smem=1,
        scratch=(flat_scratch,),
        vmem=LARGE_VMEM,
    )(meta, ordered_beside, spread_own, *tables)[0]
    spread, straight = lax.optimization_barrier((spread, along_slab(direction[:2])))
    grid = lax.all_to_all(spread, CHIPS, 0, 0, tiled=True)
    last = across_space(straight)
    applied, sums = call(
        final_field_kernel,
        [((8, atoms), F32), ((8, TILE), F32)],
        10**9,
        smem=1,
        scratch=sweep_scratch + (local_scratch,),
    )(meta, geometry, direction, *last, pairs_a, pairs_b, tile_order)
    ids = jnp.arange(G, dtype=jnp.int32)
    factor = multiplier(ids[None, :], ids[:, None], slab_index * n_space + space_index)
    planes = call(
        functools.partial(plane_kernel, (n_slab, n_pair, x_rows, pair_rows)),
        [message],
        10**9,
        scratch=(flat_scratch,),
        vmem=LARGE_VMEM,
    )(
        grid,
        factor,
        sums,
        *split_constant(wide_x.reshape(-1, G)),
        *split_constant(cas_y),
    )[0]
    returned = lax.all_to_all(planes, CHIPS, 0, 0, tiled=True)

    def probe(side):
        return call(
            functools.partial(probe_kernel, side, shift), [((8, atoms), F32)], 10**9, smem=1, vmem=LARGE_VMEM
        )(meta, returned, *tables)[0]

    beside = from_core_beside(probe(1))
    three = ((3, atoms), F32)
    return tuple(
        call(finish_kernel, [three, three, three], 10**6)(
            probe(0), beside, ordered, applied, dipoles, residual
        )
    )


def solution(mesh):
    slab, space = (mesh.shape["slab"], mesh.shape["space"])
    mesh = Mesh(mesh.devices.reshape(slab, space // 2, 2), BOTH)
    in_specs = (
        P(None, BOTH),
        P(None, BOTH),
        P(None, BOTH),
        P(None, BOTH),
        P(BOTH),
        P(BOTH, None),
        P(BOTH, None),
        P(BOTH, None, None),
        P(BOTH, None),
    )
    out_specs = (P(None, BOTH), P(None, BOTH), P(None, BOTH))
    return jax.shard_map(local, mesh=mesh, in_specs=in_specs, out_specs=out_specs, check_vma=False)
```

```python
import functools
import math

import jax
import jax.numpy as jnp
import ml_dtypes
import numpy as np
from jax import lax
from jax.experimental import pallas as pl
from jax.experimental.pallas import tpu as pltpu
from jax.sharding import Mesh
from jax.sharding import PartitionSpec as P

G = 256
TILE = 128
SPACE = ("pair", "core")
BOTH = ("slab", "pair", "core")
CHIPS = ("slab", "pair")
BETA = 0.4
THOLE = 0.39
ROOT_PI = math.sqrt(math.pi)
SELF_FIELD = 4.0 * BETA**3 / (3.0 * ROOT_PI)
F32 = jnp.float32
BF16 = jnp.bfloat16
SCALED_ERFC_T = 0.45
SCALED_ERFC = (
    0.25388532876968384,
    0.25388309359550476,
    0.22827406227588654,
    0.17522020637989044,
    0.1201537474989891,
    -0.023065825924277306,
    0.14381752908229828,
    -0.3022053837776184,
    0.19167575240135193,
    -0.04163854941725731,
)
NT = (((1,), (1,)), ((), ()))
NN = (((1,), (0,)), ((), ()))
TN = (((0,), (0,)), ((), ()))
SMALL_VMEM = 6 * 1024 * 1024
LARGE_VMEM = 16 * 1024 * 1024


def halves(values):
    high = values.astype(BF16)
    return (high, (values - high.astype(F32)).astype(BF16))


def product(left, right, dims):
    def one(a, b):
        return lax.dot_general(a, b, dims, preferred_element_type=F32)

    (left_dim,), (right_dim,) = dims[0]
    if left[0].shape[left_dim] % TILE:
        return one(left[0], right[0]) + (one(left[0], right[1]) + one(left[1], right[0]))
    return one(
        jnp.concatenate([left[0], left[0], left[1]], left_dim),
        jnp.concatenate([right[0], right[1], right[0]], right_dim),
    )


def thirds(values):
    high = values.astype(BF16).astype(F32)
    rest = values - high
    middle = rest.astype(BF16).astype(F32)
    return jnp.concatenate([high, middle, rest - middle], 0).astype(BF16)


def selected(values, one_hot, dims):
    rows = values.shape[0]
    picked = lax.dot_general(thirds(values), one_hot, dims, preferred_element_type=F32)
    return picked[:rows] + (picked[rows : 2 * rows] + picked[2 * rows :])


def order_matrix(order_row, count):
    ids = lax.broadcasted_iota(jnp.int32, (count, count), 0)
    return jnp.where(ids == order_row, 1.0, 0.0).astype(BF16)


COUNTS_AT = 32
ORDER_AT = 36
PARITY_AT = 40


def meta_kernel(lists, counts, send, after, meta):
    parity = lax.axis_index("core")
    for tile in range(4):

        def remap(place, carry):
            entry = lists[0, tile, place]
            remote = entry - 4
            pair = lax.shift_right_arithmetic(remote, 1)
            pair = pair + jnp.where(pair >= 4, 1, 0)
            along = jnp.where(pair >= 3, 1, 0) + jnp.where(pair >= 6, 1, 0)
            across = pair - 3 * along
            base = jnp.where(across == 1, 4, jnp.where(across == 2 - 2 * parity, 10, 16))
            slot = base + along * 2 + (remote & 1)
            meta[tile * 8 + place] = jnp.where(entry < 4, entry, slot)
            return carry

        lax.fori_loop(0, 8, remap, 0)
        meta[COUNTS_AT + tile] = counts[0, tile]
    first, second = (send[0, 0], send[0, 1])
    third = jnp.where(
        (first != 0) & (second != 0), 0, jnp.where((first != 1) & (second != 1), 1, 2)
    )
    meta[ORDER_AT] = first
    meta[ORDER_AT + 1] = second
    meta[ORDER_AT + 2] = third
    meta[ORDER_AT + 3] = 6 - first - second - third
    meta[PARITY_AT] = parity


def call(kernel, outs, flops, smem=0, scratch=(), vmem=SMALL_VMEM, hbm=0):
    def run(*args):
        kept = len(args) - hbm
        args = args[:kept] + tuple(
            pltpu.with_memory_space_constraint(array, pltpu.HBM) for array in args[kept:]
        )
        in_specs = [pl.BlockSpec(memory_space=pltpu.SMEM)] * smem
        in_specs += [pl.BlockSpec(memory_space=pltpu.VMEM)] * (kept - smem)
        in_specs += [pl.BlockSpec(memory_space=pltpu.HBM)] * hbm
        return pl.pallas_call(
            kernel,
            out_shape=[jax.ShapeDtypeStruct(shape, dtype) for shape, dtype in outs],
            in_specs=in_specs,
            out_specs=[pl.BlockSpec(memory_space=pltpu.VMEM)] * len(outs),
            scratch_shapes=list(scratch),
            compiler_params=pltpu.CompilerParams(vmem_limit_bytes=vmem),
            cost_estimate=pl.CostEstimate(
                flops=flops, bytes_accessed=1 << 20, transcendentals=0
            ),
        )(*args)

    return run


def gather_kernel(send, *refs):
    sources, (own, sent, bundle), held, sems = (refs[:5], refs[5:8], refs[8:13], refs[13])
    copies = [
        pltpu.make_async_copy(source, target, sems.at[at])
        for at, (source, target) in enumerate(zip(sources, held))
    ]
    for copy in copies:
        copy.start()
    for copy in copies:
        copy.wait()
    residual, cells, fraction, alphas, order = held
    atoms = residual.shape[1]
    in_cells = cells[...].astype(F32)
    bundle[0:3, :atoms] = in_cells
    bundle[3:6, :atoms] = fraction[...]
    bundle[6:8, :atoms] = jnp.zeros((2, atoms), F32)
    position = in_cells + fraction[...]
    rows = jnp.concatenate(
        [position, alphas[...].reshape(1, atoms), residual[...], jnp.zeros((1, atoms), F32)], 0
    )
    picked = selected(rows, order_matrix(order[...], atoms), NN)
    for tile in range(atoms // TILE):
        own[tile] = picked[:, tile * TILE : (tile + 1) * TILE]
    for place in range(2):
        block = own[send[0, place]]
        sent[place] = block
        bundle[:, atoms + place * TILE : atoms + (place + 1) * TILE] = block


def search_rows(block):
    return block[3:4] * block[4:7]


def fill_pool(pool, extents, own, level, before, after, meta):
    inner_step = jnp.where(meta[PARITY_AT] == 0, 1.0, -1.0)
    rows = lax.broadcasted_iota(jnp.int32, (8, TILE), 0)
    for tile in range(4):
        pool[tile] = own[tile]
    for along, source in enumerate((before, level, after)):
        for kind, step in enumerate((0.0, inner_step, -inner_step)):
            shift = jnp.where(
                rows == 0,
                float((along - 1) * extents[0]),
                jnp.where(rows == 1, step * float(extents[1]), 0.0),
            )
            for member in range(2):
                pool[4 + 6 * kind + 2 * along + member] = source[kind, member] + shift


def own_columns(columns, block, count):
    turned = block.T
    for row in range(count):
        columns[row] = jnp.broadcast_to(turned[:, row : row + 1], (TILE, TILE))


def wrap_depth(depth):
    half = 0.5 * G
    return jnp.where(depth > half, depth - G, jnp.where(depth < -half, depth + G, depth))


PAIR_ROWS = 32
GROUP = 4


def pair_kernel(first_place, extents, meta, own, level, before, after, pool, pairs, found, columns, totals):
    fill_pool(pool, extents, own, level, before, after, meta)

    def tile_step(at, carry):
        tile = meta[ORDER_AT + first_place + at]
        block = own[tile]
        own_columns(columns, jnp.concatenate([block[:3], lax.rsqrt(block[3:4]), block[4:]], 0), 4)
        live = meta[COUNTS_AT + tile]

        def chunk_step(chunk, carry):
            start = pl.multiple_of(chunk * PAIR_ROWS, PAIR_ROWS)
            rows = pl.ds(start, PAIR_ROWS)
            shape = (PAIR_ROWS, TILE)
            ahead = lax.broadcasted_iota(jnp.int32, shape, 0) - lax.broadcasted_iota(
                jnp.int32, shape, 1
            )
            diagonal = jnp.where(ahead == -start, 1.0, 0.0)

            def group_step(group, sums):
                for member in range(GROUP):
                    entry = group * GROUP + member
                    slot = meta[tile * 8 + entry]
                    other = pool[slot]
                    itself = diagonal * jnp.where(slot == tile, 1.0, 0.0)
                    d_x = other[0:1] - columns[0, rows]
                    d_y = other[1:2] - columns[1, rows]
                    d_z = wrap_depth(other[2:3] - columns[2, rows])
                    square = d_x * d_x + d_y * d_y + d_z * d_z + itself
                    inverse = lax.rsqrt(square)
                    distance = square * inverse
                    inverse_sq = inverse * inverse
                    gauss = jnp.exp(-(BETA**2) * square)
                    stretch = 1.0 + (SCALED_ERFC_T * BETA) * distance
                    t = lax.rsqrt(stretch * stretch)
                    series = SCALED_ERFC[-1] * t + SCALED_ERFC[-2]
                    for term in SCALED_ERFC[-3::-1]:
                        series = series * t + term
                    bare_one = gauss * (series * t * inverse + 2.0 * BETA / ROOT_PI) * inverse_sq
                    bare_two = (3.0 * bare_one + (4.0 * BETA**3 / ROOT_PI) * gauss) * inverse_sq
                    damping = (square * distance) * columns[3, rows] * (THOLE * lax.rsqrt(other[3:4]))
                    decay = jnp.exp(-damping) * inverse * inverse_sq
                    keep = jnp.where(entry < live, 1.0, 0.0) * (1.0 - itself)
                    three = keep * (bare_one - decay)
                    five = keep * (bare_two - (3.0 + 3.0 * damping) * decay * inverse_sq)
                    pairs[0, at * 8 + entry, rows] = five
                    pairs[1, at * 8 + entry, rows] = three
                    pairs[2, at * 8 + entry, rows] = d_z
                    v = search_rows(other)
                    along = five * (d_x * v[0:1] + d_y * v[1:2] + d_z * v[2:3])
                    sums = (
                        sums[0] + (along * d_x - three * v[0:1]),
                        sums[1] + (along * d_y - three * v[1:2]),
                        sums[2] + (along * d_z - three * v[2:3]),
                    )
                return sums

            zero = jnp.zeros(shape, F32)
            sums = lax.fori_loop(0, (live + GROUP - 1) // GROUP, group_step, (zero, zero, zero))
            for part in range(3):
                totals[part, rows] = sums[part]
            return carry

        lax.fori_loop(0, TILE // PAIR_ROWS, chunk_step, 0)
        found[at] = updated(block, totals)
        return carry

    lax.fori_loop(0, 2, tile_step, 0)


def field_rows(totals):
    return [jnp.sum(totals[part].T, axis=0, keepdims=True) for part in range(3)]


def updated(block, totals):
    alpha = block[3:4]
    field = field_rows(totals)
    rows = [alpha * (block[4 + part : 5 + part] + field[part]) for part in range(3)]
    return jnp.concatenate(rows + [jnp.zeros((5, TILE), F32)], 0)


APPLY_ROWS = 64


def fill_search(pool, own_first, own_rest, level, before, after, meta):
    for place in range(4):
        pool[meta[ORDER_AT + place]] = own_first[place] if place < 2 else own_rest[place - 2]
    for along, source in enumerate((before, level, after)):
        for kind in range(3):
            for member in range(2):
                pool[4 + 6 * kind + 2 * along + member] = source[kind, member]


def join_kernel(own, inner, outer, level):
    for member in range(2):
        level[0, member] = own[member]
        if len(inner.shape) == 3:
            level[1, member] = inner[member]
        else:
            start = inner.shape[1] - (2 - member) * TILE
            level[1, member] = inner[:, start : start + TILE]
        level[2, member] = outer[member]


def apply_tile(meta, tile, at, pairs, geometry, pool, columns, totals):
    block = geometry[tile]
    own_columns(columns, block, 2)
    live = meta[COUNTS_AT + tile]

    def chunk_step(chunk, carry):
        rows = pl.ds(pl.multiple_of(chunk * APPLY_ROWS, APPLY_ROWS), APPLY_ROWS)

        def group_step(group, sums):
            for member in range(GROUP):
                entry = group * GROUP + member
                slot = meta[tile * 8 + entry]
                other = geometry[slot]
                v = pool[slot]
                d_x = other[0:1] - columns[0, rows]
                d_y = other[1:2] - columns[1, rows]
                d_z = pairs[2, at * 8 + entry, rows]
                three = pairs[1, at * 8 + entry, rows]
                along = pairs[0, at * 8 + entry, rows] * (d_x * v[0:1] + d_y * v[1:2] + d_z * v[2:3])
                sums = (
                    sums[0] + (along * d_x - three * v[0:1]),
                    sums[1] + (along * d_y - three * v[1:2]),
                    sums[2] + (along * d_z - three * v[2:3]),
                )
            return sums

        zero = jnp.zeros((APPLY_ROWS, TILE), F32)
        sums = lax.fori_loop(0, (live + GROUP - 1) // GROUP, group_step, (zero, zero, zero))
        for part in range(3):
            totals[part, rows] = sums[part]
        return carry

    lax.fori_loop(0, TILE // APPLY_ROWS, chunk_step, 0)


def sweep_tiles(first_place, meta, geometry, banks, found, pool, columns, totals, local=None):
    for bank, pairs in enumerate(banks):

        def tile_step(at, carry):
            tile = meta[ORDER_AT + first_place + 2 * bank + at]
            apply_tile(meta, tile, at, pairs, geometry, pool, columns, totals)
            rows = updated(geometry[tile], totals)
            found[2 * bank + at] = rows
            if local is not None:
                local[tile] = rows
            return carry

        lax.fori_loop(0, 2, tile_step, 0)


def sweep_kernel(
    first_place, meta, geometry, own_first, own_rest, level, before, after, pairs, found, pool, columns, totals
):
    fill_search(pool, own_first, own_rest, level, before, after, meta)
    sweep_tiles(first_place, meta, geometry, (pairs,), found, pool, columns, totals)


def direction_kernel(
    meta, geometry, own_first, own_rest, level, before, after, pairs_a, pairs_b, order, found, sent, bundle, pool, columns, totals, local
):
    atoms = order.shape[1]
    fill_search(pool, own_first, own_rest, level, before, after, meta)
    sweep_tiles(0, meta, geometry, (pairs_a, pairs_b), found, pool, columns, totals, local)
    in_tiles = jnp.concatenate([local[tile] for tile in range(4)], 1)
    bundle[:, :atoms] = selected(in_tiles, order_matrix(order[...], atoms), NT)
    for place in range(2):
        block = found[place]
        sent[place] = block
        bundle[:, atoms + place * TILE : atoms + (place + 1) * TILE] = block


def final_field_kernel(
    meta, geometry, direction, level, before, after, pairs_a, order, stored_b, applied, sums, pool, columns, totals, local, pairs_b, sem
):
    copy = pltpu.make_async_copy(stored_b, pairs_b, sem.at[0])
    copy.start()
    atoms = order.shape[1]
    fill_search(pool, direction, direction.at[2:4], level, before, after, meta)
    both = (jnp.zeros((1, TILE), F32), jnp.zeros((1, TILE), F32))
    for bank, pairs in enumerate((pairs_a, pairs_b)):
        if bank == 1:
            copy.wait()

        def tile_step(at, both):
            curve, dots = both
            place = 2 * bank + at
            tile = meta[ORDER_AT + place]
            apply_tile(meta, tile, at, pairs, geometry, pool, columns, totals)
            block = geometry[tile]
            ahead = direction[place]
            field = field_rows(totals)
            rows = []
            for part in range(3):
                d = ahead[part : part + 1]
                value = d / block[3:4] - field[part] - SELF_FIELD * d
                curve = curve + d * value
                dots = dots + d * block[4 + part : 5 + part]
                rows.append(value)
            local[tile] = jnp.concatenate(rows + [jnp.zeros((5, TILE), F32)], 0)
            return (curve, dots)

        both = lax.fori_loop(0, 2, tile_step, both)
    in_tiles = jnp.concatenate([local[tile] for tile in range(4)], 1)
    applied[...] = selected(in_tiles, order_matrix(order[...], atoms), NT)
    lane = lax.broadcasted_iota(jnp.int32, (8, TILE), 1)
    curve_sum = jnp.sum(both[0], axis=1, keepdims=True)
    dot_sum = jnp.sum(both[1], axis=1, keepdims=True)
    sums[...] = jnp.where(lane == 1, curve_sum, jnp.where(lane == 2, dot_sum, 0.0))


def spline(fraction):
    centre_arg = fraction - 0.5

    def middle(u):
        return (55.0 + u * (20.0 + u * (-120.0 + u * (80.0 - 16.0 * u)))) / 96.0

    def middle_slope(u):
        return (20.0 + u * (-240.0 + u * (240.0 - 64.0 * u))) / 96.0

    def outer(u):
        w = 5.0 - 2.0 * u
        return (w * w) * (w * w) / 384.0

    def outer_slope(u):
        w = 5.0 - 2.0 * u
        return -(w * w * w) / 48.0

    sq = centre_arg * centre_arg
    weights = (
        outer(fraction + 1.5),
        middle(fraction + 0.5),
        115.0 / 192.0 - 0.625 * sq + 0.25 * sq * sq,
        middle(1.5 - fraction),
        outer(2.5 - fraction),
    )
    slopes = (
        outer_slope(fraction + 1.5),
        middle_slope(fraction + 0.5),
        -1.25 * centre_arg + centre_arg * sq,
        -middle_slope(1.5 - fraction),
        -outer_slope(2.5 - fraction),
    )
    return (weights, slopes)


def table(cell_row, values, length, wrapped):
    atoms = cell_row.shape[1]
    ids = lax.broadcasted_iota(jnp.int32, (length, atoms), 0)
    if wrapped:
        ahead = ids - cell_row + 2
        ahead = jnp.where(ahead >= G, ahead - G, jnp.where(ahead < 0, ahead + G, ahead))
    else:
        ahead = ids - cell_row
    total = jnp.zeros((length, atoms), F32)
    for step in range(5):
        total = jnp.where(ahead == step, values[step], total)
    return total


def tables_kernel(meta, mine, beside, cas_high, cas_low, tab_x, tab_y, w_high, w_low, slope_z):
    cas = (cas_high[meta[PARITY_AT]], cas_low[meta[PARITY_AT]])
    for side, statics in enumerate((mine, beside)):
        atoms = tab_x.shape[3]
        cells = statics[0:3, :atoms].astype(jnp.int32)
        for dim, out in ((0, tab_x), (1, tab_y)):
            weights, slopes = spline(statics[3 + dim : 4 + dim, :atoms])
            out[side, 0] = table(cells[dim : dim + 1], weights, out.shape[2], False)
            out[side, 1] = table(cells[dim : dim + 1], slopes, out.shape[2], False)
        weights, slopes = spline(statics[5:6, :atoms])
        high, low = halves(product(cas, halves(table(cells[2:3], weights, G, True)), NN))
        w_high[side] = high
        w_low[side] = low
        slope_z[side] = product(cas, halves(table(cells[2:3], slopes, G, True)), NN)


def spread_part(side, d, tab_x, tab_y, w_high, w_low, slope_z):
    w_z = (w_high[side], w_low[side])
    s_z = halves(slope_z[side] * d[2:3])
    weight_x = tab_x[side, 0]
    slope_part = tab_x[side, 1] * d[0:1]
    weight_part = weight_x * d[1:2]
    sides = []
    for y in range(tab_y.shape[2]):
        w_y, s_y = (tab_y[side, 0, y : y + 1], tab_y[side, 1, y : y + 1])
        sides.append((slope_part * w_y + weight_part * s_y, weight_x * w_y))
    rows = halves(jnp.concatenate([pair[0] for pair in sides], 0))
    flat = halves(jnp.concatenate([pair[1] for pair in sides], 0))
    return product(w_z, rows, NT) + product(s_z, flat, NT)


def spread_own_kernel(ordered, tab_x, tab_y, w_high, w_low, slope_z, out):
    out[...] = spread_part(0, ordered[:, : tab_x.shape[3]], tab_x, tab_y, w_high, w_low, slope_z)


def put_lanes(out, flat):
    for row in range(8):
        out[:, row, :] = flat[:, row * TILE : (row + 1) * TILE]


def get_lanes(grid):
    return jnp.concatenate([grid[:, row, :] for row in range(8)], 1)


def spread_both_kernel(shift, meta, ordered, mine, tab_x, tab_y, w_high, w_low, slope_z, out, flat):
    theirs = spread_part(1, ordered[:, : tab_x.shape[3]], tab_x, tab_y, w_high, w_low, slope_z)
    ours = mine[...]
    width = ours.shape[1]
    even = meta[PARITY_AT] == 0
    lower = jnp.where(even, ours, theirs)
    upper = jnp.where(even, theirs, ours)
    flat[:, :shift] = lower[:, :shift]
    flat[:, shift:width] = lower[:, shift:] + upper[:, : width - shift]
    flat[:, width : width + shift] = upper[:, width - shift :]
    flat[:, width + shift :] = jnp.zeros((flat.shape[0], flat.shape[1] - width - shift), F32)
    put_lanes(out, flat)


def plane_kernel(shapes, grid, waves, sums, *refs):
    stored, out, flat, padded = (refs[:6], refs[6], refs[7], refs[8])
    held, sems = (refs[9:15], refs[15])
    copies = [
        pltpu.make_async_copy(source, target, sems.at[at])
        for at, (source, target) in enumerate(zip(stored, held))
    ]
    for copy in copies:
        copy.start()
    x_high, x_low, yt_high, yt_low, y_high, y_low = held
    n_slab, n_pair, x_rows, y_rows = shapes
    width = x_rows * y_rows
    flat[...] = get_lanes(grid)
    padded[...] = jnp.zeros(padded.shape, F32)
    for s in range(n_slab):
        for y in range(y_rows):
            padded[y * n_pair : (y + 1) * n_pair, s * TILE : s * TILE + x_rows] = flat[
                s * n_pair : (s + 1) * n_pair, y * x_rows : (y + 1) * x_rows
            ]
    copies[0].wait()
    copies[1].wait()
    cas_x = (x_high[...], x_low[...])
    along_x = product(halves(padded[...]), cas_x, NN)
    for copy in copies[2:]:
        copy.wait()
    spectrum = product((yt_high[...], yt_low[...]), halves(along_x), NN)
    freq_z = lax.axis_index("slab") * (2 * n_pair) + 2 * lax.axis_index("pair") + lax.axis_index("core")
    ids_x = lax.broadcasted_iota(jnp.int32, (1, G), 1)
    by_x = waves[...]
    by_z = jnp.sum(jnp.where(ids_x == freq_z, by_x, 0.0), axis=1, keepdims=True)
    by_y = by_x.T
    anchor = jnp.where(
        (lax.broadcasted_iota(jnp.int32, (G, G), 0) + lax.broadcasted_iota(jnp.int32, (G, G), 1) + freq_z) == 0, 1.0, 0.0
    )
    squares = by_x[0:1] + by_y[:, 0:1] + (by_z[0:1] + anchor)
    factor = (1.0 - anchor) * (by_x[1:2] * by_z[1:2]) * by_y[:, 1:2] / (math.pi * float(G) ** 3 * squares)
    scaled = spectrum * factor
    energy = jnp.sum(jnp.sum(spectrum * scaled, axis=0, keepdims=True), axis=1, keepdims=True)
    back = halves(product((y_high[...], y_low[...]), halves(scaled), NN))
    planes = product(back, cas_x, NT)
    for s in range(n_slab):
        for y in range(y_rows):
            flat[s * n_pair : (s + 1) * n_pair, y * x_rows : (y + 1) * x_rows] = planes[
                y * n_pair : (y + 1) * n_pair, s * TILE : s * TILE + x_rows
            ]
    spare = flat.shape[1] - width
    lane = lax.broadcasted_iota(jnp.int32, (1, spare), 1)
    known = jnp.concatenate([sums[0:1], jnp.zeros((1, spare - TILE), F32)], 1)
    tail = jnp.where(lane == 0, energy, known)
    flat[:, width:] = jnp.broadcast_to(tail, (flat.shape[0], spare))
    put_lanes(out, flat)


def probe_part(side, planes, tab_x, tab_y, w_high, w_low, slope_z):
    x_rows = tab_x.shape[2]
    by_weight = product(planes, (w_high[side], w_low[side]), TN)
    by_slope = product(planes, halves(slope_z[side]), TN)
    weight_x, slope_x = (tab_x[side, 0], tab_x[side, 1])
    fields = [0.0, 0.0, 0.0]
    for y in range(tab_y.shape[2]):
        rows = slice(y * x_rows, (y + 1) * x_rows)
        w_y, s_y = (tab_y[side, 0, y : y + 1], tab_y[side, 1, y : y + 1])
        weighted = by_weight[rows]
        fields[0] += w_y * jnp.sum(slope_x * weighted, axis=0, keepdims=True)
        fields[1] += s_y * jnp.sum(weight_x * weighted, axis=0, keepdims=True)
        fields[2] += w_y * jnp.sum(weight_x * by_slope[rows], axis=0, keepdims=True)
    return fields


def probe_kernel(side, shift, meta, grid, tab_x, tab_y, w_high, w_low, slope_z, out):
    matrix = get_lanes(grid)
    width = tab_x.shape[2] * tab_y.shape[2]
    low_side = 0 if side == 0 else 1
    planes = jnp.where(
        meta[PARITY_AT] == low_side, matrix[:, :width], matrix[:, shift : shift + width]
    )
    fields = probe_part(side, halves(planes), tab_x, tab_y, w_high, w_low, slope_z)
    atoms = out.shape[1]
    scalars = jnp.sum(matrix[:, width + shift :], axis=0, keepdims=True)[:, :TILE]
    padded = jnp.concatenate([scalars, jnp.zeros((1, atoms - TILE), F32)], 1)
    out[...] = jnp.concatenate(fields + [padded, jnp.zeros((4, atoms), F32)], 0)


def finish_kernel(mine, theirs, ordered, applied, dipoles, residual, next_dipoles, next_residual, direction):
    total = mine[...] + theirs[...]
    step = total[3:4, 2:3] / (total[3:4, 0:1] + total[3:4, 1:2])
    d = ordered[0:3, : dipoles.shape[1]]
    next_dipoles[...] = dipoles[...] + step * d
    next_residual[...] = residual[...] - step * (applied[0:3] + total[0:3])
    direction[...] = d


def cas_matrix(first, second):
    angles = 2.0 * np.pi / G * (np.outer(first, second) % G)
    return np.cos(angles) + np.sin(angles)


def split_constant(values):
    whole = values.astype(np.float32)
    high = whole.astype(ml_dtypes.bfloat16)
    low = (values - high.astype(np.float64)).astype(ml_dtypes.bfloat16)
    return (jnp.asarray(high), jnp.asarray(low))


def wave_factors():
    freq = np.arange(G)
    wrapped = np.where(freq > G // 2, freq - G, freq) / G
    angles = 2.0 * np.pi / G * freq
    modulus = 115.0 / 192.0 + 19.0 / 48.0 * np.cos(angles) + 1.0 / 192.0 * np.cos(2.0 * angles)
    rows = np.zeros((8, G), np.float32)
    rows[0] = wrapped * wrapped
    rows[1] = np.exp(-((np.pi / BETA) ** 2) * wrapped * wrapped) / (modulus * modulus)
    return jnp.asarray(rows)


def swap_pairs(n_slab, n_space, odd):
    pairs = []
    for s in range(n_slab):
        for q in range(n_space):
            partner = (q + 1 if (q % 2 == 1) == odd else q - 1) % n_space
            pairs.append((s * n_space + q, s * n_space + partner))
    return pairs


def beside(block, odd):
    n_slab, n_space = (lax.axis_size("slab"), lax.axis_size(SPACE))
    return lax.ppermute(block, BOTH, swap_pairs(n_slab, n_space, odd))


def along_slab(level):
    n_slab = lax.axis_size("slab")
    up = [(i, (i + 1) % n_slab) for i in range(n_slab)]
    down = [(j, i) for i, j in up]
    return (level, lax.ppermute(level, "slab", up), lax.ppermute(level, "slab", down))


def joined(block, inner, outer):
    return call(join_kernel, [((3, 2, 8, TILE), F32)], 10**6)(block, inner, outer)[0]


def around(block, bundle=None):
    inner = beside(block if bundle is None else bundle, False)
    return along_slab(joined(block, inner, beside(block, True))), inner


def local(
    dipoles, residual, cells, fraction, polarizability, tile_order, send_tiles, tile_lists, tile_counts
):
    n_slab, n_space = (lax.axis_size("slab"), lax.axis_size(SPACE))
    n_pair = n_space // 2
    atoms = residual.shape[1]
    extents = (G // n_slab, G // n_space)
    x_rows = -(-(extents[0] + 4) // 8) * 8
    y_rows = extents[1] + 4
    pair_rows = 2 * extents[1] + 4
    shift = extents[1] * x_rows
    half = G // 2
    tile_shape = ((4, 8, TILE), F32)
    two_shape = ((2, 8, TILE), F32)
    bank_shape = ((3, 16, TILE, TILE), F32)
    pool_scratch = pltpu.VMEM((22, 8, TILE), F32)
    total_scratch = pltpu.VMEM((3, TILE, TILE), F32)
    own, sent, statics = pl.pallas_call(
        gather_kernel,
        out_shape=[
            jax.ShapeDtypeStruct(*tile_shape),
            jax.ShapeDtypeStruct(*two_shape),
            jax.ShapeDtypeStruct((8, atoms + 2 * TILE), F32),
        ],
        in_specs=[pl.BlockSpec(memory_space=pltpu.SMEM)] + [pl.BlockSpec(memory_space=pltpu.HBM)] * 5,
        out_specs=[pl.BlockSpec(memory_space=pltpu.VMEM)] * 3,
        scratch_shapes=[
            pltpu.VMEM((3, atoms), F32),
            pltpu.VMEM((3, atoms), jnp.int32),
            pltpu.VMEM((3, atoms), F32),
            pltpu.VMEM((atoms,), F32),
            pltpu.VMEM((1, atoms), jnp.int32),
            pltpu.SemaphoreType.DMA((5,)),
        ],
        compiler_params=pltpu.CompilerParams(vmem_limit_bytes=SMALL_VMEM),
    )(
        send_tiles,
        *[
            pltpu.with_memory_space_constraint(array, pltpu.HBM)
            for array in (residual, cells, fraction, polarizability, tile_order)
        ],
    )
    smem, anywhere = (pl.BlockSpec(memory_space=pltpu.SMEM), pl.BlockSpec(memory_space=pltpu.HBM))
    meta = pl.pallas_call(
        meta_kernel,
        out_shape=jax.ShapeDtypeStruct((48,), jnp.int32),
        in_specs=[smem, smem, smem, pl.BlockSpec(memory_space=pltpu.VMEM)],
        out_specs=smem,
        cost_estimate=pl.CostEstimate(flops=10**8, bytes_accessed=1 << 20, transcendentals=0),
    )(tile_lists, tile_counts, send_tiles, sent)
    first, statics_beside = around(sent, statics)

    def pairs_of(first_place):
        return call(
            functools.partial(pair_kernel, first_place, extents),
            [((22, 8, TILE), F32), bank_shape, two_shape],
            10**9,
            smem=1,
            scratch=(pltpu.VMEM((4, TILE, TILE), F32), total_scratch),
        )(meta, own, *first)

    geometry, pairs_a, search_a = pairs_of(0)
    _, pairs_b, search_b = pairs_of(2)
    sweep_scratch = (pool_scratch, pltpu.VMEM((3, TILE, TILE), F32), total_scratch)
    second, _ = around(search_a)

    def sweep(first_place, pairs):
        return call(
            functools.partial(sweep_kernel, first_place),
            [two_shape],
            10**8,
            smem=1,
            scratch=sweep_scratch,
        )(meta, geometry, search_a, search_b, *second, pairs)[0]

    next_a = sweep(0, pairs_a)
    next_b = sweep(2, pairs_b)
    third, _ = around(next_a)
    local_scratch = pltpu.VMEM((4, 8, TILE), F32)
    direction, sent, ordered = call(
        direction_kernel,
        [tile_shape, two_shape, ((8, atoms + 2 * TILE), F32)],
        10**8,
        smem=1,
        scratch=sweep_scratch + (local_scratch,),
    )(meta, geometry, next_a, next_b, *third, pairs_a, pairs_b, tile_order)
    ordered_beside, outer = (beside(ordered, False), beside(sent, True))
    freq = np.arange(G)
    padded_x = np.stack([(s * extents[0] + np.arange(x_rows) - 2) % G for s in range(n_slab)])
    real_x = np.tile(np.arange(x_rows) < extents[0] + 4, n_slab)
    cas_x = cas_matrix(padded_x.reshape(-1), freq) * real_x[:, None]
    rows_y = (np.arange(n_pair)[None] * 2 * extents[1] + np.arange(pair_rows)[:, None] - 2) % G
    cas_y = cas_matrix(rows_y.reshape(-1), freq)
    freq_by_core = np.stack([freq[0::2], freq[1::2]])
    cas_z = cas_matrix(freq_by_core.reshape(-1), freq).reshape(2, half, G)
    wide_x = np.zeros((n_slab, TILE, G))
    wide_x[:, :x_rows] = cas_x.reshape(n_slab, x_rows, G)
    tables = call(
        tables_kernel,
        [
            ((2, 2, x_rows, atoms), F32),
            ((2, 2, y_rows, atoms), F32),
            ((2, half, atoms), BF16),
            ((2, half, atoms), BF16),
            ((2, half, atoms), F32),
        ],
        10**8,
        smem=1,
        vmem=LARGE_VMEM,
    )(meta, statics, statics_beside, *split_constant(cas_z))
    message = ((half, 8, TILE), F32)
    flat_scratch = pltpu.VMEM((half, 8 * TILE), F32)
    spread_own = call(spread_own_kernel, [((half, x_rows * y_rows), F32)], 10**9, vmem=LARGE_VMEM)(ordered, *tables)[0]
    spread = call(
        functools.partial(spread_both_kernel, shift),
        [message],
        10**9,
        smem=1,
        scratch=(flat_scratch,),
        vmem=LARGE_VMEM,
    )(meta, ordered_beside, spread_own, *tables)[0]
    spread, outer = lax.optimization_barrier((spread, outer))
    grid = lax.all_to_all(spread, CHIPS, 0, 0, tiled=True)
    last = along_slab(joined(sent, ordered_beside, outer))
    applied, sums = call(
        final_field_kernel,
        [((8, atoms), F32), ((8, TILE), F32)],
        10**9,
        smem=1,
        scratch=sweep_scratch
        + (local_scratch, pltpu.VMEM(*bank_shape), pltpu.SemaphoreType.DMA((1,))),
        vmem=LARGE_VMEM,
        hbm=1,
    )(meta, geometry, direction, *last, pairs_a, tile_order, pairs_b)
    planes = call(
        functools.partial(plane_kernel, (n_slab, n_pair, x_rows, pair_rows)),
        [message],
        10**9,
        scratch=(flat_scratch, pltpu.VMEM((n_pair * pair_rows, n_slab * TILE), F32))
        + (pltpu.VMEM((n_slab * TILE, G), BF16),) * 2
        + (pltpu.VMEM((G, n_pair * pair_rows), BF16),) * 2
        + (pltpu.VMEM((n_pair * pair_rows, G), BF16),) * 2
        + (pltpu.SemaphoreType.DMA((6,)),),
        vmem=LARGE_VMEM,
        hbm=6,
    )(
        grid,
        wave_factors(),
        sums,
        *split_constant(wide_x.reshape(-1, G)),
        *split_constant(cas_y.T),
        *split_constant(cas_y),
    )[0]
    returned = lax.all_to_all(planes, CHIPS, 0, 0, tiled=True)

    def probe(side):
        return call(
            functools.partial(probe_kernel, side, shift), [((8, atoms), F32)], 10**9, smem=1, vmem=LARGE_VMEM
        )(meta, returned, *tables)[0]

    theirs = beside(probe(1), False)
    three = ((3, atoms), F32)
    return tuple(
        call(finish_kernel, [three, three, three], 10**6)(
            probe(0), theirs, ordered, applied, dipoles, residual
        )
    )


def solution(mesh):
    slab, space = (mesh.shape["slab"], mesh.shape["space"])
    mesh = Mesh(mesh.devices.reshape(slab, space // 2, 2), BOTH)
    in_specs = (
        P(None, BOTH),
        P(None, BOTH),
        P(None, BOTH),
        P(None, BOTH),
        P(BOTH),
        P(BOTH, None),
        P(BOTH, None),
        P(BOTH, None, None),
        P(BOTH, None),
    )
    out_specs = (P(None, BOTH), P(None, BOTH), P(None, BOTH))
    return jax.shard_map(local, mesh=mesh, in_specs=in_specs, out_specs=out_specs, check_vma=False)
```

```python
import functools
import math

import jax
import jax.numpy as jnp
import ml_dtypes
import numpy as np
from jax import lax
from jax.experimental import pallas as pl
from jax.experimental.pallas import tpu as pltpu
from jax.sharding import Mesh
from jax.sharding import PartitionSpec as P

G = 256
TILE = 128
SPACE = ("pair", "core")
BOTH = ("slab", "pair", "core")
CHIPS = ("slab", "pair")
BETA = 0.4
THOLE = 0.39
ROOT_PI = math.sqrt(math.pi)
SELF_FIELD = 4.0 * BETA**3 / (3.0 * ROOT_PI)
F32 = jnp.float32
BF16 = jnp.bfloat16
SCALED_ERFC_T = 0.45
SCALED_ERFC = (
    0.25388532876968384,
    0.25388309359550476,
    0.22827406227588654,
    0.17522020637989044,
    0.1201537474989891,
    -0.023065825924277306,
    0.14381752908229828,
    -0.3022053837776184,
    0.19167575240135193,
    -0.04163854941725731,
)
NT = (((1,), (1,)), ((), ()))
NN = (((1,), (0,)), ((), ()))
TN = (((0,), (0,)), ((), ()))
SMALL_VMEM = 6 * 1024 * 1024
LARGE_VMEM = 16 * 1024 * 1024


def halves(values):
    high = values.astype(BF16)
    return (high, (values - high.astype(F32)).astype(BF16))


def product(left, right, dims):
    def one(a, b):
        return lax.dot_general(a, b, dims, preferred_element_type=F32)

    (left_dim,), (right_dim,) = dims[0]
    if left[0].shape[left_dim] % TILE:
        return one(left[0], right[0]) + (one(left[0], right[1]) + one(left[1], right[0]))
    return one(
        jnp.concatenate([left[0], left[0], left[1]], left_dim),
        jnp.concatenate([right[0], right[1], right[0]], right_dim),
    )


def thirds(values):
    high = values.astype(BF16).astype(F32)
    rest = values - high
    middle = rest.astype(BF16).astype(F32)
    return jnp.concatenate([high, middle, rest - middle], 0).astype(BF16)


def selected(values, one_hot, dims):
    rows = values.shape[0]
    picked = lax.dot_general(thirds(values), one_hot, dims, preferred_element_type=F32)
    return picked[:rows] + (picked[rows : 2 * rows] + picked[2 * rows :])


def order_matrix(order_row, count):
    ids = lax.broadcasted_iota(jnp.int32, (count, count), 0)
    return jnp.where(ids == order_row, 1.0, 0.0).astype(BF16)


COUNTS_AT = 32
ORDER_AT = 36
PARITY_AT = 40


def meta_kernel(lists, counts, send, after, meta):
    parity = lax.axis_index("core")
    for tile in range(4):

        def remap(place, carry):
            entry = lists[0, tile, place]
            remote = entry - 4
            pair = lax.shift_right_arithmetic(remote, 1)
            pair = pair + jnp.where(pair >= 4, 1, 0)
            along = jnp.where(pair >= 3, 1, 0) + jnp.where(pair >= 6, 1, 0)
            across = pair - 3 * along
            base = jnp.where(across == 1, 4, jnp.where(across == 2 - 2 * parity, 10, 16))
            slot = base + along * 2 + (remote & 1)
            meta[tile * 8 + place] = jnp.where(entry < 4, entry, slot)
            return carry

        lax.fori_loop(0, 8, remap, 0)
        meta[COUNTS_AT + tile] = counts[0, tile]
    first, second = (send[0, 0], send[0, 1])
    third = jnp.where(
        (first != 0) & (second != 0), 0, jnp.where((first != 1) & (second != 1), 1, 2)
    )
    meta[ORDER_AT] = first
    meta[ORDER_AT + 1] = second
    meta[ORDER_AT + 2] = third
    meta[ORDER_AT + 3] = 6 - first - second - third
    meta[PARITY_AT] = parity


def call(kernel, outs, flops, smem=0, scratch=(), vmem=SMALL_VMEM, hbm=0):
    def run(*args):
        kept = len(args) - hbm
        args = args[:kept] + tuple(
            pltpu.with_memory_space_constraint(array, pltpu.HBM) for array in args[kept:]
        )
        in_specs = [pl.BlockSpec(memory_space=pltpu.SMEM)] * smem
        in_specs += [pl.BlockSpec(memory_space=pltpu.VMEM)] * (kept - smem)
        in_specs += [pl.BlockSpec(memory_space=pltpu.HBM)] * hbm
        return pl.pallas_call(
            kernel,
            out_shape=[jax.ShapeDtypeStruct(shape, dtype) for shape, dtype in outs],
            in_specs=in_specs,
            out_specs=[pl.BlockSpec(memory_space=pltpu.VMEM)] * len(outs),
            scratch_shapes=list(scratch),
            compiler_params=pltpu.CompilerParams(vmem_limit_bytes=vmem),
            cost_estimate=pl.CostEstimate(
                flops=flops, bytes_accessed=1 << 20, transcendentals=0
            ),
        )(*args)

    return run


def gather_kernel(send, *refs):
    sources, (own, sent, bundle), held, sems = (refs[:5], refs[5:8], refs[8:13], refs[13])
    copies = [
        pltpu.make_async_copy(source, target, sems.at[at])
        for at, (source, target) in enumerate(zip(sources, held))
    ]
    for copy in copies:
        copy.start()
    for copy in copies:
        copy.wait()
    residual, cells, fraction, alphas, order = held
    atoms = residual.shape[1]
    in_cells = cells[...].astype(F32)
    bundle[0:3, :atoms] = in_cells
    bundle[3:6, :atoms] = fraction[...]
    bundle[6:8, :atoms] = jnp.zeros((2, atoms), F32)
    position = in_cells + fraction[...]
    rows = jnp.concatenate(
        [position, alphas[...].reshape(1, atoms), residual[...], jnp.zeros((1, atoms), F32)], 0
    )
    picked = selected(rows, order_matrix(order[...], atoms), NN)
    for tile in range(atoms // TILE):
        own[tile] = picked[:, tile * TILE : (tile + 1) * TILE]
    for place in range(2):
        block = own[send[0, place]]
        sent[place] = block
        bundle[:, atoms + place * TILE : atoms + (place + 1) * TILE] = block


def search_rows(block):
    return block[3:4] * block[4:7]


def fill_pool(pool, extents, own, level, before, after, meta):
    inner_step = jnp.where(meta[PARITY_AT] == 0, 1.0, -1.0)
    rows = lax.broadcasted_iota(jnp.int32, (8, TILE), 0)
    for tile in range(4):
        pool[tile] = own[tile]
    for along, source in enumerate((before, level, after)):
        for kind, step in enumerate((0.0, inner_step, -inner_step)):
            shift = jnp.where(
                rows == 0,
                float((along - 1) * extents[0]),
                jnp.where(rows == 1, step * float(extents[1]), 0.0),
            )
            for member in range(2):
                pool[4 + 6 * kind + 2 * along + member] = source[kind, member] + shift


def own_columns(columns, block, count):
    turned = block.T
    for row in range(count):
        columns[row] = jnp.broadcast_to(turned[:, row : row + 1], (TILE, TILE))


def wrap_depth(depth):
    half = 0.5 * G
    return jnp.where(depth > half, depth - G, jnp.where(depth < -half, depth + G, depth))


PAIR_ROWS = 32
GROUP = 4


def pair_kernel(first_place, count, extents, meta, own, level, before, after, pool, pairs, found, columns, totals):
    fill_pool(pool, extents, own, level, before, after, meta)

    def tile_step(at, carry):
        tile = meta[ORDER_AT + first_place + at]
        block = own[tile]
        own_columns(columns, jnp.concatenate([block[:3], lax.rsqrt(block[3:4]), block[4:]], 0), 4)
        live = meta[COUNTS_AT + tile]

        def chunk_step(chunk, carry):
            start = pl.multiple_of(chunk * PAIR_ROWS, PAIR_ROWS)
            rows = pl.ds(start, PAIR_ROWS)
            shape = (PAIR_ROWS, TILE)
            ahead = lax.broadcasted_iota(jnp.int32, shape, 0) - lax.broadcasted_iota(
                jnp.int32, shape, 1
            )
            diagonal = jnp.where(ahead == -start, 1.0, 0.0)

            def group_step(group, sums):
                for member in range(GROUP):
                    entry = group * GROUP + member
                    slot = meta[tile * 8 + entry]
                    other = pool[slot]
                    itself = diagonal * jnp.where(slot == tile, 1.0, 0.0)
                    d_x = other[0:1] - columns[0, rows]
                    d_y = other[1:2] - columns[1, rows]
                    d_z = wrap_depth(other[2:3] - columns[2, rows])
                    square = d_x * d_x + d_y * d_y + d_z * d_z + itself
                    inverse = lax.rsqrt(square)
                    distance = square * inverse
                    inverse_sq = inverse * inverse
                    gauss = jnp.exp(-(BETA**2) * square)
                    stretch = 1.0 + (SCALED_ERFC_T * BETA) * distance
                    t = lax.rsqrt(stretch * stretch)
                    series = SCALED_ERFC[-1] * t + SCALED_ERFC[-2]
                    for term in SCALED_ERFC[-3::-1]:
                        series = series * t + term
                    bare_one = gauss * (series * t * inverse + 2.0 * BETA / ROOT_PI) * inverse_sq
                    bare_two = (3.0 * bare_one + (4.0 * BETA**3 / ROOT_PI) * gauss) * inverse_sq
                    damping = (square * distance) * columns[3, rows] * (THOLE * lax.rsqrt(other[3:4]))
                    decay = jnp.exp(-damping) * inverse * inverse_sq
                    keep = jnp.where(entry < live, 1.0, 0.0) * (1.0 - itself)
                    three = keep * (bare_one - decay)
                    five = keep * (bare_two - (3.0 + 3.0 * damping) * decay * inverse_sq)
                    pairs[0, at * 8 + entry, rows] = five
                    pairs[1, at * 8 + entry, rows] = three
                    pairs[2, at * 8 + entry, rows] = d_z
                    v = search_rows(other)
                    along = five * (d_x * v[0:1] + d_y * v[1:2] + d_z * v[2:3])
                    sums = (
                        sums[0] + (along * d_x - three * v[0:1]),
                        sums[1] + (along * d_y - three * v[1:2]),
                        sums[2] + (along * d_z - three * v[2:3]),
                    )
                return sums

            zero = jnp.zeros(shape, F32)
            sums = lax.fori_loop(0, (live + GROUP - 1) // GROUP, group_step, (zero, zero, zero))
            for part in range(3):
                totals[part, rows] = sums[part]
            return carry

        lax.fori_loop(0, TILE // PAIR_ROWS, chunk_step, 0)
        found[at] = updated(block, totals)
        return carry

    lax.fori_loop(0, count, tile_step, 0)


def field_rows(totals):
    return [jnp.sum(totals[part].T, axis=0, keepdims=True) for part in range(3)]


def updated(block, totals):
    alpha = block[3:4]
    field = field_rows(totals)
    rows = [alpha * (block[4 + part : 5 + part] + field[part]) for part in range(3)]
    return jnp.concatenate(rows + [jnp.zeros((5, TILE), F32)], 0)


APPLY_ROWS = 64


def fill_search(pool, owns, level, before, after, meta):
    place = 0
    for own in owns:
        for at in range(own.shape[0]):
            pool[meta[ORDER_AT + place]] = own[at]
            place += 1
    for along, source in enumerate((before, level, after)):
        for kind in range(3):
            for member in range(2):
                pool[4 + 6 * kind + 2 * along + member] = source[kind, member]


def join_kernel(own, inner, outer, level):
    for member in range(2):
        level[0, member] = own[member]
        if len(inner.shape) == 3:
            level[1, member] = inner[member]
        else:
            start = inner.shape[1] - (2 - member) * TILE
            level[1, member] = inner[:, start : start + TILE]
        level[2, member] = outer[member]


def apply_tile(meta, tile, at, pairs, geometry, pool, columns, totals):
    block = geometry[tile]
    own_columns(columns, block, 2)
    live = meta[COUNTS_AT + tile]

    def chunk_step(chunk, carry):
        rows = pl.ds(pl.multiple_of(chunk * APPLY_ROWS, APPLY_ROWS), APPLY_ROWS)

        def group_step(group, sums):
            for member in range(GROUP):
                entry = group * GROUP + member
                slot = meta[tile * 8 + entry]
                other = geometry[slot]
                v = pool[slot]
                d_x = other[0:1] - columns[0, rows]
                d_y = other[1:2] - columns[1, rows]
                d_z = pairs[2, at * 8 + entry, rows]
                three = pairs[1, at * 8 + entry, rows]
                along = pairs[0, at * 8 + entry, rows] * (d_x * v[0:1] + d_y * v[1:2] + d_z * v[2:3])
                sums = (
                    sums[0] + (along * d_x - three * v[0:1]),
                    sums[1] + (along * d_y - three * v[1:2]),
                    sums[2] + (along * d_z - three * v[2:3]),
                )
            return sums

        zero = jnp.zeros((APPLY_ROWS, TILE), F32)
        sums = lax.fori_loop(0, (live + GROUP - 1) // GROUP, group_step, (zero, zero, zero))
        for part in range(3):
            totals[part, rows] = sums[part]
        return carry

    lax.fori_loop(0, TILE // APPLY_ROWS, chunk_step, 0)


def sweep_tiles(place, meta, geometry, banks, found, pool, columns, totals, local=None):
    done = 0
    for pairs in banks:
        count = pairs.shape[1] // 8

        def tile_step(at, carry):
            tile = meta[ORDER_AT + place + done + at]
            apply_tile(meta, tile, at, pairs, geometry, pool, columns, totals)
            rows = updated(geometry[tile], totals)
            found[done + at] = rows
            if local is not None:
                local[tile] = rows
            return carry

        lax.fori_loop(0, count, tile_step, 0)
        done += count


def sweep_kernel(place, owns, meta, geometry, *refs):
    own_refs, (level, before, after) = (refs[:owns], refs[owns : owns + 3])
    banks, (found, pool, columns, totals) = (refs[owns + 3 : -4], refs[-4:])
    fill_search(pool, own_refs, level, before, after, meta)
    sweep_tiles(place, meta, geometry, banks, found, pool, columns, totals)


def direction_kernel(
    meta, geometry, own_a, own_b, level, before, after, pairs_a, pairs_b, pairs_c, order, found, sent, bundle, pool, columns, totals, local
):
    atoms = order.shape[1]
    fill_search(pool, (own_a, own_b), level, before, after, meta)
    sweep_tiles(0, meta, geometry, (pairs_a, pairs_b, pairs_c), found, pool, columns, totals, local)
    in_tiles = jnp.concatenate([local[tile] for tile in range(4)], 1)
    bundle[:, :atoms] = selected(in_tiles, order_matrix(order[...], atoms), NT)
    for place in range(2):
        block = found[place]
        sent[place] = block
        bundle[:, atoms + place * TILE : atoms + (place + 1) * TILE] = block


def final_field_kernel(
    meta, geometry, direction, level, before, after, pairs_a, order, stored_b, stored_c, applied, sums, pool, columns, totals, local, pairs_b, pairs_c, sems
):
    copies = [
        pltpu.make_async_copy(source, target, sems.at[at])
        for at, (source, target) in enumerate(((stored_b, pairs_b), (stored_c, pairs_c)))
    ]
    for copy in copies:
        copy.start()
    atoms = order.shape[1]
    fill_search(pool, (direction,), level, before, after, meta)
    both = (jnp.zeros((1, TILE), F32), jnp.zeros((1, TILE), F32))
    for first, pairs in ((0, pairs_a), (2, pairs_b), (3, pairs_c)):
        if first:
            copies[first - 2].wait()

        def tile_step(at, both):
            curve, dots = both
            place = first + at
            tile = meta[ORDER_AT + place]
            apply_tile(meta, tile, at, pairs, geometry, pool, columns, totals)
            block = geometry[tile]
            ahead = direction[place]
            field = field_rows(totals)
            rows = []
            for part in range(3):
                d = ahead[part : part + 1]
                value = d / block[3:4] - field[part] - SELF_FIELD * d
                curve = curve + d * value
                dots = dots + d * block[4 + part : 5 + part]
                rows.append(value)
            local[tile] = jnp.concatenate(rows + [jnp.zeros((5, TILE), F32)], 0)
            return (curve, dots)

        both = lax.fori_loop(0, pairs.shape[1] // 8, tile_step, both)
    in_tiles = jnp.concatenate([local[tile] for tile in range(4)], 1)
    applied[...] = selected(in_tiles, order_matrix(order[...], atoms), NT)
    lane = lax.broadcasted_iota(jnp.int32, (8, TILE), 1)
    curve_sum = jnp.sum(both[0], axis=1, keepdims=True)
    dot_sum = jnp.sum(both[1], axis=1, keepdims=True)
    sums[...] = jnp.where(lane == 1, curve_sum, jnp.where(lane == 2, dot_sum, 0.0))


def spline(fraction):
    centre_arg = fraction - 0.5

    def middle(u):
        return (55.0 + u * (20.0 + u * (-120.0 + u * (80.0 - 16.0 * u)))) / 96.0

    def middle_slope(u):
        return (20.0 + u * (-240.0 + u * (240.0 - 64.0 * u))) / 96.0

    def outer(u):
        w = 5.0 - 2.0 * u
        return (w * w) * (w * w) / 384.0

    def outer_slope(u):
        w = 5.0 - 2.0 * u
        return -(w * w * w) / 48.0

    sq = centre_arg * centre_arg
    weights = (
        outer(fraction + 1.5),
        middle(fraction + 0.5),
        115.0 / 192.0 - 0.625 * sq + 0.25 * sq * sq,
        middle(1.5 - fraction),
        outer(2.5 - fraction),
    )
    slopes = (
        outer_slope(fraction + 1.5),
        middle_slope(fraction + 0.5),
        -1.25 * centre_arg + centre_arg * sq,
        -middle_slope(1.5 - fraction),
        -outer_slope(2.5 - fraction),
    )
    return (weights, slopes)


def table(cell_row, values, length, wrapped):
    atoms = cell_row.shape[1]
    ids = lax.broadcasted_iota(jnp.int32, (length, atoms), 0)
    if wrapped:
        ahead = ids - cell_row + 2
        ahead = jnp.where(ahead >= G, ahead - G, jnp.where(ahead < 0, ahead + G, ahead))
    else:
        ahead = ids - cell_row
    total = jnp.zeros((length, atoms), F32)
    for step in range(5):
        total = jnp.where(ahead == step, values[step], total)
    return total


def tables_kernel(meta, mine, beside, cas_high, cas_low, tab_x, tab_y, w_high, w_low, slope_z):
    cas = (cas_high[meta[PARITY_AT]], cas_low[meta[PARITY_AT]])
    for side, statics in enumerate((mine, beside)):
        atoms = tab_x.shape[3]
        cells = statics[0:3, :atoms].astype(jnp.int32)
        for dim, out in ((0, tab_x), (1, tab_y)):
            weights, slopes = spline(statics[3 + dim : 4 + dim, :atoms])
            out[side, 0] = table(cells[dim : dim + 1], weights, out.shape[2], False)
            out[side, 1] = table(cells[dim : dim + 1], slopes, out.shape[2], False)
        weights, slopes = spline(statics[5:6, :atoms])
        high, low = halves(product(cas, halves(table(cells[2:3], weights, G, True)), NN))
        w_high[side] = high
        w_low[side] = low
        slope_z[side] = product(cas, halves(table(cells[2:3], slopes, G, True)), NN)


def spread_part(side, d, tab_x, tab_y, w_high, w_low, slope_z):
    w_z = (w_high[side], w_low[side])
    s_z = halves(slope_z[side] * d[2:3])
    weight_x = tab_x[side, 0]
    slope_part = tab_x[side, 1] * d[0:1]
    weight_part = weight_x * d[1:2]
    sides = []
    for y in range(tab_y.shape[2]):
        w_y, s_y = (tab_y[side, 0, y : y + 1], tab_y[side, 1, y : y + 1])
        sides.append((slope_part * w_y + weight_part * s_y, weight_x * w_y))
    rows = halves(jnp.concatenate([pair[0] for pair in sides], 0))
    flat = halves(jnp.concatenate([pair[1] for pair in sides], 0))
    return product(w_z, rows, NT) + product(s_z, flat, NT)


def spread_own_kernel(ordered, tab_x, tab_y, w_high, w_low, slope_z, out):
    out[...] = spread_part(0, ordered[:, : tab_x.shape[3]], tab_x, tab_y, w_high, w_low, slope_z)


def put_lanes(out, flat):
    for row in range(8):
        out[:, row, :] = flat[:, row * TILE : (row + 1) * TILE]


def get_lanes(grid):
    return jnp.concatenate([grid[:, row, :] for row in range(8)], 1)


def spread_both_kernel(shift, meta, ordered, mine, tab_x, tab_y, w_high, w_low, slope_z, out, flat):
    theirs = spread_part(1, ordered[:, : tab_x.shape[3]], tab_x, tab_y, w_high, w_low, slope_z)
    ours = mine[...]
    width = ours.shape[1]
    even = meta[PARITY_AT] == 0
    lower = jnp.where(even, ours, theirs)
    upper = jnp.where(even, theirs, ours)
    flat[:, :shift] = lower[:, :shift]
    flat[:, shift:width] = lower[:, shift:] + upper[:, : width - shift]
    flat[:, width : width + shift] = upper[:, width - shift :]
    flat[:, width + shift :] = jnp.zeros((flat.shape[0], flat.shape[1] - width - shift), F32)
    put_lanes(out, flat)


def plane_kernel(shapes, grid, waves, sums, *refs):
    stored, out, flat, padded = (refs[:6], refs[6], refs[7], refs[8])
    held, sems = (refs[9:15], refs[15])
    copies = [
        pltpu.make_async_copy(source, target, sems.at[at])
        for at, (source, target) in enumerate(zip(stored, held))
    ]
    for copy in copies:
        copy.start()
    x_high, x_low, yt_high, yt_low, y_high, y_low = held
    n_slab, n_pair, x_rows, y_rows = shapes
    width = x_rows * y_rows
    flat[...] = get_lanes(grid)
    padded[...] = jnp.zeros(padded.shape, F32)
    for s in range(n_slab):
        for y in range(y_rows):
            padded[y * n_pair : (y + 1) * n_pair, s * TILE : s * TILE + x_rows] = flat[
                s * n_pair : (s + 1) * n_pair, y * x_rows : (y + 1) * x_rows
            ]
    copies[0].wait()
    copies[1].wait()
    cas_x = (x_high[...], x_low[...])
    along_x = product(halves(padded[...]), cas_x, NN)
    for copy in copies[2:]:
        copy.wait()
    spectrum = product((yt_high[...], yt_low[...]), halves(along_x), NN)
    freq_z = lax.axis_index("slab") * (2 * n_pair) + 2 * lax.axis_index("pair") + lax.axis_index("core")
    ids_x = lax.broadcasted_iota(jnp.int32, (1, G), 1)
    by_x = waves[...]
    by_z = jnp.sum(jnp.where(ids_x == freq_z, by_x, 0.0), axis=1, keepdims=True)
    by_y = by_x.T
    anchor = jnp.where(
        (lax.broadcasted_iota(jnp.int32, (G, G), 0) + lax.broadcasted_iota(jnp.int32, (G, G), 1) + freq_z) == 0, 1.0, 0.0
    )
    squares = by_x[0:1] + by_y[:, 0:1] + (by_z[0:1] + anchor)
    factor = (1.0 - anchor) * (by_x[1:2] * by_z[1:2]) * by_y[:, 1:2] / (math.pi * float(G) ** 3 * squares)
    scaled = spectrum * factor
    energy = jnp.sum(jnp.sum(spectrum * scaled, axis=0, keepdims=True), axis=1, keepdims=True)
    back = halves(product((y_high[...], y_low[...]), halves(scaled), NN))
    planes = product(back, cas_x, NT)
    for s in range(n_slab):
        for y in range(y_rows):
            flat[s * n_pair : (s + 1) * n_pair, y * x_rows : (y + 1) * x_rows] = planes[
                y * n_pair : (y + 1) * n_pair, s * TILE : s * TILE + x_rows
            ]
    spare = flat.shape[1] - width
    lane = lax.broadcasted_iota(jnp.int32, (1, spare), 1)
    known = jnp.concatenate([sums[0:1], jnp.zeros((1, spare - TILE), F32)], 1)
    tail = jnp.where(lane == 0, energy, known)
    flat[:, width:] = jnp.broadcast_to(tail, (flat.shape[0], spare))
    put_lanes(out, flat)


def probe_part(side, planes, tab_x, tab_y, w_high, w_low, slope_z):
    x_rows = tab_x.shape[2]
    by_weight = product(planes, (w_high[side], w_low[side]), TN)
    by_slope = product(planes, halves(slope_z[side]), TN)
    weight_x, slope_x = (tab_x[side, 0], tab_x[side, 1])
    fields = [0.0, 0.0, 0.0]
    for y in range(tab_y.shape[2]):
        rows = slice(y * x_rows, (y + 1) * x_rows)
        w_y, s_y = (tab_y[side, 0, y : y + 1], tab_y[side, 1, y : y + 1])
        weighted = by_weight[rows]
        fields[0] += w_y * jnp.sum(slope_x * weighted, axis=0, keepdims=True)
        fields[1] += s_y * jnp.sum(weight_x * weighted, axis=0, keepdims=True)
        fields[2] += w_y * jnp.sum(weight_x * by_slope[rows], axis=0, keepdims=True)
    return fields


def probe_kernel(side, shift, meta, grid, tab_x, tab_y, w_high, w_low, slope_z, out):
    matrix = get_lanes(grid)
    width = tab_x.shape[2] * tab_y.shape[2]
    low_side = 0 if side == 0 else 1
    planes = jnp.where(
        meta[PARITY_AT] == low_side, matrix[:, :width], matrix[:, shift : shift + width]
    )
    fields = probe_part(side, halves(planes), tab_x, tab_y, w_high, w_low, slope_z)
    atoms = out.shape[1]
    scalars = jnp.sum(matrix[:, width + shift :], axis=0, keepdims=True)[:, :TILE]
    padded = jnp.concatenate([scalars, jnp.zeros((1, atoms - TILE), F32)], 1)
    out[...] = jnp.concatenate(fields + [padded, jnp.zeros((4, atoms), F32)], 0)


def finish_kernel(mine, theirs, ordered, applied, dipoles, residual, next_dipoles, next_residual, direction):
    total = mine[...] + theirs[...]
    step = total[3:4, 2:3] / (total[3:4, 0:1] + total[3:4, 1:2])
    d = ordered[0:3, : dipoles.shape[1]]
    next_dipoles[...] = dipoles[...] + step * d
    next_residual[...] = residual[...] - step * (applied[0:3] + total[0:3])
    direction[...] = d


def cas_matrix(first, second):
    angles = 2.0 * np.pi / G * (np.outer(first, second) % G)
    return np.cos(angles) + np.sin(angles)


def split_constant(values):
    whole = values.astype(np.float32)
    high = whole.astype(ml_dtypes.bfloat16)
    low = (values - high.astype(np.float64)).astype(ml_dtypes.bfloat16)
    return (jnp.asarray(high), jnp.asarray(low))


def wave_factors():
    freq = np.arange(G)
    wrapped = np.where(freq > G // 2, freq - G, freq) / G
    angles = 2.0 * np.pi / G * freq
    modulus = 115.0 / 192.0 + 19.0 / 48.0 * np.cos(angles) + 1.0 / 192.0 * np.cos(2.0 * angles)
    rows = np.zeros((8, G), np.float32)
    rows[0] = wrapped * wrapped
    rows[1] = np.exp(-((np.pi / BETA) ** 2) * wrapped * wrapped) / (modulus * modulus)
    return jnp.asarray(rows)


def swap_pairs(n_slab, n_space, odd):
    pairs = []
    for s in range(n_slab):
        for q in range(n_space):
            partner = (q + 1 if (q % 2 == 1) == odd else q - 1) % n_space
            pairs.append((s * n_space + q, s * n_space + partner))
    return pairs


def beside(block, odd):
    n_slab, n_space = (lax.axis_size("slab"), lax.axis_size(SPACE))
    return lax.ppermute(block, BOTH, swap_pairs(n_slab, n_space, odd))


def along_slab(level):
    n_slab = lax.axis_size("slab")
    up = [(i, (i + 1) % n_slab) for i in range(n_slab)]
    down = [(j, i) for i, j in up]
    return (level, lax.ppermute(level, "slab", up), lax.ppermute(level, "slab", down))


def joined(block, inner, outer):
    return call(join_kernel, [((3, 2, 8, TILE), F32)], 10**6)(block, inner, outer)[0]


def around(block, bundle=None, beneath=None):
    inner = beside(block if bundle is None else bundle, False)
    outer, _ = lax.optimization_barrier((beside(block, True), beneath))
    return along_slab(joined(block, inner, outer)), inner


def local(
    dipoles, residual, cells, fraction, polarizability, tile_order, send_tiles, tile_lists, tile_counts
):
    n_slab, n_space = (lax.axis_size("slab"), lax.axis_size(SPACE))
    n_pair = n_space // 2
    atoms = residual.shape[1]
    extents = (G // n_slab, G // n_space)
    x_rows = -(-(extents[0] + 4) // 8) * 8
    y_rows = extents[1] + 4
    pair_rows = 2 * extents[1] + 4
    shift = extents[1] * x_rows
    half = G // 2
    tile_shape = ((4, 8, TILE), F32)
    two_shape = ((2, 8, TILE), F32)
    one_bank = ((3, 8, TILE, TILE), F32)
    pool_scratch = pltpu.VMEM((22, 8, TILE), F32)
    total_scratch = pltpu.VMEM((3, TILE, TILE), F32)
    own, sent, statics = pl.pallas_call(
        gather_kernel,
        out_shape=[
            jax.ShapeDtypeStruct(*tile_shape),
            jax.ShapeDtypeStruct(*two_shape),
            jax.ShapeDtypeStruct((8, atoms + 2 * TILE), F32),
        ],
        in_specs=[pl.BlockSpec(memory_space=pltpu.SMEM)] + [pl.BlockSpec(memory_space=pltpu.HBM)] * 5,
        out_specs=[pl.BlockSpec(memory_space=pltpu.VMEM)] * 3,
        scratch_shapes=[
            pltpu.VMEM((3, atoms), F32),
            pltpu.VMEM((3, atoms), jnp.int32),
            pltpu.VMEM((3, atoms), F32),
            pltpu.VMEM((atoms,), F32),
            pltpu.VMEM((1, atoms), jnp.int32),
            pltpu.SemaphoreType.DMA((5,)),
        ],
        compiler_params=pltpu.CompilerParams(vmem_limit_bytes=SMALL_VMEM),
    )(
        send_tiles,
        *[
            pltpu.with_memory_space_constraint(array, pltpu.HBM)
            for array in (residual, cells, fraction, polarizability, tile_order)
        ],
    )
    smem, anywhere = (pl.BlockSpec(memory_space=pltpu.SMEM), pl.BlockSpec(memory_space=pltpu.HBM))
    meta = pl.pallas_call(
        meta_kernel,
        out_shape=jax.ShapeDtypeStruct((48,), jnp.int32),
        in_specs=[smem, smem, smem, pl.BlockSpec(memory_space=pltpu.VMEM)],
        out_specs=smem,
        cost_estimate=pl.CostEstimate(flops=10**8, bytes_accessed=1 << 20, transcendentals=0),
    )(tile_lists, tile_counts, send_tiles, sent)
    first, statics_beside = around(sent, statics, beneath=meta)

    freq = np.arange(G)
    padded_x = np.stack([(s * extents[0] + np.arange(x_rows) - 2) % G for s in range(n_slab)])
    real_x = np.tile(np.arange(x_rows) < extents[0] + 4, n_slab)
    cas_x = cas_matrix(padded_x.reshape(-1), freq) * real_x[:, None]
    rows_y = (np.arange(n_pair)[None] * 2 * extents[1] + np.arange(pair_rows)[:, None] - 2) % G
    cas_y = cas_matrix(rows_y.reshape(-1), freq)
    freq_by_core = np.stack([freq[0::2], freq[1::2]])
    cas_z = cas_matrix(freq_by_core.reshape(-1), freq).reshape(2, half, G)
    wide_x = np.zeros((n_slab, TILE, G))
    wide_x[:, :x_rows] = cas_x.reshape(n_slab, x_rows, G)
    tables = call(
        tables_kernel,
        [
            ((2, 2, x_rows, atoms), F32),
            ((2, 2, y_rows, atoms), F32),
            ((2, half, atoms), BF16),
            ((2, half, atoms), BF16),
            ((2, half, atoms), F32),
        ],
        10**8,
        smem=1,
        vmem=LARGE_VMEM,
    )(meta, statics, statics_beside, *split_constant(cas_z))
    level, before, after = first
    after, _ = lax.optimization_barrier((after, tables[1]))
    first = (level, before, after)

    def pairs_of(place, count):
        return call(
            functools.partial(pair_kernel, place, count, extents),
            [((22, 8, TILE), F32), ((3, 8 * count, TILE, TILE), F32), ((count, 8, TILE), F32)],
            10**9,
            smem=1,
            scratch=(pltpu.VMEM((4, TILE, TILE), F32), total_scratch),
        )(meta, own, *first)

    geometry, pairs_a, search_a = pairs_of(0, 2)
    _, pairs_b, search_b = pairs_of(2, 1)
    _, pairs_c, search_c = pairs_of(3, 1)
    sweep_scratch = (pool_scratch, pltpu.VMEM((3, TILE, TILE), F32), total_scratch)
    second, _ = around(search_a, beneath=search_b)

    def sweep(place, banks):
        owns = (search_a, search_b, search_c)
        return call(
            functools.partial(sweep_kernel, place, len(owns)),
            [two_shape],
            10**8,
            smem=1,
            scratch=sweep_scratch,
        )(meta, geometry, *owns, *second, *banks)[0]

    next_a = sweep(0, (pairs_a,))
    next_b = sweep(2, (pairs_b, pairs_c))
    third, _ = around(next_a, beneath=next_b)
    local_scratch = pltpu.VMEM((4, 8, TILE), F32)
    direction, sent, ordered = call(
        direction_kernel,
        [tile_shape, two_shape, ((8, atoms + 2 * TILE), F32)],
        10**8,
        smem=1,
        scratch=sweep_scratch + (local_scratch,),
    )(meta, geometry, next_a, next_b, *third, pairs_a, pairs_b, pairs_c, tile_order)
    ordered_beside = beside(ordered, False)
    message = ((half, 8, TILE), F32)
    flat_scratch = pltpu.VMEM((half, 8 * TILE), F32)
    spread_own = call(spread_own_kernel, [((half, x_rows * y_rows), F32)], 10**9, vmem=LARGE_VMEM)(ordered, *tables)[0]
    spread = call(
        functools.partial(spread_both_kernel, shift),
        [message],
        10**9,
        smem=1,
        scratch=(flat_scratch,),
        vmem=LARGE_VMEM,
    )(meta, ordered_beside, spread_own, *tables)[0]
    late, _ = lax.optimization_barrier((sent, spread_own))
    spread, outer = lax.optimization_barrier((spread, beside(late, True)))
    grid = lax.all_to_all(spread, CHIPS, 0, 0, tiled=True)
    last = along_slab(joined(sent, ordered_beside, outer))
    applied, sums = call(
        final_field_kernel,
        [((8, atoms), F32), ((8, TILE), F32)],
        10**9,
        smem=1,
        scratch=sweep_scratch
        + (local_scratch, pltpu.VMEM(*one_bank), pltpu.VMEM(*one_bank), pltpu.SemaphoreType.DMA((2,))),
        vmem=LARGE_VMEM,
        hbm=2,
    )(meta, geometry, direction, *last, pairs_a, tile_order, pairs_b, pairs_c)
    planes = call(
        functools.partial(plane_kernel, (n_slab, n_pair, x_rows, pair_rows)),
        [message],
        10**9,
        scratch=(flat_scratch, pltpu.VMEM((n_pair * pair_rows, n_slab * TILE), F32))
        + (pltpu.VMEM((n_slab * TILE, G), BF16),) * 2
        + (pltpu.VMEM((G, n_pair * pair_rows), BF16),) * 2
        + (pltpu.VMEM((n_pair * pair_rows, G), BF16),) * 2
        + (pltpu.SemaphoreType.DMA((6,)),),
        vmem=LARGE_VMEM,
        hbm=6,
    )(
        grid,
        wave_factors(),
        sums,
        *split_constant(wide_x.reshape(-1, G)),
        *split_constant(cas_y.T),
        *split_constant(cas_y),
    )[0]
    returned = lax.all_to_all(planes, CHIPS, 0, 0, tiled=True)

    def probe(side):
        return call(
            functools.partial(probe_kernel, side, shift), [((8, atoms), F32)], 10**9, smem=1, vmem=LARGE_VMEM
        )(meta, returned, *tables)[0]

    theirs = beside(probe(1), False)
    three = ((3, atoms), F32)
    return tuple(
        call(finish_kernel, [three, three, three], 10**6)(
            probe(0), theirs, ordered, applied, dipoles, residual
        )
    )


def solution(mesh):
    slab, space = (mesh.shape["slab"], mesh.shape["space"])
    mesh = Mesh(mesh.devices.reshape(slab, space // 2, 2), BOTH)
    in_specs = (
        P(None, BOTH),
        P(None, BOTH),
        P(None, BOTH),
        P(None, BOTH),
        P(BOTH),
        P(BOTH, None),
        P(BOTH, None),
        P(BOTH, None, None),
        P(BOTH, None),
    )
    out_specs = (P(None, BOTH), P(None, BOTH), P(None, BOTH))
    return jax.shard_map(local, mesh=mesh, in_specs=in_specs, out_specs=out_specs, check_vma=False)
```

```python
import functools
import math

import jax
import jax.numpy as jnp
import ml_dtypes
import numpy as np
from jax import lax
from jax.experimental import pallas as pl
from jax.experimental.pallas import tpu as pltpu
from jax.sharding import Mesh
from jax.sharding import PartitionSpec as P

G = 256
TILE = 128
SPACE = ("pair", "core")
BOTH = ("slab", "pair", "core")
CHIPS = ("slab", "pair")
BETA = 0.4
THOLE = 0.39
ROOT_PI = math.sqrt(math.pi)
SELF_FIELD = 4.0 * BETA**3 / (3.0 * ROOT_PI)
F32 = jnp.float32
BF16 = jnp.bfloat16
SCALED_ERFC_T = 0.45
SCALED_ERFC = (
    0.25388532876968384,
    0.25388309359550476,
    0.22827406227588654,
    0.17522020637989044,
    0.1201537474989891,
    -0.023065825924277306,
    0.14381752908229828,
    -0.3022053837776184,
    0.19167575240135193,
    -0.04163854941725731,
)
NT = (((1,), (1,)), ((), ()))
NN = (((1,), (0,)), ((), ()))
TN = (((0,), (0,)), ((), ()))
SMALL_VMEM = 6 * 1024 * 1024
LARGE_VMEM = 16 * 1024 * 1024


def halves(values):
    high = values.astype(BF16)
    return (high, (values - high.astype(F32)).astype(BF16))


def product(left, right, dims, stacked=True):
    def one(a, b):
        return lax.dot_general(a, b, dims, preferred_element_type=F32)

    (left_dim,), (right_dim,) = dims[0]
    if not stacked:
        return one(left[0], right[0]) + (one(left[0], right[1]) + one(left[1], right[0]))
    return one(
        jnp.concatenate([left[0], left[0], left[1]], left_dim),
        jnp.concatenate([right[0], right[1], right[0]], right_dim),
    )


def thirds(values):
    high = values.astype(BF16).astype(F32)
    rest = values - high
    middle = rest.astype(BF16).astype(F32)
    return jnp.concatenate([high, middle, rest - middle], 0).astype(BF16)


def selected(values, one_hot, dims):
    rows = values.shape[0]
    picked = lax.dot_general(thirds(values), one_hot, dims, preferred_element_type=F32)
    return picked[:rows] + (picked[rows : 2 * rows] + picked[2 * rows :])


def order_matrix(order_row, count):
    ids = lax.broadcasted_iota(jnp.int32, (count, count), 0)
    return jnp.where(ids == order_row, 1.0, 0.0).astype(BF16)


COUNTS_AT = 32
ORDER_AT = 36
PARITY_AT = 40


def meta_kernel(lists, counts, send, after, meta):
    parity = lax.axis_index("core")
    for tile in range(4):

        def remap(place, carry):
            entry = lists[0, tile, place]
            remote = entry - 4
            pair = lax.shift_right_arithmetic(remote, 1)
            pair = pair + jnp.where(pair >= 4, 1, 0)
            along = jnp.where(pair >= 3, 1, 0) + jnp.where(pair >= 6, 1, 0)
            across = pair - 3 * along
            base = jnp.where(across == 1, 4, jnp.where(across == 2 - 2 * parity, 10, 16))
            slot = base + along * 2 + (remote & 1)
            meta[tile * 8 + place] = jnp.where(entry < 4, entry, slot)
            return carry

        lax.fori_loop(0, 8, remap, 0)
        meta[COUNTS_AT + tile] = counts[0, tile]
    first, second = (send[0, 0], send[0, 1])
    third = jnp.where(
        (first != 0) & (second != 0), 0, jnp.where((first != 1) & (second != 1), 1, 2)
    )
    meta[ORDER_AT] = first
    meta[ORDER_AT + 1] = second
    meta[ORDER_AT + 2] = third
    meta[ORDER_AT + 3] = 6 - first - second - third
    meta[PARITY_AT] = parity


def call(kernel, outs, flops, smem=0, scratch=(), vmem=SMALL_VMEM, hbm=0):
    def run(*args):
        kept = len(args) - hbm
        args = args[:kept] + tuple(
            pltpu.with_memory_space_constraint(array, pltpu.HBM) for array in args[kept:]
        )
        in_specs = [pl.BlockSpec(memory_space=pltpu.SMEM)] * smem
        in_specs += [pl.BlockSpec(memory_space=pltpu.VMEM)] * (kept - smem)
        in_specs += [pl.BlockSpec(memory_space=pltpu.HBM)] * hbm
        return pl.pallas_call(
            kernel,
            out_shape=[jax.ShapeDtypeStruct(shape, dtype) for shape, dtype in outs],
            in_specs=in_specs,
            out_specs=[pl.BlockSpec(memory_space=pltpu.VMEM)] * len(outs),
            scratch_shapes=list(scratch),
            compiler_params=pltpu.CompilerParams(vmem_limit_bytes=vmem),
            cost_estimate=pl.CostEstimate(
                flops=flops, bytes_accessed=1 << 20, transcendentals=0
            ),
        )(*args)

    return run


def gather_kernel(send, *refs):
    sources, (own, sent, bundle), held, sems = (refs[:5], refs[5:8], refs[8:13], refs[13])
    copies = [
        pltpu.make_async_copy(source, target, sems.at[at])
        for at, (source, target) in enumerate(zip(sources, held))
    ]
    for copy in copies:
        copy.start()
    for copy in copies:
        copy.wait()
    residual, cells, fraction, alphas, order = held
    atoms = residual.shape[1]
    in_cells = cells[...].astype(F32)
    bundle[0:3, :atoms] = in_cells
    bundle[3:6, :atoms] = fraction[...]
    bundle[6:8, :atoms] = jnp.zeros((2, atoms), F32)
    position = in_cells + fraction[...]
    rows = jnp.concatenate(
        [position, alphas[...].reshape(1, atoms), residual[...], jnp.zeros((1, atoms), F32)], 0
    )
    picked = selected(rows, order_matrix(order[...], atoms), NN)
    for tile in range(atoms // TILE):
        own[tile] = picked[:, tile * TILE : (tile + 1) * TILE]
    for place in range(2):
        block = own[send[0, place]]
        sent[place] = block
        bundle[:, atoms + place * TILE : atoms + (place + 1) * TILE] = block


def search_rows(block):
    return block[3:4] * block[4:7]


def fill_pool(pool, extents, own, level, before, after, meta):
    inner_step = jnp.where(meta[PARITY_AT] == 0, 1.0, -1.0)
    rows = lax.broadcasted_iota(jnp.int32, (8, TILE), 0)
    for tile in range(4):
        pool[tile] = own[tile]
    for along, source in enumerate((before, level, after)):
        for kind, step in enumerate((0.0, inner_step, -inner_step)):
            shift = jnp.where(
                rows == 0,
                float((along - 1) * extents[0]),
                jnp.where(rows == 1, step * float(extents[1]), 0.0),
            )
            for member in range(2):
                pool[4 + 6 * kind + 2 * along + member] = source[kind, member] + shift


def own_columns(columns, block, count):
    turned = block.T
    for row in range(count):
        columns[row] = jnp.broadcast_to(turned[:, row : row + 1], (TILE, TILE))


def wrap_depth(depth):
    half = 0.5 * G
    return jnp.where(depth > half, depth - G, jnp.where(depth < -half, depth + G, depth))


PAIR_ROWS = 32
GROUP = 4


def pair_kernel(first_place, count, extents, meta, own, level, before, after, pool, pairs, found, columns, totals):
    fill_pool(pool, extents, own, level, before, after, meta)

    def tile_step(at, carry):
        tile = meta[ORDER_AT + first_place + at]
        block = own[tile]
        own_columns(columns, jnp.concatenate([block[:3], lax.rsqrt(block[3:4]), block[4:]], 0), 4)
        live = meta[COUNTS_AT + tile]

        def chunk_step(chunk, carry):
            start = pl.multiple_of(chunk * PAIR_ROWS, PAIR_ROWS)
            rows = pl.ds(start, PAIR_ROWS)
            shape = (PAIR_ROWS, TILE)
            ahead = lax.broadcasted_iota(jnp.int32, shape, 0) - lax.broadcasted_iota(
                jnp.int32, shape, 1
            )
            diagonal = jnp.where(ahead == -start, 1.0, 0.0)

            def group_step(group, sums):
                for member in range(GROUP):
                    entry = group * GROUP + member
                    slot = meta[tile * 8 + entry]
                    other = pool[slot]
                    itself = diagonal * jnp.where(slot == tile, 1.0, 0.0)
                    d_x = other[0:1] - columns[0, rows]
                    d_y = other[1:2] - columns[1, rows]
                    d_z = wrap_depth(other[2:3] - columns[2, rows])
                    square = d_x * d_x + d_y * d_y + d_z * d_z + itself
                    inverse = lax.rsqrt(square)
                    distance = square * inverse
                    inverse_sq = inverse * inverse
                    gauss = jnp.exp(-(BETA**2) * square)
                    stretch = 1.0 + (SCALED_ERFC_T * BETA) * distance
                    t = lax.rsqrt(stretch * stretch)
                    series = SCALED_ERFC[-1] * t + SCALED_ERFC[-2]
                    for term in SCALED_ERFC[-3::-1]:
                        series = series * t + term
                    bare_one = gauss * (series * t * inverse + 2.0 * BETA / ROOT_PI) * inverse_sq
                    bare_two = (3.0 * bare_one + (4.0 * BETA**3 / ROOT_PI) * gauss) * inverse_sq
                    damping = (square * distance) * columns[3, rows] * (THOLE * lax.rsqrt(other[3:4]))
                    decay = jnp.exp(-damping) * inverse * inverse_sq
                    keep = jnp.where(entry < live, 1.0, 0.0) * (1.0 - itself)
                    three = keep * (bare_one - decay)
                    five = keep * (bare_two - (3.0 + 3.0 * damping) * decay * inverse_sq)
                    pairs[0, at * 8 + entry, rows] = five
                    pairs[1, at * 8 + entry, rows] = three
                    pairs[2, at * 8 + entry, rows] = d_z
                    v = search_rows(other)
                    along = five * (d_x * v[0:1] + d_y * v[1:2] + d_z * v[2:3])
                    sums = (
                        sums[0] + (along * d_x - three * v[0:1]),
                        sums[1] + (along * d_y - three * v[1:2]),
                        sums[2] + (along * d_z - three * v[2:3]),
                    )
                return sums

            zero = jnp.zeros(shape, F32)
            sums = lax.fori_loop(0, (live + GROUP - 1) // GROUP, group_step, (zero, zero, zero))
            for part in range(3):
                totals[part, rows] = sums[part]
            return carry

        lax.fori_loop(0, TILE // PAIR_ROWS, chunk_step, 0)
        found[at] = updated(block, totals)
        return carry

    lax.fori_loop(0, count, tile_step, 0)


def field_rows(totals):
    return [jnp.sum(totals[part].T, axis=0, keepdims=True) for part in range(3)]


def updated(block, totals):
    alpha = block[3:4]
    field = field_rows(totals)
    rows = [alpha * (block[4 + part : 5 + part] + field[part]) for part in range(3)]
    return jnp.concatenate(rows + [jnp.zeros((5, TILE), F32)], 0)


APPLY_ROWS = 64


def fill_search(pool, owns, level, before, after, meta):
    place = 0
    for own in owns:
        for at in range(own.shape[0]):
            pool[meta[ORDER_AT + place]] = own[at]
            place += 1
    for along, source in enumerate((before, level, after)):
        for kind in range(3):
            for member in range(2):
                pool[4 + 6 * kind + 2 * along + member] = source[kind, member]


def join_kernel(own, inner, outer, level):
    for member in range(2):
        level[0, member] = own[member]
        if len(inner.shape) == 3:
            level[1, member] = inner[member]
        else:
            start = inner.shape[1] - (2 - member) * TILE
            level[1, member] = inner[:, start : start + TILE]
        level[2, member] = outer[member]


def apply_tile(meta, tile, at, pairs, geometry, pool, columns, totals):
    block = geometry[tile]
    own_columns(columns, block, 2)
    live = meta[COUNTS_AT + tile]

    def chunk_step(chunk, carry):
        rows = pl.ds(pl.multiple_of(chunk * APPLY_ROWS, APPLY_ROWS), APPLY_ROWS)

        def group_step(group, sums):
            for member in range(GROUP):
                entry = group * GROUP + member
                slot = meta[tile * 8 + entry]
                other = geometry[slot]
                v = pool[slot]
                d_x = other[0:1] - columns[0, rows]
                d_y = other[1:2] - columns[1, rows]
                d_z = pairs[2, at * 8 + entry, rows]
                three = pairs[1, at * 8 + entry, rows]
                along = pairs[0, at * 8 + entry, rows] * (d_x * v[0:1] + d_y * v[1:2] + d_z * v[2:3])
                sums = (
                    sums[0] + (along * d_x - three * v[0:1]),
                    sums[1] + (along * d_y - three * v[1:2]),
                    sums[2] + (along * d_z - three * v[2:3]),
                )
            return sums

        zero = jnp.zeros((APPLY_ROWS, TILE), F32)
        sums = lax.fori_loop(0, (live + GROUP - 1) // GROUP, group_step, (zero, zero, zero))
        for part in range(3):
            totals[part, rows] = sums[part]
        return carry

    lax.fori_loop(0, TILE // APPLY_ROWS, chunk_step, 0)


def sweep_tiles(place, meta, geometry, banks, found, pool, columns, totals, local=None):
    done = 0
    for pairs in banks:
        count = pairs.shape[1] // 8

        def tile_step(at, carry):
            tile = meta[ORDER_AT + place + done + at]
            apply_tile(meta, tile, at, pairs, geometry, pool, columns, totals)
            rows = updated(geometry[tile], totals)
            found[done + at] = rows
            if local is not None:
                local[tile] = rows
            return carry

        lax.fori_loop(0, count, tile_step, 0)
        done += count


def sweep_kernel(place, owns, meta, geometry, *refs):
    own_refs, (level, before, after) = (refs[:owns], refs[owns : owns + 3])
    banks, (found, pool, columns, totals) = (refs[owns + 3 : -4], refs[-4:])
    fill_search(pool, own_refs, level, before, after, meta)
    sweep_tiles(place, meta, geometry, banks, found, pool, columns, totals)


def direction_kernel(
    meta, geometry, own_a, own_b, level, before, after, sent, pairs_b, pairs_c, order, found, bundle, pool, columns, totals, local
):
    atoms = order.shape[1]
    fill_search(pool, (own_a, own_b), level, before, after, meta)
    sweep_tiles(2, meta, geometry, (pairs_b, pairs_c), found, pool, columns, totals, local)
    for place in range(2):
        block = sent[place]
        local[meta[ORDER_AT + place]] = block
        bundle[:, atoms + place * TILE : atoms + (place + 1) * TILE] = block
    in_tiles = jnp.concatenate([local[tile] for tile in range(4)], 1)
    bundle[:, :atoms] = selected(in_tiles, order_matrix(order[...], atoms), NT)


def final_field_kernel(
    meta, geometry, sent, rest, level, before, after, pairs_a, order, stored_b, stored_c, applied, sums, pool, columns, totals, local, pairs_b, pairs_c, sems
):
    copies = [
        pltpu.make_async_copy(source, target, sems.at[at])
        for at, (source, target) in enumerate(((stored_b, pairs_b), (stored_c, pairs_c)))
    ]
    for copy in copies:
        copy.start()
    atoms = order.shape[1]
    fill_search(pool, (sent, rest), level, before, after, meta)
    both = (jnp.zeros((1, TILE), F32), jnp.zeros((1, TILE), F32))
    for first, pairs in ((0, pairs_a), (2, pairs_b), (3, pairs_c)):
        if first:
            copies[first - 2].wait()

        def tile_step(at, both):
            curve, dots = both
            place = first + at
            tile = meta[ORDER_AT + place]
            apply_tile(meta, tile, at, pairs, geometry, pool, columns, totals)
            block = geometry[tile]
            ahead = rest[first - 2 + at] if first else sent[at]
            field = field_rows(totals)
            rows = []
            for part in range(3):
                d = ahead[part : part + 1]
                value = d / block[3:4] - field[part] - SELF_FIELD * d
                curve = curve + d * value
                dots = dots + d * block[4 + part : 5 + part]
                rows.append(value)
            local[tile] = jnp.concatenate(rows + [jnp.zeros((5, TILE), F32)], 0)
            return (curve, dots)

        both = lax.fori_loop(0, pairs.shape[1] // 8, tile_step, both)
    in_tiles = jnp.concatenate([local[tile] for tile in range(4)], 1)
    applied[...] = selected(in_tiles, order_matrix(order[...], atoms), NT)
    lane = lax.broadcasted_iota(jnp.int32, (8, TILE), 1)
    curve_sum = jnp.sum(both[0], axis=1, keepdims=True)
    dot_sum = jnp.sum(both[1], axis=1, keepdims=True)
    sums[...] = jnp.where(lane == 1, curve_sum, jnp.where(lane == 2, dot_sum, 0.0))


def spline(fraction):
    centre_arg = fraction - 0.5

    def middle(u):
        return (55.0 + u * (20.0 + u * (-120.0 + u * (80.0 - 16.0 * u)))) / 96.0

    def middle_slope(u):
        return (20.0 + u * (-240.0 + u * (240.0 - 64.0 * u))) / 96.0

    def outer(u):
        w = 5.0 - 2.0 * u
        return (w * w) * (w * w) / 384.0

    def outer_slope(u):
        w = 5.0 - 2.0 * u
        return -(w * w * w) / 48.0

    sq = centre_arg * centre_arg
    weights = (
        outer(fraction + 1.5),
        middle(fraction + 0.5),
        115.0 / 192.0 - 0.625 * sq + 0.25 * sq * sq,
        middle(1.5 - fraction),
        outer(2.5 - fraction),
    )
    slopes = (
        outer_slope(fraction + 1.5),
        middle_slope(fraction + 0.5),
        -1.25 * centre_arg + centre_arg * sq,
        -middle_slope(1.5 - fraction),
        -outer_slope(2.5 - fraction),
    )
    return (weights, slopes)


def table(cell_row, values, length, wrapped):
    atoms = cell_row.shape[1]
    ids = lax.broadcasted_iota(jnp.int32, (length, atoms), 0)
    if wrapped:
        ahead = ids - cell_row + 2
        ahead = jnp.where(ahead >= G, ahead - G, jnp.where(ahead < 0, ahead + G, ahead))
    else:
        ahead = ids - cell_row
    total = jnp.zeros((length, atoms), F32)
    for step in range(5):
        total = jnp.where(ahead == step, values[step], total)
    return total


def tables_kernel(
    meta, mine, beside, stored_high, stored_low, tab_x, tab_y, w_high, w_low, slope_z, cas_high, cas_low, sems
):
    core = meta[PARITY_AT]
    copies = [
        pltpu.make_async_copy(stored_high.at[core], cas_high, sems.at[0]),
        pltpu.make_async_copy(stored_low.at[core], cas_low, sems.at[1]),
    ]
    for copy in copies:
        copy.start()
    for copy in copies:
        copy.wait()
    cas = (cas_high[...], cas_low[...])
    for side, statics in enumerate((mine, beside)):
        atoms = tab_x.shape[3]
        cells = statics[0:3, :atoms].astype(jnp.int32)
        for dim, out in ((0, tab_x), (1, tab_y)):
            weights, slopes = spline(statics[3 + dim : 4 + dim, :atoms])
            out[side, 0] = table(cells[dim : dim + 1], weights, out.shape[2], False)
            out[side, 1] = table(cells[dim : dim + 1], slopes, out.shape[2], False)
        weights, slopes = spline(statics[5:6, :atoms])
        high, low = halves(product(cas, halves(table(cells[2:3], weights, G, True)), NN))
        w_high[side] = high
        w_low[side] = low
        slope_z[side] = product(cas, halves(table(cells[2:3], slopes, G, True)), NN)


def spread_part(side, d, tab_x, tab_y, w_high, w_low, slope_z):
    w_z = (w_high[side], w_low[side])
    s_z = halves(slope_z[side] * d[2:3])
    weight_x = tab_x[side, 0]
    slope_part = tab_x[side, 1] * d[0:1]
    weight_part = weight_x * d[1:2]
    sides = []
    for y in range(tab_y.shape[2]):
        w_y, s_y = (tab_y[side, 0, y : y + 1], tab_y[side, 1, y : y + 1])
        sides.append((slope_part * w_y + weight_part * s_y, weight_x * w_y))
    rows = halves(jnp.concatenate([pair[0] for pair in sides], 0))
    flat = halves(jnp.concatenate([pair[1] for pair in sides], 0))
    return product(w_z, rows, NT) + product(s_z, flat, NT)


def spread_own_kernel(ordered, tab_x, tab_y, w_high, w_low, slope_z, out):
    out[...] = spread_part(0, ordered[:, : tab_x.shape[3]], tab_x, tab_y, w_high, w_low, slope_z)


def put_lanes(out, flat):
    for row in range(8):
        out[:, row, :] = flat[:, row * TILE : (row + 1) * TILE]


def get_lanes(grid):
    return jnp.concatenate([grid[:, row, :] for row in range(8)], 1)


def spread_both_kernel(shift, meta, ordered, mine, tab_x, tab_y, w_high, w_low, slope_z, out, flat):
    theirs = spread_part(1, ordered[:, : tab_x.shape[3]], tab_x, tab_y, w_high, w_low, slope_z)
    ours = mine[...]
    width = ours.shape[1]
    even = meta[PARITY_AT] == 0
    lower = jnp.where(even, ours, theirs)
    upper = jnp.where(even, theirs, ours)
    flat[:, :shift] = lower[:, :shift]
    flat[:, shift:width] = lower[:, shift:] + upper[:, : width - shift]
    flat[:, width : width + shift] = upper[:, width - shift :]
    flat[:, width + shift :] = jnp.zeros((flat.shape[0], flat.shape[1] - width - shift), F32)
    put_lanes(out, flat)


def plane_kernel(shapes, grid, waves, sums, *refs):
    stored, out, flat, padded = (refs[:6], refs[6], refs[7], refs[8])
    held, sems = (refs[9:15], refs[15])
    copies = [
        pltpu.make_async_copy(source, target, sems.at[at])
        for at, (source, target) in enumerate(zip(stored, held))
    ]
    for copy in copies:
        copy.start()
    x_high, x_low, yt_high, yt_low, y_high, y_low = held
    n_slab, n_pair, x_rows, y_rows = shapes
    width = x_rows * y_rows
    flat[...] = get_lanes(grid)
    padded[...] = jnp.zeros(padded.shape, F32)
    for s in range(n_slab):
        for y in range(y_rows):
            padded[y * n_pair : (y + 1) * n_pair, s * TILE : s * TILE + x_rows] = flat[
                s * n_pair : (s + 1) * n_pair, y * x_rows : (y + 1) * x_rows
            ]
    copies[0].wait()
    copies[1].wait()
    cas_x = (x_high[...], x_low[...])
    along_x = product(halves(padded[...]), cas_x, NN, False)
    for copy in copies[2:]:
        copy.wait()
    spectrum = product((yt_high[...], yt_low[...]), halves(along_x), NN, False)
    freq_z = lax.axis_index("slab") * (2 * n_pair) + 2 * lax.axis_index("pair") + lax.axis_index("core")
    ids_x = lax.broadcasted_iota(jnp.int32, (1, G), 1)
    by_x = waves[...]
    by_z = jnp.sum(jnp.where(ids_x == freq_z, by_x, 0.0), axis=1, keepdims=True)
    by_y = by_x.T
    anchor = jnp.where(
        (lax.broadcasted_iota(jnp.int32, (G, G), 0) + lax.broadcasted_iota(jnp.int32, (G, G), 1) + freq_z) == 0, 1.0, 0.0
    )
    squares = by_x[0:1] + by_y[:, 0:1] + (by_z[0:1] + anchor)
    factor = (1.0 - anchor) * (by_x[1:2] * by_z[1:2]) * by_y[:, 1:2] / (math.pi * float(G) ** 3 * squares)
    scaled = spectrum * factor
    energy = jnp.sum(jnp.sum(spectrum * scaled, axis=0, keepdims=True), axis=1, keepdims=True)
    back = halves(product((y_high[...], y_low[...]), halves(scaled), NN, False))
    planes = product(back, cas_x, NT, False)
    for s in range(n_slab):
        for y in range(y_rows):
            flat[s * n_pair : (s + 1) * n_pair, y * x_rows : (y + 1) * x_rows] = planes[
                y * n_pair : (y + 1) * n_pair, s * TILE : s * TILE + x_rows
            ]
    spare = flat.shape[1] - width
    lane = lax.broadcasted_iota(jnp.int32, (1, spare), 1)
    known = jnp.concatenate([sums[0:1], jnp.zeros((1, spare - TILE), F32)], 1)
    tail = jnp.where(lane == 0, energy, known)
    flat[:, width:] = jnp.broadcast_to(tail, (flat.shape[0], spare))
    put_lanes(out, flat)


def probe_part(side, planes, tab_x, tab_y, w_high, w_low, slope_z):
    x_rows = tab_x.shape[2]
    by_weight = product(planes, (w_high[side], w_low[side]), TN)
    by_slope = product(planes, halves(slope_z[side]), TN)
    weight_x, slope_x = (tab_x[side, 0], tab_x[side, 1])
    fields = [0.0, 0.0, 0.0]
    for y in range(tab_y.shape[2]):
        rows = slice(y * x_rows, (y + 1) * x_rows)
        w_y, s_y = (tab_y[side, 0, y : y + 1], tab_y[side, 1, y : y + 1])
        weighted = by_weight[rows]
        fields[0] += w_y * jnp.sum(slope_x * weighted, axis=0, keepdims=True)
        fields[1] += s_y * jnp.sum(weight_x * weighted, axis=0, keepdims=True)
        fields[2] += w_y * jnp.sum(weight_x * by_slope[rows], axis=0, keepdims=True)
    return fields


def probe_kernel(side, shift, meta, grid, tab_x, tab_y, w_high, w_low, slope_z, out):
    matrix = get_lanes(grid)
    width = tab_x.shape[2] * tab_y.shape[2]
    low_side = 0 if side == 0 else 1
    planes = jnp.where(
        meta[PARITY_AT] == low_side, matrix[:, :width], matrix[:, shift : shift + width]
    )
    fields = probe_part(side, halves(planes), tab_x, tab_y, w_high, w_low, slope_z)
    atoms = out.shape[1]
    scalars = jnp.sum(matrix[:, width + shift :], axis=0, keepdims=True)[:, :TILE]
    padded = jnp.concatenate([scalars, jnp.zeros((1, atoms - TILE), F32)], 1)
    out[...] = jnp.concatenate(fields + [padded, jnp.zeros((4, atoms), F32)], 0)


def finish_kernel(mine, theirs, ordered, applied, dipoles, residual, next_dipoles, next_residual, direction):
    total = mine[...] + theirs[...]
    step = total[3:4, 2:3] / (total[3:4, 0:1] + total[3:4, 1:2])
    d = ordered[0:3, : dipoles.shape[1]]
    next_dipoles[...] = dipoles[...] + step * d
    next_residual[...] = residual[...] - step * (applied[0:3] + total[0:3])
    direction[...] = d


def cas_matrix(first, second):
    angles = 2.0 * np.pi / G * (np.outer(first, second) % G)
    return np.cos(angles) + np.sin(angles)


def split_constant(values):
    whole = values.astype(np.float32)
    high = whole.astype(ml_dtypes.bfloat16)
    low = (values - high.astype(np.float64)).astype(ml_dtypes.bfloat16)
    return (jnp.asarray(high), jnp.asarray(low))


def wave_factors():
    freq = np.arange(G)
    wrapped = np.where(freq > G // 2, freq - G, freq) / G
    angles = 2.0 * np.pi / G * freq
    modulus = 115.0 / 192.0 + 19.0 / 48.0 * np.cos(angles) + 1.0 / 192.0 * np.cos(2.0 * angles)
    rows = np.zeros((8, G), np.float32)
    rows[0] = wrapped * wrapped
    rows[1] = np.exp(-((np.pi / BETA) ** 2) * wrapped * wrapped) / (modulus * modulus)
    return jnp.asarray(rows)


def swap_pairs(n_slab, n_space, odd):
    pairs = []
    for s in range(n_slab):
        for q in range(n_space):
            partner = (q + 1 if (q % 2 == 1) == odd else q - 1) % n_space
            pairs.append((s * n_space + q, s * n_space + partner))
    return pairs


def beside(block, odd):
    n_slab, n_space = (lax.axis_size("slab"), lax.axis_size(SPACE))
    return lax.ppermute(block, BOTH, swap_pairs(n_slab, n_space, odd))


def along_slab(level):
    n_slab = lax.axis_size("slab")
    up = [(i, (i + 1) % n_slab) for i in range(n_slab)]
    down = [(j, i) for i, j in up]
    return (level, lax.ppermute(level, "slab", up), lax.ppermute(level, "slab", down))


def joined(block, inner, outer):
    return call(join_kernel, [((3, 2, 8, TILE), F32)], 10**6)(block, inner, outer)[0]


def around(block, bundle=None, beneath=None):
    inner = beside(block if bundle is None else bundle, False)
    outer, _ = lax.optimization_barrier((beside(block, True), beneath))
    return along_slab(joined(block, inner, outer)), inner


def local(
    dipoles, residual, cells, fraction, polarizability, tile_order, send_tiles, tile_lists, tile_counts
):
    n_slab, n_space = (lax.axis_size("slab"), lax.axis_size(SPACE))
    n_pair = n_space // 2
    atoms = residual.shape[1]
    extents = (G // n_slab, G // n_space)
    x_rows = -(-(extents[0] + 4) // 8) * 8
    y_rows = extents[1] + 4
    pair_rows = 2 * extents[1] + 4
    shift = extents[1] * x_rows
    half = G // 2
    tile_shape = ((4, 8, TILE), F32)
    two_shape = ((2, 8, TILE), F32)
    one_bank = ((3, 8, TILE, TILE), F32)
    pool_scratch = pltpu.VMEM((22, 8, TILE), F32)
    total_scratch = pltpu.VMEM((3, TILE, TILE), F32)
    own, sent, statics = pl.pallas_call(
        gather_kernel,
        out_shape=[
            jax.ShapeDtypeStruct(*tile_shape),
            jax.ShapeDtypeStruct(*two_shape),
            jax.ShapeDtypeStruct((8, atoms + 2 * TILE), F32),
        ],
        in_specs=[pl.BlockSpec(memory_space=pltpu.SMEM)] + [pl.BlockSpec(memory_space=pltpu.HBM)] * 5,
        out_specs=[pl.BlockSpec(memory_space=pltpu.VMEM)] * 3,
        scratch_shapes=[
            pltpu.VMEM((3, atoms), F32),
            pltpu.VMEM((3, atoms), jnp.int32),
            pltpu.VMEM((3, atoms), F32),
            pltpu.VMEM((atoms,), F32),
            pltpu.VMEM((1, atoms), jnp.int32),
            pltpu.SemaphoreType.DMA((5,)),
        ],
        compiler_params=pltpu.CompilerParams(vmem_limit_bytes=SMALL_VMEM),
    )(
        send_tiles,
        *[
            pltpu.with_memory_space_constraint(array, pltpu.HBM)
            for array in (residual, cells, fraction, polarizability, tile_order)
        ],
    )
    smem, anywhere = (pl.BlockSpec(memory_space=pltpu.SMEM), pl.BlockSpec(memory_space=pltpu.HBM))
    meta = pl.pallas_call(
        meta_kernel,
        out_shape=jax.ShapeDtypeStruct((48,), jnp.int32),
        in_specs=[smem, smem, smem, pl.BlockSpec(memory_space=pltpu.VMEM)],
        out_specs=smem,
        compiler_params=pltpu.CompilerParams(vmem_limit_bytes=SMALL_VMEM),
        cost_estimate=pl.CostEstimate(flops=10**8, bytes_accessed=1 << 20, transcendentals=0),
    )(tile_lists, tile_counts, send_tiles, sent)
    first, statics_beside = around(sent, statics, beneath=meta)

    freq = np.arange(G)
    padded_x = np.stack([(s * extents[0] + np.arange(x_rows) - 2) % G for s in range(n_slab)])
    real_x = np.tile(np.arange(x_rows) < extents[0] + 4, n_slab)
    cas_x = cas_matrix(padded_x.reshape(-1), freq) * real_x[:, None]
    rows_y = (np.arange(n_pair)[None] * 2 * extents[1] + np.arange(pair_rows)[:, None] - 2) % G
    cas_y = cas_matrix(rows_y.reshape(-1), freq)
    freq_by_core = np.stack([freq[0::2], freq[1::2]])
    cas_z = cas_matrix(freq_by_core.reshape(-1), freq).reshape(2, half, G)
    wide_x = np.zeros((n_slab, TILE, G))
    wide_x[:, :x_rows] = cas_x.reshape(n_slab, x_rows, G)
    def pairs_of(place, count):
        return call(
            functools.partial(pair_kernel, place, count, extents),
            [((22, 8, TILE), F32), ((3, 8 * count, TILE, TILE), F32), ((count, 8, TILE), F32)],
            10**9,
            smem=1,
            scratch=(pltpu.VMEM((4, TILE, TILE), F32), total_scratch),
        )(meta, own, *first)

    geometry, pairs_a, search_a = pairs_of(0, 2)
    _, pairs_b, search_b = pairs_of(2, 1)
    _, pairs_c, search_c = pairs_of(3, 1)
    sweep_scratch = (pool_scratch, pltpu.VMEM((3, TILE, TILE), F32), total_scratch)
    second, _ = around(search_a, beneath=search_b)

    def sweep(place, owns, received, banks):
        return call(
            functools.partial(sweep_kernel, place, len(owns)),
            [two_shape],
            10**8,
            smem=1,
            scratch=sweep_scratch,
        )(meta, geometry, *owns, *received, *banks)[0]

    searches = (search_a, search_b, search_c)
    next_a = sweep(0, searches, second, (pairs_a,))
    next_b = sweep(2, searches, second, (pairs_b, pairs_c))
    third, _ = around(next_a, beneath=next_b)
    statics_beside, _ = lax.optimization_barrier((statics_beside, third[0]))
    tables = call(
        tables_kernel,
        [
            ((2, 2, x_rows, atoms), F32),
            ((2, 2, y_rows, atoms), F32),
            ((2, half, atoms), BF16),
            ((2, half, atoms), BF16),
            ((2, half, atoms), F32),
        ],
        10**8,
        smem=1,
        vmem=LARGE_VMEM,
        scratch=(pltpu.VMEM((half, G), BF16),) * 2 + (pltpu.SemaphoreType.DMA((2,)),),
        hbm=2,
    )(meta, statics, statics_beside, *split_constant(cas_z))
    level, before, after = third
    after, _ = lax.optimization_barrier((after, tables[1]))
    third = (level, before, after)
    local_scratch = pltpu.VMEM((4, 8, TILE), F32)
    sent = sweep(0, (next_a, next_b), third, (pairs_a,))
    outer = beside(sent, True)
    rest, ordered = call(
        direction_kernel,
        [two_shape, ((8, atoms + 2 * TILE), F32)],
        10**8,
        smem=1,
        scratch=sweep_scratch + (local_scratch,),
    )(meta, geometry, next_a, next_b, *third, sent, pairs_b, pairs_c, tile_order)
    ordered_beside = beside(ordered, False)
    message = ((half, 8, TILE), F32)
    flat_scratch = pltpu.VMEM((half, 8 * TILE), F32)
    spread_own = call(spread_own_kernel, [((half, x_rows * y_rows), F32)], 10**9, vmem=LARGE_VMEM)(ordered, *tables)[0]
    spread = call(
        functools.partial(spread_both_kernel, shift),
        [message],
        10**9,
        smem=1,
        scratch=(flat_scratch,),
        vmem=LARGE_VMEM,
    )(meta, ordered_beside, spread_own, *tables)[0]
    spread, outer = lax.optimization_barrier((spread, outer))
    grid = lax.all_to_all(spread, CHIPS, 0, 0, tiled=True)
    last = along_slab(joined(sent, ordered_beside, outer))
    applied, sums = call(
        final_field_kernel,
        [((8, atoms), F32), ((8, TILE), F32)],
        10**9,
        smem=1,
        scratch=sweep_scratch
        + (local_scratch, pltpu.VMEM(*one_bank), pltpu.VMEM(*one_bank), pltpu.SemaphoreType.DMA((2,))),
        vmem=LARGE_VMEM,
        hbm=2,
    )(meta, geometry, sent, rest, *last, pairs_a, tile_order, pairs_b, pairs_c)
    planes = call(
        functools.partial(plane_kernel, (n_slab, n_pair, x_rows, pair_rows)),
        [message],
        10**9,
        scratch=(flat_scratch, pltpu.VMEM((n_pair * pair_rows, n_slab * TILE), F32))
        + (pltpu.VMEM((n_slab * TILE, G), BF16),) * 2
        + (pltpu.VMEM((G, n_pair * pair_rows), BF16),) * 2
        + (pltpu.VMEM((n_pair * pair_rows, G), BF16),) * 2
        + (pltpu.SemaphoreType.DMA((6,)),),
        vmem=LARGE_VMEM,
        hbm=6,
    )(
        grid,
        wave_factors(),
        sums,
        *split_constant(wide_x.reshape(-1, G)),
        *split_constant(cas_y.T),
        *split_constant(cas_y),
    )[0]
    returned = lax.all_to_all(planes, CHIPS, 0, 0, tiled=True)

    def probe(side):
        return call(
            functools.partial(probe_kernel, side, shift), [((8, atoms), F32)], 10**9, smem=1, vmem=LARGE_VMEM
        )(meta, returned, *tables)[0]

    theirs = beside(probe(1), False)
    three = ((3, atoms), F32)
    return tuple(
        call(finish_kernel, [three, three, three], 10**6)(
            probe(0), theirs, ordered, applied, dipoles, residual
        )
    )


def solution(mesh):
    slab, space = (mesh.shape["slab"], mesh.shape["space"])
    mesh = Mesh(mesh.devices.reshape(slab, space // 2, 2), BOTH)
    in_specs = (
        P(None, BOTH),
        P(None, BOTH),
        P(None, BOTH),
        P(None, BOTH),
        P(BOTH),
        P(BOTH, None),
        P(BOTH, None),
        P(BOTH, None, None),
        P(BOTH, None),
    )
    out_specs = (P(None, BOTH), P(None, BOTH), P(None, BOTH))
    return jax.shard_map(local, mesh=mesh, in_specs=in_specs, out_specs=out_specs, check_vma=False)
```

```python
import functools
import math

import jax
import jax.numpy as jnp
import ml_dtypes
import numpy as np
from jax import lax
from jax.experimental import pallas as pl
from jax.experimental.pallas import tpu as pltpu
from jax.sharding import Mesh
from jax.sharding import PartitionSpec as P

G = 256
TILE = 128
SPACE = ("pair", "core")
BOTH = ("slab", "pair", "core")
CHIPS = ("slab", "pair")
BETA = 0.4
THOLE = 0.39
ROOT_PI = math.sqrt(math.pi)
SELF_FIELD = 4.0 * BETA**3 / (3.0 * ROOT_PI)
F32 = jnp.float32
BF16 = jnp.bfloat16
SCALED_ERFC_T = 0.45
SCALED_ERFC = (
    0.25388532876968384,
    0.25388309359550476,
    0.22827406227588654,
    0.17522020637989044,
    0.1201537474989891,
    -0.023065825924277306,
    0.14381752908229828,
    -0.3022053837776184,
    0.19167575240135193,
    -0.04163854941725731,
)
NT = (((1,), (1,)), ((), ()))
NN = (((1,), (0,)), ((), ()))
TN = (((0,), (0,)), ((), ()))
SMALL_VMEM = 6 * 1024 * 1024
LARGE_VMEM = 16 * 1024 * 1024


def halves(values):
    high = values.astype(BF16)
    return (high, (values - high.astype(F32)).astype(BF16))


def product(left, right, dims, stacked=True):
    def one(a, b):
        return lax.dot_general(a, b, dims, preferred_element_type=F32)

    (left_dim,), (right_dim,) = dims[0]
    if not stacked:
        return one(left[0], right[0]) + (one(left[0], right[1]) + one(left[1], right[0]))
    return one(
        jnp.concatenate([left[0], left[0], left[1]], left_dim),
        jnp.concatenate([right[0], right[1], right[0]], right_dim),
    )


def thirds(values):
    high = values.astype(BF16).astype(F32)
    rest = values - high
    middle = rest.astype(BF16).astype(F32)
    return jnp.concatenate([high, middle, rest - middle], 0).astype(BF16)


def selected(values, one_hot, dims):
    rows = values.shape[0]
    picked = lax.dot_general(thirds(values), one_hot, dims, preferred_element_type=F32)
    return picked[:rows] + (picked[rows : 2 * rows] + picked[2 * rows :])


def order_matrix(order_row, count):
    ids = lax.broadcasted_iota(jnp.int32, (count, count), 0)
    return jnp.where(ids == order_row, 1.0, 0.0).astype(BF16)


COUNTS_AT = 32
ORDER_AT = 36
PARITY_AT = 40


def meta_kernel(lists, counts, send, after, meta):
    parity = lax.axis_index("core")
    for tile in range(4):

        def remap(place, carry):
            entry = lists[0, tile, place]
            remote = entry - 4
            pair = lax.shift_right_arithmetic(remote, 1)
            pair = pair + jnp.where(pair >= 4, 1, 0)
            along = jnp.where(pair >= 3, 1, 0) + jnp.where(pair >= 6, 1, 0)
            across = pair - 3 * along
            base = jnp.where(across == 1, 4, jnp.where(across == 2 - 2 * parity, 10, 16))
            slot = base + along * 2 + (remote & 1)
            meta[tile * 8 + place] = jnp.where(entry < 4, entry, slot)
            return carry

        lax.fori_loop(0, 8, remap, 0)
        meta[COUNTS_AT + tile] = counts[0, tile]
    first, second = (send[0, 0], send[0, 1])
    third = jnp.where(
        (first != 0) & (second != 0), 0, jnp.where((first != 1) & (second != 1), 1, 2)
    )
    meta[ORDER_AT] = first
    meta[ORDER_AT + 1] = second
    meta[ORDER_AT + 2] = third
    meta[ORDER_AT + 3] = 6 - first - second - third
    meta[PARITY_AT] = parity


def call(kernel, outs, flops, smem=0, scratch=(), vmem=SMALL_VMEM, hbm=0, hbm_outs=False):
    def run(*args):
        kept = len(args) - hbm
        args = args[:kept] + tuple(
            pltpu.with_memory_space_constraint(array, pltpu.HBM) for array in args[kept:]
        )
        in_specs = [pl.BlockSpec(memory_space=pltpu.SMEM)] * smem
        in_specs += [pl.BlockSpec(memory_space=pltpu.VMEM)] * (kept - smem)
        in_specs += [pl.BlockSpec(memory_space=pltpu.HBM)] * hbm
        return pl.pallas_call(
            kernel,
            out_shape=[
                (pltpu.HBM if hbm_outs else jax.ShapeDtypeStruct)(shape, dtype) for shape, dtype in outs
            ],
            in_specs=in_specs,
            out_specs=[pl.BlockSpec(memory_space=pltpu.HBM if hbm_outs else pltpu.VMEM)] * len(outs),
            scratch_shapes=list(scratch),
            compiler_params=pltpu.CompilerParams(vmem_limit_bytes=vmem),
            cost_estimate=pl.CostEstimate(
                flops=flops, bytes_accessed=1 << 20, transcendentals=0
            ),
        )(*args)

    return run


def gather_kernel(*refs):
    sources, (own, sent, bundle), held, sems = (refs[:6], refs[6:9], refs[9:15], refs[15])
    copies = [
        pltpu.make_async_copy(source, target, sems.at[at])
        for at, (source, target) in enumerate(zip(sources, held))
    ]
    for copy in copies:
        copy.start()
    for copy in copies:
        copy.wait()
    residual, cells, fraction, alphas, order, send = held
    atoms = residual.shape[1]
    in_cells = cells[...].astype(F32)
    bundle[0:3, :atoms] = in_cells
    bundle[3:6, :atoms] = fraction[...]
    bundle[6:8, :atoms] = jnp.zeros((2, atoms), F32)
    position = in_cells + fraction[...]
    rows = jnp.concatenate(
        [position, alphas[...].reshape(1, atoms), residual[...], jnp.zeros((1, atoms), F32)], 0
    )
    picked = selected(rows, order_matrix(order[...], atoms), NN)
    for tile in range(atoms // TILE):
        own[tile] = picked[:, tile * TILE : (tile + 1) * TILE]
    for place in range(2):
        block = own[send[0, place]]
        sent[place] = block
        bundle[:, atoms + place * TILE : atoms + (place + 1) * TILE] = block


def search_rows(block):
    return block[3:4] * block[4:7]


def fill_pool(pool, extents, own, level, before, after, meta):
    inner_step = jnp.where(meta[PARITY_AT] == 0, 1.0, -1.0)
    rows = lax.broadcasted_iota(jnp.int32, (8, TILE), 0)
    for tile in range(4):
        pool[tile] = own[tile]
    for along, source in enumerate((before, level, after)):
        for kind, step in enumerate((0.0, inner_step, -inner_step)):
            shift = jnp.where(
                rows == 0,
                float((along - 1) * extents[0]),
                jnp.where(rows == 1, step * float(extents[1]), 0.0),
            )
            for member in range(2):
                pool[4 + 6 * kind + 2 * along + member] = source[kind, member] + shift


def own_columns(columns, block, count):
    turned = block.T
    for row in range(count):
        columns[row] = jnp.broadcast_to(turned[:, row : row + 1], (TILE, TILE))


def wrap_depth(depth):
    half = 0.5 * G
    return jnp.where(depth > half, depth - G, jnp.where(depth < -half, depth + G, depth))


PAIR_ROWS = 32
GROUP = 4


def pair_kernel(first_place, count, extents, meta, own, level, before, after, pool, pairs, found, columns, totals):
    fill_pool(pool, extents, own, level, before, after, meta)

    def tile_step(at, carry):
        tile = meta[ORDER_AT + first_place + at]
        block = own[tile]
        own_columns(columns, jnp.concatenate([block[:3], lax.rsqrt(block[3:4]), block[4:]], 0), 4)
        live = meta[COUNTS_AT + tile]

        def chunk_step(chunk, carry):
            start = pl.multiple_of(chunk * PAIR_ROWS, PAIR_ROWS)
            rows = pl.ds(start, PAIR_ROWS)
            shape = (PAIR_ROWS, TILE)
            ahead = lax.broadcasted_iota(jnp.int32, shape, 0) - lax.broadcasted_iota(
                jnp.int32, shape, 1
            )
            diagonal = jnp.where(ahead == -start, 1.0, 0.0)

            def group_step(group, sums):
                for member in range(GROUP):
                    entry = group * GROUP + member
                    slot = meta[tile * 8 + entry]
                    other = pool[slot]
                    itself = diagonal * jnp.where(slot == tile, 1.0, 0.0)
                    d_x = other[0:1] - columns[0, rows]
                    d_y = other[1:2] - columns[1, rows]
                    d_z = wrap_depth(other[2:3] - columns[2, rows])
                    square = d_x * d_x + d_y * d_y + d_z * d_z + itself
                    inverse = lax.rsqrt(square)
                    distance = square * inverse
                    inverse_sq = inverse * inverse
                    gauss = jnp.exp(-(BETA**2) * square)
                    stretch = 1.0 + (SCALED_ERFC_T * BETA) * distance
                    t = lax.rsqrt(stretch * stretch)
                    series = SCALED_ERFC[-1] * t + SCALED_ERFC[-2]
                    for term in SCALED_ERFC[-3::-1]:
                        series = series * t + term
                    bare_one = gauss * (series * t * inverse + 2.0 * BETA / ROOT_PI) * inverse_sq
                    bare_two = (3.0 * bare_one + (4.0 * BETA**3 / ROOT_PI) * gauss) * inverse_sq
                    damping = (square * distance) * columns[3, rows] * (THOLE * lax.rsqrt(other[3:4]))
                    decay = jnp.exp(-damping) * inverse * inverse_sq
                    keep = jnp.where(entry < live, 1.0, 0.0) * (1.0 - itself)
                    three = keep * (bare_one - decay)
                    five = keep * (bare_two - (3.0 + 3.0 * damping) * decay * inverse_sq)
                    pairs[0, at * 8 + entry, rows] = five
                    pairs[1, at * 8 + entry, rows] = three
                    pairs[2, at * 8 + entry, rows] = d_z
                    v = search_rows(other)
                    along = five * (d_x * v[0:1] + d_y * v[1:2] + d_z * v[2:3])
                    sums = (
                        sums[0] + (along * d_x - three * v[0:1]),
                        sums[1] + (along * d_y - three * v[1:2]),
                        sums[2] + (along * d_z - three * v[2:3]),
                    )
                return sums

            zero = jnp.zeros(shape, F32)
            sums = lax.fori_loop(0, (live + GROUP - 1) // GROUP, group_step, (zero, zero, zero))
            for part in range(3):
                totals[part, rows] = sums[part]
            return carry

        lax.fori_loop(0, TILE // PAIR_ROWS, chunk_step, 0)
        found[at] = updated(block, totals)
        return carry

    lax.fori_loop(0, count, tile_step, 0)


def field_rows(totals):
    return [jnp.sum(totals[part].T, axis=0, keepdims=True) for part in range(3)]


def updated(block, totals):
    alpha = block[3:4]
    field = field_rows(totals)
    rows = [alpha * (block[4 + part : 5 + part] + field[part]) for part in range(3)]
    return jnp.concatenate(rows + [jnp.zeros((5, TILE), F32)], 0)


APPLY_ROWS = 64


def fill_search(pool, owns, level, before, after, meta):
    place = 0
    for own in owns:
        for at in range(own.shape[0]):
            pool[meta[ORDER_AT + place]] = own[at]
            place += 1
    for along, source in enumerate((before, level, after)):
        for kind in range(3):
            for member in range(2):
                pool[4 + 6 * kind + 2 * along + member] = source[kind, member]


def join_kernel(own, inner, outer, level):
    for member in range(2):
        level[0, member] = own[member]
        if len(inner.shape) == 3:
            level[1, member] = inner[member]
        else:
            start = inner.shape[1] - (2 - member) * TILE
            level[1, member] = inner[:, start : start + TILE]
        level[2, member] = outer[member]


def apply_tile(meta, tile, at, pairs, geometry, pool, columns, totals):
    block = geometry[tile]
    own_columns(columns, block, 2)
    live = meta[COUNTS_AT + tile]

    def chunk_step(chunk, carry):
        rows = pl.ds(pl.multiple_of(chunk * APPLY_ROWS, APPLY_ROWS), APPLY_ROWS)

        def group_step(group, sums):
            for member in range(GROUP):
                entry = group * GROUP + member
                slot = meta[tile * 8 + entry]
                other = geometry[slot]
                v = pool[slot]
                d_x = other[0:1] - columns[0, rows]
                d_y = other[1:2] - columns[1, rows]
                d_z = pairs[2, at * 8 + entry, rows]
                three = pairs[1, at * 8 + entry, rows]
                along = pairs[0, at * 8 + entry, rows] * (d_x * v[0:1] + d_y * v[1:2] + d_z * v[2:3])
                sums = (
                    sums[0] + (along * d_x - three * v[0:1]),
                    sums[1] + (along * d_y - three * v[1:2]),
                    sums[2] + (along * d_z - three * v[2:3]),
                )
            return sums

        zero = jnp.zeros((APPLY_ROWS, TILE), F32)
        sums = lax.fori_loop(0, (live + GROUP - 1) // GROUP, group_step, (zero, zero, zero))
        for part in range(3):
            totals[part, rows] = sums[part]
        return carry

    lax.fori_loop(0, TILE // APPLY_ROWS, chunk_step, 0)


def sweep_tiles(place, meta, geometry, banks, found, pool, columns, totals, local=None):
    done = 0
    for pairs in banks:
        count = pairs.shape[1] // 8

        def tile_step(at, carry):
            tile = meta[ORDER_AT + place + done + at]
            apply_tile(meta, tile, at, pairs, geometry, pool, columns, totals)
            rows = updated(geometry[tile], totals)
            found[done + at] = rows
            if local is not None:
                local[tile] = rows
            return carry

        lax.fori_loop(0, count, tile_step, 0)
        done += count


def sweep_kernel(place, owns, meta, geometry, *refs):
    own_refs, (level, before, after) = (refs[:owns], refs[owns : owns + 3])
    banks, (found, pool, columns, totals) = (refs[owns + 3 : -4], refs[-4:])
    fill_search(pool, own_refs, level, before, after, meta)
    sweep_tiles(place, meta, geometry, banks, found, pool, columns, totals)


def direction_kernel(
    meta, geometry, own_a, own_b, level, before, after, sent, pairs_b, pairs_c, order, found, bundle, pool, columns, totals, local
):
    atoms = order.shape[1]
    fill_search(pool, (own_a, own_b), level, before, after, meta)
    sweep_tiles(2, meta, geometry, (pairs_b, pairs_c), found, pool, columns, totals, local)
    for place in range(2):
        block = sent[place]
        local[meta[ORDER_AT + place]] = block
        bundle[:, atoms + place * TILE : atoms + (place + 1) * TILE] = block
    in_tiles = jnp.concatenate([local[tile] for tile in range(4)], 1)
    bundle[:, :atoms] = selected(in_tiles, order_matrix(order[...], atoms), NT)


def final_field_kernel(
    meta, geometry, sent, rest, level, before, after, pairs_a, order, stored_b, stored_c, applied, sums, pool, columns, totals, local, pairs_b, pairs_c, sems
):
    copies = [
        pltpu.make_async_copy(source, target, sems.at[at])
        for at, (source, target) in enumerate(((stored_b, pairs_b), (stored_c, pairs_c)))
    ]
    for copy in copies:
        copy.start()
    atoms = order.shape[1]
    fill_search(pool, (sent, rest), level, before, after, meta)
    both = (jnp.zeros((1, TILE), F32), jnp.zeros((1, TILE), F32))
    for first, pairs in ((0, pairs_a), (2, pairs_b), (3, pairs_c)):
        if first:
            copies[first - 2].wait()

        def tile_step(at, both):
            curve, dots = both
            place = first + at
            tile = meta[ORDER_AT + place]
            apply_tile(meta, tile, at, pairs, geometry, pool, columns, totals)
            block = geometry[tile]
            ahead = rest[first - 2 + at] if first else sent[at]
            field = field_rows(totals)
            rows = []
            for part in range(3):
                d = ahead[part : part + 1]
                value = d / block[3:4] - field[part] - SELF_FIELD * d
                curve = curve + d * value
                dots = dots + d * block[4 + part : 5 + part]
                rows.append(value)
            local[tile] = jnp.concatenate(rows + [jnp.zeros((5, TILE), F32)], 0)
            return (curve, dots)

        both = lax.fori_loop(0, pairs.shape[1] // 8, tile_step, both)
    in_tiles = jnp.concatenate([local[tile] for tile in range(4)], 1)
    applied[...] = selected(in_tiles, order_matrix(order[...], atoms), NT)
    lane = lax.broadcasted_iota(jnp.int32, (8, TILE), 1)
    curve_sum = jnp.sum(both[0], axis=1, keepdims=True)
    dot_sum = jnp.sum(both[1], axis=1, keepdims=True)
    sums[...] = jnp.where(lane == 1, curve_sum, jnp.where(lane == 2, dot_sum, 0.0))


def spline(fraction):
    centre_arg = fraction - 0.5

    def middle(u):
        return (55.0 + u * (20.0 + u * (-120.0 + u * (80.0 - 16.0 * u)))) / 96.0

    def middle_slope(u):
        return (20.0 + u * (-240.0 + u * (240.0 - 64.0 * u))) / 96.0

    def outer(u):
        w = 5.0 - 2.0 * u
        return (w * w) * (w * w) / 384.0

    def outer_slope(u):
        w = 5.0 - 2.0 * u
        return -(w * w * w) / 48.0

    sq = centre_arg * centre_arg
    weights = (
        outer(fraction + 1.5),
        middle(fraction + 0.5),
        115.0 / 192.0 - 0.625 * sq + 0.25 * sq * sq,
        middle(1.5 - fraction),
        outer(2.5 - fraction),
    )
    slopes = (
        outer_slope(fraction + 1.5),
        middle_slope(fraction + 0.5),
        -1.25 * centre_arg + centre_arg * sq,
        -middle_slope(1.5 - fraction),
        -outer_slope(2.5 - fraction),
    )
    return (weights, slopes)


def table(cell_row, values, length, wrapped):
    atoms = cell_row.shape[1]
    ids = lax.broadcasted_iota(jnp.int32, (length, atoms), 0)
    if wrapped:
        ahead = ids - cell_row + 2
        ahead = jnp.where(ahead >= G, ahead - G, jnp.where(ahead < 0, ahead + G, ahead))
    else:
        ahead = ids - cell_row
    total = jnp.zeros((length, atoms), F32)
    for step in range(5):
        total = jnp.where(ahead == step, values[step], total)
    return total


def tables_kernel(
    mine, beside, stored_high, stored_low, tab_x, tab_y, w_high, w_low, slope_z, cas_high, cas_low, sems
):
    core = lax.axis_index("core")
    copies = [
        pltpu.make_async_copy(stored_high.at[core], cas_high, sems.at[0]),
        pltpu.make_async_copy(stored_low.at[core], cas_low, sems.at[1]),
    ]
    for copy in copies:
        copy.start()
    for copy in copies:
        copy.wait()
    cas = (cas_high[...], cas_low[...])
    for side, statics in enumerate((mine, beside)):
        atoms = tab_x.shape[3]
        cells = statics[0:3, :atoms].astype(jnp.int32)
        for dim, out in ((0, tab_x), (1, tab_y)):
            weights, slopes = spline(statics[3 + dim : 4 + dim, :atoms])
            out[side, 0] = table(cells[dim : dim + 1], weights, out.shape[2], False)
            out[side, 1] = table(cells[dim : dim + 1], slopes, out.shape[2], False)
        weights, slopes = spline(statics[5:6, :atoms])
        high, low = halves(product(cas, halves(table(cells[2:3], weights, G, True)), NN))
        w_high[side] = high
        w_low[side] = low
        slope_z[side] = product(cas, halves(table(cells[2:3], slopes, G, True)), NN)


def spread_part(side, d, tab_x, tab_y, w_high, w_low, slope_z):
    w_z = (w_high[side], w_low[side])
    s_z = halves(slope_z[side] * d[2:3])
    weight_x = tab_x[side, 0]
    slope_part = tab_x[side, 1] * d[0:1]
    weight_part = weight_x * d[1:2]
    sides = []
    for y in range(tab_y.shape[2]):
        w_y, s_y = (tab_y[side, 0, y : y + 1], tab_y[side, 1, y : y + 1])
        sides.append((slope_part * w_y + weight_part * s_y, weight_x * w_y))
    rows = halves(jnp.concatenate([pair[0] for pair in sides], 0))
    flat = halves(jnp.concatenate([pair[1] for pair in sides], 0))
    return product(w_z, rows, NT) + product(s_z, flat, NT)


def spread_own_kernel(ordered, tab_x, tab_y, w_high, w_low, slope_z, out):
    out[...] = spread_part(0, ordered[:, : tab_x.shape[3]], tab_x, tab_y, w_high, w_low, slope_z)


def put_lanes(out, flat):
    for row in range(8):
        out[:, row, :] = flat[:, row * TILE : (row + 1) * TILE]


def get_lanes(grid):
    return jnp.concatenate([grid[:, row, :] for row in range(8)], 1)


def spread_both_kernel(shift, ordered, mine, tab_x, tab_y, w_high, w_low, slope_z, out, flat, message, sems):
    theirs = spread_part(1, ordered[:, : tab_x.shape[3]], tab_x, tab_y, w_high, w_low, slope_z)
    ours = mine[...]
    width = ours.shape[1]
    even = lax.axis_index("core") == 0
    lower = jnp.where(even, ours, theirs)
    upper = jnp.where(even, theirs, ours)
    flat[:, :shift] = lower[:, :shift]
    flat[:, shift:width] = lower[:, shift:] + upper[:, : width - shift]
    flat[:, width : width + shift] = upper[:, width - shift :]
    flat[:, width + shift :] = jnp.zeros((flat.shape[0], flat.shape[1] - width - shift), F32)
    pieces = sems.shape[0]
    size = flat.shape[0] // pieces
    copies = []
    for piece in range(pieces):
        rows = slice(piece * size, (piece + 1) * size)
        for row in range(8):
            message[rows, row, :] = flat[rows, row * TILE : (row + 1) * TILE]
        copies.append(pltpu.make_async_copy(message.at[rows], out.at[rows], sems.at[piece]))
        copies[-1].start()
    for copy in copies:
        copy.wait()


def factor_of(waves, freq_z):
    ids_x = lax.broadcasted_iota(jnp.int32, (1, G), 1)
    by_x = waves[...]
    by_z = jnp.sum(jnp.where(ids_x == freq_z, by_x, 0.0), axis=1, keepdims=True)
    by_y = by_x.T
    anchor = jnp.where(
        (lax.broadcasted_iota(jnp.int32, (G, G), 0) + lax.broadcasted_iota(jnp.int32, (G, G), 1) + freq_z) == 0, 1.0, 0.0
    )
    squares = by_x[0:1] + by_y[:, 0:1] + (by_z[0:1] + anchor)
    return (1.0 - anchor) * (by_x[1:2] * by_z[1:2]) * by_y[:, 1:2] / (math.pi * float(G) ** 3 * squares)


def plane_kernel(shapes, waves, sums, *refs):
    stored, out, flat, padded = (refs[:7], refs[7], refs[8], refs[9])
    held, sems = (refs[10:17], refs[17])
    copies = [
        pltpu.make_async_copy(source, target, sems.at[at])
        for at, (source, target) in enumerate(zip(stored, held))
    ]
    for copy in copies:
        copy.start()
    grid, x_high, x_low, yt_high, yt_low, y_high, y_low = held
    n_slab, n_pair, x_rows, y_rows = shapes
    width = x_rows * y_rows
    freq_z = lax.axis_index("slab") * (2 * n_pair) + 2 * lax.axis_index("pair") + lax.axis_index("core")
    factor = factor_of(waves, freq_z)
    copies[0].wait()
    flat[...] = get_lanes(grid)
    padded[...] = jnp.zeros(padded.shape, F32)
    for s in range(n_slab):
        for y in range(y_rows):
            padded[y * n_pair : (y + 1) * n_pair, s * TILE : s * TILE + x_rows] = flat[
                s * n_pair : (s + 1) * n_pair, y * x_rows : (y + 1) * x_rows
            ]
    for copy in copies[1:]:
        copy.wait()
    cas_x = (x_high[...], x_low[...])
    along_x = product(halves(padded[...]), cas_x, NN, False)
    spectrum = product((yt_high[...], yt_low[...]), halves(along_x), NN, False)
    scaled = spectrum * factor
    energy = jnp.sum(jnp.sum(spectrum * scaled, axis=0, keepdims=True), axis=1, keepdims=True)
    back = halves(product((y_high[...], y_low[...]), halves(scaled), NN, False))
    planes = product(back, cas_x, NT, False)
    for s in range(n_slab):
        for y in range(y_rows):
            flat[s * n_pair : (s + 1) * n_pair, y * x_rows : (y + 1) * x_rows] = planes[
                y * n_pair : (y + 1) * n_pair, s * TILE : s * TILE + x_rows
            ]
    spare = flat.shape[1] - width
    lane = lax.broadcasted_iota(jnp.int32, (1, spare), 1)
    known = jnp.concatenate([sums[0:1], jnp.zeros((1, spare - TILE), F32)], 1)
    tail = jnp.where(lane == 0, energy, known)
    flat[:, width:] = jnp.broadcast_to(tail, (flat.shape[0], spare))
    put_lanes(out, flat)


def probe_part(side, planes, tab_x, tab_y, w_high, w_low, slope_z):
    x_rows = tab_x.shape[2]
    by_weight = product(planes, (w_high[side], w_low[side]), TN)
    by_slope = product(planes, halves(slope_z[side]), TN)
    weight_x, slope_x = (tab_x[side, 0], tab_x[side, 1])
    fields = [0.0, 0.0, 0.0]
    for y in range(tab_y.shape[2]):
        rows = slice(y * x_rows, (y + 1) * x_rows)
        w_y, s_y = (tab_y[side, 0, y : y + 1], tab_y[side, 1, y : y + 1])
        weighted = by_weight[rows]
        fields[0] += w_y * jnp.sum(slope_x * weighted, axis=0, keepdims=True)
        fields[1] += s_y * jnp.sum(weight_x * weighted, axis=0, keepdims=True)
        fields[2] += w_y * jnp.sum(weight_x * by_slope[rows], axis=0, keepdims=True)
    return fields


def probe_kernel(side, shift, grid, tab_x, tab_y, w_high, w_low, slope_z, out):
    matrix = get_lanes(grid)
    width = tab_x.shape[2] * tab_y.shape[2]
    low_side = 0 if side == 0 else 1
    planes = jnp.where(
        lax.axis_index("core") == low_side, matrix[:, :width], matrix[:, shift : shift + width]
    )
    fields = probe_part(side, halves(planes), tab_x, tab_y, w_high, w_low, slope_z)
    atoms = out.shape[1]
    scalars = jnp.sum(matrix[:, width + shift :], axis=0, keepdims=True)[:, :TILE]
    padded = jnp.concatenate([scalars, jnp.zeros((1, atoms - TILE), F32)], 1)
    out[...] = jnp.concatenate(fields + [padded, jnp.zeros((4, atoms), F32)], 0)


def finish_kernel(mine, theirs, ordered, applied, dipoles, residual, next_dipoles, next_residual, direction):
    total = mine[...] + theirs[...]
    step = total[3:4, 2:3] / (total[3:4, 0:1] + total[3:4, 1:2])
    d = ordered[0:3, : dipoles.shape[1]]
    next_dipoles[...] = dipoles[...] + step * d
    next_residual[...] = residual[...] - step * (applied[0:3] + total[0:3])
    direction[...] = d


def cas_matrix(first, second):
    angles = 2.0 * np.pi / G * (np.outer(first, second) % G)
    return np.cos(angles) + np.sin(angles)


def split_constant(values):
    whole = values.astype(np.float32)
    high = whole.astype(ml_dtypes.bfloat16)
    low = (values - high.astype(np.float64)).astype(ml_dtypes.bfloat16)
    return (jnp.asarray(high), jnp.asarray(low))


def wave_factors():
    freq = np.arange(G)
    wrapped = np.where(freq > G // 2, freq - G, freq) / G
    angles = 2.0 * np.pi / G * freq
    modulus = 115.0 / 192.0 + 19.0 / 48.0 * np.cos(angles) + 1.0 / 192.0 * np.cos(2.0 * angles)
    rows = np.zeros((8, G), np.float32)
    rows[0] = wrapped * wrapped
    rows[1] = np.exp(-((np.pi / BETA) ** 2) * wrapped * wrapped) / (modulus * modulus)
    return jnp.asarray(rows)


def swap_pairs(n_slab, n_space, odd):
    pairs = []
    for s in range(n_slab):
        for q in range(n_space):
            partner = (q + 1 if (q % 2 == 1) == odd else q - 1) % n_space
            pairs.append((s * n_space + q, s * n_space + partner))
    return pairs


def beside(block, odd):
    n_slab, n_space = (lax.axis_size("slab"), lax.axis_size(SPACE))
    return lax.ppermute(block, BOTH, swap_pairs(n_slab, n_space, odd))


def along_slab(level):
    n_slab = lax.axis_size("slab")
    up = [(i, (i + 1) % n_slab) for i in range(n_slab)]
    down = [(j, i) for i, j in up]
    return (level, lax.ppermute(level, "slab", up), lax.ppermute(level, "slab", down))


def joined(block, inner, outer):
    return call(join_kernel, [((3, 2, 8, TILE), F32)], 10**6)(block, inner, outer)[0]


def around(block, bundle=None, beneath=None):
    inner = beside(block if bundle is None else bundle, False)
    outer, _ = lax.optimization_barrier((beside(block, True), beneath))
    return along_slab(joined(block, inner, outer)), inner


def local(
    dipoles, residual, cells, fraction, polarizability, tile_order, send_tiles, tile_lists, tile_counts
):
    n_slab, n_space = (lax.axis_size("slab"), lax.axis_size(SPACE))
    n_pair = n_space // 2
    atoms = residual.shape[1]
    extents = (G // n_slab, G // n_space)
    x_rows = -(-(extents[0] + 4) // 8) * 8
    y_rows = extents[1] + 4
    pair_rows = 2 * extents[1] + 4
    shift = extents[1] * x_rows
    half = G // 2
    tile_shape = ((4, 8, TILE), F32)
    two_shape = ((2, 8, TILE), F32)
    one_bank = ((3, 8, TILE, TILE), F32)
    pool_scratch = pltpu.VMEM((22, 8, TILE), F32)
    total_scratch = pltpu.VMEM((3, TILE, TILE), F32)
    own, sent, statics = pl.pallas_call(
        gather_kernel,
        out_shape=[
            jax.ShapeDtypeStruct(*tile_shape),
            jax.ShapeDtypeStruct(*two_shape),
            jax.ShapeDtypeStruct((8, atoms + 2 * TILE), F32),
        ],
        in_specs=[pl.BlockSpec(memory_space=pltpu.HBM)] * 6,
        out_specs=[pl.BlockSpec(memory_space=pltpu.VMEM)] * 3,
        scratch_shapes=[
            pltpu.VMEM((3, atoms), F32),
            pltpu.VMEM((3, atoms), jnp.int32),
            pltpu.VMEM((3, atoms), F32),
            pltpu.VMEM((atoms,), F32),
            pltpu.VMEM((1, atoms), jnp.int32),
            pltpu.SMEM((1, 2), jnp.int32),
            pltpu.SemaphoreType.DMA((6,)),
        ],
        compiler_params=pltpu.CompilerParams(vmem_limit_bytes=SMALL_VMEM),
    )(
        *[
            pltpu.with_memory_space_constraint(array, pltpu.HBM)
            for array in (residual, cells, fraction, polarizability, tile_order, send_tiles)
        ],
    )
    smem, anywhere = (pl.BlockSpec(memory_space=pltpu.SMEM), pl.BlockSpec(memory_space=pltpu.HBM))
    meta = pl.pallas_call(
        meta_kernel,
        out_shape=jax.ShapeDtypeStruct((48,), jnp.int32),
        in_specs=[smem, smem, smem, pl.BlockSpec(memory_space=pltpu.VMEM)],
        out_specs=smem,
        compiler_params=pltpu.CompilerParams(vmem_limit_bytes=SMALL_VMEM),
        cost_estimate=pl.CostEstimate(flops=10**8, bytes_accessed=1 << 20, transcendentals=0),
    )(tile_lists, tile_counts, send_tiles, sent)
    first, statics_beside = around(sent, statics, beneath=meta)

    freq = np.arange(G)
    padded_x = np.stack([(s * extents[0] + np.arange(x_rows) - 2) % G for s in range(n_slab)])
    real_x = np.tile(np.arange(x_rows) < extents[0] + 4, n_slab)
    cas_x = cas_matrix(padded_x.reshape(-1), freq) * real_x[:, None]
    rows_y = (np.arange(n_pair)[None] * 2 * extents[1] + np.arange(pair_rows)[:, None] - 2) % G
    cas_y = cas_matrix(rows_y.reshape(-1), freq)
    freq_by_core = np.stack([freq[0::2], freq[1::2]])
    cas_z = cas_matrix(freq_by_core.reshape(-1), freq).reshape(2, half, G)
    wide_x = np.zeros((n_slab, TILE, G))
    wide_x[:, :x_rows] = cas_x.reshape(n_slab, x_rows, G)
    def pairs_of(place, count):
        return call(
            functools.partial(pair_kernel, place, count, extents),
            [((22, 8, TILE), F32), ((3, 8 * count, TILE, TILE), F32), ((count, 8, TILE), F32)],
            10**9,
            smem=1,
            scratch=(pltpu.VMEM((4, TILE, TILE), F32), total_scratch),
        )(meta, own, *first)

    geometry, pairs_a, search_a = pairs_of(0, 2)
    _, pairs_b, search_b = pairs_of(2, 1)
    _, pairs_c, search_c = pairs_of(3, 1)
    sweep_scratch = (pool_scratch, pltpu.VMEM((3, TILE, TILE), F32), total_scratch)
    second, _ = around(search_a, beneath=search_b)

    def sweep(place, owns, received, banks):
        return call(
            functools.partial(sweep_kernel, place, len(owns)),
            [two_shape],
            10**8,
            smem=1,
            scratch=sweep_scratch,
        )(meta, geometry, *owns, *received, *banks)[0]

    searches = (search_a, search_b, search_c)
    next_a = sweep(0, searches, second, (pairs_a,))
    next_b = sweep(2, searches, second, (pairs_b, pairs_c))
    third, _ = around(next_a, beneath=next_b)
    statics_beside, _ = lax.optimization_barrier((statics_beside, third[0]))
    tables = call(
        tables_kernel,
        [
            ((2, 2, x_rows, atoms), F32),
            ((2, 2, y_rows, atoms), F32),
            ((2, half, atoms), BF16),
            ((2, half, atoms), BF16),
            ((2, half, atoms), F32),
        ],
        10**8,
        vmem=LARGE_VMEM,
        scratch=(pltpu.VMEM((half, G), BF16),) * 2 + (pltpu.SemaphoreType.DMA((2,)),),
        hbm=2,
    )(statics, statics_beside, *split_constant(cas_z))
    level, before, after = third
    after, _ = lax.optimization_barrier((after, tables[1]))
    third = (level, before, after)
    local_scratch = pltpu.VMEM((4, 8, TILE), F32)
    sent = sweep(0, (next_a, next_b), third, (pairs_a,))
    outer = beside(sent, True)
    rest, ordered = call(
        direction_kernel,
        [two_shape, ((8, atoms + 2 * TILE), F32)],
        10**8,
        smem=1,
        scratch=sweep_scratch + (local_scratch,),
    )(meta, geometry, next_a, next_b, *third, sent, pairs_b, pairs_c, tile_order)
    ordered_beside = beside(ordered, False)
    message = ((half, 8, TILE), F32)
    flat_scratch = pltpu.VMEM((half, 8 * TILE), F32)
    spread_own = call(spread_own_kernel, [((half, x_rows * y_rows), F32)], 10**9, vmem=LARGE_VMEM)(ordered, *tables)[0]
    spread = call(
        functools.partial(spread_both_kernel, shift),
        [message],
        10**9,
        scratch=(flat_scratch, pltpu.VMEM(*message), pltpu.SemaphoreType.DMA((4,))),
        vmem=LARGE_VMEM,
        hbm_outs=True,
    )(ordered_beside, spread_own, *tables)[0]
    spread, outer = lax.optimization_barrier((spread, outer))
    grid = lax.all_to_all(spread, CHIPS, 0, 0, tiled=True)
    last = along_slab(joined(sent, ordered_beside, outer))
    applied, sums = call(
        final_field_kernel,
        [((8, atoms), F32), ((8, TILE), F32)],
        10**9,
        smem=1,
        scratch=sweep_scratch
        + (local_scratch, pltpu.VMEM(*one_bank), pltpu.VMEM(*one_bank), pltpu.SemaphoreType.DMA((2,))),
        vmem=LARGE_VMEM,
        hbm=2,
    )(meta, geometry, sent, rest, *last, pairs_a, tile_order, pairs_b, pairs_c)
    planes = call(
        functools.partial(plane_kernel, (n_slab, n_pair, x_rows, pair_rows)),
        [message],
        10**9,
        scratch=(flat_scratch, pltpu.VMEM((n_pair * pair_rows, n_slab * TILE), F32), pltpu.VMEM(*message))
        + (pltpu.VMEM((n_slab * TILE, G), BF16),) * 2
        + (pltpu.VMEM((G, n_pair * pair_rows), BF16),) * 2
        + (pltpu.VMEM((n_pair * pair_rows, G), BF16),) * 2
        + (pltpu.SemaphoreType.DMA((7,)),),
        vmem=LARGE_VMEM,
        hbm=7,
    )(
        wave_factors(),
        sums,
        grid,
        *split_constant(wide_x.reshape(-1, G)),
        *split_constant(cas_y.T),
        *split_constant(cas_y),
    )[0]
    returned = lax.all_to_all(planes, CHIPS, 0, 0, tiled=True)

    def probe(side):
        return call(
            functools.partial(probe_kernel, side, shift), [((8, atoms), F32)], 10**9, vmem=LARGE_VMEM
        )(returned, *tables)[0]

    theirs = beside(probe(1), False)
    three = ((3, atoms), F32)
    return tuple(
        call(finish_kernel, [three, three, three], 10**6)(
            probe(0), theirs, ordered, applied, dipoles, residual
        )
    )


def solution(mesh):
    slab, space = (mesh.shape["slab"], mesh.shape["space"])
    mesh = Mesh(mesh.devices.reshape(slab, space // 2, 2), BOTH)
    in_specs = (
        P(None, BOTH),
        P(None, BOTH),
        P(None, BOTH),
        P(None, BOTH),
        P(BOTH),
        P(BOTH, None),
        P(BOTH, None),
        P(BOTH, None, None),
        P(BOTH, None),
    )
    out_specs = (P(None, BOTH), P(None, BOTH), P(None, BOTH))
    return jax.shard_map(local, mesh=mesh, in_specs=in_specs, out_specs=out_specs, check_vma=False)
```

```python
import functools
import math

import jax
import jax.numpy as jnp
import ml_dtypes
import numpy as np
from jax import lax
from jax.experimental import pallas as pl
from jax.experimental.pallas import tpu as pltpu
from jax.sharding import Mesh
from jax.sharding import PartitionSpec as P

G = 256
TILE = 128
SPACE = ("pair", "core")
BOTH = ("slab", "pair", "core")
CHIPS = ("slab", "pair")
BETA = 0.4
THOLE = 0.39
ROOT_PI = math.sqrt(math.pi)
SELF_FIELD = 4.0 * BETA**3 / (3.0 * ROOT_PI)
F32 = jnp.float32
BF16 = jnp.bfloat16
SCALED_ERFC_T = 0.45
SCALED_ERFC = (
    0.25388532876968384,
    0.25388309359550476,
    0.22827406227588654,
    0.17522020637989044,
    0.1201537474989891,
    -0.023065825924277306,
    0.14381752908229828,
    -0.3022053837776184,
    0.19167575240135193,
    -0.04163854941725731,
)
NT = (((1,), (1,)), ((), ()))
NN = (((1,), (0,)), ((), ()))
TN = (((0,), (0,)), ((), ()))
SMALL_VMEM = 6 * 1024 * 1024
LARGE_VMEM = 16 * 1024 * 1024


def halves(values):
    high = values.astype(BF16)
    return (high, (values - high.astype(F32)).astype(BF16))


def product(left, right, dims, stacked=True):
    def one(a, b):
        return lax.dot_general(a, b, dims, preferred_element_type=F32)

    (left_dim,), (right_dim,) = dims[0]
    if not stacked:
        return one(left[0], right[0]) + (one(left[0], right[1]) + one(left[1], right[0]))
    return one(
        jnp.concatenate([left[0], left[0], left[1]], left_dim),
        jnp.concatenate([right[0], right[1], right[0]], right_dim),
    )


def thirds(values):
    high = values.astype(BF16).astype(F32)
    rest = values - high
    middle = rest.astype(BF16).astype(F32)
    return jnp.concatenate([high, middle, rest - middle], 0).astype(BF16)


def selected(values, one_hot, dims):
    rows = values.shape[0]
    picked = lax.dot_general(thirds(values), one_hot, dims, preferred_element_type=F32)
    return picked[:rows] + (picked[rows : 2 * rows] + picked[2 * rows :])


def order_matrix(order_row, count):
    ids = lax.broadcasted_iota(jnp.int32, (count, count), 0)
    return jnp.where(ids == order_row, 1.0, 0.0).astype(BF16)


COUNTS_AT = 32
ORDER_AT = 36
PARITY_AT = 40


def meta_kernel(lists, counts, send, after, meta):
    parity = lax.axis_index("core")
    for tile in range(4):

        def remap(place, carry):
            entry = lists[0, tile, place]
            remote = entry - 4
            pair = lax.shift_right_arithmetic(remote, 1)
            pair = pair + jnp.where(pair >= 4, 1, 0)
            along = jnp.where(pair >= 3, 1, 0) + jnp.where(pair >= 6, 1, 0)
            across = pair - 3 * along
            base = jnp.where(across == 1, 4, jnp.where(across == 2 - 2 * parity, 10, 16))
            slot = base + along * 2 + (remote & 1)
            meta[tile * 8 + place] = jnp.where(entry < 4, entry, slot)
            return carry

        lax.fori_loop(0, 8, remap, 0)
        meta[COUNTS_AT + tile] = counts[0, tile]
    first, second = (send[0, 0], send[0, 1])
    third = jnp.where(
        (first != 0) & (second != 0), 0, jnp.where((first != 1) & (second != 1), 1, 2)
    )
    meta[ORDER_AT] = first
    meta[ORDER_AT + 1] = second
    meta[ORDER_AT + 2] = third
    meta[ORDER_AT + 3] = 6 - first - second - third
    meta[PARITY_AT] = parity


def call(kernel, outs, flops, smem=0, scratch=(), vmem=SMALL_VMEM, hbm=0, hbm_outs=False):
    def run(*args):
        kept = len(args) - hbm
        args = args[:kept] + tuple(
            pltpu.with_memory_space_constraint(array, pltpu.HBM) for array in args[kept:]
        )
        in_specs = [pl.BlockSpec(memory_space=pltpu.SMEM)] * smem
        in_specs += [pl.BlockSpec(memory_space=pltpu.VMEM)] * (kept - smem)
        in_specs += [pl.BlockSpec(memory_space=pltpu.HBM)] * hbm
        return pl.pallas_call(
            kernel,
            out_shape=[
                (pltpu.HBM if hbm_outs else jax.ShapeDtypeStruct)(shape, dtype) for shape, dtype in outs
            ],
            in_specs=in_specs,
            out_specs=[pl.BlockSpec(memory_space=pltpu.HBM if hbm_outs else pltpu.VMEM)] * len(outs),
            scratch_shapes=list(scratch),
            compiler_params=pltpu.CompilerParams(vmem_limit_bytes=vmem),
            cost_estimate=pl.CostEstimate(
                flops=flops, bytes_accessed=1 << 20, transcendentals=0
            ),
        )(*args)

    return run


def gather_kernel(*refs):
    sources, (own, sent, bundle), held, sems = (refs[:6], refs[6:9], refs[9:15], refs[15])
    copies = [
        pltpu.make_async_copy(source, target, sems.at[at])
        for at, (source, target) in enumerate(zip(sources, held))
    ]
    for copy in copies:
        copy.start()
    for copy in copies:
        copy.wait()
    residual, cells, fraction, alphas, order, send = held
    atoms = residual.shape[1]
    in_cells = cells[...].astype(F32)
    bundle[0:3, :atoms] = in_cells
    bundle[3:6, :atoms] = fraction[...]
    bundle[6:8, :atoms] = jnp.zeros((2, atoms), F32)
    position = in_cells + fraction[...]
    rows = jnp.concatenate(
        [position, alphas[...].reshape(1, atoms), residual[...], jnp.zeros((1, atoms), F32)], 0
    )
    picked = selected(rows, order_matrix(order[...], atoms), NN)
    for tile in range(atoms // TILE):
        own[tile] = picked[:, tile * TILE : (tile + 1) * TILE]
    for place in range(2):
        block = own[send[0, place]]
        sent[place] = block
        bundle[:, atoms + place * TILE : atoms + (place + 1) * TILE] = block


def search_rows(block):
    return block[3:4] * block[4:7]


def fill_pool(pool, extents, own, level, before, after, meta):
    inner_step = jnp.where(meta[PARITY_AT] == 0, 1.0, -1.0)
    rows = lax.broadcasted_iota(jnp.int32, (8, TILE), 0)
    for tile in range(4):
        pool[tile] = own[tile]
    for along, source in enumerate((before, level, after)):
        for kind, step in enumerate((0.0, inner_step, -inner_step)):
            shift = jnp.where(
                rows == 0,
                float((along - 1) * extents[0]),
                jnp.where(rows == 1, step * float(extents[1]), 0.0),
            )
            for member in range(2):
                pool[4 + 6 * kind + 2 * along + member] = source[kind, member] + shift


def own_columns(columns, block, count):
    turned = block.T
    for row in range(count):
        columns[row] = jnp.broadcast_to(turned[:, row : row + 1], (TILE, TILE))


def wrap_depth(depth):
    half = 0.5 * G
    return jnp.where(depth > half, depth - G, jnp.where(depth < -half, depth + G, depth))


PAIR_ROWS = 32
GROUP = 4


def pair_kernel(first_place, count, extents, meta, own, level, before, after, pool, pairs, found, columns, totals):
    fill_pool(pool, extents, own, level, before, after, meta)

    def tile_step(at, carry):
        tile = meta[ORDER_AT + first_place + at]
        block = own[tile]
        own_columns(columns, jnp.concatenate([block[:3], lax.rsqrt(block[3:4]), block[4:]], 0), 4)
        live = meta[COUNTS_AT + tile]

        def chunk_step(chunk, carry):
            start = pl.multiple_of(chunk * PAIR_ROWS, PAIR_ROWS)
            rows = pl.ds(start, PAIR_ROWS)
            shape = (PAIR_ROWS, TILE)
            ahead = lax.broadcasted_iota(jnp.int32, shape, 0) - lax.broadcasted_iota(
                jnp.int32, shape, 1
            )
            diagonal = jnp.where(ahead == -start, 1.0, 0.0)

            def group_step(group, sums):
                for member in range(GROUP):
                    entry = group * GROUP + member
                    slot = meta[tile * 8 + entry]
                    other = pool[slot]
                    itself = diagonal * jnp.where(slot == tile, 1.0, 0.0)
                    d_x = other[0:1] - columns[0, rows]
                    d_y = other[1:2] - columns[1, rows]
                    d_z = wrap_depth(other[2:3] - columns[2, rows])
                    square = d_x * d_x + d_y * d_y + d_z * d_z + itself
                    inverse = lax.rsqrt(square)
                    distance = square * inverse
                    inverse_sq = inverse * inverse
                    gauss = jnp.exp(-(BETA**2) * square)
                    stretch = 1.0 + (SCALED_ERFC_T * BETA) * distance
                    t = lax.rsqrt(stretch * stretch)
                    series = SCALED_ERFC[-1] * t + SCALED_ERFC[-2]
                    for term in SCALED_ERFC[-3::-1]:
                        series = series * t + term
                    bare_one = gauss * (series * t * inverse + 2.0 * BETA / ROOT_PI) * inverse_sq
                    bare_two = (3.0 * bare_one + (4.0 * BETA**3 / ROOT_PI) * gauss) * inverse_sq
                    damping = (square * distance) * columns[3, rows] * (THOLE * lax.rsqrt(other[3:4]))
                    decay = jnp.exp(-damping) * inverse * inverse_sq
                    keep = jnp.where(entry < live, 1.0, 0.0) * (1.0 - itself)
                    three = keep * (bare_one - decay)
                    five = keep * (bare_two - (3.0 + 3.0 * damping) * decay * inverse_sq)
                    pairs[0, at * 8 + entry, rows] = five
                    pairs[1, at * 8 + entry, rows] = three
                    pairs[2, at * 8 + entry, rows] = d_z
                    v = search_rows(other)
                    along = five * (d_x * v[0:1] + d_y * v[1:2] + d_z * v[2:3])
                    sums = (
                        sums[0] + (along * d_x - three * v[0:1]),
                        sums[1] + (along * d_y - three * v[1:2]),
                        sums[2] + (along * d_z - three * v[2:3]),
                    )
                return sums

            zero = jnp.zeros(shape, F32)
            sums = lax.fori_loop(0, (live + GROUP - 1) // GROUP, group_step, (zero, zero, zero))
            for part in range(3):
                totals[part, rows] = sums[part]
            return carry

        lax.fori_loop(0, TILE // PAIR_ROWS, chunk_step, 0)
        found[at] = updated(block, totals)
        return carry

    lax.fori_loop(0, count, tile_step, 0)


def field_rows(totals):
    return [jnp.sum(totals[part].T, axis=0, keepdims=True) for part in range(3)]


def updated(block, totals):
    alpha = block[3:4]
    field = field_rows(totals)
    rows = [alpha * (block[4 + part : 5 + part] + field[part]) for part in range(3)]
    return jnp.concatenate(rows + [jnp.zeros((5, TILE), F32)], 0)


APPLY_ROWS = 64


def fill_search(pool, owns, level, before, after, meta):
    place = 0
    for own in owns:
        for at in range(own.shape[0]):
            pool[meta[ORDER_AT + place]] = own[at]
            place += 1
    for along, source in enumerate((before, level, after)):
        for kind in range(3):
            for member in range(2):
                pool[4 + 6 * kind + 2 * along + member] = source[kind, member]


def join_kernel(own, inner, outer, level):
    for member in range(2):
        level[0, member] = own[member]
        if len(inner.shape) == 3:
            level[1, member] = inner[member]
        else:
            start = inner.shape[1] - (2 - member) * TILE
            level[1, member] = inner[:, start : start + TILE]
        level[2, member] = outer[member]


def apply_tile(meta, tile, at, pairs, geometry, pool, columns, totals):
    block = geometry[tile]
    own_columns(columns, block, 2)
    live = meta[COUNTS_AT + tile]

    def chunk_step(chunk, carry):
        rows = pl.ds(pl.multiple_of(chunk * APPLY_ROWS, APPLY_ROWS), APPLY_ROWS)

        def group_step(group, sums):
            for member in range(GROUP):
                entry = group * GROUP + member
                slot = meta[tile * 8 + entry]
                other = geometry[slot]
                v = pool[slot]
                d_x = other[0:1] - columns[0, rows]
                d_y = other[1:2] - columns[1, rows]
                d_z = pairs[2, at * 8 + entry, rows]
                three = pairs[1, at * 8 + entry, rows]
                along = pairs[0, at * 8 + entry, rows] * (d_x * v[0:1] + d_y * v[1:2] + d_z * v[2:3])
                sums = (
                    sums[0] + (along * d_x - three * v[0:1]),
                    sums[1] + (along * d_y - three * v[1:2]),
                    sums[2] + (along * d_z - three * v[2:3]),
                )
            return sums

        zero = jnp.zeros((APPLY_ROWS, TILE), F32)
        sums = lax.fori_loop(0, (live + GROUP - 1) // GROUP, group_step, (zero, zero, zero))
        for part in range(3):
            totals[part, rows] = sums[part]
        return carry

    lax.fori_loop(0, TILE // APPLY_ROWS, chunk_step, 0)


def sweep_tiles(place, meta, geometry, banks, found, pool, columns, totals, local=None):
    done = 0
    for pairs in banks:
        count = pairs.shape[1] // 8

        def tile_step(at, carry):
            tile = meta[ORDER_AT + place + done + at]
            apply_tile(meta, tile, at, pairs, geometry, pool, columns, totals)
            rows = updated(geometry[tile], totals)
            found[done + at] = rows
            if local is not None:
                local[tile] = rows
            return carry

        lax.fori_loop(0, count, tile_step, 0)
        done += count


def sweep_kernel(place, owns, meta, geometry, *refs):
    own_refs, (level, before, after) = (refs[:owns], refs[owns : owns + 3])
    banks, (found, pool, columns, totals) = (refs[owns + 3 : -4], refs[-4:])
    fill_search(pool, own_refs, level, before, after, meta)
    sweep_tiles(place, meta, geometry, banks, found, pool, columns, totals)


def direction_kernel(
    meta, geometry, own_a, own_b, level, before, after, sent, pairs_b, pairs_c, order, found, bundle, pool, columns, totals, local
):
    atoms = order.shape[1]
    fill_search(pool, (own_a, own_b), level, before, after, meta)
    sweep_tiles(2, meta, geometry, (pairs_b, pairs_c), found, pool, columns, totals, local)
    for place in range(2):
        block = sent[place]
        local[meta[ORDER_AT + place]] = block
        bundle[:, atoms + place * TILE : atoms + (place + 1) * TILE] = block
    in_tiles = jnp.concatenate([local[tile] for tile in range(4)], 1)
    bundle[:, :atoms] = selected(in_tiles, order_matrix(order[...], atoms), NT)


def final_field_kernel(
    meta, geometry, sent, rest, level, before, after, pairs_a, order, stored_b, stored_c, applied, sums, pool, columns, totals, local, pairs_b, pairs_c, sems
):
    copies = [
        pltpu.make_async_copy(source, target, sems.at[at])
        for at, (source, target) in enumerate(((stored_b, pairs_b), (stored_c, pairs_c)))
    ]
    for copy in copies:
        copy.start()
    atoms = order.shape[1]
    fill_search(pool, (sent, rest), level, before, after, meta)
    both = (jnp.zeros((1, TILE), F32), jnp.zeros((1, TILE), F32))
    for first, pairs in ((0, pairs_a), (2, pairs_b), (3, pairs_c)):
        if first:
            copies[first - 2].wait()

        def tile_step(at, both):
            curve, dots = both
            place = first + at
            tile = meta[ORDER_AT + place]
            apply_tile(meta, tile, at, pairs, geometry, pool, columns, totals)
            block = geometry[tile]
            ahead = rest[first - 2 + at] if first else sent[at]
            field = field_rows(totals)
            rows = []
            for part in range(3):
                d = ahead[part : part + 1]
                value = d / block[3:4] - field[part] - SELF_FIELD * d
                curve = curve + d * value
                dots = dots + d * block[4 + part : 5 + part]
                rows.append(value)
            local[tile] = jnp.concatenate(rows + [jnp.zeros((5, TILE), F32)], 0)
            return (curve, dots)

        both = lax.fori_loop(0, pairs.shape[1] // 8, tile_step, both)
    in_tiles = jnp.concatenate([local[tile] for tile in range(4)], 1)
    applied[...] = selected(in_tiles, order_matrix(order[...], atoms), NT)
    lane = lax.broadcasted_iota(jnp.int32, (8, TILE), 1)
    curve_sum = jnp.sum(both[0], axis=1, keepdims=True)
    dot_sum = jnp.sum(both[1], axis=1, keepdims=True)
    sums[...] = jnp.where(lane == 1, curve_sum, jnp.where(lane == 2, dot_sum, 0.0))


def spline(fraction):
    centre_arg = fraction - 0.5

    def middle(u):
        return (55.0 + u * (20.0 + u * (-120.0 + u * (80.0 - 16.0 * u)))) / 96.0

    def middle_slope(u):
        return (20.0 + u * (-240.0 + u * (240.0 - 64.0 * u))) / 96.0

    def outer(u):
        w = 5.0 - 2.0 * u
        return (w * w) * (w * w) / 384.0

    def outer_slope(u):
        w = 5.0 - 2.0 * u
        return -(w * w * w) / 48.0

    sq = centre_arg * centre_arg
    weights = (
        outer(fraction + 1.5),
        middle(fraction + 0.5),
        115.0 / 192.0 - 0.625 * sq + 0.25 * sq * sq,
        middle(1.5 - fraction),
        outer(2.5 - fraction),
    )
    slopes = (
        outer_slope(fraction + 1.5),
        middle_slope(fraction + 0.5),
        -1.25 * centre_arg + centre_arg * sq,
        -middle_slope(1.5 - fraction),
        -outer_slope(2.5 - fraction),
    )
    return (weights, slopes)


def table(cell_row, values, length, wrapped):
    atoms = cell_row.shape[1]
    ids = lax.broadcasted_iota(jnp.int32, (length, atoms), 0)
    if wrapped:
        ahead = ids - cell_row + 2
        ahead = jnp.where(ahead >= G, ahead - G, jnp.where(ahead < 0, ahead + G, ahead))
    else:
        ahead = ids - cell_row
    total = jnp.zeros((length, atoms), F32)
    for step in range(5):
        total = jnp.where(ahead == step, values[step], total)
    return total


def tables_kernel(
    mine, beside, stored_high, stored_low, tab_x, tab_y, w_high, w_low, slope_z, cas_high, cas_low, sems
):
    core = lax.axis_index("core")
    copies = [
        pltpu.make_async_copy(stored_high.at[core], cas_high, sems.at[0]),
        pltpu.make_async_copy(stored_low.at[core], cas_low, sems.at[1]),
    ]
    for copy in copies:
        copy.start()
    for copy in copies:
        copy.wait()
    cas = (cas_high[...], cas_low[...])
    for side, statics in enumerate((mine, beside)):
        atoms = tab_x.shape[3]
        cells = statics[0:3, :atoms].astype(jnp.int32)
        for dim, out in ((0, tab_x), (1, tab_y)):
            weights, slopes = spline(statics[3 + dim : 4 + dim, :atoms])
            out[side, 0] = table(cells[dim : dim + 1], weights, out.shape[2], False)
            out[side, 1] = table(cells[dim : dim + 1], slopes, out.shape[2], False)
        weights, slopes = spline(statics[5:6, :atoms])
        high, low = halves(product(cas, halves(table(cells[2:3], weights, G, True)), NN))
        w_high[side] = high
        w_low[side] = low
        slope_z[side] = product(cas, halves(table(cells[2:3], slopes, G, True)), NN)


def spread_part(side, d, tab_x, tab_y, w_high, w_low, slope_z):
    w_z = (w_high[side], w_low[side])
    s_z = halves(slope_z[side] * d[2:3])
    weight_x = tab_x[side, 0]
    slope_part = tab_x[side, 1] * d[0:1]
    weight_part = weight_x * d[1:2]
    sides = []
    for y in range(tab_y.shape[2]):
        w_y, s_y = (tab_y[side, 0, y : y + 1], tab_y[side, 1, y : y + 1])
        sides.append((slope_part * w_y + weight_part * s_y, weight_x * w_y))
    rows = halves(jnp.concatenate([pair[0] for pair in sides], 0))
    flat = halves(jnp.concatenate([pair[1] for pair in sides], 0))
    return product(w_z, rows, NT) + product(s_z, flat, NT)


def spread_own_kernel(ordered, tab_x, tab_y, w_high, w_low, slope_z, out):
    out[...] = spread_part(0, ordered[:, : tab_x.shape[3]], tab_x, tab_y, w_high, w_low, slope_z)


def put_lanes(out, flat):
    for row in range(8):
        out[:, row, :] = flat[:, row * TILE : (row + 1) * TILE]


def get_lanes(grid):
    return jnp.concatenate([grid[:, row, :] for row in range(8)], 1)


def spread_both_kernel(shift, ordered, mine, tab_x, tab_y, w_high, w_low, slope_z, out, flat, message, sems):
    theirs = spread_part(1, ordered[:, : tab_x.shape[3]], tab_x, tab_y, w_high, w_low, slope_z)
    ours = mine[...]
    width = ours.shape[1]
    even = lax.axis_index("core") == 0
    lower = jnp.where(even, ours, theirs)
    upper = jnp.where(even, theirs, ours)
    flat[:, :shift] = lower[:, :shift]
    flat[:, shift:width] = lower[:, shift:] + upper[:, : width - shift]
    flat[:, width : width + shift] = upper[:, width - shift :]
    flat[:, width + shift :] = jnp.zeros((flat.shape[0], flat.shape[1] - width - shift), F32)
    pieces = sems.shape[0]
    size = flat.shape[0] // pieces
    copies = []
    for piece in range(pieces):
        rows = slice(piece * size, (piece + 1) * size)
        for row in range(8):
            message[rows, row, :] = flat[rows, row * TILE : (row + 1) * TILE]
        copies.append(pltpu.make_async_copy(message.at[rows], out.at[rows], sems.at[piece]))
        copies[-1].start()
    for copy in copies:
        copy.wait()


def factor_of(waves, freq_z):
    ids_x = lax.broadcasted_iota(jnp.int32, (1, G), 1)
    by_x = waves[...]
    by_z = jnp.sum(jnp.where(ids_x == freq_z, by_x, 0.0), axis=1, keepdims=True)
    by_y = by_x.T
    anchor = jnp.where(
        (lax.broadcasted_iota(jnp.int32, (G, G), 0) + lax.broadcasted_iota(jnp.int32, (G, G), 1) + freq_z) == 0, 1.0, 0.0
    )
    squares = by_x[0:1] + by_y[:, 0:1] + (by_z[0:1] + anchor)
    return (1.0 - anchor) * (by_x[1:2] * by_z[1:2]) * by_y[:, 1:2] / (math.pi * float(G) ** 3 * squares)


def rolled(flat, rows, start, size, amount):
    low = start // TILE * TILE
    high = -(-(start + size) // TILE) * TILE
    return pltpu.roll(flat[rows, low:high], amount, 0)[:, start - low : start - low + size]


def plane_kernel(shapes, waves, sums, *refs):
    stored, out, flat, plane = (refs[:7], refs[7], refs[8], refs[9])
    held, sems = (refs[10:17], refs[17])
    copies = [
        pltpu.make_async_copy(source, target, sems.at[at])
        for at, (source, target) in enumerate(zip(stored, held))
    ]
    for copy in copies:
        copy.start()
    grid, x_high, x_low, yt_high, yt_low, y_high, y_low = held
    n_slab, n_pair, x_rows, y_rows = shapes
    x_own, y_own = (G // n_slab, y_rows - 4)
    width = x_rows * y_rows
    freq_z = lax.axis_index("slab") * (2 * n_pair) + 2 * lax.axis_index("pair") + lax.axis_index("core")
    factor = factor_of(waves, freq_z)
    copies[0].wait()
    flat[...] = get_lanes(grid)
    two = 2 * x_rows
    first_own, last_own = (slice(two, 2 * two), slice(y_own * x_rows, y_own * x_rows + two))
    slabs = [slice(s * n_pair, (s + 1) * n_pair) for s in range(n_slab)]
    for rows in slabs:
        from_next = rolled(flat, rows, 0, two, n_pair - 1)
        from_last = rolled(flat, rows, width - two, two, 1)
        flat[rows, last_own] = flat[rows, last_own] + from_next
        flat[rows, first_own] = flat[rows, first_own] + from_last
    padded = [
        jnp.concatenate(
            [flat[rows, (y + 2) * x_rows : (y + 3) * x_rows] for y in range(y_own)], 0
        )
        for rows in slabs
    ]
    for s, block in enumerate(padded):
        plane[:, s * x_own : (s + 1) * x_own] = block[:, 2 : x_own + 2]
    for s, block in enumerate(padded):
        for at, part in (
            ((s * x_own - 2) % G, block[:, :2]),
            ((s + 1) * x_own % G, block[:, x_own + 2 : x_own + 4]),
        ):
            plane[:, at : at + 2] = plane[:, at : at + 2] + part
    for copy in copies[1:]:
        copy.wait()
    cas_x = (x_high[...], x_low[...])
    along_x = product(halves(plane[...]), cas_x, NN, False)
    spectrum = product((yt_high[...], yt_low[...]), halves(along_x), NN, False)
    scaled = spectrum * factor
    energy = jnp.sum(jnp.sum(spectrum * scaled, axis=0, keepdims=True), axis=1, keepdims=True)
    back = halves(product((y_high[...], y_low[...]), halves(scaled), NN, False))
    plane[...] = product(back, cas_x, NN, False)
    for s, rows in enumerate(slabs):
        start, stop = (s * x_own - 2, (s + 1) * x_own + 2)
        pieces = [plane[:, max(start, 0) : min(stop, G)]]
        if start < 0:
            pieces = [plane[:, G + start :]] + pieces
        if stop > G:
            pieces = pieces + [plane[:, : stop - G]]
        block = pieces[0] if len(pieces) == 1 else jnp.concatenate(pieces, 1)
        for y in range(y_own):
            at = (y + 2) * x_rows
            flat[rows, at : at + x_own + 4] = block[y * n_pair : (y + 1) * n_pair]
        flat[rows, :two] = rolled(flat, rows, y_own * x_rows, two, 1)
        flat[rows, width - two : width] = rolled(flat, rows, two, two, n_pair - 1)
    spare = flat.shape[1] - width
    lane = lax.broadcasted_iota(jnp.int32, (1, spare), 1)
    known = jnp.concatenate([sums[0:1], jnp.zeros((1, spare - TILE), F32)], 1)
    tail = jnp.where(lane == 0, energy, known)
    flat[:, width:] = jnp.broadcast_to(tail, (flat.shape[0], spare))
    put_lanes(out, flat)


def probe_part(side, planes, tab_x, tab_y, w_high, w_low, slope_z):
    x_rows = tab_x.shape[2]
    by_weight = product(planes, (w_high[side], w_low[side]), TN)
    by_slope = product(planes, halves(slope_z[side]), TN)
    weight_x, slope_x = (tab_x[side, 0], tab_x[side, 1])
    fields = [0.0, 0.0, 0.0]
    for y in range(tab_y.shape[2]):
        rows = slice(y * x_rows, (y + 1) * x_rows)
        w_y, s_y = (tab_y[side, 0, y : y + 1], tab_y[side, 1, y : y + 1])
        weighted = by_weight[rows]
        fields[0] += w_y * jnp.sum(slope_x * weighted, axis=0, keepdims=True)
        fields[1] += s_y * jnp.sum(weight_x * weighted, axis=0, keepdims=True)
        fields[2] += w_y * jnp.sum(weight_x * by_slope[rows], axis=0, keepdims=True)
    return fields


def probe_kernel(side, shift, grid, tab_x, tab_y, w_high, w_low, slope_z, out):
    matrix = get_lanes(grid)
    width = tab_x.shape[2] * tab_y.shape[2]
    low_side = 0 if side == 0 else 1
    planes = jnp.where(
        lax.axis_index("core") == low_side, matrix[:, :width], matrix[:, shift : shift + width]
    )
    fields = probe_part(side, halves(planes), tab_x, tab_y, w_high, w_low, slope_z)
    atoms = out.shape[1]
    scalars = jnp.sum(matrix[:, width + shift :], axis=0, keepdims=True)[:, :TILE]
    padded = jnp.concatenate([scalars, jnp.zeros((1, atoms - TILE), F32)], 1)
    out[...] = jnp.concatenate(fields + [padded, jnp.zeros((4, atoms), F32)], 0)


def finish_kernel(mine, theirs, ordered, applied, dipoles, residual, next_dipoles, next_residual, direction):
    total = mine[...] + theirs[...]
    step = total[3:4, 2:3] / (total[3:4, 0:1] + total[3:4, 1:2])
    d = ordered[0:3, : dipoles.shape[1]]
    next_dipoles[...] = dipoles[...] + step * d
    next_residual[...] = residual[...] - step * (applied[0:3] + total[0:3])
    direction[...] = d


def cas_matrix(first, second):
    angles = 2.0 * np.pi / G * (np.outer(first, second) % G)
    return np.cos(angles) + np.sin(angles)


def split_constant(values):
    whole = values.astype(np.float32)
    high = whole.astype(ml_dtypes.bfloat16)
    low = (values - high.astype(np.float64)).astype(ml_dtypes.bfloat16)
    return (jnp.asarray(high), jnp.asarray(low))


def wave_factors():
    freq = np.arange(G)
    wrapped = np.where(freq > G // 2, freq - G, freq) / G
    angles = 2.0 * np.pi / G * freq
    modulus = 115.0 / 192.0 + 19.0 / 48.0 * np.cos(angles) + 1.0 / 192.0 * np.cos(2.0 * angles)
    rows = np.zeros((8, G), np.float32)
    rows[0] = wrapped * wrapped
    rows[1] = np.exp(-((np.pi / BETA) ** 2) * wrapped * wrapped) / (modulus * modulus)
    return jnp.asarray(rows)


def swap_pairs(n_slab, n_space, odd):
    pairs = []
    for s in range(n_slab):
        for q in range(n_space):
            partner = (q + 1 if (q % 2 == 1) == odd else q - 1) % n_space
            pairs.append((s * n_space + q, s * n_space + partner))
    return pairs


def beside(block, odd):
    n_slab, n_space = (lax.axis_size("slab"), lax.axis_size(SPACE))
    return lax.ppermute(block, BOTH, swap_pairs(n_slab, n_space, odd))


def along_slab(level):
    n_slab = lax.axis_size("slab")
    up = [(i, (i + 1) % n_slab) for i in range(n_slab)]
    down = [(j, i) for i, j in up]
    return (level, lax.ppermute(level, "slab", up), lax.ppermute(level, "slab", down))


def joined(block, inner, outer):
    return call(join_kernel, [((3, 2, 8, TILE), F32)], 10**6)(block, inner, outer)[0]


def around(block, bundle=None, beneath=None):
    inner = beside(block if bundle is None else bundle, False)
    outer, _ = lax.optimization_barrier((beside(block, True), beneath))
    return along_slab(joined(block, inner, outer)), inner


def local(
    dipoles, residual, cells, fraction, polarizability, tile_order, send_tiles, tile_lists, tile_counts
):
    n_slab, n_space = (lax.axis_size("slab"), lax.axis_size(SPACE))
    n_pair = n_space // 2
    atoms = residual.shape[1]
    extents = (G // n_slab, G // n_space)
    x_rows = -(-(extents[0] + 4) // 8) * 8
    y_rows = extents[1] + 4
    pair_rows = 2 * extents[1] + 4
    shift = extents[1] * x_rows
    half = G // 2
    tile_shape = ((4, 8, TILE), F32)
    two_shape = ((2, 8, TILE), F32)
    one_bank = ((3, 8, TILE, TILE), F32)
    pool_scratch = pltpu.VMEM((22, 8, TILE), F32)
    total_scratch = pltpu.VMEM((3, TILE, TILE), F32)
    own, sent, statics = pl.pallas_call(
        gather_kernel,
        out_shape=[
            jax.ShapeDtypeStruct(*tile_shape),
            jax.ShapeDtypeStruct(*two_shape),
            jax.ShapeDtypeStruct((8, atoms + 2 * TILE), F32),
        ],
        in_specs=[pl.BlockSpec(memory_space=pltpu.HBM)] * 6,
        out_specs=[pl.BlockSpec(memory_space=pltpu.VMEM)] * 3,
        scratch_shapes=[
            pltpu.VMEM((3, atoms), F32),
            pltpu.VMEM((3, atoms), jnp.int32),
            pltpu.VMEM((3, atoms), F32),
            pltpu.VMEM((atoms,), F32),
            pltpu.VMEM((1, atoms), jnp.int32),
            pltpu.SMEM((1, 2), jnp.int32),
            pltpu.SemaphoreType.DMA((6,)),
        ],
        compiler_params=pltpu.CompilerParams(vmem_limit_bytes=SMALL_VMEM),
    )(
        *[
            pltpu.with_memory_space_constraint(array, pltpu.HBM)
            for array in (residual, cells, fraction, polarizability, tile_order, send_tiles)
        ],
    )
    smem, anywhere = (pl.BlockSpec(memory_space=pltpu.SMEM), pl.BlockSpec(memory_space=pltpu.HBM))
    meta = pl.pallas_call(
        meta_kernel,
        out_shape=jax.ShapeDtypeStruct((48,), jnp.int32),
        in_specs=[smem, smem, smem, pl.BlockSpec(memory_space=pltpu.VMEM)],
        out_specs=smem,
        compiler_params=pltpu.CompilerParams(vmem_limit_bytes=SMALL_VMEM),
        cost_estimate=pl.CostEstimate(flops=10**8, bytes_accessed=1 << 20, transcendentals=0),
    )(tile_lists, tile_counts, send_tiles, sent)
    first, statics_beside = around(sent, statics, beneath=meta)

    freq = np.arange(G)
    rows_y = np.arange(n_pair)[None] * 2 * extents[1] + np.arange(2 * extents[1])[:, None]
    cas_y = cas_matrix(rows_y.reshape(-1), freq)
    freq_by_core = np.stack([freq[0::2], freq[1::2]])
    cas_z = cas_matrix(freq_by_core.reshape(-1), freq).reshape(2, half, G)
    def pairs_of(place, count):
        return call(
            functools.partial(pair_kernel, place, count, extents),
            [((22, 8, TILE), F32), ((3, 8 * count, TILE, TILE), F32), ((count, 8, TILE), F32)],
            10**9,
            smem=1,
            scratch=(pltpu.VMEM((4, TILE, TILE), F32), total_scratch),
        )(meta, own, *first)

    geometry, pairs_a, search_a = pairs_of(0, 2)
    _, pairs_b, search_b = pairs_of(2, 1)
    _, pairs_c, search_c = pairs_of(3, 1)
    sweep_scratch = (pool_scratch, pltpu.VMEM((3, TILE, TILE), F32), total_scratch)
    second, _ = around(search_a, beneath=search_b)

    def sweep(place, owns, received, banks):
        return call(
            functools.partial(sweep_kernel, place, len(owns)),
            [two_shape],
            10**8,
            smem=1,
            scratch=sweep_scratch,
        )(meta, geometry, *owns, *received, *banks)[0]

    searches = (search_a, search_b, search_c)
    next_a = sweep(0, searches, second, (pairs_a,))
    next_b = sweep(2, searches, second, (pairs_b, pairs_c))
    third, _ = around(next_a, beneath=next_b)
    statics_beside, _ = lax.optimization_barrier((statics_beside, third[0]))
    tables = call(
        tables_kernel,
        [
            ((2, 2, x_rows, atoms), F32),
            ((2, 2, y_rows, atoms), F32),
            ((2, half, atoms), BF16),
            ((2, half, atoms), BF16),
            ((2, half, atoms), F32),
        ],
        10**8,
        vmem=LARGE_VMEM,
        scratch=(pltpu.VMEM((half, G), BF16),) * 2 + (pltpu.SemaphoreType.DMA((2,)),),
        hbm=2,
    )(statics, statics_beside, *split_constant(cas_z))
    level, before, after = third
    after, _ = lax.optimization_barrier((after, tables[1]))
    third = (level, before, after)
    local_scratch = pltpu.VMEM((4, 8, TILE), F32)
    sent = sweep(0, (next_a, next_b), third, (pairs_a,))
    outer = beside(sent, True)
    rest, ordered = call(
        direction_kernel,
        [two_shape, ((8, atoms + 2 * TILE), F32)],
        10**8,
        smem=1,
        scratch=sweep_scratch + (local_scratch,),
    )(meta, geometry, next_a, next_b, *third, sent, pairs_b, pairs_c, tile_order)
    ordered_beside = beside(ordered, False)
    message = ((half, 8, TILE), F32)
    flat_scratch = pltpu.VMEM((half, 8 * TILE), F32)
    spread_own = call(spread_own_kernel, [((half, x_rows * y_rows), F32)], 10**9, vmem=LARGE_VMEM)(ordered, *tables)[0]
    spread = call(
        functools.partial(spread_both_kernel, shift),
        [message],
        10**9,
        scratch=(flat_scratch, pltpu.VMEM(*message), pltpu.SemaphoreType.DMA((4,))),
        vmem=LARGE_VMEM,
        hbm_outs=True,
    )(ordered_beside, spread_own, *tables)[0]
    spread, outer = lax.optimization_barrier((spread, outer))
    grid = lax.all_to_all(spread, CHIPS, 0, 0, tiled=True)
    last = along_slab(joined(sent, ordered_beside, outer))
    applied, sums = call(
        final_field_kernel,
        [((8, atoms), F32), ((8, TILE), F32)],
        10**9,
        smem=1,
        scratch=sweep_scratch
        + (local_scratch, pltpu.VMEM(*one_bank), pltpu.VMEM(*one_bank), pltpu.SemaphoreType.DMA((2,))),
        vmem=LARGE_VMEM,
        hbm=2,
    )(meta, geometry, sent, rest, *last, pairs_a, tile_order, pairs_b, pairs_c)
    planes = call(
        functools.partial(plane_kernel, (n_slab, n_pair, x_rows, pair_rows)),
        [message],
        10**9,
        scratch=(flat_scratch, pltpu.VMEM((G, G), F32), pltpu.VMEM(*message))
        + (pltpu.VMEM((G, G), BF16),) * 6
        + (pltpu.SemaphoreType.DMA((7,)),),
        vmem=LARGE_VMEM,
        hbm=7,
    )(
        wave_factors(),
        sums,
        grid,
        *split_constant(cas_matrix(freq, freq)),
        *split_constant(cas_y.T),
        *split_constant(cas_y),
    )[0]
    returned = lax.all_to_all(planes, CHIPS, 0, 0, tiled=True)

    def probe(side):
        return call(
            functools.partial(probe_kernel, side, shift), [((8, atoms), F32)], 10**9, vmem=LARGE_VMEM
        )(returned, *tables)[0]

    theirs = beside(probe(1), False)
    three = ((3, atoms), F32)
    return tuple(
        call(finish_kernel, [three, three, three], 10**6)(
            probe(0), theirs, ordered, applied, dipoles, residual
        )
    )


def solution(mesh):
    slab, space = (mesh.shape["slab"], mesh.shape["space"])
    mesh = Mesh(mesh.devices.reshape(slab, space // 2, 2), BOTH)
    in_specs = (
        P(None, BOTH),
        P(None, BOTH),
        P(None, BOTH),
        P(None, BOTH),
        P(BOTH),
        P(BOTH, None),
        P(BOTH, None),
        P(BOTH, None, None),
        P(BOTH, None),
    )
    out_specs = (P(None, BOTH), P(None, BOTH), P(None, BOTH))
    return jax.shard_map(local, mesh=mesh, in_specs=in_specs, out_specs=out_specs, check_vma=False)
```

```python
import functools
import math

import jax
import jax.numpy as jnp
import ml_dtypes
import numpy as np
from jax import lax
from jax.experimental import pallas as pl
from jax.experimental.pallas import tpu as pltpu
from jax.sharding import Mesh
from jax.sharding import PartitionSpec as P

G = 256
TILE = 128
SPACE = ("pair", "core")
BOTH = ("slab", "pair", "core")
CHIPS = ("slab", "pair")
BETA = 0.4
THOLE = 0.39
ROOT_PI = math.sqrt(math.pi)
SELF_FIELD = 4.0 * BETA**3 / (3.0 * ROOT_PI)
F32 = jnp.float32
BF16 = jnp.bfloat16
SCALED_ERFC_T = 0.45
SCALED_ERFC = (
    0.25388532876968384,
    0.25388309359550476,
    0.22827406227588654,
    0.17522020637989044,
    0.1201537474989891,
    -0.023065825924277306,
    0.14381752908229828,
    -0.3022053837776184,
    0.19167575240135193,
    -0.04163854941725731,
)
NT = (((1,), (1,)), ((), ()))
NN = (((1,), (0,)), ((), ()))
TN = (((0,), (0,)), ((), ()))
SMALL_VMEM = 6 * 1024 * 1024
LARGE_VMEM = 16 * 1024 * 1024


def halves(values):
    high = values.astype(BF16)
    return (high, (values - high.astype(F32)).astype(BF16))


def product(left, right, dims, stacked=True):
    def one(a, b):
        return lax.dot_general(a, b, dims, preferred_element_type=F32)

    (left_dim,), (right_dim,) = dims[0]
    if not stacked:
        return one(left[0], right[0]) + (one(left[0], right[1]) + one(left[1], right[0]))
    return one(
        jnp.concatenate([left[0], left[0], left[1]], left_dim),
        jnp.concatenate([right[0], right[1], right[0]], right_dim),
    )


def thirds(values):
    high = values.astype(BF16).astype(F32)
    rest = values - high
    middle = rest.astype(BF16).astype(F32)
    return jnp.concatenate([high, middle, rest - middle], 0).astype(BF16)


def selected(values, one_hot, dims):
    rows = values.shape[0]
    picked = lax.dot_general(thirds(values), one_hot, dims, preferred_element_type=F32)
    return picked[:rows] + (picked[rows : 2 * rows] + picked[2 * rows :])


def order_matrix(order_row, count):
    ids = lax.broadcasted_iota(jnp.int32, (count, count), 0)
    return jnp.where(ids == order_row, 1.0, 0.0).astype(BF16)


COUNTS_AT = 32
ORDER_AT = 36
PARITY_AT = 40


def meta_kernel(stored_lists, stored_counts, stored_send, after, meta, lists, counts, send, sems):
    copies = [
        pltpu.make_async_copy(source, target, sems.at[at])
        for at, (source, target) in enumerate(
            ((stored_lists, lists), (stored_counts, counts), (stored_send, send))
        )
    ]
    for copy in copies:
        copy.start()
    for copy in copies:
        copy.wait()
    parity = lax.axis_index("core")
    for tile in range(4):

        def remap(place, carry):
            entry = lists[0, tile, place]
            remote = entry - 4
            pair = lax.shift_right_arithmetic(remote, 1)
            pair = pair + jnp.where(pair >= 4, 1, 0)
            along = jnp.where(pair >= 3, 1, 0) + jnp.where(pair >= 6, 1, 0)
            across = pair - 3 * along
            base = jnp.where(across == 1, 4, jnp.where(across == 2 - 2 * parity, 10, 16))
            slot = base + along * 2 + (remote & 1)
            meta[tile * 8 + place] = jnp.where(entry < 4, entry, slot)
            return carry

        lax.fori_loop(0, 8, remap, 0)
        meta[COUNTS_AT + tile] = counts[0, tile]
    first, second = (send[0, 0], send[0, 1])
    third = jnp.where(
        (first != 0) & (second != 0), 0, jnp.where((first != 1) & (second != 1), 1, 2)
    )
    meta[ORDER_AT] = first
    meta[ORDER_AT + 1] = second
    meta[ORDER_AT + 2] = third
    meta[ORDER_AT + 3] = 6 - first - second - third
    meta[PARITY_AT] = parity


def call(kernel, outs, flops, smem=0, scratch=(), vmem=SMALL_VMEM, hbm=0, hbm_outs=False):
    def run(*args):
        kept = len(args) - hbm
        args = args[:kept] + tuple(
            pltpu.with_memory_space_constraint(array, pltpu.HBM) for array in args[kept:]
        )
        in_specs = [pl.BlockSpec(memory_space=pltpu.SMEM)] * smem
        in_specs += [pl.BlockSpec(memory_space=pltpu.VMEM)] * (kept - smem)
        in_specs += [pl.BlockSpec(memory_space=pltpu.HBM)] * hbm
        return pl.pallas_call(
            kernel,
            out_shape=[
                (pltpu.HBM if hbm_outs else jax.ShapeDtypeStruct)(shape, dtype) for shape, dtype in outs
            ],
            in_specs=in_specs,
            out_specs=[pl.BlockSpec(memory_space=pltpu.HBM if hbm_outs else pltpu.VMEM)] * len(outs),
            scratch_shapes=list(scratch),
            compiler_params=pltpu.CompilerParams(vmem_limit_bytes=vmem),
            cost_estimate=pl.CostEstimate(
                flops=flops, bytes_accessed=1 << 20, transcendentals=0
            ),
        )(*args)

    return run


def gather_kernel(*refs):
    sources, (own, sent, bundle), held, sems = (refs[:6], refs[6:9], refs[9:15], refs[15])
    copies = [
        pltpu.make_async_copy(source, target, sems.at[at])
        for at, (source, target) in enumerate(zip(sources, held))
    ]
    for copy in copies:
        copy.start()
    for copy in copies:
        copy.wait()
    residual, cells, fraction, alphas, order, send = held
    atoms = residual.shape[1]
    in_cells = cells[...].astype(F32)
    bundle[0:3, :atoms] = in_cells
    bundle[3:6, :atoms] = fraction[...]
    bundle[6:8, :atoms] = jnp.zeros((2, atoms), F32)
    position = in_cells + fraction[...]
    rows = jnp.concatenate(
        [position, alphas[...].reshape(1, atoms), residual[...], jnp.zeros((1, atoms), F32)], 0
    )
    picked = selected(rows, order_matrix(order[...], atoms), NN)
    for tile in range(atoms // TILE):
        own[tile] = picked[:, tile * TILE : (tile + 1) * TILE]
    for place in range(2):
        block = own[send[0, place]]
        sent[place] = block
        bundle[:, atoms + place * TILE : atoms + (place + 1) * TILE] = block


def search_rows(block):
    return block[3:4] * block[4:7]


def fill_pool(pool, extents, own, level, before, after, meta):
    inner_step = jnp.where(meta[PARITY_AT] == 0, 1.0, -1.0)
    rows = lax.broadcasted_iota(jnp.int32, (8, TILE), 0)
    for tile in range(4):
        pool[tile] = own[tile]
    for along, source in enumerate((before, level, after)):
        for kind, step in enumerate((0.0, inner_step, -inner_step)):
            shift = jnp.where(
                rows == 0,
                float((along - 1) * extents[0]),
                jnp.where(rows == 1, step * float(extents[1]), 0.0),
            )
            for member in range(2):
                pool[4 + 6 * kind + 2 * along + member] = source[kind, member] + shift


def own_columns(columns, block, count):
    turned = block.T
    for row in range(count):
        columns[row] = jnp.broadcast_to(turned[:, row : row + 1], (TILE, TILE))


def wrap_depth(depth):
    half = 0.5 * G
    return jnp.where(depth > half, depth - G, jnp.where(depth < -half, depth + G, depth))


PAIR_ROWS = 32
GROUP = 4


def pair_kernel(extents, meta, own, level, before, after, pool, pairs, found, columns, totals):
    fill_pool(pool, extents, own, level, before, after, meta)
    pair_tiles(0, meta, pool, pairs, found, columns, totals)


def pair_tiles(first_place, meta, pool, pairs, found, columns, totals):
    def tile_step(at, carry):
        tile = meta[ORDER_AT + first_place + at]
        block = pool[tile]
        own_columns(columns, jnp.concatenate([block[:3], lax.rsqrt(block[3:4]), block[4:]], 0), 4)
        live = meta[COUNTS_AT + tile]

        def chunk_step(chunk, carry):
            start = pl.multiple_of(chunk * PAIR_ROWS, PAIR_ROWS)
            rows = pl.ds(start, PAIR_ROWS)
            shape = (PAIR_ROWS, TILE)
            ahead = lax.broadcasted_iota(jnp.int32, shape, 0) - lax.broadcasted_iota(
                jnp.int32, shape, 1
            )
            diagonal = jnp.where(ahead == -start, 1.0, 0.0)

            def group_step(group, sums):
                for member in range(GROUP):
                    entry = group * GROUP + member
                    slot = meta[tile * 8 + entry]
                    other = pool[slot]
                    itself = diagonal * jnp.where(slot == tile, 1.0, 0.0)
                    d_x = other[0:1] - columns[0, rows]
                    d_y = other[1:2] - columns[1, rows]
                    d_z = wrap_depth(other[2:3] - columns[2, rows])
                    square = d_x * d_x + d_y * d_y + d_z * d_z + itself
                    inverse = lax.rsqrt(square)
                    distance = square * inverse
                    inverse_sq = inverse * inverse
                    gauss = jnp.exp(-(BETA**2) * square)
                    stretch = 1.0 + (SCALED_ERFC_T * BETA) * distance
                    t = lax.rsqrt(stretch * stretch)
                    series = SCALED_ERFC[-1] * t + SCALED_ERFC[-2]
                    for term in SCALED_ERFC[-3::-1]:
                        series = series * t + term
                    bare_one = gauss * (series * t * inverse + 2.0 * BETA / ROOT_PI) * inverse_sq
                    bare_two = (3.0 * bare_one + (4.0 * BETA**3 / ROOT_PI) * gauss) * inverse_sq
                    damping = (square * distance) * columns[3, rows] * (THOLE * lax.rsqrt(other[3:4]))
                    decay = jnp.exp(-damping) * inverse * inverse_sq
                    keep = jnp.where(entry < live, 1.0, 0.0) * (1.0 - itself)
                    three = keep * (bare_one - decay)
                    five = keep * (bare_two - (3.0 + 3.0 * damping) * decay * inverse_sq)
                    pairs[0, at * 8 + entry, rows] = five
                    pairs[1, at * 8 + entry, rows] = three
                    pairs[2, at * 8 + entry, rows] = d_z
                    v = search_rows(other)
                    along = five * (d_x * v[0:1] + d_y * v[1:2] + d_z * v[2:3])
                    sums = (
                        sums[0] + (along * d_x - three * v[0:1]),
                        sums[1] + (along * d_y - three * v[1:2]),
                        sums[2] + (along * d_z - three * v[2:3]),
                    )
                return sums

            zero = jnp.zeros(shape, F32)
            sums = lax.fori_loop(0, (live + GROUP - 1) // GROUP, group_step, (zero, zero, zero))
            for part in range(3):
                totals[part, rows] = sums[part]
            return carry

        lax.fori_loop(0, TILE // PAIR_ROWS, chunk_step, 0)
        found[at] = updated(block, totals)
        return carry

    lax.fori_loop(0, found.shape[0], tile_step, 0)


def field_rows(totals):
    return [jnp.sum(totals[part].T, axis=0, keepdims=True) for part in range(3)]


def updated(block, totals):
    alpha = block[3:4]
    field = field_rows(totals)
    rows = [alpha * (block[4 + part : 5 + part] + field[part]) for part in range(3)]
    return jnp.concatenate(rows + [jnp.zeros((5, TILE), F32)], 0)


APPLY_ROWS = 64


def fill_search(pool, owns, level, before, after, meta):
    place = 0
    for own in owns:
        for at in range(own.shape[0]):
            pool[meta[ORDER_AT + place]] = own[at]
            place += 1
    for along, source in enumerate((before, level, after)):
        for kind in range(3):
            for member in range(2):
                pool[4 + 6 * kind + 2 * along + member] = source[kind, member]


def join_kernel(own, inner, outer, level):
    for member in range(2):
        level[0, member] = own[member]
        if len(inner.shape) == 3:
            level[1, member] = inner[member]
        else:
            start = inner.shape[1] - (2 - member) * TILE
            level[1, member] = inner[:, start : start + TILE]
        level[2, member] = outer[member]


def apply_tile(meta, tile, at, pairs, geometry, pool, columns, totals):
    block = geometry[tile]
    own_columns(columns, block, 2)
    live = meta[COUNTS_AT + tile]

    def chunk_step(chunk, carry):
        rows = pl.ds(pl.multiple_of(chunk * APPLY_ROWS, APPLY_ROWS), APPLY_ROWS)

        def group_step(group, sums):
            for member in range(GROUP):
                entry = group * GROUP + member
                slot = meta[tile * 8 + entry]
                other = geometry[slot]
                v = pool[slot]
                d_x = other[0:1] - columns[0, rows]
                d_y = other[1:2] - columns[1, rows]
                d_z = pairs[2, at * 8 + entry, rows]
                three = pairs[1, at * 8 + entry, rows]
                along = pairs[0, at * 8 + entry, rows] * (d_x * v[0:1] + d_y * v[1:2] + d_z * v[2:3])
                sums = (
                    sums[0] + (along * d_x - three * v[0:1]),
                    sums[1] + (along * d_y - three * v[1:2]),
                    sums[2] + (along * d_z - three * v[2:3]),
                )
            return sums

        zero = jnp.zeros((APPLY_ROWS, TILE), F32)
        sums = lax.fori_loop(0, (live + GROUP - 1) // GROUP, group_step, (zero, zero, zero))
        for part in range(3):
            totals[part, rows] = sums[part]
        return carry

    lax.fori_loop(0, TILE // APPLY_ROWS, chunk_step, 0)


def sweep_tiles(place, meta, geometry, banks, found, pool, columns, totals, local=None):
    done = 0
    for pairs in banks:
        count = pairs.shape[1] // 8

        def tile_step(at, carry):
            tile = meta[ORDER_AT + place + done + at]
            apply_tile(meta, tile, at, pairs, geometry, pool, columns, totals)
            rows = updated(geometry[tile], totals)
            found[done + at] = rows
            if local is not None:
                local[tile] = rows
            return carry

        lax.fori_loop(0, count, tile_step, 0)
        done += count


def sweep_kernel(place, owns, meta, geometry, *refs):
    own_refs, (level, before, after) = (refs[:owns], refs[owns : owns + 3])
    banks, (found, pool, columns, totals) = (refs[owns + 3 : -4], refs[-4:])
    fill_search(pool, own_refs, level, before, after, meta)
    sweep_tiles(place, meta, geometry, banks, found, pool, columns, totals)


def direction_kernel(
    meta, geometry, own_a, own_b, level, before, after, sent, pairs_b, pairs_c, order, found, bundle, pool, columns, totals, local
):
    atoms = order.shape[1]
    fill_search(pool, (own_a, own_b), level, before, after, meta)
    sweep_tiles(2, meta, geometry, (pairs_b, pairs_c), found, pool, columns, totals, local)
    for place in range(2):
        block = sent[place]
        local[meta[ORDER_AT + place]] = block
        bundle[:, atoms + place * TILE : atoms + (place + 1) * TILE] = block
    in_tiles = jnp.concatenate([local[tile] for tile in range(4)], 1)
    bundle[:, :atoms] = selected(in_tiles, order_matrix(order[...], atoms), NT)


def final_field_kernel(
    meta, geometry, sent, rest, level, before, after, pairs_a, order, stored_b, stored_c, applied, sums, pool, columns, totals, local, pairs_b, pairs_c, sems
):
    copies = [
        pltpu.make_async_copy(source, target, sems.at[at])
        for at, (source, target) in enumerate(((stored_b, pairs_b), (stored_c, pairs_c)))
    ]
    for copy in copies:
        copy.start()
    atoms = order.shape[1]
    fill_search(pool, (sent, rest), level, before, after, meta)
    both = (jnp.zeros((1, TILE), F32), jnp.zeros((1, TILE), F32))
    for first, pairs in ((0, pairs_a), (2, pairs_b), (3, pairs_c)):
        if first:
            copies[first - 2].wait()

        def tile_step(at, both):
            curve, dots = both
            place = first + at
            tile = meta[ORDER_AT + place]
            apply_tile(meta, tile, at, pairs, geometry, pool, columns, totals)
            block = geometry[tile]
            ahead = rest[first - 2 + at] if first else sent[at]
            field = field_rows(totals)
            rows = []
            for part in range(3):
                d = ahead[part : part + 1]
                value = d / block[3:4] - field[part] - SELF_FIELD * d
                curve = curve + d * value
                dots = dots + d * block[4 + part : 5 + part]
                rows.append(value)
            local[tile] = jnp.concatenate(rows + [jnp.zeros((5, TILE), F32)], 0)
            return (curve, dots)

        both = lax.fori_loop(0, pairs.shape[1] // 8, tile_step, both)
    in_tiles = jnp.concatenate([local[tile] for tile in range(4)], 1)
    applied[...] = selected(in_tiles, order_matrix(order[...], atoms), NT)
    lane = lax.broadcasted_iota(jnp.int32, (8, TILE), 1)
    curve_sum = jnp.sum(both[0], axis=1, keepdims=True)
    dot_sum = jnp.sum(both[1], axis=1, keepdims=True)
    sums[...] = jnp.where(lane == 1, curve_sum, jnp.where(lane == 2, dot_sum, 0.0))


def spline(fraction):
    centre_arg = fraction - 0.5

    def middle(u):
        return (55.0 + u * (20.0 + u * (-120.0 + u * (80.0 - 16.0 * u)))) / 96.0

    def middle_slope(u):
        return (20.0 + u * (-240.0 + u * (240.0 - 64.0 * u))) / 96.0

    def outer(u):
        w = 5.0 - 2.0 * u
        return (w * w) * (w * w) / 384.0

    def outer_slope(u):
        w = 5.0 - 2.0 * u
        return -(w * w * w) / 48.0

    sq = centre_arg * centre_arg
    weights = (
        outer(fraction + 1.5),
        middle(fraction + 0.5),
        115.0 / 192.0 - 0.625 * sq + 0.25 * sq * sq,
        middle(1.5 - fraction),
        outer(2.5 - fraction),
    )
    slopes = (
        outer_slope(fraction + 1.5),
        middle_slope(fraction + 0.5),
        -1.25 * centre_arg + centre_arg * sq,
        -middle_slope(1.5 - fraction),
        -outer_slope(2.5 - fraction),
    )
    return (weights, slopes)


def table(cell_row, values, length, wrapped):
    atoms = cell_row.shape[1]
    ids = lax.broadcasted_iota(jnp.int32, (length, atoms), 0)
    if wrapped:
        ahead = ids - cell_row + 2
        ahead = jnp.where(ahead >= G, ahead - G, jnp.where(ahead < 0, ahead + G, ahead))
    else:
        ahead = ids - cell_row
    total = jnp.zeros((length, atoms), F32)
    for step in range(5):
        total = jnp.where(ahead == step, values[step], total)
    return total


def tables_kernel(
    mine, beside, stored_high, stored_low, tab_x, tab_y, w_high, w_low, slope_z, cas_high, cas_low, sems
):
    core = lax.axis_index("core")
    copies = [
        pltpu.make_async_copy(stored_high.at[core], cas_high, sems.at[0]),
        pltpu.make_async_copy(stored_low.at[core], cas_low, sems.at[1]),
    ]
    for copy in copies:
        copy.start()
    for copy in copies:
        copy.wait()
    cas = (cas_high[...], cas_low[...])
    for side, statics in enumerate((mine, beside)):
        atoms = tab_x.shape[3]
        cells = statics[0:3, :atoms].astype(jnp.int32)
        for dim, out in ((0, tab_x), (1, tab_y)):
            weights, slopes = spline(statics[3 + dim : 4 + dim, :atoms])
            out[side, 0] = table(cells[dim : dim + 1], weights, out.shape[2], False)
            out[side, 1] = table(cells[dim : dim + 1], slopes, out.shape[2], False)
        weights, slopes = spline(statics[5:6, :atoms])
        high, low = halves(product(cas, halves(table(cells[2:3], weights, G, True)), NN))
        w_high[side] = high
        w_low[side] = low
        slope_z[side] = product(cas, halves(table(cells[2:3], slopes, G, True)), NN)


def spread_part(side, d, tab_x, tab_y, w_high, w_low, slope_z):
    w_z = (w_high[side], w_low[side])
    s_z = halves(slope_z[side] * d[2:3])
    weight_x = tab_x[side, 0]
    slope_part = tab_x[side, 1] * d[0:1]
    weight_part = weight_x * d[1:2]
    sides = []
    for y in range(tab_y.shape[2]):
        w_y, s_y = (tab_y[side, 0, y : y + 1], tab_y[side, 1, y : y + 1])
        sides.append((slope_part * w_y + weight_part * s_y, weight_x * w_y))
    rows = halves(jnp.concatenate([pair[0] for pair in sides], 0))
    flat = halves(jnp.concatenate([pair[1] for pair in sides], 0))
    return product(w_z, rows, NT) + product(s_z, flat, NT)


def spread_own_kernel(ordered, tab_x, tab_y, w_high, w_low, slope_z, out):
    out[...] = spread_part(0, ordered[:, : tab_x.shape[3]], tab_x, tab_y, w_high, w_low, slope_z)


def put_lanes(out, flat):
    for row in range(8):
        out[:, row, :] = flat[:, row * TILE : (row + 1) * TILE]


def get_lanes(grid):
    return jnp.concatenate([grid[:, row, :] for row in range(8)], 1)


def spread_both_kernel(shift, ordered, mine, tab_x, tab_y, w_high, w_low, slope_z, out, flat, message, sems):
    theirs = spread_part(1, ordered[:, : tab_x.shape[3]], tab_x, tab_y, w_high, w_low, slope_z)
    ours = mine[...]
    width = ours.shape[1]
    even = lax.axis_index("core") == 0
    lower = jnp.where(even, ours, theirs)
    upper = jnp.where(even, theirs, ours)
    flat[:, :shift] = lower[:, :shift]
    flat[:, shift:width] = lower[:, shift:] + upper[:, : width - shift]
    flat[:, width : width + shift] = upper[:, width - shift :]
    flat[:, width + shift :] = jnp.zeros((flat.shape[0], flat.shape[1] - width - shift), F32)
    pieces = sems.shape[0]
    size = flat.shape[0] // pieces
    copies = []
    for piece in range(pieces):
        rows = slice(piece * size, (piece + 1) * size)
        for row in range(8):
            message[rows, row, :] = flat[rows, row * TILE : (row + 1) * TILE]
        copies.append(pltpu.make_async_copy(message.at[rows], out.at[rows], sems.at[piece]))
        copies[-1].start()
    for copy in copies:
        copy.wait()


def factor_of(waves, freq_z):
    ids_x = lax.broadcasted_iota(jnp.int32, (1, G), 1)
    by_x = waves[...]
    by_z = jnp.sum(jnp.where(ids_x == freq_z, by_x, 0.0), axis=1, keepdims=True)
    by_y = by_x.T
    anchor = jnp.where(
        (lax.broadcasted_iota(jnp.int32, (G, G), 0) + lax.broadcasted_iota(jnp.int32, (G, G), 1) + freq_z) == 0, 1.0, 0.0
    )
    squares = by_x[0:1] + by_y[:, 0:1] + (by_z[0:1] + anchor)
    return (1.0 - anchor) * (by_x[1:2] * by_z[1:2]) * by_y[:, 1:2] / (math.pi * float(G) ** 3 * squares)


def rolled(flat, rows, start, size, amount):
    low = start // TILE * TILE
    high = -(-(start + size) // TILE) * TILE
    return pltpu.roll(flat[rows, low:high], amount, 0)[:, start - low : start - low + size]


def plane_kernel(shapes, waves, sums, *refs):
    stored, out, flat, plane = (refs[:7], refs[7], refs[8], refs[9])
    held, sems = (refs[10:17], refs[17])
    copies = [
        pltpu.make_async_copy(source, target, sems.at[at])
        for at, (source, target) in enumerate(zip(stored, held))
    ]
    for copy in copies:
        copy.start()
    grid, x_high, x_low, yt_high, yt_low, y_high, y_low = held
    n_slab, n_pair, x_rows, y_rows = shapes
    x_own, y_own = (G // n_slab, y_rows - 4)
    width = x_rows * y_rows
    freq_z = lax.axis_index("slab") * (2 * n_pair) + 2 * lax.axis_index("pair") + lax.axis_index("core")
    factor = factor_of(waves, freq_z)
    copies[0].wait()
    flat[...] = get_lanes(grid)
    two = 2 * x_rows
    first_own, last_own = (slice(two, 2 * two), slice(y_own * x_rows, y_own * x_rows + two))
    slabs = [slice(s * n_pair, (s + 1) * n_pair) for s in range(n_slab)]
    for rows in slabs:
        from_next = rolled(flat, rows, 0, two, n_pair - 1)
        from_last = rolled(flat, rows, width - two, two, 1)
        flat[rows, last_own] = flat[rows, last_own] + from_next
        flat[rows, first_own] = flat[rows, first_own] + from_last
    padded = [
        jnp.concatenate(
            [flat[rows, (y + 2) * x_rows : (y + 3) * x_rows] for y in range(y_own)], 0
        )
        for rows in slabs
    ]
    for s, block in enumerate(padded):
        plane[:, s * x_own : (s + 1) * x_own] = block[:, 2 : x_own + 2]
    for s, block in enumerate(padded):
        for at, part in (
            ((s * x_own - 2) % G, block[:, :2]),
            ((s + 1) * x_own % G, block[:, x_own + 2 : x_own + 4]),
        ):
            plane[:, at : at + 2] = plane[:, at : at + 2] + part
    for copy in copies[1:]:
        copy.wait()
    cas_x = (x_high[...], x_low[...])
    along_x = product(halves(plane[...]), cas_x, NN, False)
    spectrum = product((yt_high[...], yt_low[...]), halves(along_x), NN, False)
    scaled = spectrum * factor
    energy = jnp.sum(jnp.sum(spectrum * scaled, axis=0, keepdims=True), axis=1, keepdims=True)
    back = halves(product((y_high[...], y_low[...]), halves(scaled), NN, False))
    plane[...] = product(back, cas_x, NN, False)
    for s, rows in enumerate(slabs):
        start, stop = (s * x_own - 2, (s + 1) * x_own + 2)
        pieces = [plane[:, max(start, 0) : min(stop, G)]]
        if start < 0:
            pieces = [plane[:, G + start :]] + pieces
        if stop > G:
            pieces = pieces + [plane[:, : stop - G]]
        block = pieces[0] if len(pieces) == 1 else jnp.concatenate(pieces, 1)
        for y in range(y_own):
            at = (y + 2) * x_rows
            flat[rows, at : at + x_own + 4] = block[y * n_pair : (y + 1) * n_pair]
        flat[rows, :two] = rolled(flat, rows, y_own * x_rows, two, 1)
        flat[rows, width - two : width] = rolled(flat, rows, two, two, n_pair - 1)
    spare = flat.shape[1] - width
    lane = lax.broadcasted_iota(jnp.int32, (1, spare), 1)
    known = jnp.concatenate([sums[0:1], jnp.zeros((1, spare - TILE), F32)], 1)
    tail = jnp.where(lane == 0, energy, known)
    flat[:, width:] = jnp.broadcast_to(tail, (flat.shape[0], spare))
    put_lanes(out, flat)


def probe_part(side, planes, tab_x, tab_y, w_high, w_low, slope_z):
    x_rows = tab_x.shape[2]
    by_weight = product(planes, (w_high[side], w_low[side]), TN)
    by_slope = product(planes, halves(slope_z[side]), TN)
    weight_x, slope_x = (tab_x[side, 0], tab_x[side, 1])
    fields = [0.0, 0.0, 0.0]
    for y in range(tab_y.shape[2]):
        rows = slice(y * x_rows, (y + 1) * x_rows)
        w_y, s_y = (tab_y[side, 0, y : y + 1], tab_y[side, 1, y : y + 1])
        weighted = by_weight[rows]
        fields[0] += w_y * jnp.sum(slope_x * weighted, axis=0, keepdims=True)
        fields[1] += s_y * jnp.sum(weight_x * weighted, axis=0, keepdims=True)
        fields[2] += w_y * jnp.sum(weight_x * by_slope[rows], axis=0, keepdims=True)
    return fields


def probe_kernel(side, shift, grid, tab_x, tab_y, w_high, w_low, slope_z, out):
    matrix = get_lanes(grid)
    width = tab_x.shape[2] * tab_y.shape[2]
    low_side = 0 if side == 0 else 1
    planes = jnp.where(
        lax.axis_index("core") == low_side, matrix[:, :width], matrix[:, shift : shift + width]
    )
    fields = probe_part(side, halves(planes), tab_x, tab_y, w_high, w_low, slope_z)
    atoms = out.shape[1]
    scalars = jnp.sum(matrix[:, width + shift :], axis=0, keepdims=True)[:, :TILE]
    padded = jnp.concatenate([scalars, jnp.zeros((1, atoms - TILE), F32)], 1)
    out[...] = jnp.concatenate(fields + [padded, jnp.zeros((4, atoms), F32)], 0)


def finish_kernel(mine, theirs, ordered, applied, dipoles, residual, next_dipoles, next_residual, direction):
    total = mine[...] + theirs[...]
    step = total[3:4, 2:3] / (total[3:4, 0:1] + total[3:4, 1:2])
    d = ordered[0:3, : dipoles.shape[1]]
    next_dipoles[...] = dipoles[...] + step * d
    next_residual[...] = residual[...] - step * (applied[0:3] + total[0:3])
    direction[...] = d


def cas_matrix(first, second):
    angles = 2.0 * np.pi / G * (np.outer(first, second) % G)
    return np.cos(angles) + np.sin(angles)


def split_constant(values):
    whole = values.astype(np.float32)
    high = whole.astype(ml_dtypes.bfloat16)
    low = (values - high.astype(np.float64)).astype(ml_dtypes.bfloat16)
    return (jnp.asarray(high), jnp.asarray(low))


def wave_factors():
    freq = np.arange(G)
    wrapped = np.where(freq > G // 2, freq - G, freq) / G
    angles = 2.0 * np.pi / G * freq
    modulus = 115.0 / 192.0 + 19.0 / 48.0 * np.cos(angles) + 1.0 / 192.0 * np.cos(2.0 * angles)
    rows = np.zeros((8, G), np.float32)
    rows[0] = wrapped * wrapped
    rows[1] = np.exp(-((np.pi / BETA) ** 2) * wrapped * wrapped) / (modulus * modulus)
    return jnp.asarray(rows)


def swap_pairs(n_slab, n_space, odd):
    pairs = []
    for s in range(n_slab):
        for q in range(n_space):
            partner = (q + 1 if (q % 2 == 1) == odd else q - 1) % n_space
            pairs.append((s * n_space + q, s * n_space + partner))
    return pairs


def beside(block, odd):
    n_slab, n_space = (lax.axis_size("slab"), lax.axis_size(SPACE))
    return lax.ppermute(block, BOTH, swap_pairs(n_slab, n_space, odd))


def along_slab(level):
    n_slab = lax.axis_size("slab")
    up = [(i, (i + 1) % n_slab) for i in range(n_slab)]
    down = [(j, i) for i, j in up]
    return (level, lax.ppermute(level, "slab", up), lax.ppermute(level, "slab", down))


def joined(block, inner, outer):
    return call(join_kernel, [((3, 2, 8, TILE), F32)], 10**6)(block, inner, outer)[0]


def around(block, inner=None, beneath=None):
    inner = beside(block, False) if inner is None else inner
    outer, _ = lax.optimization_barrier((beside(block, True), beneath))
    return along_slab(joined(block, inner, outer))


def local(
    dipoles, residual, cells, fraction, polarizability, tile_order, send_tiles, tile_lists, tile_counts
):
    n_slab, n_space = (lax.axis_size("slab"), lax.axis_size(SPACE))
    n_pair = n_space // 2
    atoms = residual.shape[1]
    extents = (G // n_slab, G // n_space)
    x_rows = -(-(extents[0] + 4) // 8) * 8
    y_rows = extents[1] + 4
    pair_rows = 2 * extents[1] + 4
    shift = extents[1] * x_rows
    half = G // 2
    tile_shape = ((4, 8, TILE), F32)
    two_shape = ((2, 8, TILE), F32)
    one_bank = ((3, 8, TILE, TILE), F32)
    pool_scratch = pltpu.VMEM((22, 8, TILE), F32)
    total_scratch = pltpu.VMEM((3, TILE, TILE), F32)
    own, sent, statics = pl.pallas_call(
        gather_kernel,
        out_shape=[
            jax.ShapeDtypeStruct(*tile_shape),
            jax.ShapeDtypeStruct(*two_shape),
            jax.ShapeDtypeStruct((8, atoms + 2 * TILE), F32),
        ],
        in_specs=[pl.BlockSpec(memory_space=pltpu.HBM)] * 6,
        out_specs=[pl.BlockSpec(memory_space=pltpu.VMEM)] * 3,
        scratch_shapes=[
            pltpu.VMEM((3, atoms), F32),
            pltpu.VMEM((3, atoms), jnp.int32),
            pltpu.VMEM((3, atoms), F32),
            pltpu.VMEM((atoms,), F32),
            pltpu.VMEM((1, atoms), jnp.int32),
            pltpu.SMEM((1, 2), jnp.int32),
            pltpu.SemaphoreType.DMA((6,)),
        ],
        compiler_params=pltpu.CompilerParams(vmem_limit_bytes=SMALL_VMEM),
    )(
        *[
            pltpu.with_memory_space_constraint(array, pltpu.HBM)
            for array in (residual, cells, fraction, polarizability, tile_order, send_tiles)
        ],
    )
    smem, anywhere = (pl.BlockSpec(memory_space=pltpu.SMEM), pl.BlockSpec(memory_space=pltpu.HBM))
    meta = pl.pallas_call(
        meta_kernel,
        out_shape=jax.ShapeDtypeStruct((48,), jnp.int32),
        in_specs=[anywhere, anywhere, anywhere, pl.BlockSpec(memory_space=pltpu.VMEM)],
        out_specs=smem,
        scratch_shapes=[
            pltpu.SMEM(tile_lists.shape, jnp.int32),
            pltpu.SMEM(tile_counts.shape, jnp.int32),
            pltpu.SMEM(send_tiles.shape, jnp.int32),
            pltpu.SemaphoreType.DMA((3,)),
        ],
        compiler_params=pltpu.CompilerParams(vmem_limit_bytes=SMALL_VMEM),
        cost_estimate=pl.CostEstimate(flops=10**8, bytes_accessed=1 << 20, transcendentals=0),
    )(
        *[
            pltpu.with_memory_space_constraint(array, pltpu.HBM)
            for array in (tile_lists, tile_counts, send_tiles)
        ],
        sent,
    )
    statics_beside = beside(statics, False)
    freq = np.arange(G)
    rows_y = np.arange(n_pair)[None] * 2 * extents[1] + np.arange(2 * extents[1])[:, None]
    cas_y = cas_matrix(rows_y.reshape(-1), freq)
    freq_by_core = np.stack([freq[0::2], freq[1::2]])
    cas_z = cas_matrix(freq_by_core.reshape(-1), freq).reshape(2, half, G)
    tables = call(
        tables_kernel,
        [
            ((2, 2, x_rows, atoms), F32),
            ((2, 2, y_rows, atoms), F32),
            ((2, half, atoms), BF16),
            ((2, half, atoms), BF16),
            ((2, half, atoms), F32),
        ],
        10**8,
        vmem=LARGE_VMEM,
        scratch=(pltpu.VMEM((half, G), BF16),) * 2 + (pltpu.SemaphoreType.DMA((2,)),),
        hbm=2,
    )(statics, statics_beside, *split_constant(cas_z))
    first = around(sent, statics_beside, beneath=(meta, tables[1]))

    pair_scratch = (pltpu.VMEM((4, TILE, TILE), F32), total_scratch)
    geometry, pairs_a, search_a = call(
        functools.partial(pair_kernel, extents),
        [((22, 8, TILE), F32), ((3, 16, TILE, TILE), F32), two_shape],
        10**9,
        smem=1,
        scratch=pair_scratch,
    )(meta, own, *first)

    def pairs_of(place):
        return call(
            functools.partial(pair_tiles, place),
            [one_bank, ((1, 8, TILE), F32)],
            10**9,
            smem=1,
            scratch=pair_scratch,
        )(meta, geometry)

    pairs_b, search_b = pairs_of(2)
    pairs_c, search_c = pairs_of(3)
    sweep_scratch = (pool_scratch, pltpu.VMEM((3, TILE, TILE), F32), total_scratch)
    second = around(search_a, beneath=search_b)

    def sweep(place, owns, received, banks):
        return call(
            functools.partial(sweep_kernel, place, len(owns)),
            [two_shape],
            10**8,
            smem=1,
            scratch=sweep_scratch,
        )(meta, geometry, *owns, *received, *banks)[0]

    searches = (search_a, search_b, search_c)
    next_a = sweep(0, searches, second, (pairs_a,))
    next_b = sweep(2, searches, second, (pairs_b, pairs_c))
    third = around(next_a, beneath=next_b)
    local_scratch = pltpu.VMEM((4, 8, TILE), F32)
    sent = sweep(0, (next_a, next_b), third, (pairs_a,))
    outer = beside(sent, True)
    rest, ordered = call(
        direction_kernel,
        [two_shape, ((8, atoms + 2 * TILE), F32)],
        10**8,
        smem=1,
        scratch=sweep_scratch + (local_scratch,),
    )(meta, geometry, next_a, next_b, *third, sent, pairs_b, pairs_c, tile_order)
    ordered_beside = beside(ordered, False)
    message = ((half, 8, TILE), F32)
    flat_scratch = pltpu.VMEM((half, 8 * TILE), F32)
    spread_own = call(spread_own_kernel, [((half, x_rows * y_rows), F32)], 10**9, vmem=LARGE_VMEM)(ordered, *tables)[0]
    spread = call(
        functools.partial(spread_both_kernel, shift),
        [message],
        10**9,
        scratch=(flat_scratch, pltpu.VMEM(*message), pltpu.SemaphoreType.DMA((4,))),
        vmem=LARGE_VMEM,
        hbm_outs=True,
    )(ordered_beside, spread_own, *tables)[0]
    spread, outer = lax.optimization_barrier((spread, outer))
    grid = lax.all_to_all(spread, CHIPS, 0, 0, tiled=True)
    last = along_slab(joined(sent, ordered_beside, outer))
    applied, sums = call(
        final_field_kernel,
        [((8, atoms), F32), ((8, TILE), F32)],
        10**9,
        smem=1,
        scratch=sweep_scratch
        + (local_scratch, pltpu.VMEM(*one_bank), pltpu.VMEM(*one_bank), pltpu.SemaphoreType.DMA((2,))),
        vmem=LARGE_VMEM,
        hbm=2,
    )(meta, geometry, sent, rest, *last, pairs_a, tile_order, pairs_b, pairs_c)
    planes = call(
        functools.partial(plane_kernel, (n_slab, n_pair, x_rows, pair_rows)),
        [message],
        10**9,
        scratch=(flat_scratch, pltpu.VMEM((G, G), F32), pltpu.VMEM(*message))
        + (pltpu.VMEM((G, G), BF16),) * 6
        + (pltpu.SemaphoreType.DMA((7,)),),
        vmem=LARGE_VMEM,
        hbm=7,
    )(
        wave_factors(),
        sums,
        grid,
        *split_constant(cas_matrix(freq, freq)),
        *split_constant(cas_y.T),
        *split_constant(cas_y),
    )[0]
    returned = lax.all_to_all(planes, CHIPS, 0, 0, tiled=True)

    def probe(side):
        return call(
            functools.partial(probe_kernel, side, shift), [((8, atoms), F32)], 10**9, vmem=LARGE_VMEM
        )(returned, *tables)[0]

    theirs = beside(probe(1), False)
    three = ((3, atoms), F32)
    return tuple(
        call(finish_kernel, [three, three, three], 10**6)(
            probe(0), theirs, ordered, applied, dipoles, residual
        )
    )


def solution(mesh):
    slab, space = (mesh.shape["slab"], mesh.shape["space"])
    mesh = Mesh(mesh.devices.reshape(slab, space // 2, 2), BOTH)
    in_specs = (
        P(None, BOTH),
        P(None, BOTH),
        P(None, BOTH),
        P(None, BOTH),
        P(BOTH),
        P(BOTH, None),
        P(BOTH, None),
        P(BOTH, None, None),
        P(BOTH, None),
    )
    out_specs = (P(None, BOTH), P(None, BOTH), P(None, BOTH))
    return jax.shard_map(local, mesh=mesh, in_specs=in_specs, out_specs=out_specs, check_vma=False)
```

```python
import functools
import math

import jax
import jax.numpy as jnp
import ml_dtypes
import numpy as np
from jax import lax
from jax.experimental import pallas as pl
from jax.experimental.pallas import tpu as pltpu
from jax.sharding import Mesh
from jax.sharding import PartitionSpec as P

G = 256
TILE = 128
SPACE = ("pair", "core")
BOTH = ("slab", "pair", "core")
CHIPS = ("slab", "pair")
BETA = 0.4
THOLE = 0.39
ROOT_PI = math.sqrt(math.pi)
SELF_FIELD = 4.0 * BETA**3 / (3.0 * ROOT_PI)
F32 = jnp.float32
BF16 = jnp.bfloat16
SCALED_ERFC_T = 0.45
SCALED_ERFC = (
    0.25388532876968384,
    0.25388309359550476,
    0.22827406227588654,
    0.17522020637989044,
    0.1201537474989891,
    -0.023065825924277306,
    0.14381752908229828,
    -0.3022053837776184,
    0.19167575240135193,
    -0.04163854941725731,
)
NT = (((1,), (1,)), ((), ()))
NN = (((1,), (0,)), ((), ()))
TN = (((0,), (0,)), ((), ()))
SMALL_VMEM = 6 * 1024 * 1024
LARGE_VMEM = 16 * 1024 * 1024


def halves(values):
    high = values.astype(BF16)
    return (high, (values - high.astype(F32)).astype(BF16))


def product(left, right, dims, stacked=True):
    def one(a, b):
        return lax.dot_general(a, b, dims, preferred_element_type=F32)

    (left_dim,), (right_dim,) = dims[0]
    if not stacked:
        return one(left[0], right[0]) + (one(left[0], right[1]) + one(left[1], right[0]))
    return one(
        jnp.concatenate([left[0], left[0], left[1]], left_dim),
        jnp.concatenate([right[0], right[1], right[0]], right_dim),
    )


def thirds(values):
    high = values.astype(BF16).astype(F32)
    rest = values - high
    middle = rest.astype(BF16).astype(F32)
    return jnp.concatenate([high, middle, rest - middle], 0).astype(BF16)


def selected(values, one_hot, dims):
    rows = values.shape[0]
    picked = lax.dot_general(thirds(values), one_hot, dims, preferred_element_type=F32)
    return picked[:rows] + (picked[rows : 2 * rows] + picked[2 * rows :])


def order_matrix(order_row, count):
    ids = lax.broadcasted_iota(jnp.int32, (count, count), 0)
    return jnp.where(ids == order_row, 1.0, 0.0).astype(BF16)


COUNTS_AT = 32
ORDER_AT = 36
PARITY_AT = 40


def meta_kernel(stored_lists, stored_counts, stored_send, after, meta, lists, counts, send, sems):
    copies = [
        pltpu.make_async_copy(source, target, sems.at[at])
        for at, (source, target) in enumerate(
            ((stored_lists, lists), (stored_counts, counts), (stored_send, send))
        )
    ]
    for copy in copies:
        copy.start()
    for copy in copies:
        copy.wait()
    parity = lax.axis_index("core")
    for tile in range(4):

        def remap(place, carry):
            entry = lists[0, tile, place]
            remote = entry - 4
            pair = lax.shift_right_arithmetic(remote, 1)
            pair = pair + jnp.where(pair >= 4, 1, 0)
            along = jnp.where(pair >= 3, 1, 0) + jnp.where(pair >= 6, 1, 0)
            across = pair - 3 * along
            base = jnp.where(across == 1, 4, jnp.where(across == 2 - 2 * parity, 10, 16))
            slot = base + along * 2 + (remote & 1)
            meta[tile * 8 + place] = jnp.where(entry < 4, entry, slot)
            return carry

        lax.fori_loop(0, 8, remap, 0)
        meta[COUNTS_AT + tile] = counts[0, tile]
    first, second = (send[0, 0], send[0, 1])
    third = jnp.where(
        (first != 0) & (second != 0), 0, jnp.where((first != 1) & (second != 1), 1, 2)
    )
    meta[ORDER_AT] = first
    meta[ORDER_AT + 1] = second
    meta[ORDER_AT + 2] = third
    meta[ORDER_AT + 3] = 6 - first - second - third
    meta[PARITY_AT] = parity


def call(kernel, outs, flops, smem=0, scratch=(), vmem=SMALL_VMEM, hbm=0, hbm_outs=False):
    def run(*args):
        kept = len(args) - hbm
        args = args[:kept] + tuple(
            pltpu.with_memory_space_constraint(array, pltpu.HBM) for array in args[kept:]
        )
        in_specs = [pl.BlockSpec(memory_space=pltpu.SMEM)] * smem
        in_specs += [pl.BlockSpec(memory_space=pltpu.VMEM)] * (kept - smem)
        in_specs += [pl.BlockSpec(memory_space=pltpu.HBM)] * hbm
        return pl.pallas_call(
            kernel,
            out_shape=[
                (pltpu.HBM if hbm_outs else jax.ShapeDtypeStruct)(shape, dtype) for shape, dtype in outs
            ],
            in_specs=in_specs,
            out_specs=[pl.BlockSpec(memory_space=pltpu.HBM if hbm_outs else pltpu.VMEM)] * len(outs),
            scratch_shapes=list(scratch),
            compiler_params=pltpu.CompilerParams(vmem_limit_bytes=vmem),
            cost_estimate=pl.CostEstimate(
                flops=flops, bytes_accessed=1 << 20, transcendentals=0
            ),
        )(*args)

    return run


def gather_kernel(*refs):
    sources, (own, sent, bundle), held, sems = (refs[:6], refs[6:9], refs[9:15], refs[15])
    copies = [
        pltpu.make_async_copy(source, target, sems.at[at])
        for at, (source, target) in enumerate(zip(sources, held))
    ]
    for copy in copies:
        copy.start()
    for copy in copies:
        copy.wait()
    residual, cells, fraction, alphas, order, send = held
    atoms = residual.shape[1]
    in_cells = cells[...].astype(F32)
    bundle[0:3, :atoms] = in_cells
    bundle[3:6, :atoms] = fraction[...]
    bundle[6:8, :atoms] = jnp.zeros((2, atoms), F32)
    position = in_cells + fraction[...]
    rows = jnp.concatenate(
        [position, alphas[...].reshape(1, atoms), residual[...], jnp.zeros((1, atoms), F32)], 0
    )
    picked = selected(rows, order_matrix(order[...], atoms), NN)
    for tile in range(atoms // TILE):
        own[tile] = picked[:, tile * TILE : (tile + 1) * TILE]
    for place in range(2):
        block = own[send[0, place]]
        sent[place] = block
        bundle[:, atoms + place * TILE : atoms + (place + 1) * TILE] = block


def search_rows(block):
    return block[3:4] * block[4:7]


def fill_pool(pool, extents, own, level, before, after, meta):
    inner_step = jnp.where(meta[PARITY_AT] == 0, 1.0, -1.0)
    rows = lax.broadcasted_iota(jnp.int32, (8, TILE), 0)
    for tile in range(4):
        pool[tile] = own[tile]
    for along, source in enumerate((before, level, after)):
        for kind, step in enumerate((0.0, inner_step, -inner_step)):
            shift = jnp.where(
                rows == 0,
                float((along - 1) * extents[0]),
                jnp.where(rows == 1, step * float(extents[1]), 0.0),
            )
            for member in range(2):
                pool[4 + 6 * kind + 2 * along + member] = source[kind, member] + shift


def own_columns(columns, block, count):
    turned = block.T
    for row in range(count):
        columns[row] = jnp.broadcast_to(turned[:, row : row + 1], (TILE, TILE))


def wrap_depth(depth):
    half = 0.5 * G
    return jnp.where(depth > half, depth - G, jnp.where(depth < -half, depth + G, depth))


PAIR_ROWS = 32
GROUP = 4


def pair_kernel(extents, meta, own, level, before, after, pool, pairs, found, columns, totals):
    fill_pool(pool, extents, own, level, before, after, meta)
    pair_tiles(0, meta, pool, pairs, found, columns, totals)


def pair_tiles(first_place, meta, pool, pairs, found, columns, totals):
    def tile_step(at, carry):
        tile = meta[ORDER_AT + first_place + at]
        block = pool[tile]
        own_columns(columns, jnp.concatenate([block[:3], lax.rsqrt(block[3:4]), block[4:]], 0), 4)
        live = meta[COUNTS_AT + tile]

        def chunk_step(chunk, carry):
            start = pl.multiple_of(chunk * PAIR_ROWS, PAIR_ROWS)
            rows = pl.ds(start, PAIR_ROWS)
            shape = (PAIR_ROWS, TILE)
            ahead = lax.broadcasted_iota(jnp.int32, shape, 0) - lax.broadcasted_iota(
                jnp.int32, shape, 1
            )
            diagonal = jnp.where(ahead == -start, 1.0, 0.0)

            def group_step(group, sums):
                for member in range(GROUP):
                    entry = group * GROUP + member
                    slot = meta[tile * 8 + entry]
                    other = pool[slot]
                    itself = diagonal * jnp.where(slot == tile, 1.0, 0.0)
                    d_x = other[0:1] - columns[0, rows]
                    d_y = other[1:2] - columns[1, rows]
                    d_z = wrap_depth(other[2:3] - columns[2, rows])
                    square = d_x * d_x + d_y * d_y + d_z * d_z + itself
                    inverse = lax.rsqrt(square)
                    distance = square * inverse
                    inverse_sq = inverse * inverse
                    gauss = jnp.exp(-(BETA**2) * square)
                    stretch = 1.0 + (SCALED_ERFC_T * BETA) * distance
                    t = lax.rsqrt(stretch * stretch)
                    series = SCALED_ERFC[-1] * t + SCALED_ERFC[-2]
                    for term in SCALED_ERFC[-3::-1]:
                        series = series * t + term
                    bare_one = gauss * (series * t * inverse + 2.0 * BETA / ROOT_PI) * inverse_sq
                    bare_two = (3.0 * bare_one + (4.0 * BETA**3 / ROOT_PI) * gauss) * inverse_sq
                    damping = (square * distance) * columns[3, rows] * (THOLE * lax.rsqrt(other[3:4]))
                    decay = jnp.exp(-damping) * inverse * inverse_sq
                    keep = jnp.where(entry < live, 1.0, 0.0) * (1.0 - itself)
                    three = keep * (bare_one - decay)
                    five = keep * (bare_two - (3.0 + 3.0 * damping) * decay * inverse_sq)
                    pairs[0, at * 8 + entry, rows] = five
                    pairs[1, at * 8 + entry, rows] = three
                    pairs[2, at * 8 + entry, rows] = d_z
                    v = search_rows(other)
                    along = five * (d_x * v[0:1] + d_y * v[1:2] + d_z * v[2:3])
                    sums = (
                        sums[0] + (along * d_x - three * v[0:1]),
                        sums[1] + (along * d_y - three * v[1:2]),
                        sums[2] + (along * d_z - three * v[2:3]),
                    )
                return sums

            zero = jnp.zeros(shape, F32)
            sums = lax.fori_loop(0, (live + GROUP - 1) // GROUP, group_step, (zero, zero, zero))
            for part in range(3):
                totals[part, rows] = sums[part]
            return carry

        lax.fori_loop(0, TILE // PAIR_ROWS, chunk_step, 0)
        found[at] = updated(block, totals)
        return carry

    lax.fori_loop(0, found.shape[0], tile_step, 0)


def field_rows(totals):
    return [jnp.sum(totals[part].T, axis=0, keepdims=True) for part in range(3)]


def updated(block, totals):
    alpha = block[3:4]
    field = field_rows(totals)
    rows = [alpha * (block[4 + part : 5 + part] + field[part]) for part in range(3)]
    return jnp.concatenate(rows + [jnp.zeros((5, TILE), F32)], 0)


APPLY_ROWS = 64


def fill_search(pool, owns, level, before, after, meta):
    place = 0
    for own in owns:
        for at in range(own.shape[0]):
            pool[meta[ORDER_AT + place]] = own[at]
            place += 1
    for along, source in enumerate((before, level, after)):
        for kind in range(3):
            for member in range(2):
                pool[4 + 6 * kind + 2 * along + member] = source[kind, member]


def join_kernel(own, inner, outer, level):
    for member in range(2):
        level[0, member] = own[member]
        if len(inner.shape) == 3:
            level[1, member] = inner[member]
        else:
            start = inner.shape[1] - (2 - member) * TILE
            level[1, member] = inner[:, start : start + TILE]
        level[2, member] = outer[member]


def apply_tile(meta, tile, at, pairs, geometry, pool, columns, totals):
    block = geometry[tile]
    own_columns(columns, block, 2)
    live = meta[COUNTS_AT + tile]

    def chunk_step(chunk, carry):
        rows = pl.ds(pl.multiple_of(chunk * APPLY_ROWS, APPLY_ROWS), APPLY_ROWS)

        def group_step(group, sums):
            for member in range(GROUP):
                entry = group * GROUP + member
                slot = meta[tile * 8 + entry]
                other = geometry[slot]
                v = pool[slot]
                d_x = other[0:1] - columns[0, rows]
                d_y = other[1:2] - columns[1, rows]
                d_z = pairs[2, at * 8 + entry, rows]
                three = pairs[1, at * 8 + entry, rows]
                along = pairs[0, at * 8 + entry, rows] * (d_x * v[0:1] + d_y * v[1:2] + d_z * v[2:3])
                sums = (
                    sums[0] + (along * d_x - three * v[0:1]),
                    sums[1] + (along * d_y - three * v[1:2]),
                    sums[2] + (along * d_z - three * v[2:3]),
                )
            return sums

        zero = jnp.zeros((APPLY_ROWS, TILE), F32)
        sums = lax.fori_loop(0, (live + GROUP - 1) // GROUP, group_step, (zero, zero, zero))
        for part in range(3):
            totals[part, rows] = sums[part]
        return carry

    lax.fori_loop(0, TILE // APPLY_ROWS, chunk_step, 0)


def sweep_tiles(place, meta, geometry, banks, found, pool, columns, totals, local=None):
    done = 0
    for pairs in banks:
        count = pairs.shape[1] // 8

        def tile_step(at, carry):
            tile = meta[ORDER_AT + place + done + at]
            apply_tile(meta, tile, at, pairs, geometry, pool, columns, totals)
            rows = updated(geometry[tile], totals)
            found[done + at] = rows
            if local is not None:
                local[tile] = rows
            return carry

        lax.fori_loop(0, count, tile_step, 0)
        done += count


def sweep_kernel(place, owns, meta, geometry, *refs):
    own_refs, (level, before, after) = (refs[:owns], refs[owns : owns + 3])
    banks, (found, pool, columns, totals) = (refs[owns + 3 : -4], refs[-4:])
    fill_search(pool, own_refs, level, before, after, meta)
    sweep_tiles(place, meta, geometry, banks, found, pool, columns, totals)


def direction_kernel(
    meta, geometry, own_a, own_b, level, before, after, pairs_a, pairs_b, pairs_c, order, sent, rest, bundle, pool, columns, totals, local
):
    atoms = order.shape[1]
    fill_search(pool, (own_a, own_b), level, before, after, meta)
    sweep_tiles(0, meta, geometry, (pairs_a,), sent, pool, columns, totals, local)
    sweep_tiles(2, meta, geometry, (pairs_b, pairs_c), rest, pool, columns, totals, local)
    for place in range(2):
        bundle[:, atoms + place * TILE : atoms + (place + 1) * TILE] = sent[place]
    in_tiles = jnp.concatenate([local[tile] for tile in range(4)], 1)
    bundle[:, :atoms] = selected(in_tiles, order_matrix(order[...], atoms), NT)


def final_field_kernel(
    meta, geometry, sent, rest, level, before, after, pairs_a, order, stored_b, stored_c, applied, sums, pool, columns, totals, local, pairs_b, pairs_c, sems
):
    copies = [
        pltpu.make_async_copy(source, target, sems.at[at])
        for at, (source, target) in enumerate(((stored_b, pairs_b), (stored_c, pairs_c)))
    ]
    for copy in copies:
        copy.start()
    atoms = order.shape[1]
    fill_search(pool, (sent, rest), level, before, after, meta)
    both = (jnp.zeros((1, TILE), F32), jnp.zeros((1, TILE), F32))
    for first, pairs in ((0, pairs_a), (2, pairs_b), (3, pairs_c)):
        if first:
            copies[first - 2].wait()

        def tile_step(at, both):
            curve, dots = both
            place = first + at
            tile = meta[ORDER_AT + place]
            apply_tile(meta, tile, at, pairs, geometry, pool, columns, totals)
            block = geometry[tile]
            ahead = rest[first - 2 + at] if first else sent[at]
            field = field_rows(totals)
            rows = []
            for part in range(3):
                d = ahead[part : part + 1]
                value = d / block[3:4] - field[part] - SELF_FIELD * d
                curve = curve + d * value
                dots = dots + d * block[4 + part : 5 + part]
                rows.append(value)
            local[tile] = jnp.concatenate(rows + [jnp.zeros((5, TILE), F32)], 0)
            return (curve, dots)

        both = lax.fori_loop(0, pairs.shape[1] // 8, tile_step, both)
    in_tiles = jnp.concatenate([local[tile] for tile in range(4)], 1)
    applied[...] = selected(in_tiles, order_matrix(order[...], atoms), NT)
    lane = lax.broadcasted_iota(jnp.int32, (8, TILE), 1)
    curve_sum = jnp.sum(both[0], axis=1, keepdims=True)
    dot_sum = jnp.sum(both[1], axis=1, keepdims=True)
    sums[...] = jnp.where(lane == 1, curve_sum, jnp.where(lane == 2, dot_sum, 0.0))


def spline(fraction):
    centre_arg = fraction - 0.5

    def middle(u):
        return (55.0 + u * (20.0 + u * (-120.0 + u * (80.0 - 16.0 * u)))) / 96.0

    def middle_slope(u):
        return (20.0 + u * (-240.0 + u * (240.0 - 64.0 * u))) / 96.0

    def outer(u):
        w = 5.0 - 2.0 * u
        return (w * w) * (w * w) / 384.0

    def outer_slope(u):
        w = 5.0 - 2.0 * u
        return -(w * w * w) / 48.0

    sq = centre_arg * centre_arg
    weights = (
        outer(fraction + 1.5),
        middle(fraction + 0.5),
        115.0 / 192.0 - 0.625 * sq + 0.25 * sq * sq,
        middle(1.5 - fraction),
        outer(2.5 - fraction),
    )
    slopes = (
        outer_slope(fraction + 1.5),
        middle_slope(fraction + 0.5),
        -1.25 * centre_arg + centre_arg * sq,
        -middle_slope(1.5 - fraction),
        -outer_slope(2.5 - fraction),
    )
    return (weights, slopes)


def table(cell_row, values, length, wrapped):
    atoms = cell_row.shape[1]
    ids = lax.broadcasted_iota(jnp.int32, (length, atoms), 0)
    if wrapped:
        ahead = ids - cell_row + 2
        ahead = jnp.where(ahead >= G, ahead - G, jnp.where(ahead < 0, ahead + G, ahead))
    else:
        ahead = ids - cell_row
    total = jnp.zeros((length, atoms), F32)
    for step in range(5):
        total = jnp.where(ahead == step, values[step], total)
    return total


def tables_kernel(
    mine, beside, stored_high, stored_low, tab_x, tab_y, w_high, w_low, slope_z, cas_high, cas_low, sems
):
    core = lax.axis_index("core")
    copies = [
        pltpu.make_async_copy(stored_high.at[core], cas_high, sems.at[0]),
        pltpu.make_async_copy(stored_low.at[core], cas_low, sems.at[1]),
    ]
    for copy in copies:
        copy.start()
    for copy in copies:
        copy.wait()
    cas = (cas_high[...], cas_low[...])
    for side, statics in enumerate((mine, beside)):
        atoms = tab_x.shape[3]
        cells = statics[0:3, :atoms].astype(jnp.int32)
        for dim, out in ((0, tab_x), (1, tab_y)):
            weights, slopes = spline(statics[3 + dim : 4 + dim, :atoms])
            out[side, 0] = table(cells[dim : dim + 1], weights, out.shape[2], False)
            out[side, 1] = table(cells[dim : dim + 1], slopes, out.shape[2], False)
        weights, slopes = spline(statics[5:6, :atoms])
        high, low = halves(product(cas, halves(table(cells[2:3], weights, G, True)), NN))
        w_high[side] = high
        w_low[side] = low
        slope_z[side] = product(cas, halves(table(cells[2:3], slopes, G, True)), NN)


def spread_part(side, d, tab_x, tab_y, w_high, w_low, slope_z):
    w_z = (w_high[side], w_low[side])
    s_z = halves(slope_z[side] * d[2:3])
    weight_x = tab_x[side, 0]
    slope_part = tab_x[side, 1] * d[0:1]
    weight_part = weight_x * d[1:2]
    sides = []
    for y in range(tab_y.shape[2]):
        w_y, s_y = (tab_y[side, 0, y : y + 1], tab_y[side, 1, y : y + 1])
        sides.append((slope_part * w_y + weight_part * s_y, weight_x * w_y))
    rows = halves(jnp.concatenate([pair[0] for pair in sides], 0))
    flat = halves(jnp.concatenate([pair[1] for pair in sides], 0))
    return product(w_z, rows, NT) + product(s_z, flat, NT)


def spread_own_kernel(ordered, tab_x, tab_y, w_high, w_low, slope_z, out):
    out[...] = spread_part(0, ordered[:, : tab_x.shape[3]], tab_x, tab_y, w_high, w_low, slope_z)


def put_lanes(out, flat):
    for row in range(8):
        out[:, row, :] = flat[:, row * TILE : (row + 1) * TILE]


def get_lanes(grid):
    return jnp.concatenate([grid[:, row, :] for row in range(8)], 1)


def spread_both_kernel(shift, ordered, mine, tab_x, tab_y, w_high, w_low, slope_z, out, flat, message, sems):
    theirs = spread_part(1, ordered[:, : tab_x.shape[3]], tab_x, tab_y, w_high, w_low, slope_z)
    ours = mine[...]
    width = ours.shape[1]
    even = lax.axis_index("core") == 0
    lower = jnp.where(even, ours, theirs)
    upper = jnp.where(even, theirs, ours)
    flat[:, :shift] = lower[:, :shift]
    flat[:, shift:width] = lower[:, shift:] + upper[:, : width - shift]
    flat[:, width : width + shift] = upper[:, width - shift :]
    flat[:, width + shift :] = jnp.zeros((flat.shape[0], flat.shape[1] - width - shift), F32)
    pieces = sems.shape[0]
    size = flat.shape[0] // pieces
    copies = []
    for piece in range(pieces):
        rows = slice(piece * size, (piece + 1) * size)
        for row in range(8):
            message[rows, row, :] = flat[rows, row * TILE : (row + 1) * TILE]
        copies.append(pltpu.make_async_copy(message.at[rows], out.at[rows], sems.at[piece]))
        copies[-1].start()
    for copy in copies:
        copy.wait()


def factor_of(waves, freq_z):
    ids_x = lax.broadcasted_iota(jnp.int32, (1, G), 1)
    by_x = waves[...]
    by_z = jnp.sum(jnp.where(ids_x == freq_z, by_x, 0.0), axis=1, keepdims=True)
    by_y = by_x.T
    anchor = jnp.where(
        (lax.broadcasted_iota(jnp.int32, (G, G), 0) + lax.broadcasted_iota(jnp.int32, (G, G), 1) + freq_z) == 0, 1.0, 0.0
    )
    squares = by_x[0:1] + by_y[:, 0:1] + (by_z[0:1] + anchor)
    return (1.0 - anchor) * (by_x[1:2] * by_z[1:2]) * by_y[:, 1:2] / (math.pi * float(G) ** 3 * squares)


def rolled(flat, rows, start, size, amount):
    low = start // TILE * TILE
    high = -(-(start + size) // TILE) * TILE
    return pltpu.roll(flat[rows, low:high], amount, 0)[:, start - low : start - low + size]


def plane_kernel(shapes, waves, sums, *refs):
    stored, out, flat, plane = (refs[:7], refs[7], refs[8], refs[9])
    held, sems = (refs[10:17], refs[17])
    copies = [
        pltpu.make_async_copy(source, target, sems.at[at])
        for at, (source, target) in enumerate(zip(stored, held))
    ]
    for copy in copies:
        copy.start()
    grid, x_high, x_low, yt_high, yt_low, y_high, y_low = held
    n_slab, n_pair, x_rows, y_rows = shapes
    x_own, y_own = (G // n_slab, y_rows - 4)
    width = x_rows * y_rows
    freq_z = lax.axis_index("slab") * (2 * n_pair) + 2 * lax.axis_index("pair") + lax.axis_index("core")
    factor = factor_of(waves, freq_z)
    copies[0].wait()
    flat[...] = get_lanes(grid)
    two = 2 * x_rows
    first_own, last_own = (slice(two, 2 * two), slice(y_own * x_rows, y_own * x_rows + two))
    slabs = [slice(s * n_pair, (s + 1) * n_pair) for s in range(n_slab)]
    for rows in slabs:
        from_next = rolled(flat, rows, 0, two, n_pair - 1)
        from_last = rolled(flat, rows, width - two, two, 1)
        flat[rows, last_own] = flat[rows, last_own] + from_next
        flat[rows, first_own] = flat[rows, first_own] + from_last
    padded = [
        jnp.concatenate(
            [flat[rows, (y + 2) * x_rows : (y + 3) * x_rows] for y in range(y_own)], 0
        )
        for rows in slabs
    ]
    for s, block in enumerate(padded):
        plane[:, s * x_own : (s + 1) * x_own] = block[:, 2 : x_own + 2]
    for s, block in enumerate(padded):
        for at, part in (
            ((s * x_own - 2) % G, block[:, :2]),
            ((s + 1) * x_own % G, block[:, x_own + 2 : x_own + 4]),
        ):
            plane[:, at : at + 2] = plane[:, at : at + 2] + part
    for copy in copies[1:]:
        copy.wait()
    cas_x = (x_high[...], x_low[...])
    along_x = product(halves(plane[...]), cas_x, NN, False)
    spectrum = product((yt_high[...], yt_low[...]), halves(along_x), NN, False)
    scaled = spectrum * factor
    energy = jnp.sum(jnp.sum(spectrum * scaled, axis=0, keepdims=True), axis=1, keepdims=True)
    back = halves(product((y_high[...], y_low[...]), halves(scaled), NN, False))
    plane[...] = product(back, cas_x, NN, False)
    for s, rows in enumerate(slabs):
        start, stop = (s * x_own - 2, (s + 1) * x_own + 2)
        pieces = [plane[:, max(start, 0) : min(stop, G)]]
        if start < 0:
            pieces = [plane[:, G + start :]] + pieces
        if stop > G:
            pieces = pieces + [plane[:, : stop - G]]
        block = pieces[0] if len(pieces) == 1 else jnp.concatenate(pieces, 1)
        for y in range(y_own):
            at = (y + 2) * x_rows
            flat[rows, at : at + x_own + 4] = block[y * n_pair : (y + 1) * n_pair]
        flat[rows, :two] = rolled(flat, rows, y_own * x_rows, two, 1)
        flat[rows, width - two : width] = rolled(flat, rows, two, two, n_pair - 1)
    spare = flat.shape[1] - width
    lane = lax.broadcasted_iota(jnp.int32, (1, spare), 1)
    known = jnp.concatenate([sums[0:1], jnp.zeros((1, spare - TILE), F32)], 1)
    tail = jnp.where(lane == 0, energy, known)
    flat[:, width:] = jnp.broadcast_to(tail, (flat.shape[0], spare))
    put_lanes(out, flat)


def probe_part(side, planes, tab_x, tab_y, w_high, w_low, slope_z):
    x_rows = tab_x.shape[2]
    by_weight = product(planes, (w_high[side], w_low[side]), TN)
    by_slope = product(planes, halves(slope_z[side]), TN)
    weight_x, slope_x = (tab_x[side, 0], tab_x[side, 1])
    fields = [0.0, 0.0, 0.0]
    for y in range(tab_y.shape[2]):
        rows = slice(y * x_rows, (y + 1) * x_rows)
        w_y, s_y = (tab_y[side, 0, y : y + 1], tab_y[side, 1, y : y + 1])
        weighted = by_weight[rows]
        fields[0] += w_y * jnp.sum(slope_x * weighted, axis=0, keepdims=True)
        fields[1] += s_y * jnp.sum(weight_x * weighted, axis=0, keepdims=True)
        fields[2] += w_y * jnp.sum(weight_x * by_slope[rows], axis=0, keepdims=True)
    return fields


def probe_kernel(side, shift, grid, tab_x, tab_y, w_high, w_low, slope_z, out):
    matrix = get_lanes(grid)
    width = tab_x.shape[2] * tab_y.shape[2]
    low_side = 0 if side == 0 else 1
    planes = jnp.where(
        lax.axis_index("core") == low_side, matrix[:, :width], matrix[:, shift : shift + width]
    )
    fields = probe_part(side, halves(planes), tab_x, tab_y, w_high, w_low, slope_z)
    atoms = out.shape[1]
    scalars = jnp.sum(matrix[:, width + shift :], axis=0, keepdims=True)[:, :TILE]
    padded = jnp.concatenate([scalars, jnp.zeros((1, atoms - TILE), F32)], 1)
    out[...] = jnp.concatenate(fields + [padded, jnp.zeros((4, atoms), F32)], 0)


def finish_kernel(mine, theirs, ordered, applied, dipoles, residual, next_dipoles, next_residual, direction):
    total = mine[...] + theirs[...]
    step = total[3:4, 2:3] / (total[3:4, 0:1] + total[3:4, 1:2])
    d = ordered[0:3, : dipoles.shape[1]]
    next_dipoles[...] = dipoles[...] + step * d
    next_residual[...] = residual[...] - step * (applied[0:3] + total[0:3])
    direction[...] = d


def cas_matrix(first, second):
    angles = 2.0 * np.pi / G * (np.outer(first, second) % G)
    return np.cos(angles) + np.sin(angles)


def split_constant(values):
    whole = values.astype(np.float32)
    high = whole.astype(ml_dtypes.bfloat16)
    low = (values - high.astype(np.float64)).astype(ml_dtypes.bfloat16)
    return (jnp.asarray(high), jnp.asarray(low))


def wave_factors():
    freq = np.arange(G)
    wrapped = np.where(freq > G // 2, freq - G, freq) / G
    angles = 2.0 * np.pi / G * freq
    modulus = 115.0 / 192.0 + 19.0 / 48.0 * np.cos(angles) + 1.0 / 192.0 * np.cos(2.0 * angles)
    rows = np.zeros((8, G), np.float32)
    rows[0] = wrapped * wrapped
    rows[1] = np.exp(-((np.pi / BETA) ** 2) * wrapped * wrapped) / (modulus * modulus)
    return jnp.asarray(rows)


def swap_pairs(n_slab, n_space, odd):
    pairs = []
    for s in range(n_slab):
        for q in range(n_space):
            partner = (q + 1 if (q % 2 == 1) == odd else q - 1) % n_space
            pairs.append((s * n_space + q, s * n_space + partner))
    return pairs


def beside(block, odd):
    n_slab, n_space = (lax.axis_size("slab"), lax.axis_size(SPACE))
    return lax.ppermute(block, BOTH, swap_pairs(n_slab, n_space, odd))


def along_slab(level):
    n_slab = lax.axis_size("slab")
    up = [(i, (i + 1) % n_slab) for i in range(n_slab)]
    down = [(j, i) for i, j in up]
    return (level, lax.ppermute(level, "slab", up), lax.ppermute(level, "slab", down))


def joined(block, inner, outer):
    return call(join_kernel, [((3, 2, 8, TILE), F32)], 10**6)(block, inner, outer)[0]


def around(block, inner=None, beneath=None):
    inner = beside(block, False) if inner is None else inner
    outer, _ = lax.optimization_barrier((beside(block, True), beneath))
    return along_slab(joined(block, inner, outer))


def local(
    dipoles, residual, cells, fraction, polarizability, tile_order, send_tiles, tile_lists, tile_counts
):
    n_slab, n_space = (lax.axis_size("slab"), lax.axis_size(SPACE))
    n_pair = n_space // 2
    atoms = residual.shape[1]
    extents = (G // n_slab, G // n_space)
    x_rows = -(-(extents[0] + 4) // 8) * 8
    y_rows = extents[1] + 4
    pair_rows = 2 * extents[1] + 4
    shift = extents[1] * x_rows
    half = G // 2
    tile_shape = ((4, 8, TILE), F32)
    two_shape = ((2, 8, TILE), F32)
    one_bank = ((3, 8, TILE, TILE), F32)
    pool_scratch = pltpu.VMEM((22, 8, TILE), F32)
    total_scratch = pltpu.VMEM((3, TILE, TILE), F32)
    own, sent, statics = pl.pallas_call(
        gather_kernel,
        out_shape=[
            jax.ShapeDtypeStruct(*tile_shape),
            jax.ShapeDtypeStruct(*two_shape),
            jax.ShapeDtypeStruct((8, atoms + 2 * TILE), F32),
        ],
        in_specs=[pl.BlockSpec(memory_space=pltpu.HBM)] * 6,
        out_specs=[pl.BlockSpec(memory_space=pltpu.VMEM)] * 3,
        scratch_shapes=[
            pltpu.VMEM((3, atoms), F32),
            pltpu.VMEM((3, atoms), jnp.int32),
            pltpu.VMEM((3, atoms), F32),
            pltpu.VMEM((atoms,), F32),
            pltpu.VMEM((1, atoms), jnp.int32),
            pltpu.SMEM((1, 2), jnp.int32),
            pltpu.SemaphoreType.DMA((6,)),
        ],
        compiler_params=pltpu.CompilerParams(vmem_limit_bytes=SMALL_VMEM),
    )(
        *[
            pltpu.with_memory_space_constraint(array, pltpu.HBM)
            for array in (residual, cells, fraction, polarizability, tile_order, send_tiles)
        ],
    )
    smem, anywhere = (pl.BlockSpec(memory_space=pltpu.SMEM), pl.BlockSpec(memory_space=pltpu.HBM))
    meta = pl.pallas_call(
        meta_kernel,
        out_shape=jax.ShapeDtypeStruct((48,), jnp.int32),
        in_specs=[anywhere, anywhere, anywhere, pl.BlockSpec(memory_space=pltpu.VMEM)],
        out_specs=smem,
        scratch_shapes=[
            pltpu.SMEM(tile_lists.shape, jnp.int32),
            pltpu.SMEM(tile_counts.shape, jnp.int32),
            pltpu.SMEM(send_tiles.shape, jnp.int32),
            pltpu.SemaphoreType.DMA((3,)),
        ],
        compiler_params=pltpu.CompilerParams(vmem_limit_bytes=SMALL_VMEM),
        cost_estimate=pl.CostEstimate(flops=10**8, bytes_accessed=1 << 20, transcendentals=0),
    )(
        *[
            pltpu.with_memory_space_constraint(array, pltpu.HBM)
            for array in (tile_lists, tile_counts, send_tiles)
        ],
        sent,
    )
    statics_beside = beside(statics, False)
    freq = np.arange(G)
    rows_y = np.arange(n_pair)[None] * 2 * extents[1] + np.arange(2 * extents[1])[:, None]
    cas_y = cas_matrix(rows_y.reshape(-1), freq)
    freq_by_core = np.stack([freq[0::2], freq[1::2]])
    cas_z = cas_matrix(freq_by_core.reshape(-1), freq).reshape(2, half, G)
    tables = call(
        tables_kernel,
        [
            ((2, 2, x_rows, atoms), F32),
            ((2, 2, y_rows, atoms), F32),
            ((2, half, atoms), BF16),
            ((2, half, atoms), BF16),
            ((2, half, atoms), F32),
        ],
        10**8,
        vmem=LARGE_VMEM,
        scratch=(pltpu.VMEM((half, G), BF16),) * 2 + (pltpu.SemaphoreType.DMA((2,)),),
        hbm=2,
    )(statics, statics_beside, *split_constant(cas_z))
    first = around(sent, statics_beside, beneath=(meta, tables[1]))

    pair_scratch = (pltpu.VMEM((4, TILE, TILE), F32), total_scratch)
    geometry, pairs_a, search_a = call(
        functools.partial(pair_kernel, extents),
        [((22, 8, TILE), F32), ((3, 16, TILE, TILE), F32), two_shape],
        10**9,
        smem=1,
        scratch=pair_scratch,
    )(meta, own, *first)

    def pairs_of(place):
        return call(
            functools.partial(pair_tiles, place),
            [one_bank, ((1, 8, TILE), F32)],
            10**9,
            smem=1,
            scratch=pair_scratch,
        )(meta, geometry)

    pairs_b, search_b = pairs_of(2)
    pairs_c, search_c = pairs_of(3)
    sweep_scratch = (pool_scratch, pltpu.VMEM((3, TILE, TILE), F32), total_scratch)
    second = around(search_a, beneath=search_b)

    def sweep(place, owns, received, banks):
        return call(
            functools.partial(sweep_kernel, place, len(owns)),
            [two_shape],
            10**8,
            smem=1,
            scratch=sweep_scratch,
        )(meta, geometry, *owns, *received, *banks)[0]

    searches = (search_a, search_b, search_c)
    next_a = sweep(0, searches, second, (pairs_a,))
    next_b = sweep(2, searches, second, (pairs_b, pairs_c))
    third = around(next_a, beneath=next_b)
    local_scratch = pltpu.VMEM((4, 8, TILE), F32)
    sent, rest, ordered = call(
        direction_kernel,
        [two_shape, two_shape, ((8, atoms + 2 * TILE), F32)],
        10**8,
        smem=1,
        scratch=sweep_scratch + (local_scratch,),
    )(meta, geometry, next_a, next_b, *third, pairs_a, pairs_b, pairs_c, tile_order)
    ordered_beside = beside(ordered, False)
    message = ((half, 8, TILE), F32)
    flat_scratch = pltpu.VMEM((half, 8 * TILE), F32)
    spread_own = call(spread_own_kernel, [((half, x_rows * y_rows), F32)], 10**9, vmem=LARGE_VMEM)(ordered, *tables)[0]
    spread = call(
        functools.partial(spread_both_kernel, shift),
        [message],
        10**9,
        scratch=(flat_scratch, pltpu.VMEM(*message), pltpu.SemaphoreType.DMA((4,))),
        vmem=LARGE_VMEM,
        hbm_outs=True,
    )(ordered_beside, spread_own, *tables)[0]
    late, _ = lax.optimization_barrier((sent, spread))
    grid = lax.all_to_all(spread, CHIPS, 0, 0, tiled=True)
    last = along_slab(joined(sent, ordered_beside, beside(late, True)))
    applied, sums = call(
        final_field_kernel,
        [((8, atoms), F32), ((8, TILE), F32)],
        10**9,
        smem=1,
        scratch=sweep_scratch
        + (local_scratch, pltpu.VMEM(*one_bank), pltpu.VMEM(*one_bank), pltpu.SemaphoreType.DMA((2,))),
        vmem=LARGE_VMEM,
        hbm=2,
    )(meta, geometry, sent, rest, *last, pairs_a, tile_order, pairs_b, pairs_c)
    planes = call(
        functools.partial(plane_kernel, (n_slab, n_pair, x_rows, pair_rows)),
        [message],
        10**9,
        scratch=(flat_scratch, pltpu.VMEM((G, G), F32), pltpu.VMEM(*message))
        + (pltpu.VMEM((G, G), BF16),) * 6
        + (pltpu.SemaphoreType.DMA((7,)),),
        vmem=LARGE_VMEM,
        hbm=7,
    )(
        wave_factors(),
        sums,
        grid,
        *split_constant(cas_matrix(freq, freq)),
        *split_constant(cas_y.T),
        *split_constant(cas_y),
    )[0]
    returned = lax.all_to_all(planes, CHIPS, 0, 0, tiled=True)

    def probe(side):
        return call(
            functools.partial(probe_kernel, side, shift), [((8, atoms), F32)], 10**9, vmem=LARGE_VMEM
        )(returned, *tables)[0]

    theirs = beside(probe(1), False)
    three = ((3, atoms), F32)
    return tuple(
        call(finish_kernel, [three, three, three], 10**6)(
            probe(0), theirs, ordered, applied, dipoles, residual
        )
    )


def solution(mesh):
    slab, space = (mesh.shape["slab"], mesh.shape["space"])
    mesh = Mesh(mesh.devices.reshape(slab, space // 2, 2), BOTH)
    in_specs = (
        P(None, BOTH),
        P(None, BOTH),
        P(None, BOTH),
        P(None, BOTH),
        P(BOTH),
        P(BOTH, None),
        P(BOTH, None),
        P(BOTH, None, None),
        P(BOTH, None),
    )
    out_specs = (P(None, BOTH), P(None, BOTH), P(None, BOTH))
    return jax.shard_map(local, mesh=mesh, in_specs=in_specs, out_specs=out_specs, check_vma=False)
```

```python
import functools
import math

import jax
import jax.numpy as jnp
import ml_dtypes
import numpy as np
from jax import lax
from jax.experimental import pallas as pl
from jax.experimental.pallas import tpu as pltpu
from jax.sharding import Mesh
from jax.sharding import PartitionSpec as P

G = 256
TILE = 128
SPACE = ("pair", "core")
BOTH = ("slab", "pair", "core")
CHIPS = ("slab", "pair")
BETA = 0.4
THOLE = 0.39
ROOT_PI = math.sqrt(math.pi)
SELF_FIELD = 4.0 * BETA**3 / (3.0 * ROOT_PI)
F32 = jnp.float32
BF16 = jnp.bfloat16
SCALED_ERFC_T = 0.45
SCALED_ERFC = (
    0.25388532876968384,
    0.25388309359550476,
    0.22827406227588654,
    0.17522020637989044,
    0.1201537474989891,
    -0.023065825924277306,
    0.14381752908229828,
    -0.3022053837776184,
    0.19167575240135193,
    -0.04163854941725731,
)
NT = (((1,), (1,)), ((), ()))
NN = (((1,), (0,)), ((), ()))
TN = (((0,), (0,)), ((), ()))
SMALL_VMEM = 6 * 1024 * 1024
LARGE_VMEM = 16 * 1024 * 1024


def halves(values):
    high = values.astype(BF16)
    return (high, (values - high.astype(F32)).astype(BF16))


def product(left, right, dims, stacked=True):
    def one(a, b):
        return lax.dot_general(a, b, dims, preferred_element_type=F32)

    (left_dim,), (right_dim,) = dims[0]
    if not stacked:
        return one(left[0], right[0]) + (one(left[0], right[1]) + one(left[1], right[0]))
    return one(
        jnp.concatenate([left[0], left[0], left[1]], left_dim),
        jnp.concatenate([right[0], right[1], right[0]], right_dim),
    )


def thirds(values):
    high = values.astype(BF16).astype(F32)
    rest = values - high
    middle = rest.astype(BF16).astype(F32)
    return jnp.concatenate([high, middle, rest - middle], 0).astype(BF16)


def selected(values, one_hot, dims):
    rows = values.shape[0]
    picked = lax.dot_general(thirds(values), one_hot, dims, preferred_element_type=F32)
    return picked[:rows] + (picked[rows : 2 * rows] + picked[2 * rows :])


def order_matrix(order_row, count):
    ids = lax.broadcasted_iota(jnp.int32, (count, count), 0)
    return jnp.where(ids == order_row, 1.0, 0.0).astype(BF16)


COUNTS_AT = 32
ORDER_AT = 36
PARITY_AT = 40


def meta_kernel(stored_lists, stored_counts, stored_send, after, meta, lists, counts, send, sems):
    copies = [
        pltpu.make_async_copy(source, target, sems.at[at])
        for at, (source, target) in enumerate(
            ((stored_lists, lists), (stored_counts, counts), (stored_send, send))
        )
    ]
    for copy in copies:
        copy.start()
    for copy in copies:
        copy.wait()
    parity = lax.axis_index("core")
    for tile in range(4):

        def remap(place, carry):
            entry = lists[0, tile, place]
            remote = entry - 4
            pair = lax.shift_right_arithmetic(remote, 1)
            pair = pair + jnp.where(pair >= 4, 1, 0)
            along = jnp.where(pair >= 3, 1, 0) + jnp.where(pair >= 6, 1, 0)
            across = pair - 3 * along
            base = jnp.where(across == 1, 4, jnp.where(across == 2 - 2 * parity, 10, 16))
            slot = base + along * 2 + (remote & 1)
            meta[tile * 8 + place] = jnp.where(entry < 4, entry, slot)
            return carry

        lax.fori_loop(0, 8, remap, 0)
        meta[COUNTS_AT + tile] = counts[0, tile]
    first, second = (send[0, 0], send[0, 1])
    third = jnp.where(
        (first != 0) & (second != 0), 0, jnp.where((first != 1) & (second != 1), 1, 2)
    )
    meta[ORDER_AT] = first
    meta[ORDER_AT + 1] = second
    meta[ORDER_AT + 2] = third
    meta[ORDER_AT + 3] = 6 - first - second - third
    meta[PARITY_AT] = parity


def call(kernel, outs, flops, smem=0, scratch=(), vmem=SMALL_VMEM, hbm=0, hbm_outs=False):
    def run(*args):
        kept = len(args) - hbm
        args = args[:kept] + tuple(
            pltpu.with_memory_space_constraint(array, pltpu.HBM) for array in args[kept:]
        )
        in_specs = [pl.BlockSpec(memory_space=pltpu.SMEM)] * smem
        in_specs += [pl.BlockSpec(memory_space=pltpu.VMEM)] * (kept - smem)
        in_specs += [pl.BlockSpec(memory_space=pltpu.HBM)] * hbm
        return pl.pallas_call(
            kernel,
            out_shape=[
                (pltpu.HBM if hbm_outs else jax.ShapeDtypeStruct)(shape, dtype) for shape, dtype in outs
            ],
            in_specs=in_specs,
            out_specs=[pl.BlockSpec(memory_space=pltpu.HBM if hbm_outs else pltpu.VMEM)] * len(outs),
            scratch_shapes=list(scratch),
            compiler_params=pltpu.CompilerParams(vmem_limit_bytes=vmem),
            cost_estimate=pl.CostEstimate(
                flops=flops, bytes_accessed=1 << 20, transcendentals=0
            ),
        )(*args)

    return run


def gather_kernel(*refs):
    sources, (own, sent, bundle), held, sems = (refs[:6], refs[6:9], refs[9:15], refs[15])
    copies = [
        pltpu.make_async_copy(source, target, sems.at[at])
        for at, (source, target) in enumerate(zip(sources, held))
    ]
    for copy in copies:
        copy.start()
    for copy in copies:
        copy.wait()
    residual, cells, fraction, alphas, order, send = held
    atoms = residual.shape[1]
    in_cells = cells[...].astype(F32)
    bundle[0:3, :atoms] = in_cells
    bundle[3:6, :atoms] = fraction[...]
    bundle[6:8, :atoms] = jnp.zeros((2, atoms), F32)
    position = in_cells + fraction[...]
    rows = jnp.concatenate(
        [position, alphas[...].reshape(1, atoms), residual[...], jnp.zeros((1, atoms), F32)], 0
    )
    picked = selected(rows, order_matrix(order[...], atoms), NN)
    for tile in range(atoms // TILE):
        own[tile] = picked[:, tile * TILE : (tile + 1) * TILE]
    for place in range(2):
        block = own[send[0, place]]
        sent[place] = block
        bundle[:, atoms + place * TILE : atoms + (place + 1) * TILE] = block


def search_rows(block):
    return block[3:4] * block[4:7]


def fill_pool(pool, extents, own, level, before, after, meta):
    inner_step = jnp.where(meta[PARITY_AT] == 0, 1.0, -1.0)
    rows = lax.broadcasted_iota(jnp.int32, (8, TILE), 0)
    for tile in range(4):
        pool[tile] = own[tile]
    for along, source in enumerate((before, level, after)):
        for kind, step in enumerate((0.0, inner_step, -inner_step)):
            shift = jnp.where(
                rows == 0,
                float((along - 1) * extents[0]),
                jnp.where(rows == 1, step * float(extents[1]), 0.0),
            )
            for member in range(2):
                pool[4 + 6 * kind + 2 * along + member] = source[kind, member] + shift


def own_columns(columns, block, count):
    turned = block.T
    for row in range(count):
        columns[row] = jnp.broadcast_to(turned[:, row : row + 1], (TILE, TILE))


def wrap_depth(depth):
    half = 0.5 * G
    return jnp.where(depth > half, depth - G, jnp.where(depth < -half, depth + G, depth))


PAIR_ROWS = 32
GROUP = 4


def pair_kernel(extents, meta, own, level, before, after, pool, pairs, found, columns, totals):
    fill_pool(pool, extents, own, level, before, after, meta)
    pair_tiles(0, meta, pool, pairs, found, columns, totals)


def pair_tiles(first_place, meta, pool, pairs, found, columns, totals):
    def tile_step(at, carry):
        tile = meta[ORDER_AT + first_place + at]
        block = pool[tile]
        own_columns(columns, jnp.concatenate([block[:3], lax.rsqrt(block[3:4]), block[4:]], 0), 4)
        live = meta[COUNTS_AT + tile]

        def chunk_step(chunk, carry):
            start = pl.multiple_of(chunk * PAIR_ROWS, PAIR_ROWS)
            rows = pl.ds(start, PAIR_ROWS)
            shape = (PAIR_ROWS, TILE)
            ahead = lax.broadcasted_iota(jnp.int32, shape, 0) - lax.broadcasted_iota(
                jnp.int32, shape, 1
            )
            diagonal = jnp.where(ahead == -start, 1.0, 0.0)

            def group_step(group, sums):
                for member in range(GROUP):
                    entry = group * GROUP + member
                    slot = meta[tile * 8 + entry]
                    other = pool[slot]
                    itself = diagonal * jnp.where(slot == tile, 1.0, 0.0)
                    d_x = other[0:1] - columns[0, rows]
                    d_y = other[1:2] - columns[1, rows]
                    d_z = wrap_depth(other[2:3] - columns[2, rows])
                    square = d_x * d_x + d_y * d_y + d_z * d_z + itself
                    inverse = lax.rsqrt(square)
                    distance = square * inverse
                    inverse_sq = inverse * inverse
                    gauss = jnp.exp(-(BETA**2) * square)
                    stretch = 1.0 + (SCALED_ERFC_T * BETA) * distance
                    t = lax.rsqrt(stretch * stretch)
                    series = SCALED_ERFC[-1] * t + SCALED_ERFC[-2]
                    for term in SCALED_ERFC[-3::-1]:
                        series = series * t + term
                    bare_one = gauss * (series * t * inverse + 2.0 * BETA / ROOT_PI) * inverse_sq
                    bare_two = (3.0 * bare_one + (4.0 * BETA**3 / ROOT_PI) * gauss) * inverse_sq
                    damping = (square * distance) * columns[3, rows] * (THOLE * lax.rsqrt(other[3:4]))
                    decay = jnp.exp(-damping) * inverse * inverse_sq
                    keep = jnp.where(entry < live, 1.0, 0.0) * (1.0 - itself)
                    three = keep * (bare_one - decay)
                    five = keep * (bare_two - (3.0 + 3.0 * damping) * decay * inverse_sq)
                    pairs[0, at * 8 + entry, rows] = five
                    pairs[1, at * 8 + entry, rows] = three
                    pairs[2, at * 8 + entry, rows] = d_z
                    v = search_rows(other)
                    along = five * (d_x * v[0:1] + d_y * v[1:2] + d_z * v[2:3])
                    sums = (
                        sums[0] + (along * d_x - three * v[0:1]),
                        sums[1] + (along * d_y - three * v[1:2]),
                        sums[2] + (along * d_z - three * v[2:3]),
                    )
                return sums

            zero = jnp.zeros(shape, F32)
            sums = lax.fori_loop(0, (live + GROUP - 1) // GROUP, group_step, (zero, zero, zero))
            for part in range(3):
                totals[part, rows] = sums[part]
            return carry

        lax.fori_loop(0, TILE // PAIR_ROWS, chunk_step, 0)
        found[at] = updated(block, totals)
        return carry

    lax.fori_loop(0, found.shape[0], tile_step, 0)


def field_rows(totals):
    return [jnp.sum(totals[part].T, axis=0, keepdims=True) for part in range(3)]


def updated(block, totals):
    alpha = block[3:4]
    field = field_rows(totals)
    rows = [alpha * (block[4 + part : 5 + part] + field[part]) for part in range(3)]
    return jnp.concatenate(rows + [jnp.zeros((5, TILE), F32)], 0)


APPLY_ROWS = 64


def fill_search(pool, owns, level, before, after, meta):
    place = 0
    for own in owns:
        for at in range(own.shape[0]):
            pool[meta[ORDER_AT + place]] = own[at]
            place += 1
    for along, source in enumerate((before, level, after)):
        for kind in range(3):
            for member in range(2):
                pool[4 + 6 * kind + 2 * along + member] = source[kind, member]


def join_kernel(own, inner, outer, level):
    for member in range(2):
        level[0, member] = own[member]
        if len(inner.shape) == 3:
            level[1, member] = inner[member]
        else:
            start = inner.shape[1] - (2 - member) * TILE
            level[1, member] = inner[:, start : start + TILE]
        level[2, member] = outer[member]


def apply_tile(meta, tile, at, pairs, geometry, pool, columns, totals):
    block = geometry[tile]
    own_columns(columns, block, 2)
    live = meta[COUNTS_AT + tile]

    def chunk_step(chunk, carry):
        rows = pl.ds(pl.multiple_of(chunk * APPLY_ROWS, APPLY_ROWS), APPLY_ROWS)

        def group_step(group, sums):
            for member in range(GROUP):
                entry = group * GROUP + member
                slot = meta[tile * 8 + entry]
                other = geometry[slot]
                v = pool[slot]
                d_x = other[0:1] - columns[0, rows]
                d_y = other[1:2] - columns[1, rows]
                d_z = pairs[2, at * 8 + entry, rows]
                three = pairs[1, at * 8 + entry, rows]
                along = pairs[0, at * 8 + entry, rows] * (d_x * v[0:1] + d_y * v[1:2] + d_z * v[2:3])
                sums = (
                    sums[0] + (along * d_x - three * v[0:1]),
                    sums[1] + (along * d_y - three * v[1:2]),
                    sums[2] + (along * d_z - three * v[2:3]),
                )
            return sums

        zero = jnp.zeros((APPLY_ROWS, TILE), F32)
        sums = lax.fori_loop(0, (live + GROUP - 1) // GROUP, group_step, (zero, zero, zero))
        for part in range(3):
            totals[part, rows] = sums[part]
        return carry

    lax.fori_loop(0, TILE // APPLY_ROWS, chunk_step, 0)


def sweep_tiles(place, meta, geometry, banks, found, pool, columns, totals, local=None):
    done = 0
    for pairs in banks:
        count = pairs.shape[1] // 8

        def tile_step(at, carry):
            tile = meta[ORDER_AT + place + done + at]
            apply_tile(meta, tile, at, pairs, geometry, pool, columns, totals)
            rows = updated(geometry[tile], totals)
            found[done + at] = rows
            if local is not None:
                local[tile] = rows
            return carry

        lax.fori_loop(0, count, tile_step, 0)
        done += count


def sweep_kernel(place, owns, meta, geometry, *refs):
    own_refs, (level, before, after) = (refs[:owns], refs[owns : owns + 3])
    banks, (found, pool, columns, totals) = (refs[owns + 3 : -4], refs[-4:])
    fill_search(pool, own_refs, level, before, after, meta)
    sweep_tiles(place, meta, geometry, banks, found, pool, columns, totals)


def direction_kernel(
    meta, geometry, own_a, own_b, level, before, after, pairs_a, pairs_b, pairs_c, order, sent, rest, bundle, pool, columns, totals, local
):
    atoms = order.shape[1]
    fill_search(pool, (own_a, own_b), level, before, after, meta)
    sweep_tiles(0, meta, geometry, (pairs_a,), sent, pool, columns, totals, local)
    sweep_tiles(2, meta, geometry, (pairs_b, pairs_c), rest, pool, columns, totals, local)
    for place in range(2):
        bundle[:, atoms + place * TILE : atoms + (place + 1) * TILE] = sent[place]
    in_tiles = jnp.concatenate([local[tile] for tile in range(4)], 1)
    bundle[:, :atoms] = selected(in_tiles, order_matrix(order[...], atoms), NT)


def final_field_kernel(
    meta, geometry, sent, rest, level, before, after, pairs_a, order, stored_b, stored_c, applied, sums, pool, columns, totals, local, pairs_b, pairs_c, sems
):
    copies = [
        pltpu.make_async_copy(source, target, sems.at[at])
        for at, (source, target) in enumerate(((stored_b, pairs_b), (stored_c, pairs_c)))
    ]
    for copy in copies:
        copy.start()
    atoms = order.shape[1]
    fill_search(pool, (sent, rest), level, before, after, meta)
    both = (jnp.zeros((1, TILE), F32), jnp.zeros((1, TILE), F32))
    for first, pairs in ((0, pairs_a), (2, pairs_b), (3, pairs_c)):
        if first:
            copies[first - 2].wait()

        def tile_step(at, both):
            curve, dots = both
            place = first + at
            tile = meta[ORDER_AT + place]
            apply_tile(meta, tile, at, pairs, geometry, pool, columns, totals)
            block = geometry[tile]
            ahead = rest[first - 2 + at] if first else sent[at]
            field = field_rows(totals)
            rows = []
            for part in range(3):
                d = ahead[part : part + 1]
                value = d / block[3:4] - field[part] - SELF_FIELD * d
                curve = curve + d * value
                dots = dots + d * block[4 + part : 5 + part]
                rows.append(value)
            local[tile] = jnp.concatenate(rows + [jnp.zeros((5, TILE), F32)], 0)
            return (curve, dots)

        both = lax.fori_loop(0, pairs.shape[1] // 8, tile_step, both)
    in_tiles = jnp.concatenate([local[tile] for tile in range(4)], 1)
    applied[...] = selected(in_tiles, order_matrix(order[...], atoms), NT)
    lane = lax.broadcasted_iota(jnp.int32, (8, TILE), 1)
    curve_sum = jnp.sum(both[0], axis=1, keepdims=True)
    dot_sum = jnp.sum(both[1], axis=1, keepdims=True)
    sums[...] = jnp.where(lane == 1, curve_sum, jnp.where(lane == 2, dot_sum, 0.0))


def spline(fraction):
    centre_arg = fraction - 0.5

    def middle(u):
        return (55.0 + u * (20.0 + u * (-120.0 + u * (80.0 - 16.0 * u)))) / 96.0

    def middle_slope(u):
        return (20.0 + u * (-240.0 + u * (240.0 - 64.0 * u))) / 96.0

    def outer(u):
        w = 5.0 - 2.0 * u
        return (w * w) * (w * w) / 384.0

    def outer_slope(u):
        w = 5.0 - 2.0 * u
        return -(w * w * w) / 48.0

    sq = centre_arg * centre_arg
    weights = (
        outer(fraction + 1.5),
        middle(fraction + 0.5),
        115.0 / 192.0 - 0.625 * sq + 0.25 * sq * sq,
        middle(1.5 - fraction),
        outer(2.5 - fraction),
    )
    slopes = (
        outer_slope(fraction + 1.5),
        middle_slope(fraction + 0.5),
        -1.25 * centre_arg + centre_arg * sq,
        -middle_slope(1.5 - fraction),
        -outer_slope(2.5 - fraction),
    )
    return (weights, slopes)


def table(cell_row, values, length, wrapped):
    atoms = cell_row.shape[1]
    ids = lax.broadcasted_iota(jnp.int32, (length, atoms), 0)
    if wrapped:
        ahead = ids - cell_row + 2
        ahead = jnp.where(ahead >= G, ahead - G, jnp.where(ahead < 0, ahead + G, ahead))
    else:
        ahead = ids - cell_row
    total = jnp.zeros((length, atoms), F32)
    for step in range(5):
        total = jnp.where(ahead == step, values[step], total)
    return total


def tables_kernel(
    mine, beside, stored_high, stored_low, tab_x, tab_y, w_high, w_low, slope_z, cas_high, cas_low, sems
):
    core = lax.axis_index("core")
    copies = [
        pltpu.make_async_copy(stored_high.at[core], cas_high, sems.at[0]),
        pltpu.make_async_copy(stored_low.at[core], cas_low, sems.at[1]),
    ]
    for copy in copies:
        copy.start()
    for copy in copies:
        copy.wait()
    cas = (cas_high[...], cas_low[...])
    for side, statics in enumerate((mine, beside)):
        atoms = tab_x.shape[3]
        cells = statics[0:3, :atoms].astype(jnp.int32)
        for dim, out in ((0, tab_x), (1, tab_y)):
            weights, slopes = spline(statics[3 + dim : 4 + dim, :atoms])
            out[side, 0] = table(cells[dim : dim + 1], weights, out.shape[2], False)
            out[side, 1] = table(cells[dim : dim + 1], slopes, out.shape[2], False)
        weights, slopes = spline(statics[5:6, :atoms])
        high, low = halves(product(cas, halves(table(cells[2:3], weights, G, True)), NN))
        w_high[side] = high
        w_low[side] = low
        slope_z[side] = product(cas, halves(table(cells[2:3], slopes, G, True)), NN)


def spread_part(side, d, tab_x, tab_y, w_high, w_low, slope_z):
    w_z = (w_high[side], w_low[side])
    s_z = halves(slope_z[side] * d[2:3])
    weight_x = tab_x[side, 0]
    slope_part = tab_x[side, 1] * d[0:1]
    weight_part = weight_x * d[1:2]
    sides = []
    for y in range(tab_y.shape[2]):
        w_y, s_y = (tab_y[side, 0, y : y + 1], tab_y[side, 1, y : y + 1])
        sides.append((slope_part * w_y + weight_part * s_y, weight_x * w_y))
    rows = halves(jnp.concatenate([pair[0] for pair in sides], 0))
    flat = halves(jnp.concatenate([pair[1] for pair in sides], 0))
    return product(w_z, rows, NT) + product(s_z, flat, NT)


def spread_own_kernel(ordered, tab_x, tab_y, w_high, w_low, slope_z, out):
    out[...] = spread_part(0, ordered[:, : tab_x.shape[3]], tab_x, tab_y, w_high, w_low, slope_z)


def put_lanes(out, flat):
    for row in range(8):
        out[:, row, :] = flat[:, row * TILE : (row + 1) * TILE]


def get_lanes(grid):
    return jnp.concatenate([grid[:, row, :] for row in range(8)], 1)


def spread_both_kernel(shift, ordered, mine, tab_x, tab_y, w_high, w_low, slope_z, out, flat, message, sems):
    theirs = spread_part(1, ordered[:, : tab_x.shape[3]], tab_x, tab_y, w_high, w_low, slope_z)
    ours = mine[...]
    width = ours.shape[1]
    even = lax.axis_index("core") == 0
    lower = jnp.where(even, ours, theirs)
    upper = jnp.where(even, theirs, ours)
    flat[:, :shift] = lower[:, :shift]
    flat[:, shift:width] = lower[:, shift:] + upper[:, : width - shift]
    flat[:, width : width + shift] = upper[:, width - shift :]
    flat[:, width + shift :] = jnp.zeros((flat.shape[0], flat.shape[1] - width - shift), F32)
    pieces = sems.shape[0]
    size = flat.shape[0] // pieces
    copies = []
    for piece in range(pieces):
        rows = slice(piece * size, (piece + 1) * size)
        for row in range(8):
            message[rows, row, :] = flat[rows, row * TILE : (row + 1) * TILE]
        copies.append(pltpu.make_async_copy(message.at[rows], out.at[rows], sems.at[piece]))
        copies[-1].start()
    for copy in copies:
        copy.wait()


def factor_of(waves, freq_z):
    ids_x = lax.broadcasted_iota(jnp.int32, (1, G), 1)
    by_x = waves[...]
    by_z = jnp.sum(jnp.where(ids_x == freq_z, by_x, 0.0), axis=1, keepdims=True)
    by_y = by_x.T
    anchor = jnp.where(
        (lax.broadcasted_iota(jnp.int32, (G, G), 0) + lax.broadcasted_iota(jnp.int32, (G, G), 1) + freq_z) == 0, 1.0, 0.0
    )
    squares = by_x[0:1] + by_y[:, 0:1] + (by_z[0:1] + anchor)
    return (1.0 - anchor) * (by_x[1:2] * by_z[1:2]) * by_y[:, 1:2] / (math.pi * float(G) ** 3 * squares)


def rolled(flat, rows, start, size, amount):
    low = start // TILE * TILE
    high = -(-(start + size) // TILE) * TILE
    return pltpu.roll(flat[rows, low:high], amount, 0)[:, start - low : start - low + size]


def plane_kernel(shapes, waves, sums, *refs):
    stored, out, flat, plane = (refs[:7], refs[7], refs[8], refs[9])
    held, sems = (refs[10:17], refs[17])
    copies = [
        pltpu.make_async_copy(source, target, sems.at[at])
        for at, (source, target) in enumerate(zip(stored, held))
    ]
    for copy in copies:
        copy.start()
    grid, x_high, x_low, yt_high, yt_low, y_high, y_low = held
    n_slab, n_pair, x_rows, y_rows = shapes
    x_own, y_own = (G // n_slab, y_rows - 4)
    width = x_rows * y_rows
    freq_z = lax.axis_index("slab") * (2 * n_pair) + 2 * lax.axis_index("pair") + lax.axis_index("core")
    factor = factor_of(waves, freq_z)
    copies[0].wait()
    flat[...] = get_lanes(grid)
    two = 2 * x_rows
    first_own, last_own = (slice(two, 2 * two), slice(y_own * x_rows, y_own * x_rows + two))
    slabs = [slice(s * n_pair, (s + 1) * n_pair) for s in range(n_slab)]
    for rows in slabs:
        from_next = rolled(flat, rows, 0, two, n_pair - 1)
        from_last = rolled(flat, rows, width - two, two, 1)
        flat[rows, last_own] = flat[rows, last_own] + from_next
        flat[rows, first_own] = flat[rows, first_own] + from_last
    padded = [
        jnp.concatenate(
            [flat[rows, (y + 2) * x_rows : (y + 3) * x_rows] for y in range(y_own)], 0
        )
        for rows in slabs
    ]
    for s, block in enumerate(padded):
        plane[:, s * x_own : (s + 1) * x_own] = block[:, 2 : x_own + 2]
    for s, block in enumerate(padded):
        for at, part in (
            ((s * x_own - 2) % G, block[:, :2]),
            ((s + 1) * x_own % G, block[:, x_own + 2 : x_own + 4]),
        ):
            plane[:, at : at + 2] = plane[:, at : at + 2] + part
    for copy in copies[1:]:
        copy.wait()
    cas_x = (x_high[...], x_low[...])
    along_x = product(halves(plane[...]), cas_x, NN, False)
    spectrum = product((yt_high[...], yt_low[...]), halves(along_x), NN, False)
    scaled = spectrum * factor
    energy = jnp.sum(jnp.sum(spectrum * scaled, axis=0, keepdims=True), axis=1, keepdims=True)
    back = halves(product((y_high[...], y_low[...]), halves(scaled), NN, False))
    plane[...] = product(back, cas_x, NN, False)
    for s, rows in enumerate(slabs):
        start, stop = (s * x_own - 2, (s + 1) * x_own + 2)
        pieces = [plane[:, max(start, 0) : min(stop, G)]]
        if start < 0:
            pieces = [plane[:, G + start :]] + pieces
        if stop > G:
            pieces = pieces + [plane[:, : stop - G]]
        block = pieces[0] if len(pieces) == 1 else jnp.concatenate(pieces, 1)
        for y in range(y_own):
            at = (y + 2) * x_rows
            flat[rows, at : at + x_own + 4] = block[y * n_pair : (y + 1) * n_pair]
        flat[rows, :two] = rolled(flat, rows, y_own * x_rows, two, 1)
        flat[rows, width - two : width] = rolled(flat, rows, two, two, n_pair - 1)
    spare = flat.shape[1] - width
    lane = lax.broadcasted_iota(jnp.int32, (1, spare), 1)
    known = jnp.concatenate([sums[0:1], jnp.zeros((1, spare - TILE), F32)], 1)
    tail = jnp.where(lane == 0, energy, known)
    flat[:, width:] = jnp.broadcast_to(tail, (flat.shape[0], spare))
    put_lanes(out, flat)


def probe_part(side, planes, tab_x, tab_y, w_high, w_low, slope_z):
    x_rows = tab_x.shape[2]
    by_weight = product(planes, (w_high[side], w_low[side]), TN)
    by_slope = product(planes, halves(slope_z[side]), TN)
    weight_x, slope_x = (tab_x[side, 0], tab_x[side, 1])
    fields = [0.0, 0.0, 0.0]
    for y in range(tab_y.shape[2]):
        rows = slice(y * x_rows, (y + 1) * x_rows)
        w_y, s_y = (tab_y[side, 0, y : y + 1], tab_y[side, 1, y : y + 1])
        weighted = by_weight[rows]
        fields[0] += w_y * jnp.sum(slope_x * weighted, axis=0, keepdims=True)
        fields[1] += s_y * jnp.sum(weight_x * weighted, axis=0, keepdims=True)
        fields[2] += w_y * jnp.sum(weight_x * by_slope[rows], axis=0, keepdims=True)
    return fields


def probe_kernel(side, shift, grid, tab_x, tab_y, w_high, w_low, slope_z, out):
    matrix = get_lanes(grid)
    width = tab_x.shape[2] * tab_y.shape[2]
    low_side = 0 if side == 0 else 1
    planes = jnp.where(
        lax.axis_index("core") == low_side, matrix[:, :width], matrix[:, shift : shift + width]
    )
    fields = probe_part(side, halves(planes), tab_x, tab_y, w_high, w_low, slope_z)
    atoms = out.shape[1]
    scalars = jnp.sum(matrix[:, width + shift :], axis=0, keepdims=True)[:, :TILE]
    padded = jnp.concatenate([scalars, jnp.zeros((1, atoms - TILE), F32)], 1)
    out[...] = jnp.concatenate(fields + [padded, jnp.zeros((4, atoms), F32)], 0)


def finish_kernel(mine, theirs, ordered, applied, dipoles, residual, next_dipoles, next_residual, direction):
    total = mine[...] + theirs[...]
    step = total[3:4, 2:3] / (total[3:4, 0:1] + total[3:4, 1:2])
    d = ordered[0:3, : dipoles.shape[1]]
    next_dipoles[...] = dipoles[...] + step * d
    next_residual[...] = residual[...] - step * (applied[0:3] + total[0:3])
    direction[...] = d


def cas_matrix(first, second):
    angles = 2.0 * np.pi / G * (np.outer(first, second) % G)
    return np.cos(angles) + np.sin(angles)


def split_constant(values):
    whole = values.astype(np.float32)
    high = whole.astype(ml_dtypes.bfloat16)
    low = (values - high.astype(np.float64)).astype(ml_dtypes.bfloat16)
    return (jnp.asarray(high), jnp.asarray(low))


def wave_factors():
    freq = np.arange(G)
    wrapped = np.where(freq > G // 2, freq - G, freq) / G
    angles = 2.0 * np.pi / G * freq
    modulus = 115.0 / 192.0 + 19.0 / 48.0 * np.cos(angles) + 1.0 / 192.0 * np.cos(2.0 * angles)
    rows = np.zeros((8, G), np.float32)
    rows[0] = wrapped * wrapped
    rows[1] = np.exp(-((np.pi / BETA) ** 2) * wrapped * wrapped) / (modulus * modulus)
    return jnp.asarray(rows)


def swap_pairs(n_slab, n_space, odd):
    pairs = []
    for s in range(n_slab):
        for q in range(n_space):
            partner = (q + 1 if (q % 2 == 1) == odd else q - 1) % n_space
            pairs.append((s * n_space + q, s * n_space + partner))
    return pairs


def beside(block, odd):
    n_slab, n_space = (lax.axis_size("slab"), lax.axis_size(SPACE))
    return lax.ppermute(block, BOTH, swap_pairs(n_slab, n_space, odd))


def along_slab(level):
    n_slab = lax.axis_size("slab")
    up = [(i, (i + 1) % n_slab) for i in range(n_slab)]
    down = [(j, i) for i, j in up]
    return (level, lax.ppermute(level, "slab", up), lax.ppermute(level, "slab", down))


def joined(block, inner, outer):
    return call(join_kernel, [((3, 2, 8, TILE), F32)], 10**6)(block, inner, outer)[0]


def around(block, inner=None, beneath=None):
    inner = beside(block, False) if inner is None else inner
    outer, _ = lax.optimization_barrier((beside(block, True), beneath))
    return along_slab(joined(block, inner, outer))


def local(
    dipoles, residual, cells, fraction, polarizability, tile_order, send_tiles, tile_lists, tile_counts
):
    n_slab, n_space = (lax.axis_size("slab"), lax.axis_size(SPACE))
    n_pair = n_space // 2
    atoms = residual.shape[1]
    extents = (G // n_slab, G // n_space)
    x_rows = -(-(extents[0] + 4) // 8) * 8
    y_rows = extents[1] + 4
    pair_rows = 2 * extents[1] + 4
    shift = extents[1] * x_rows
    half = G // 2
    tile_shape = ((4, 8, TILE), F32)
    two_shape = ((2, 8, TILE), F32)
    one_bank = ((3, 8, TILE, TILE), F32)
    pool_scratch = pltpu.VMEM((22, 8, TILE), F32)
    total_scratch = pltpu.VMEM((3, TILE, TILE), F32)
    own, sent, statics = pl.pallas_call(
        gather_kernel,
        out_shape=[
            jax.ShapeDtypeStruct(*tile_shape),
            jax.ShapeDtypeStruct(*two_shape),
            jax.ShapeDtypeStruct((8, atoms + 2 * TILE), F32),
        ],
        in_specs=[pl.BlockSpec(memory_space=pltpu.HBM)] * 6,
        out_specs=[pl.BlockSpec(memory_space=pltpu.VMEM)] * 3,
        scratch_shapes=[
            pltpu.VMEM((3, atoms), F32),
            pltpu.VMEM((3, atoms), jnp.int32),
            pltpu.VMEM((3, atoms), F32),
            pltpu.VMEM((atoms,), F32),
            pltpu.VMEM((1, atoms), jnp.int32),
            pltpu.SMEM((1, 2), jnp.int32),
            pltpu.SemaphoreType.DMA((6,)),
        ],
        compiler_params=pltpu.CompilerParams(vmem_limit_bytes=SMALL_VMEM),
    )(
        *[
            pltpu.with_memory_space_constraint(array, pltpu.HBM)
            for array in (residual, cells, fraction, polarizability, tile_order, send_tiles)
        ],
    )
    smem, anywhere = (pl.BlockSpec(memory_space=pltpu.SMEM), pl.BlockSpec(memory_space=pltpu.HBM))
    meta = pl.pallas_call(
        meta_kernel,
        out_shape=jax.ShapeDtypeStruct((48,), jnp.int32),
        in_specs=[anywhere, anywhere, anywhere, pl.BlockSpec(memory_space=pltpu.VMEM)],
        out_specs=smem,
        scratch_shapes=[
            pltpu.SMEM(tile_lists.shape, jnp.int32),
            pltpu.SMEM(tile_counts.shape, jnp.int32),
            pltpu.SMEM(send_tiles.shape, jnp.int32),
            pltpu.SemaphoreType.DMA((3,)),
        ],
        compiler_params=pltpu.CompilerParams(vmem_limit_bytes=SMALL_VMEM),
        cost_estimate=pl.CostEstimate(flops=10**8, bytes_accessed=1 << 20, transcendentals=0),
    )(
        *[
            pltpu.with_memory_space_constraint(array, pltpu.HBM)
            for array in (tile_lists, tile_counts, send_tiles)
        ],
        sent,
    )
    statics_beside = beside(statics, False)
    freq = np.arange(G)
    rows_y = np.arange(n_pair)[None] * 2 * extents[1] + np.arange(2 * extents[1])[:, None]
    cas_y = cas_matrix(rows_y.reshape(-1), freq)
    freq_by_core = np.stack([freq[0::2], freq[1::2]])
    cas_z = cas_matrix(freq_by_core.reshape(-1), freq).reshape(2, half, G)
    tables = call(
        tables_kernel,
        [
            ((2, 2, x_rows, atoms), F32),
            ((2, 2, y_rows, atoms), F32),
            ((2, half, atoms), BF16),
            ((2, half, atoms), BF16),
            ((2, half, atoms), F32),
        ],
        10**8,
        vmem=LARGE_VMEM,
        scratch=(pltpu.VMEM((half, G), BF16),) * 2 + (pltpu.SemaphoreType.DMA((2,)),),
        hbm=2,
    )(statics, statics_beside, *split_constant(cas_z))
    first = around(sent, statics_beside, beneath=(meta, tables[1]))

    pair_scratch = (pltpu.VMEM((4, TILE, TILE), F32), total_scratch)
    geometry, pairs_a, search_a = call(
        functools.partial(pair_kernel, extents),
        [((22, 8, TILE), F32), ((3, 16, TILE, TILE), F32), two_shape],
        10**9,
        smem=1,
        scratch=pair_scratch,
    )(meta, own, *first)

    def pairs_of(place):
        return call(
            functools.partial(pair_tiles, place),
            [one_bank, ((1, 8, TILE), F32)],
            10**9,
            smem=1,
            scratch=pair_scratch,
        )(meta, geometry)

    pairs_b, search_b = pairs_of(2)
    pairs_c, search_c = pairs_of(3)
    sweep_scratch = (pool_scratch, pltpu.VMEM((3, TILE, TILE), F32), total_scratch)
    second = around(search_a, beneath=search_b)

    def sweep(place, owns, received, banks):
        return call(
            functools.partial(sweep_kernel, place, len(owns)),
            [two_shape],
            10**8,
            smem=1,
            scratch=sweep_scratch,
        )(meta, geometry, *owns, *received, *banks)[0]

    searches = (search_a, search_b, search_c)
    next_a = sweep(0, searches, second, (pairs_a,))
    next_b = sweep(2, searches, second, (pairs_b, pairs_c))
    third = around(next_a, beneath=next_b)
    local_scratch = pltpu.VMEM((4, 8, TILE), F32)
    sent, rest, ordered = call(
        direction_kernel,
        [two_shape, two_shape, ((8, atoms + 2 * TILE), F32)],
        10**8,
        smem=1,
        scratch=sweep_scratch + (local_scratch,),
    )(meta, geometry, next_a, next_b, *third, pairs_a, pairs_b, pairs_c, tile_order)
    ordered_beside, outer = (beside(ordered, False), beside(sent, True))
    message = ((half, 8, TILE), F32)
    flat_scratch = pltpu.VMEM((half, 8 * TILE), F32)
    spread_own = call(spread_own_kernel, [((half, x_rows * y_rows), F32)], 10**9, vmem=LARGE_VMEM)(ordered, *tables)[0]
    spread = call(
        functools.partial(spread_both_kernel, shift),
        [message],
        10**9,
        scratch=(flat_scratch, pltpu.VMEM(*message), pltpu.SemaphoreType.DMA((4,))),
        vmem=LARGE_VMEM,
        hbm_outs=True,
    )(ordered_beside, spread_own, *tables)[0]
    spread, outer = lax.optimization_barrier((spread, outer))
    grid = lax.all_to_all(spread, CHIPS, 0, 0, tiled=True)
    last = along_slab(joined(sent, ordered_beside, outer))
    applied, sums = call(
        final_field_kernel,
        [((8, atoms), F32), ((8, TILE), F32)],
        10**9,
        smem=1,
        scratch=sweep_scratch
        + (local_scratch, pltpu.VMEM(*one_bank), pltpu.VMEM(*one_bank), pltpu.SemaphoreType.DMA((2,))),
        vmem=LARGE_VMEM,
        hbm=2,
    )(meta, geometry, sent, rest, *last, pairs_a, tile_order, pairs_b, pairs_c)
    planes = call(
        functools.partial(plane_kernel, (n_slab, n_pair, x_rows, pair_rows)),
        [message],
        10**9,
        scratch=(flat_scratch, pltpu.VMEM((G, G), F32), pltpu.VMEM(*message))
        + (pltpu.VMEM((G, G), BF16),) * 6
        + (pltpu.SemaphoreType.DMA((7,)),),
        vmem=LARGE_VMEM,
        hbm=7,
    )(
        wave_factors(),
        sums,
        grid,
        *split_constant(cas_matrix(freq, freq)),
        *split_constant(cas_y.T),
        *split_constant(cas_y),
    )[0]
    returned = lax.all_to_all(planes, CHIPS, 0, 0, tiled=True)

    def probe(side):
        return call(
            functools.partial(probe_kernel, side, shift), [((8, atoms), F32)], 10**9, vmem=LARGE_VMEM
        )(returned, *tables)[0]

    theirs = beside(probe(1), False)
    three = ((3, atoms), F32)
    return tuple(
        call(finish_kernel, [three, three, three], 10**6)(
            probe(0), theirs, ordered, applied, dipoles, residual
        )
    )


def solution(mesh):
    slab, space = (mesh.shape["slab"], mesh.shape["space"])
    mesh = Mesh(mesh.devices.reshape(slab, space // 2, 2), BOTH)
    in_specs = (
        P(None, BOTH),
        P(None, BOTH),
        P(None, BOTH),
        P(None, BOTH),
        P(BOTH),
        P(BOTH, None),
        P(BOTH, None),
        P(BOTH, None, None),
        P(BOTH, None),
    )
    out_specs = (P(None, BOTH), P(None, BOTH), P(None, BOTH))
    return jax.shard_map(local, mesh=mesh, in_specs=in_specs, out_specs=out_specs, check_vma=False)
```

```python
import functools
import math

import jax
import jax.numpy as jnp
import ml_dtypes
import numpy as np
from jax import lax
from jax.experimental import pallas as pl
from jax.experimental.pallas import tpu as pltpu
from jax.sharding import Mesh
from jax.sharding import PartitionSpec as P

G = 256
TILE = 128
SPACE = ("pair", "core")
BOTH = ("slab", "pair", "core")
CHIPS = ("slab", "pair")
BETA = 0.4
THOLE = 0.39
ROOT_PI = math.sqrt(math.pi)
SELF_FIELD = 4.0 * BETA**3 / (3.0 * ROOT_PI)
F32 = jnp.float32
BF16 = jnp.bfloat16
SCALED_ERFC_T = 0.45
SCALED_ERFC = (
    0.25388532876968384,
    0.25388309359550476,
    0.22827406227588654,
    0.17522020637989044,
    0.1201537474989891,
    -0.023065825924277306,
    0.14381752908229828,
    -0.3022053837776184,
    0.19167575240135193,
    -0.04163854941725731,
)
NT = (((1,), (1,)), ((), ()))
NN = (((1,), (0,)), ((), ()))
TN = (((0,), (0,)), ((), ()))
SMALL_VMEM = 6 * 1024 * 1024
LARGE_VMEM = 16 * 1024 * 1024


def halves(values):
    high = values.astype(BF16)
    return (high, (values - high.astype(F32)).astype(BF16))


def product(left, right, dims, stacked=True):
    def one(a, b):
        return lax.dot_general(a, b, dims, preferred_element_type=F32)

    (left_dim,), (right_dim,) = dims[0]
    if not stacked:
        return one(left[0], right[0]) + (one(left[0], right[1]) + one(left[1], right[0]))
    return one(
        jnp.concatenate([left[0], left[0], left[1]], left_dim),
        jnp.concatenate([right[0], right[1], right[0]], right_dim),
    )


def thirds(values):
    high = values.astype(BF16).astype(F32)
    rest = values - high
    middle = rest.astype(BF16).astype(F32)
    return jnp.concatenate([high, middle, rest - middle], 0).astype(BF16)


def selected(values, one_hot, dims):
    rows = values.shape[0]
    picked = lax.dot_general(thirds(values), one_hot, dims, preferred_element_type=F32)
    return picked[:rows] + (picked[rows : 2 * rows] + picked[2 * rows :])


def order_matrix(order_row, count):
    ids = lax.broadcasted_iota(jnp.int32, (count, count), 0)
    return jnp.where(ids == order_row, 1.0, 0.0).astype(BF16)


COUNTS_AT = 32
ORDER_AT = 36
PARITY_AT = 40


def meta_kernel(lists, counts, send, after, meta):
    parity = lax.axis_index("core")
    for tile in range(4):

        def remap(place, carry):
            entry = lists[0, tile, place]
            remote = entry - 4
            pair = lax.shift_right_arithmetic(remote, 1)
            pair = pair + jnp.where(pair >= 4, 1, 0)
            along = jnp.where(pair >= 3, 1, 0) + jnp.where(pair >= 6, 1, 0)
            across = pair - 3 * along
            base = jnp.where(across == 1, 4, jnp.where(across == 2 - 2 * parity, 10, 16))
            slot = base + along * 2 + (remote & 1)
            meta[tile * 8 + place] = jnp.where(entry < 4, entry, slot)
            return carry

        lax.fori_loop(0, 8, remap, 0)
        meta[COUNTS_AT + tile] = counts[0, tile]
    first, second = (send[0, 0], send[0, 1])
    third = jnp.where(
        (first != 0) & (second != 0), 0, jnp.where((first != 1) & (second != 1), 1, 2)
    )
    meta[ORDER_AT] = first
    meta[ORDER_AT + 1] = second
    meta[ORDER_AT + 2] = third
    meta[ORDER_AT + 3] = 6 - first - second - third
    meta[PARITY_AT] = parity


def call(kernel, outs, flops, smem=0, scratch=(), vmem=SMALL_VMEM, hbm=0, hbm_outs=False):
    def run(*args):
        kept = len(args) - hbm
        args = args[:kept] + tuple(
            pltpu.with_memory_space_constraint(array, pltpu.HBM) for array in args[kept:]
        )
        in_specs = [pl.BlockSpec(memory_space=pltpu.SMEM)] * smem
        in_specs += [pl.BlockSpec(memory_space=pltpu.VMEM)] * (kept - smem)
        in_specs += [pl.BlockSpec(memory_space=pltpu.HBM)] * hbm
        return pl.pallas_call(
            kernel,
            out_shape=[
                (pltpu.HBM if hbm_outs else jax.ShapeDtypeStruct)(shape, dtype) for shape, dtype in outs
            ],
            in_specs=in_specs,
            out_specs=[pl.BlockSpec(memory_space=pltpu.HBM if hbm_outs else pltpu.VMEM)] * len(outs),
            scratch_shapes=list(scratch),
            compiler_params=pltpu.CompilerParams(vmem_limit_bytes=vmem),
            cost_estimate=pl.CostEstimate(
                flops=flops, bytes_accessed=1 << 20, transcendentals=0
            ),
        )(*args)

    return run


def gather_kernel(*refs):
    sources, (own, sent, bundle), held, sems = (refs[:6], refs[6:9], refs[9:15], refs[15])
    copies = [
        pltpu.make_async_copy(source, target, sems.at[at])
        for at, (source, target) in enumerate(zip(sources, held))
    ]
    for copy in copies:
        copy.start()
    for copy in copies:
        copy.wait()
    residual, cells, fraction, alphas, order, send = held
    atoms = residual.shape[1]
    in_cells = cells[...].astype(F32)
    bundle[0:3, :atoms] = in_cells
    bundle[3:6, :atoms] = fraction[...]
    bundle[6:8, :atoms] = jnp.zeros((2, atoms), F32)
    position = in_cells + fraction[...]
    rows = jnp.concatenate(
        [position, alphas[...].reshape(1, atoms), residual[...], jnp.zeros((1, atoms), F32)], 0
    )
    picked = selected(rows, order_matrix(order[...], atoms), NN)
    for tile in range(atoms // TILE):
        own[tile] = picked[:, tile * TILE : (tile + 1) * TILE]
    for place in range(2):
        block = own[send[0, place]]
        sent[place] = block
        bundle[:, atoms + place * TILE : atoms + (place + 1) * TILE] = block


def search_rows(block):
    return block[3:4] * block[4:7]


def fill_pool(pool, extents, own, level, before, after, meta):
    inner_step = jnp.where(meta[PARITY_AT] == 0, 1.0, -1.0)
    rows = lax.broadcasted_iota(jnp.int32, (8, TILE), 0)
    for tile in range(4):
        pool[tile] = own[tile]
    for along, source in enumerate((before, level, after)):
        for kind, step in enumerate((0.0, inner_step, -inner_step)):
            shift = jnp.where(
                rows == 0,
                float((along - 1) * extents[0]),
                jnp.where(rows == 1, step * float(extents[1]), 0.0),
            )
            for member in range(2):
                pool[4 + 6 * kind + 2 * along + member] = source[kind, member] + shift


def own_columns(columns, block, count):
    turned = block.T
    for row in range(count):
        columns[row] = jnp.broadcast_to(turned[:, row : row + 1], (TILE, TILE))


def wrap_depth(depth):
    half = 0.5 * G
    return jnp.where(depth > half, depth - G, jnp.where(depth < -half, depth + G, depth))


PAIR_ROWS = 64
GROUP = 4


def pair_kernel(first_place, count, extents, meta, own, level, before, after, pool, pairs, found, columns, totals):
    fill_pool(pool, extents, own, level, before, after, meta)

    def tile_step(at, carry):
        tile = meta[ORDER_AT + first_place + at]
        block = own[tile]
        own_columns(columns, jnp.concatenate([block[:3], lax.rsqrt(block[3:4]), block[4:]], 0), 4)
        live = meta[COUNTS_AT + tile]

        def chunk_step(chunk, carry):
            start = pl.multiple_of(chunk * PAIR_ROWS, PAIR_ROWS)
            rows = pl.ds(start, PAIR_ROWS)
            shape = (PAIR_ROWS, TILE)
            ahead = lax.broadcasted_iota(jnp.int32, shape, 0) - lax.broadcasted_iota(
                jnp.int32, shape, 1
            )
            diagonal = jnp.where(ahead == -start, 1.0, 0.0)

            def group_step(group, sums):
                for member in range(GROUP):
                    entry = group * GROUP + member
                    slot = meta[tile * 8 + entry]
                    other = pool[slot]
                    itself = diagonal * jnp.where(slot == tile, 1.0, 0.0)
                    d_x = other[0:1] - columns[0, rows]
                    d_y = other[1:2] - columns[1, rows]
                    d_z = wrap_depth(other[2:3] - columns[2, rows])
                    square = d_x * d_x + d_y * d_y + d_z * d_z + itself
                    inverse = lax.rsqrt(square)
                    distance = square * inverse
                    inverse_sq = inverse * inverse
                    gauss = jnp.exp(-(BETA**2) * square)
                    stretch = 1.0 + (SCALED_ERFC_T * BETA) * distance
                    t = lax.rsqrt(stretch * stretch)
                    series = SCALED_ERFC[-1] * t + SCALED_ERFC[-2]
                    for term in SCALED_ERFC[-3::-1]:
                        series = series * t + term
                    bare_one = gauss * (series * t * inverse + 2.0 * BETA / ROOT_PI) * inverse_sq
                    bare_two = (3.0 * bare_one + (4.0 * BETA**3 / ROOT_PI) * gauss) * inverse_sq
                    damping = (square * distance) * columns[3, rows] * (THOLE * lax.rsqrt(other[3:4]))
                    decay = jnp.exp(-damping) * inverse * inverse_sq
                    keep = jnp.where(entry < live, 1.0, 0.0) * (1.0 - itself)
                    three = keep * (bare_one - decay)
                    five = keep * (bare_two - (3.0 + 3.0 * damping) * decay * inverse_sq)
                    pairs[0, at * 8 + entry, rows] = five
                    pairs[1, at * 8 + entry, rows] = three
                    pairs[2, at * 8 + entry, rows] = d_z
                    v = search_rows(other)
                    along = five * (d_x * v[0:1] + d_y * v[1:2] + d_z * v[2:3])
                    sums = (
                        sums[0] + (along * d_x - three * v[0:1]),
                        sums[1] + (along * d_y - three * v[1:2]),
                        sums[2] + (along * d_z - three * v[2:3]),
                    )
                return sums

            zero = jnp.zeros(shape, F32)
            sums = lax.fori_loop(0, (live + GROUP - 1) // GROUP, group_step, (zero, zero, zero))
            for part in range(3):
                totals[part, rows] = sums[part]
            return carry

        lax.fori_loop(0, TILE // PAIR_ROWS, chunk_step, 0)
        found[at] = updated(block, totals)
        return carry

    lax.fori_loop(0, count, tile_step, 0)


def field_rows(totals):
    return [jnp.sum(totals[part].T, axis=0, keepdims=True) for part in range(3)]


def updated(block, totals):
    alpha = block[3:4]
    field = field_rows(totals)
    rows = [alpha * (block[4 + part : 5 + part] + field[part]) for part in range(3)]
    return jnp.concatenate(rows + [jnp.zeros((5, TILE), F32)], 0)


APPLY_ROWS = 64


def fill_search(pool, owns, level, before, after, meta):
    place = 0
    for own in owns:
        for at in range(own.shape[0]):
            pool[meta[ORDER_AT + place]] = own[at]
            place += 1
    for along, source in enumerate((before, level, after)):
        for kind in range(3):
            for member in range(2):
                pool[4 + 6 * kind + 2 * along + member] = source[kind, member]


def join_kernel(own, inner, outer, level):
    for member in range(2):
        level[0, member] = own[member]
        if len(inner.shape) == 3:
            level[1, member] = inner[member]
        else:
            start = inner.shape[1] - (2 - member) * TILE
            level[1, member] = inner[:, start : start + TILE]
        level[2, member] = outer[member]


def apply_tile(meta, tile, at, pairs, geometry, pool, columns, totals):
    block = geometry[tile]
    own_columns(columns, block, 2)
    live = meta[COUNTS_AT + tile]

    def chunk_step(chunk, carry):
        rows = pl.ds(pl.multiple_of(chunk * APPLY_ROWS, APPLY_ROWS), APPLY_ROWS)

        def group_step(group, sums):
            for member in range(GROUP):
                entry = group * GROUP + member
                slot = meta[tile * 8 + entry]
                other = geometry[slot]
                v = pool[slot]
                d_x = other[0:1] - columns[0, rows]
                d_y = other[1:2] - columns[1, rows]
                d_z = pairs[2, at * 8 + entry, rows]
                three = pairs[1, at * 8 + entry, rows]
                along = pairs[0, at * 8 + entry, rows] * (d_x * v[0:1] + d_y * v[1:2] + d_z * v[2:3])
                sums = (
                    sums[0] + (along * d_x - three * v[0:1]),
                    sums[1] + (along * d_y - three * v[1:2]),
                    sums[2] + (along * d_z - three * v[2:3]),
                )
            return sums

        zero = jnp.zeros((APPLY_ROWS, TILE), F32)
        sums = lax.fori_loop(0, (live + GROUP - 1) // GROUP, group_step, (zero, zero, zero))
        for part in range(3):
            totals[part, rows] = sums[part]
        return carry

    lax.fori_loop(0, TILE // APPLY_ROWS, chunk_step, 0)


def sweep_tiles(place, meta, geometry, banks, found, pool, columns, totals, local=None):
    done = 0
    for pairs in banks:
        count = pairs.shape[1] // 8

        def tile_step(at, carry):
            tile = meta[ORDER_AT + place + done + at]
            apply_tile(meta, tile, at, pairs, geometry, pool, columns, totals)
            rows = updated(geometry[tile], totals)
            found[done + at] = rows
            if local is not None:
                local[tile] = rows
            return carry

        lax.fori_loop(0, count, tile_step, 0)
        done += count


def sweep_kernel(place, owns, meta, geometry, *refs):
    own_refs, (level, before, after) = (refs[:owns], refs[owns : owns + 3])
    banks, (found, pool, columns, totals) = (refs[owns + 3 : -4], refs[-4:])
    fill_search(pool, own_refs, level, before, after, meta)
    sweep_tiles(place, meta, geometry, banks, found, pool, columns, totals)


def direction_kernel(
    meta, geometry, own_a, own_b, level, before, after, sent, pairs_b, pairs_c, order, found, bundle, pool, columns, totals, local
):
    atoms = order.shape[1]
    fill_search(pool, (own_a, own_b), level, before, after, meta)
    sweep_tiles(2, meta, geometry, (pairs_b, pairs_c), found, pool, columns, totals, local)
    for place in range(2):
        block = sent[place]
        local[meta[ORDER_AT + place]] = block
        bundle[:, atoms + place * TILE : atoms + (place + 1) * TILE] = block
    in_tiles = jnp.concatenate([local[tile] for tile in range(4)], 1)
    bundle[:, :atoms] = selected(in_tiles, order_matrix(order[...], atoms), NT)


def final_field_kernel(
    meta, geometry, sent, rest, level, before, after, pairs_a, order, stored_b, stored_c, applied, sums, pool, columns, totals, local, pairs_b, pairs_c, sems
):
    copies = [
        pltpu.make_async_copy(source, target, sems.at[at])
        for at, (source, target) in enumerate(((stored_b, pairs_b), (stored_c, pairs_c)))
    ]
    for copy in copies:
        copy.start()
    atoms = order.shape[1]
    fill_search(pool, (sent, rest), level, before, after, meta)
    both = (jnp.zeros((1, TILE), F32), jnp.zeros((1, TILE), F32))
    for first, pairs in ((0, pairs_a), (2, pairs_b), (3, pairs_c)):
        if first:
            copies[first - 2].wait()

        def tile_step(at, both):
            curve, dots = both
            place = first + at
            tile = meta[ORDER_AT + place]
            apply_tile(meta, tile, at, pairs, geometry, pool, columns, totals)
            block = geometry[tile]
            ahead = rest[first - 2 + at] if first else sent[at]
            field = field_rows(totals)
            rows = []
            for part in range(3):
                d = ahead[part : part + 1]
                value = d / block[3:4] - field[part] - SELF_FIELD * d
                curve = curve + d * value
                dots = dots + d * block[4 + part : 5 + part]
                rows.append(value)
            local[tile] = jnp.concatenate(rows + [jnp.zeros((5, TILE), F32)], 0)
            return (curve, dots)

        both = lax.fori_loop(0, pairs.shape[1] // 8, tile_step, both)
    in_tiles = jnp.concatenate([local[tile] for tile in range(4)], 1)
    applied[...] = selected(in_tiles, order_matrix(order[...], atoms), NT)
    lane = lax.broadcasted_iota(jnp.int32, (8, TILE), 1)
    curve_sum = jnp.sum(both[0], axis=1, keepdims=True)
    dot_sum = jnp.sum(both[1], axis=1, keepdims=True)
    sums[...] = jnp.where(lane == 1, curve_sum, jnp.where(lane == 2, dot_sum, 0.0))


def spline(fraction):
    centre_arg = fraction - 0.5

    def middle(u):
        return (55.0 + u * (20.0 + u * (-120.0 + u * (80.0 - 16.0 * u)))) / 96.0

    def middle_slope(u):
        return (20.0 + u * (-240.0 + u * (240.0 - 64.0 * u))) / 96.0

    def outer(u):
        w = 5.0 - 2.0 * u
        return (w * w) * (w * w) / 384.0

    def outer_slope(u):
        w = 5.0 - 2.0 * u
        return -(w * w * w) / 48.0

    sq = centre_arg * centre_arg
    weights = (
        outer(fraction + 1.5),
        middle(fraction + 0.5),
        115.0 / 192.0 - 0.625 * sq + 0.25 * sq * sq,
        middle(1.5 - fraction),
        outer(2.5 - fraction),
    )
    slopes = (
        outer_slope(fraction + 1.5),
        middle_slope(fraction + 0.5),
        -1.25 * centre_arg + centre_arg * sq,
        -middle_slope(1.5 - fraction),
        -outer_slope(2.5 - fraction),
    )
    return (weights, slopes)


def table(cell_row, values, length, wrapped):
    atoms = cell_row.shape[1]
    ids = lax.broadcasted_iota(jnp.int32, (length, atoms), 0)
    if wrapped:
        ahead = ids - cell_row + 2
        ahead = jnp.where(ahead >= G, ahead - G, jnp.where(ahead < 0, ahead + G, ahead))
    else:
        ahead = ids - cell_row
    total = jnp.zeros((length, atoms), F32)
    for step in range(5):
        total = jnp.where(ahead == step, values[step], total)
    return total


def tables_kernel(
    mine, beside, stored_high, stored_low, tab_x, tab_y, w_high, w_low, slope_z, cas_high, cas_low, sems
):
    core = lax.axis_index("core")
    copies = [
        pltpu.make_async_copy(stored_high.at[core], cas_high, sems.at[0]),
        pltpu.make_async_copy(stored_low.at[core], cas_low, sems.at[1]),
    ]
    for copy in copies:
        copy.start()
    for copy in copies:
        copy.wait()
    cas = (cas_high[...], cas_low[...])
    for side, statics in enumerate((mine, beside)):
        atoms = tab_x.shape[3]
        cells = statics[0:3, :atoms].astype(jnp.int32)
        for dim, out in ((0, tab_x), (1, tab_y)):
            weights, slopes = spline(statics[3 + dim : 4 + dim, :atoms])
            out[side, 0] = table(cells[dim : dim + 1], weights, out.shape[2], False)
            out[side, 1] = table(cells[dim : dim + 1], slopes, out.shape[2], False)
        weights, slopes = spline(statics[5:6, :atoms])
        high, low = halves(product(cas, halves(table(cells[2:3], weights, G, True)), NN))
        w_high[side] = high
        w_low[side] = low
        slope_z[side] = product(cas, halves(table(cells[2:3], slopes, G, True)), NN)


def spread_part(side, d, tab_x, tab_y, w_high, w_low, slope_z):
    w_z = (w_high[side], w_low[side])
    s_z = halves(slope_z[side] * d[2:3])
    weight_x = tab_x[side, 0]
    slope_part = tab_x[side, 1] * d[0:1]
    weight_part = weight_x * d[1:2]
    sides = []
    for y in range(tab_y.shape[2]):
        w_y, s_y = (tab_y[side, 0, y : y + 1], tab_y[side, 1, y : y + 1])
        sides.append((slope_part * w_y + weight_part * s_y, weight_x * w_y))
    rows = halves(jnp.concatenate([pair[0] for pair in sides], 0))
    flat = halves(jnp.concatenate([pair[1] for pair in sides], 0))
    return product(w_z, rows, NT) + product(s_z, flat, NT)


def spread_own_kernel(ordered, tab_x, tab_y, w_high, w_low, slope_z, out):
    out[...] = spread_part(0, ordered[:, : tab_x.shape[3]], tab_x, tab_y, w_high, w_low, slope_z)


def put_lanes(out, flat):
    for row in range(8):
        out[:, row, :] = flat[:, row * TILE : (row + 1) * TILE]


def get_lanes(grid):
    return jnp.concatenate([grid[:, row, :] for row in range(8)], 1)


def spread_both_kernel(shift, ordered, mine, tab_x, tab_y, w_high, w_low, slope_z, out, flat, message, sems):
    theirs = spread_part(1, ordered[:, : tab_x.shape[3]], tab_x, tab_y, w_high, w_low, slope_z)
    ours = mine[...]
    width = ours.shape[1]
    even = lax.axis_index("core") == 0
    lower = jnp.where(even, ours, theirs)
    upper = jnp.where(even, theirs, ours)
    flat[:, :shift] = lower[:, :shift]
    flat[:, shift:width] = lower[:, shift:] + upper[:, : width - shift]
    flat[:, width : width + shift] = upper[:, width - shift :]
    flat[:, width + shift :] = jnp.zeros((flat.shape[0], flat.shape[1] - width - shift), F32)
    pieces = sems.shape[0]
    size = flat.shape[0] // pieces
    copies = []
    for piece in range(pieces):
        rows = slice(piece * size, (piece + 1) * size)
        for row in range(8):
            message[rows, row, :] = flat[rows, row * TILE : (row + 1) * TILE]
        copies.append(pltpu.make_async_copy(message.at[rows], out.at[rows], sems.at[piece]))
        copies[-1].start()
    for copy in copies:
        copy.wait()


def factor_of(waves, freq_z):
    ids_x = lax.broadcasted_iota(jnp.int32, (1, G), 1)
    by_x = waves[...]
    by_z = jnp.sum(jnp.where(ids_x == freq_z, by_x, 0.0), axis=1, keepdims=True)
    by_y = by_x.T
    anchor = jnp.where(
        (lax.broadcasted_iota(jnp.int32, (G, G), 0) + lax.broadcasted_iota(jnp.int32, (G, G), 1) + freq_z) == 0, 1.0, 0.0
    )
    squares = by_x[0:1] + by_y[:, 0:1] + (by_z[0:1] + anchor)
    return (1.0 - anchor) * (by_x[1:2] * by_z[1:2]) * by_y[:, 1:2] / (math.pi * float(G) ** 3 * squares)


def plane_kernel(shapes, waves, sums, *refs):
    stored, out, flat, padded = (refs[:7], refs[7], refs[8], refs[9])
    held, sems = (refs[10:17], refs[17])
    copies = [
        pltpu.make_async_copy(source, target, sems.at[at])
        for at, (source, target) in enumerate(zip(stored, held))
    ]
    for copy in copies:
        copy.start()
    grid, x_high, x_low, yt_high, yt_low, y_high, y_low = held
    n_slab, n_pair, x_rows, y_rows = shapes
    width = x_rows * y_rows
    freq_z = lax.axis_index("slab") * (2 * n_pair) + 2 * lax.axis_index("pair") + lax.axis_index("core")
    factor = factor_of(waves, freq_z)
    copies[0].wait()
    flat[...] = get_lanes(grid)
    padded[...] = jnp.zeros(padded.shape, F32)
    for s in range(n_slab):
        for y in range(y_rows):
            padded[y * n_pair : (y + 1) * n_pair, s * TILE : s * TILE + x_rows] = flat[
                s * n_pair : (s + 1) * n_pair, y * x_rows : (y + 1) * x_rows
            ]
    for copy in copies[1:]:
        copy.wait()
    cas_x = (x_high[...], x_low[...])
    along_x = product(halves(padded[...]), cas_x, NN, False)
    spectrum = product((yt_high[...], yt_low[...]), halves(along_x), NN, False)
    scaled = spectrum * factor
    energy = jnp.sum(jnp.sum(spectrum * scaled, axis=0, keepdims=True), axis=1, keepdims=True)
    back = halves(product((y_high[...], y_low[...]), halves(scaled), NN, False))
    planes = product(back, cas_x, NT, False)
    for s in range(n_slab):
        for y in range(y_rows):
            flat[s * n_pair : (s + 1) * n_pair, y * x_rows : (y + 1) * x_rows] = planes[
                y * n_pair : (y + 1) * n_pair, s * TILE : s * TILE + x_rows
            ]
    spare = flat.shape[1] - width
    lane = lax.broadcasted_iota(jnp.int32, (1, spare), 1)
    known = jnp.concatenate([sums[0:1], jnp.zeros((1, spare - TILE), F32)], 1)
    tail = jnp.where(lane == 0, energy, known)
    flat[:, width:] = jnp.broadcast_to(tail, (flat.shape[0], spare))
    put_lanes(out, flat)


def probe_part(side, planes, tab_x, tab_y, w_high, w_low, slope_z):
    x_rows = tab_x.shape[2]
    by_weight = product(planes, (w_high[side], w_low[side]), TN)
    by_slope = product(planes, halves(slope_z[side]), TN)
    weight_x, slope_x = (tab_x[side, 0], tab_x[side, 1])
    fields = [0.0, 0.0, 0.0]
    for y in range(tab_y.shape[2]):
        rows = slice(y * x_rows, (y + 1) * x_rows)
        w_y, s_y = (tab_y[side, 0, y : y + 1], tab_y[side, 1, y : y + 1])
        weighted = by_weight[rows]
        fields[0] += w_y * jnp.sum(slope_x * weighted, axis=0, keepdims=True)
        fields[1] += s_y * jnp.sum(weight_x * weighted, axis=0, keepdims=True)
        fields[2] += w_y * jnp.sum(weight_x * by_slope[rows], axis=0, keepdims=True)
    return fields


def probe_kernel(side, shift, grid, tab_x, tab_y, w_high, w_low, slope_z, out):
    matrix = get_lanes(grid)
    width = tab_x.shape[2] * tab_y.shape[2]
    low_side = 0 if side == 0 else 1
    planes = jnp.where(
        lax.axis_index("core") == low_side, matrix[:, :width], matrix[:, shift : shift + width]
    )
    fields = probe_part(side, halves(planes), tab_x, tab_y, w_high, w_low, slope_z)
    atoms = out.shape[1]
    scalars = jnp.sum(matrix[:, width + shift :], axis=0, keepdims=True)[:, :TILE]
    padded = jnp.concatenate([scalars, jnp.zeros((1, atoms - TILE), F32)], 1)
    out[...] = jnp.concatenate(fields + [padded, jnp.zeros((4, atoms), F32)], 0)


def finish_kernel(mine, theirs, ordered, applied, dipoles, residual, next_dipoles, next_residual, direction):
    total = mine[...] + theirs[...]
    step = total[3:4, 2:3] / (total[3:4, 0:1] + total[3:4, 1:2])
    d = ordered[0:3, : dipoles.shape[1]]
    next_dipoles[...] = dipoles[...] + step * d
    next_residual[...] = residual[...] - step * (applied[0:3] + total[0:3])
    direction[...] = d


def cas_matrix(first, second):
    angles = 2.0 * np.pi / G * (np.outer(first, second) % G)
    return np.cos(angles) + np.sin(angles)


def split_constant(values):
    whole = values.astype(np.float32)
    high = whole.astype(ml_dtypes.bfloat16)
    low = (values - high.astype(np.float64)).astype(ml_dtypes.bfloat16)
    return (jnp.asarray(high), jnp.asarray(low))


def wave_factors():
    freq = np.arange(G)
    wrapped = np.where(freq > G // 2, freq - G, freq) / G
    angles = 2.0 * np.pi / G * freq
    modulus = 115.0 / 192.0 + 19.0 / 48.0 * np.cos(angles) + 1.0 / 192.0 * np.cos(2.0 * angles)
    rows = np.zeros((8, G), np.float32)
    rows[0] = wrapped * wrapped
    rows[1] = np.exp(-((np.pi / BETA) ** 2) * wrapped * wrapped) / (modulus * modulus)
    return jnp.asarray(rows)


def swap_pairs(n_slab, n_space, odd):
    pairs = []
    for s in range(n_slab):
        for q in range(n_space):
            partner = (q + 1 if (q % 2 == 1) == odd else q - 1) % n_space
            pairs.append((s * n_space + q, s * n_space + partner))
    return pairs


def beside(block, odd):
    n_slab, n_space = (lax.axis_size("slab"), lax.axis_size(SPACE))
    return lax.ppermute(block, BOTH, swap_pairs(n_slab, n_space, odd))


def along_slab(level):
    n_slab = lax.axis_size("slab")
    up = [(i, (i + 1) % n_slab) for i in range(n_slab)]
    down = [(j, i) for i, j in up]
    return (level, lax.ppermute(level, "slab", up), lax.ppermute(level, "slab", down))


def joined(block, inner, outer):
    return call(join_kernel, [((3, 2, 8, TILE), F32)], 10**6)(block, inner, outer)[0]


def around(block, bundle=None, beneath=None):
    inner = beside(block if bundle is None else bundle, False)
    outer, _ = lax.optimization_barrier((beside(block, True), beneath))
    return along_slab(joined(block, inner, outer)), inner


def local(
    dipoles, residual, cells, fraction, polarizability, tile_order, send_tiles, tile_lists, tile_counts
):
    n_slab, n_space = (lax.axis_size("slab"), lax.axis_size(SPACE))
    n_pair = n_space // 2
    atoms = residual.shape[1]
    extents = (G // n_slab, G // n_space)
    x_rows = -(-(extents[0] + 4) // 8) * 8
    y_rows = extents[1] + 4
    pair_rows = 2 * extents[1] + 4
    shift = extents[1] * x_rows
    half = G // 2
    tile_shape = ((4, 8, TILE), F32)
    two_shape = ((2, 8, TILE), F32)
    one_bank = ((3, 8, TILE, TILE), F32)
    pool_scratch = pltpu.VMEM((22, 8, TILE), F32)
    total_scratch = pltpu.VMEM((3, TILE, TILE), F32)
    own, sent, statics = pl.pallas_call(
        gather_kernel,
        out_shape=[
            jax.ShapeDtypeStruct(*tile_shape),
            jax.ShapeDtypeStruct(*two_shape),
            jax.ShapeDtypeStruct((8, atoms + 2 * TILE), F32),
        ],
        in_specs=[pl.BlockSpec(memory_space=pltpu.HBM)] * 6,
        out_specs=[pl.BlockSpec(memory_space=pltpu.VMEM)] * 3,
        scratch_shapes=[
            pltpu.VMEM((3, atoms), F32),
            pltpu.VMEM((3, atoms), jnp.int32),
            pltpu.VMEM((3, atoms), F32),
            pltpu.VMEM((atoms,), F32),
            pltpu.VMEM((1, atoms), jnp.int32),
            pltpu.SMEM((1, 2), jnp.int32),
            pltpu.SemaphoreType.DMA((6,)),
        ],
        compiler_params=pltpu.CompilerParams(vmem_limit_bytes=SMALL_VMEM),
    )(
        *[
            pltpu.with_memory_space_constraint(array, pltpu.HBM)
            for array in (residual, cells, fraction, polarizability, tile_order, send_tiles)
        ],
    )
    smem, anywhere = (pl.BlockSpec(memory_space=pltpu.SMEM), pl.BlockSpec(memory_space=pltpu.HBM))
    meta = pl.pallas_call(
        meta_kernel,
        out_shape=jax.ShapeDtypeStruct((48,), jnp.int32),
        in_specs=[smem, smem, smem, pl.BlockSpec(memory_space=pltpu.VMEM)],
        out_specs=smem,
        compiler_params=pltpu.CompilerParams(vmem_limit_bytes=SMALL_VMEM),
        cost_estimate=pl.CostEstimate(flops=10**8, bytes_accessed=1 << 20, transcendentals=0),
    )(tile_lists, tile_counts, send_tiles, sent)
    first, statics_beside = around(sent, statics, beneath=meta)

    freq = np.arange(G)
    padded_x = np.stack([(s * extents[0] + np.arange(x_rows) - 2) % G for s in range(n_slab)])
    real_x = np.tile(np.arange(x_rows) < extents[0] + 4, n_slab)
    cas_x = cas_matrix(padded_x.reshape(-1), freq) * real_x[:, None]
    rows_y = (np.arange(n_pair)[None] * 2 * extents[1] + np.arange(pair_rows)[:, None] - 2) % G
    cas_y = cas_matrix(rows_y.reshape(-1), freq)
    freq_by_core = np.stack([freq[0::2], freq[1::2]])
    cas_z = cas_matrix(freq_by_core.reshape(-1), freq).reshape(2, half, G)
    wide_x = np.zeros((n_slab, TILE, G))
    wide_x[:, :x_rows] = cas_x.reshape(n_slab, x_rows, G)
    def pairs_of(place, count):
        return call(
            functools.partial(pair_kernel, place, count, extents),
            [((22, 8, TILE), F32), ((3, 8 * count, TILE, TILE), F32), ((count, 8, TILE), F32)],
            10**9,
            smem=1,
            scratch=(pltpu.VMEM((4, TILE, TILE), F32), total_scratch),
        )(meta, own, *first)

    geometry, pairs_a, search_a = pairs_of(0, 2)
    _, pairs_b, search_b = pairs_of(2, 1)
    _, pairs_c, search_c = pairs_of(3, 1)
    sweep_scratch = (pool_scratch, pltpu.VMEM((3, TILE, TILE), F32), total_scratch)
    second, _ = around(search_a, beneath=search_b)

    def sweep(place, owns, received, banks):
        return call(
            functools.partial(sweep_kernel, place, len(owns)),
            [two_shape],
            10**8,
            smem=1,
            scratch=sweep_scratch,
        )(meta, geometry, *owns, *received, *banks)[0]

    searches = (search_a, search_b, search_c)
    next_a = sweep(0, searches, second, (pairs_a,))
    next_b = sweep(2, searches, second, (pairs_b, pairs_c))
    third, _ = around(next_a, beneath=next_b)
    statics_beside, _ = lax.optimization_barrier((statics_beside, third[0]))
    tables = call(
        tables_kernel,
        [
            ((2, 2, x_rows, atoms), F32),
            ((2, 2, y_rows, atoms), F32),
            ((2, half, atoms), BF16),
            ((2, half, atoms), BF16),
            ((2, half, atoms), F32),
        ],
        10**8,
        vmem=LARGE_VMEM,
        scratch=(pltpu.VMEM((half, G), BF16),) * 2 + (pltpu.SemaphoreType.DMA((2,)),),
        hbm=2,
    )(statics, statics_beside, *split_constant(cas_z))
    level, before, after = third
    after, _ = lax.optimization_barrier((after, tables[1]))
    third = (level, before, after)
    local_scratch = pltpu.VMEM((4, 8, TILE), F32)
    sent = sweep(0, (next_a, next_b), third, (pairs_a,))
    outer = beside(sent, True)
    rest, ordered = call(
        direction_kernel,
        [two_shape, ((8, atoms + 2 * TILE), F32)],
        10**8,
        smem=1,
        scratch=sweep_scratch + (local_scratch,),
    )(meta, geometry, next_a, next_b, *third, sent, pairs_b, pairs_c, tile_order)
    ordered_beside = beside(ordered, False)
    message = ((half, 8, TILE), F32)
    flat_scratch = pltpu.VMEM((half, 8 * TILE), F32)
    spread_own = call(spread_own_kernel, [((half, x_rows * y_rows), F32)], 10**9, vmem=LARGE_VMEM)(ordered, *tables)[0]
    spread = call(
        functools.partial(spread_both_kernel, shift),
        [message],
        10**9,
        scratch=(flat_scratch, pltpu.VMEM(*message), pltpu.SemaphoreType.DMA((4,))),
        vmem=LARGE_VMEM,
        hbm_outs=True,
    )(ordered_beside, spread_own, *tables)[0]
    spread, outer = lax.optimization_barrier((spread, outer))
    grid = lax.all_to_all(spread, CHIPS, 0, 0, tiled=True)
    last = along_slab(joined(sent, ordered_beside, outer))
    applied, sums = call(
        final_field_kernel,
        [((8, atoms), F32), ((8, TILE), F32)],
        10**9,
        smem=1,
        scratch=sweep_scratch
        + (local_scratch, pltpu.VMEM(*one_bank), pltpu.VMEM(*one_bank), pltpu.SemaphoreType.DMA((2,))),
        vmem=LARGE_VMEM,
        hbm=2,
    )(meta, geometry, sent, rest, *last, pairs_a, tile_order, pairs_b, pairs_c)
    planes = call(
        functools.partial(plane_kernel, (n_slab, n_pair, x_rows, pair_rows)),
        [message],
        10**9,
        scratch=(flat_scratch, pltpu.VMEM((n_pair * pair_rows, n_slab * TILE), F32), pltpu.VMEM(*message))
        + (pltpu.VMEM((n_slab * TILE, G), BF16),) * 2
        + (pltpu.VMEM((G, n_pair * pair_rows), BF16),) * 2
        + (pltpu.VMEM((n_pair * pair_rows, G), BF16),) * 2
        + (pltpu.SemaphoreType.DMA((7,)),),
        vmem=LARGE_VMEM,
        hbm=7,
    )(
        wave_factors(),
        sums,
        grid,
        *split_constant(wide_x.reshape(-1, G)),
        *split_constant(cas_y.T),
        *split_constant(cas_y),
    )[0]
    returned = lax.all_to_all(planes, CHIPS, 0, 0, tiled=True)

    def probe(side):
        return call(
            functools.partial(probe_kernel, side, shift), [((8, atoms), F32)], 10**9, vmem=LARGE_VMEM
        )(returned, *tables)[0]

    theirs = beside(probe(1), False)
    three = ((3, atoms), F32)
    return tuple(
        call(finish_kernel, [three, three, three], 10**6)(
            probe(0), theirs, ordered, applied, dipoles, residual
        )
    )


def solution(mesh):
    slab, space = (mesh.shape["slab"], mesh.shape["space"])
    mesh = Mesh(mesh.devices.reshape(slab, space // 2, 2), BOTH)
    in_specs = (
        P(None, BOTH),
        P(None, BOTH),
        P(None, BOTH),
        P(None, BOTH),
        P(BOTH),
        P(BOTH, None),
        P(BOTH, None),
        P(BOTH, None, None),
        P(BOTH, None),
    )
    out_specs = (P(None, BOTH), P(None, BOTH), P(None, BOTH))
    return jax.shard_map(local, mesh=mesh, in_specs=in_specs, out_specs=out_specs, check_vma=False)
```
